32 devices in a mesh: seg: 8 (over z, core), seq: 4 (over y, x).
Axes of the slice: x: 2, y: 2, z: 4, core: 2. Of those that a mesh axis runs over, the one named last changes fastest.
Arguments:
- layer_input: bfloat16 [8, 2048, 1024], P('seg', 'seq'), may hold values from -6 to 6
- output_grad: bfloat16 [8, 2048, 1024], P('seg', 'seq'), may hold values from -6 to 6
- norm1_gain: float32 [1024], replicated, may hold values from 0.5 to 1.5
- norm2_gain: float32 [1024], replicated, may hold values from 0.5 to 1.5
- w_qkv: bfloat16 [1024, 3072], replicated, may hold values from -0.25 to 0.25
- w_out: bfloat16 [1024, 1024], replicated, may hold values from -0.75 to 0.75
- w_gate: bfloat16 [1024, 2816], replicated, may hold values from -0.1875 to 0.1875
- w_up: bfloat16 [1024, 2816], replicated, may hold values from -0.1875 to 0.1875
- w_down: bfloat16 [2816, 1024], replicated, may hold values from -0.109375 to 0.109375
- mem_keys: bfloat16 [8, 1024, 1024], P('seg', 'seq'), may hold values from -8 to 8
- mem_values: bfloat16 [8, 1024, 1024], P('seg', 'seq'), may hold values from -8 to 8
- memory_flags: int32 [8], replicated, may hold values from 0 to 1, as said below
- sources: int32 [8, 3], replicated, may hold values from 0 to 7, as said below
Outputs:
- output: bfloat16 [8, 2048, 1024], P('seg', 'seq')
- input_grad: float32 [8, 2048, 1024], P('seg', 'seq')
- grad_norm1: float32 [1024], P('seq')
- grad_norm2: float32 [1024], P('seq')
- grad_qkv: float32 [1024, 3072], P('seq')
- grad_out: float32 [1024, 1024], P('seq')
- grad_gate: float32 [1024, 2816], P('seq')
- grad_up: float32 [1024, 2816], P('seq')
- grad_down: float32 [2816, 1024], P('seq')
The draws below stay inside these ranges and needn't reach their ends.
Inputs may be any that keep to these rules, and one draw needn't show every extreme that they name: `memory_flags`: exactly half of the segments have flag 1. `sources`: row s lists 3 different segments, none of them s. The first column is a permutation of the segments, and the first source of a segment has the other flag than the segment.
All inputs are finite; a program needn't handle non-finite values.
Results may differ from the reference program's by a relative error of at most 0.023.
Values may be sent and summed in bfloat16 or wider, within the bound.
A program may use at most 256 MiB of HBM per device.

```python
import jax
import jax.numpy as jnp
from jax import lax

D = 1024
HEADS = 8
HEAD_DIM = 128
FF = 2816
MEM_SEG = 1024
CROSS = 3
LEN = 2048
SEGS = 8
MEM = 4096


def segment_cycle(key):
    order = jax.random.permutation(jax.random.fold_in(key, 17), SEGS).astype(jnp.int32)
    following = jnp.zeros((SEGS,), jnp.int32).at[order].set(jnp.roll(order, -1))
    parity = (jnp.arange(SEGS, dtype=jnp.int32) % 2 == 0).astype(jnp.int32)
    flagged = jnp.zeros((SEGS,), jnp.int32).at[order].set(parity)
    return (following, flagged)


def draw_memory_flags(key, part):
    following, flagged = segment_cycle(key)
    return flagged


def draw_sources(key, part):
    following, flagged = segment_cycle(key)
    own_ids = jnp.arange(SEGS, dtype=jnp.int32)
    candidates = jnp.arange(SEGS, dtype=jnp.int32)[None, :]
    scores = jax.random.randint(jax.random.fold_in(key, 29), (SEGS, SEGS), 0, 1 << 20) * SEGS + candidates
    banned = (candidates == own_ids[:, None]) | (candidates == following[:, None])
    scores = jnp.where(banned, -1 - candidates, scores)
    extra_scores, extra_ids = lax.top_k(scores, CROSS - 1)
    return jnp.concatenate([following[:, None], extra_ids.astype(jnp.int32)], axis=1)


def shard_levels(own_key, extent, shards, smallest, top_value):
    def one(dim, parts):
        draws = jax.random.uniform(jax.random.fold_in(jax.random.fold_in(own_key, 6), dim), (parts,), jnp.float32, smallest / len(shards), top_value / len(shards))
        return jnp.repeat(jnp.exp(draws), extent[dim] // parts).reshape((-1,) + (1,) * (len(extent) - dim - 1))

    gain = one(*shards[0])
    for cut in shards[1:]:
        gain = gain * one(*cut)
    return gain


def gaussian(rng, extent, deviation, limit, cuts=(), kind=jnp.bfloat16):
    values = deviation * jax.random.normal(rng, extent, jnp.float32)
    if cuts:
        values = values * shard_levels(rng, extent, cuts, -0.22, 0.18)
    return jnp.clip(values, -limit, limit).astype(kind)


def setup_inputs(seed: int = 0) -> dict:
    arg_keys = jax.random.split(jax.random.key(seed), 14)
    layer_input = gaussian(arg_keys[0], (SEGS, LEN, D), 1.0, 6.0, ((0, 8), (1, 4)))
    output_grad = gaussian(arg_keys[1], (SEGS, LEN, D), 1.0, 6.0, ((0, 8), (1, 4)))
    norm1_gain = jnp.clip(1.0 + 0.1 * jax.random.normal(arg_keys[2], (D,), jnp.float32), 0.5, 1.5)
    norm2_gain = jnp.clip(1.0 + 0.1 * jax.random.normal(arg_keys[3], (D,), jnp.float32), 0.5, 1.5)
    w_qkv = gaussian(arg_keys[4], (D, 3 * D), (D // 2) ** -0.5, 0.25)
    w_out = gaussian(arg_keys[5], (D, D), (D // 16) ** -0.5, 0.75)
    w_gate = gaussian(arg_keys[6], (D, FF), D ** -0.5, 0.1875)
    w_up = gaussian(arg_keys[7], (D, FF), D ** -0.5, 0.1875)
    w_down = gaussian(arg_keys[8], (FF, D), FF ** -0.5, 0.109375)
    mem_keys = gaussian(arg_keys[9], (SEGS, MEM_SEG, D), 1.4, 8.0, ((0, 8), (1, 4)))
    mem_values = gaussian(arg_keys[10], (SEGS, MEM_SEG, D), 1.4, 8.0, ((0, 8), (1, 4)))
    memory_flags = draw_memory_flags(jax.random.fold_in(arg_keys[13], 71), 0)
    sources = draw_sources(jax.random.fold_in(arg_keys[13], 71), 0)
    return dict(layer_input=layer_input, output_grad=output_grad, norm1_gain=norm1_gain, norm2_gain=norm2_gain, w_qkv=w_qkv, w_out=w_out, w_gate=w_gate, w_up=w_up, w_down=w_down, mem_keys=mem_keys, mem_values=mem_values, memory_flags=memory_flags, sources=sources)


precise = lax.Precision.HIGHEST
masked_score = -1e+30
epsilon = 1e-06
rotary_base = 10000.0

@jax.custom_vjp
def low(v):
    return lax.optimization_barrier(v.astype(jnp.bfloat16)).astype(jnp.float32)

@jax.custom_vjp
def low_back(v):
    return v

def low_keep(v):
    return (low(v), None)

def low_pass(kept, grad):
    return (grad,)

def back_keep(v):
    return (v, None)

def back_low(kept, grad):
    return (low(grad),)
low.defvjp(low_keep, low_pass)
low_back.defvjp(back_keep, back_low)

def rms_norm(values, norm_gain):
    return values * lax.rsqrt(lax.optimization_barrier(jnp.mean(values * values, axis=-1, keepdims=True)) + epsilon) * norm_gain

def rotary(shaped, positions):
    half_dim = HEAD_DIM // 2
    exponent = -2.0 * jnp.arange(half_dim, dtype=jnp.float32) / HEAD_DIM
    angles = positions[:, None] * jnp.power(rotary_base, exponent)[None, :]
    angles = jnp.concatenate([angles, angles], axis=1)[:, None, :]
    turned = jnp.concatenate([-shaped[..., half_dim:], shaped[..., :half_dim]], axis=-1)
    return shaped * jnp.cos(angles) + turned * jnp.sin(angles)

def matmul(former, latter):
    return jnp.dot(former, latter, precision=precise)

def layer(inputs, norm1_gain, norm2_gain, w_qkv, w_out, w_gate, w_up, w_down, memory_keys, memory_values, flag):
    positions = jnp.arange(LEN).astype(jnp.float32)
    first_low = low(rms_norm(inputs, norm1_gain))
    projected = low_back(matmul(first_low, w_qkv))
    queries = low(rotary(projected[:, :D].reshape(LEN, HEADS, HEAD_DIM), positions))
    own_keys = low(rotary(projected[:, D:2 * D].reshape(LEN, HEADS, HEAD_DIM), positions))
    own_values = low(projected[:, 2 * D:].reshape(LEN, HEADS, HEAD_DIM))
    block_rows = min(512, LEN)
    block_count = LEN // block_rows
    score_scale = HEAD_DIM ** (-0.5)
    key_positions = jnp.arange(LEN).astype(jnp.int32)

    def attend(operands):
        query_block, block_start = operands
        memory_scores = jnp.einsum('qhd,khd->hqk', query_block, memory_keys, precision=precise) * score_scale
        own_scores = jnp.einsum('qhd,khd->hqk', query_block, own_keys, precision=precise) * score_scale
        scores = low_back(jnp.concatenate([memory_scores, own_scores], axis=-1))
        query_positions = block_start + jnp.arange(block_rows).astype(jnp.int32)
        visible = key_positions[None, :] <= query_positions[:, None]
        memory_open = jnp.broadcast_to(flag > 0, (block_rows, MEM))
        allowed = jnp.concatenate([memory_open, visible], axis=1)
        scores = jnp.where(allowed[None], scores, masked_score)
        weights = low(jax.nn.softmax(scores, axis=-1))
        mixed_memory = jnp.einsum('hqk,khd->qhd', weights[:, :, :MEM], memory_values, precision=precise)
        return mixed_memory + jnp.einsum('hqk,khd->qhd', weights[:, :, MEM:], own_values, precision=precise)
    starts = (jnp.arange(block_count) * block_rows).astype(jnp.int32)
    attended = lax.map(jax.checkpoint(attend), (queries.reshape(block_count, block_rows, HEADS, HEAD_DIM), starts))
    attended = low(low_back(attended.reshape(LEN, D)))
    residual = inputs + low_back(matmul(attended, w_out))
    second_low = low(rms_norm(residual, norm2_gain))
    gate_values = low_back(matmul(second_low, w_gate))
    up_values = low_back(matmul(second_low, w_up))
    hidden = low(jax.nn.silu(gate_values) * up_values)
    return residual + low_back(matmul(hidden, w_down))

def reference(layer_input, output_grad, norm1_gain, norm2_gain, w_qkv, w_out, w_gate, w_up, w_down, mem_keys, mem_values, memory_flags, sources):
    weights = tuple((weight.astype(jnp.float32) for weight in (norm1_gain, norm2_gain, w_qkv, w_out, w_gate, w_up, w_down)))
    keys_float = mem_keys.astype(jnp.float32)
    values_float = mem_values.astype(jnp.float32)

    def segment(carry, operands):
        seg_input, seg_grad, flag, listed, seg_index = operands
        picked = jnp.concatenate([jnp.reshape(seg_index, (1,)), listed]).astype(jnp.int32)
        memory_keys = jnp.take(keys_float, picked, axis=0).reshape(MEM, HEADS, HEAD_DIM)
        memory_values = jnp.take(values_float, picked, axis=0).reshape(MEM, HEADS, HEAD_DIM)

        def forward(inputs, *params):
            return layer(inputs, *params, memory_keys, memory_values, flag)
        result, pullback = jax.vjp(forward, seg_input.astype(jnp.float32), *weights)
        gradients = pullback(seg_grad.astype(jnp.float32))
        carry = tuple((running + addend for running, addend in zip(carry, gradients[1:])))
        return (carry, (result.astype(jnp.bfloat16), gradients[0]))
    zero_grads = tuple((jnp.zeros(weight.shape, jnp.float32) for weight in weights))
    seg_ids = jnp.arange(SEGS).astype(jnp.int32)
    totals, (output, input_grad) = lax.scan(segment, zero_grads, (layer_input, output_grad, memory_flags, sources, seg_ids))
    return (output, input_grad, totals[0], totals[1], totals[2], totals[3], totals[4], totals[5], totals[6])
```

```python
import functools
import math

import jax
import jax.numpy as jnp
from jax import lax
from jax.experimental import pallas as pl
from jax.experimental.pallas import tpu as pltpu
from jax.sharding import PartitionSpec as P

D = 1024
HEADS = 8
HEAD_DIM = 128


masked_score = -1e30
epsilon = 1e-06
rotary_base = 10000.0


def product(former, latter):
    return jnp.dot(former, latter, preferred_element_type=jnp.float32)


def product_nt(former, latter):
    return lax.dot_general(
        former, latter, (((1,), (1,)), ((), ())), preferred_element_type=jnp.float32
    )


def product_tn(former, latter):
    return lax.dot_general(
        former, latter, (((0,), (0,)), ((), ())), preferred_element_type=jnp.float32
    )


def norm_forward(values, norm_gain):
    inverse = lax.rsqrt(jnp.mean(values * values, axis=-1, keepdims=True) + epsilon)
    return (values * inverse * norm_gain, inverse)


def norm_backward(values, inverse, norm_gain, upstream):
    weighted = upstream * norm_gain
    inner_mean = jnp.mean(weighted * values, axis=-1, keepdims=True)
    grad_values = inverse * weighted - inverse * inverse * inverse * values * inner_mean
    grad_gain = jnp.sum(upstream * values * inverse, axis=0)
    return (grad_values, grad_gain)


def turn_tables(positions):
    half_dim = HEAD_DIM // 2
    exponent = -2.0 * jnp.arange(half_dim, dtype=jnp.float32) / HEAD_DIM
    angles = positions[:, None] * jnp.power(rotary_base, exponent)[None, :]
    angles = jnp.concatenate([angles, angles], axis=1)
    return (jnp.cos(angles)[:, None, :], jnp.sin(angles)[:, None, :])


def rotate(matrix, cosine_table, sine_table, direction):
    row_count = matrix.shape[0]
    half_dim = HEAD_DIM // 2
    shaped = matrix.reshape(row_count, HEADS, HEAD_DIM)
    turned = jnp.concatenate([-shaped[..., half_dim:], shaped[..., :half_dim]], axis=-1)
    return (shaped * cosine_table + direction * turned * sine_table).reshape(
        row_count, HEADS * HEAD_DIM
    )


def general_plan(
    layer_input,
    output_grad,
    norm1_gain,
    norm2_gain,
    w_qkv,
    w_out,
    w_gate,
    w_up,
    w_down,
    mem_keys,
    mem_values,
    memory_flags,
    sources,
):
    seg_index = lax.axis_index("seg")
    seq_index = lax.axis_index("seq")
    tokens = layer_input.shape[1]
    score_scale = HEAD_DIM ** (-0.5)
    flag_on = lax.dynamic_index_in_dim(memory_flags, seg_index, 0, keepdims=False) > 0
    listed = lax.dynamic_index_in_dim(sources, seg_index, 0, keepdims=False)
    picked = jnp.concatenate([jnp.reshape(seg_index, (1,)), listed])
    every_keys, every_values = (
        lax.all_gather(mem_keys, "seg", axis=0, tiled=True),
        lax.all_gather(mem_values, "seg", axis=0, tiled=True),
    )
    chosen_keys = jnp.take(every_keys, picked, axis=0)
    chosen_values = jnp.take(every_values, picked, axis=0)
    memory_keys, memory_values = (
        lax.all_gather(chosen_keys, "seq", axis=1, tiled=True),
        lax.all_gather(chosen_values, "seq", axis=1, tiled=True),
    )
    memory_key_blocks = memory_keys.reshape(-1, tokens, HEADS, HEAD_DIM)
    memory_value_blocks = memory_values.reshape(-1, tokens, HEADS, HEAD_DIM)
    memory_blocks = memory_key_blocks.shape[0]
    inputs = layer_input[0].astype(jnp.float32)
    first_norm, first_inverse = norm_forward(inputs, norm1_gain)
    first_low = first_norm.astype(jnp.bfloat16)
    projected = product(first_low, w_qkv)
    positions = seq_index * tokens + lax.iota(jnp.int32, tokens)
    cosine_table, sine_table = turn_tables(positions.astype(jnp.float32))
    queries = rotate(projected[:, :D], cosine_table, sine_table, 1.0).astype(jnp.bfloat16)
    own_keys = rotate(projected[:, D : 2 * D], cosine_table, sine_table, 1.0).astype(jnp.bfloat16)
    own_values = projected[:, 2 * D :].astype(jnp.bfloat16)
    all_keys, all_values = (
        lax.all_gather(own_keys, "seq", axis=0, tiled=True),
        lax.all_gather(own_values, "seq", axis=0, tiled=True),
    )
    key_blocks = all_keys.reshape(-1, tokens, HEADS, HEAD_DIM)
    value_blocks = all_values.reshape(-1, tokens, HEADS, HEAD_DIM)
    query_heads = queries.reshape(tokens, HEADS, HEAD_DIM)
    memory_open = jnp.broadcast_to(flag_on, (tokens, tokens))
    own_count = seq_index + 1
    key_offsets = lax.iota(jnp.int32, tokens)

    def own_open(block):
        return (block * tokens + key_offsets)[None, :] <= positions[:, None]

    def block_scores(key_block, open_mask):
        raw = (
            jnp.einsum("qhd,khd->hqk", query_heads, key_block, preferred_element_type=jnp.float32)
            * score_scale
        )
        return jnp.where(open_mask[None], raw, masked_score)

    def sweep(step, carry):

        def memory_turn(block, state):
            return step(
                state,
                block,
                memory_key_blocks[block],
                memory_value_blocks[block],
                memory_open,
                False,
            )

        def own_turn(block, state):
            return step(state, block, key_blocks[block], value_blocks[block], own_open(block), True)

        carry = lax.fori_loop(0, memory_blocks, memory_turn, carry)
        return lax.fori_loop(0, own_count, own_turn, carry)

    def max_step(carry, block, key_block, value_block, open_mask, own):
        row_max, row_sum = carry
        scores = block_scores(key_block, open_mask)
        new_max = jnp.maximum(row_max, jnp.max(scores, axis=2))
        row_sum = row_sum * jnp.exp(row_max - new_max) + jnp.sum(
            jnp.exp(scores - new_max[..., None]), axis=2
        )
        return (new_max, row_sum)

    start_max = jnp.full((HEADS, tokens), masked_score, jnp.float32)
    row_max, row_sum = sweep(max_step, (start_max, jnp.zeros((HEADS, tokens), jnp.float32)))
    log_totals = row_max + jnp.log(row_sum)

    def mix_step(total, block, key_block, value_block, open_mask, own):
        weights_low = jnp.exp(block_scores(key_block, open_mask) - log_totals[..., None]).astype(
            jnp.bfloat16
        )
        return total + jnp.einsum(
            "hqk,khd->qhd", weights_low, value_block, preferred_element_type=jnp.float32
        )

    attended = sweep(mix_step, jnp.zeros((tokens, HEADS, HEAD_DIM), jnp.float32))
    attended_low = attended.reshape(tokens, D).astype(jnp.bfloat16)
    residual = inputs + product(attended_low, w_out)
    second_norm, second_inverse = norm_forward(residual, norm2_gain)
    second_low = second_norm.astype(jnp.bfloat16)
    gate_values = product(second_low, w_gate)
    up_values = product(second_low, w_up)
    sigmoid_gate = jax.nn.sigmoid(gate_values)
    activated = gate_values * sigmoid_gate
    hidden_low = (activated * up_values).astype(jnp.bfloat16)
    output = (residual + product(hidden_low, w_down)).astype(jnp.bfloat16)
    upstream = output_grad[0]
    grad_down = product_tn(hidden_low, upstream)
    grad_hidden = product_nt(upstream, w_down)
    grad_gate_low = (
        grad_hidden * up_values * sigmoid_gate * (1.0 + gate_values * (1.0 - sigmoid_gate))
    ).astype(jnp.bfloat16)
    grad_up_low = (grad_hidden * activated).astype(jnp.bfloat16)
    grad_gate = product_tn(second_low, grad_gate_low)
    grad_up = product_tn(second_low, grad_up_low)
    grad_second = product_nt(grad_gate_low, w_gate) + product_nt(grad_up_low, w_up)
    grad_residual, grad_norm2 = norm_backward(residual, second_inverse, norm2_gain, grad_second)
    grad_residual = grad_residual + upstream.astype(jnp.float32)
    residual_low = grad_residual.astype(jnp.bfloat16)
    grad_out = product_tn(attended_low, residual_low)
    grad_attended = product_nt(residual_low, w_out).astype(jnp.bfloat16)
    grad_heads = grad_attended.reshape(tokens, HEADS, HEAD_DIM)

    def probs_pair(key_block, value_block, open_mask):
        probs = jnp.exp(block_scores(key_block, open_mask) - log_totals[..., None])
        dprobs = jnp.einsum(
            "qhd,khd->hqk", grad_heads, value_block, preferred_element_type=jnp.float32
        )
        return (probs, dprobs)

    def delta_step(total, block, key_block, value_block, open_mask, own):
        probs, dprobs = probs_pair(key_block, value_block, open_mask)
        return total + jnp.sum(probs * dprobs, axis=2)

    delta_rows = sweep(delta_step, jnp.zeros((HEADS, tokens), jnp.float32))

    def grad_step(carry, block, key_block, value_block, open_mask, own):
        grad_query, key_terms, value_terms = carry
        probs, dprobs = probs_pair(key_block, value_block, open_mask)
        dscores = (probs * (dprobs - delta_rows[..., None])).astype(jnp.bfloat16)
        grad_query = grad_query + jnp.einsum(
            "hqk,khd->qhd", dscores, key_block, preferred_element_type=jnp.float32
        )
        if own:
            key_part = (
                jnp.einsum("hqk,qhd->khd", dscores, query_heads, preferred_element_type=jnp.float32)
                * score_scale
            )
            value_part = jnp.einsum(
                "hqk,qhd->khd",
                probs.astype(jnp.bfloat16),
                grad_heads,
                preferred_element_type=jnp.float32,
            )
            key_terms = lax.dynamic_update_index_in_dim(key_terms, key_part, block, 0)
            value_terms = lax.dynamic_update_index_in_dim(value_terms, value_part, block, 0)
        return (grad_query, key_terms, value_terms)

    term_shape = key_blocks.shape
    start_grads = (
        jnp.zeros((tokens, HEADS, HEAD_DIM), jnp.float32),
        jnp.zeros(term_shape, jnp.float32),
        jnp.zeros(term_shape, jnp.float32),
    )
    grad_query, key_terms, value_terms = sweep(grad_step, start_grads)
    grad_queries = (grad_query * score_scale).reshape(tokens, D)
    grad_keys, grad_values = (
        lax.psum_scatter(
            key_terms.astype(jnp.bfloat16), "seq", scatter_dimension=0, tiled=True
        ).astype(jnp.float32),
        lax.psum_scatter(
            value_terms.astype(jnp.bfloat16), "seq", scatter_dimension=0, tiled=True
        ).astype(jnp.float32),
    )
    grad_projected = jnp.concatenate(
        [
            rotate(grad_queries, cosine_table, sine_table, -1.0),
            rotate(grad_keys.reshape(tokens, D), cosine_table, sine_table, -1.0),
            grad_values.reshape(tokens, D),
        ],
        axis=1,
    ).astype(jnp.bfloat16)
    grad_qkv = product_tn(first_low, grad_projected)
    grad_first = product_nt(grad_projected, w_qkv)
    grad_inputs, grad_norm1 = norm_backward(inputs, first_inverse, norm1_gain, grad_first)
    input_grad = (grad_inputs + grad_residual)[None]
    shares = (
        lax.psum_scatter(
            grad_norm1.astype(jnp.bfloat16), "seq", scatter_dimension=0, tiled=True
        ).astype(jnp.float32),
        lax.psum_scatter(
            grad_norm2.astype(jnp.bfloat16), "seq", scatter_dimension=0, tiled=True
        ).astype(jnp.float32),
        lax.psum_scatter(
            grad_qkv.astype(jnp.bfloat16), "seq", scatter_dimension=0, tiled=True
        ).astype(jnp.float32),
        lax.psum_scatter(
            grad_out.astype(jnp.bfloat16), "seq", scatter_dimension=0, tiled=True
        ).astype(jnp.float32),
        lax.psum_scatter(
            grad_gate.astype(jnp.bfloat16), "seq", scatter_dimension=0, tiled=True
        ).astype(jnp.float32),
        lax.psum_scatter(
            grad_up.astype(jnp.bfloat16), "seq", scatter_dimension=0, tiled=True
        ).astype(jnp.float32),
        lax.psum_scatter(
            grad_down.astype(jnp.bfloat16), "seq", scatter_dimension=0, tiled=True
        ).astype(jnp.float32),
    )
    totals = (
        lax.psum(shares[0].astype(jnp.bfloat16), "seg").astype(jnp.float32),
        lax.psum(shares[1].astype(jnp.bfloat16), "seg").astype(jnp.float32),
        lax.psum(shares[2].astype(jnp.bfloat16), "seg").astype(jnp.float32),
        lax.psum(shares[3].astype(jnp.bfloat16), "seg").astype(jnp.float32),
        lax.psum(shares[4].astype(jnp.bfloat16), "seg").astype(jnp.float32),
        lax.psum(shares[5].astype(jnp.bfloat16), "seg").astype(jnp.float32),
        lax.psum(shares[6].astype(jnp.bfloat16), "seg").astype(jnp.float32),
    )
    return (
        output[None],
        input_grad,
        totals[0],
        totals[1],
        totals[2],
        totals[3],
        totals[4],
        totals[5],
        totals[6],
    )


VMEM_BYTES = 60 * 1024 * 1024
LN2 = math.log(2.0)
SCORE_SCALE = HEAD_DIM ** (-0.5)


def lane_fold(op, tile, running):
    for column in range(tile.shape[1] // HEAD_DIM):
        piece = tile[:, column * HEAD_DIM : (column + 1) * HEAD_DIM]
        running = piece if running is None else op(running, piece)
    return running


def causal(scores):
    rows = lax.broadcasted_iota(jnp.int32, scores.shape, 0)
    columns = lax.broadcasted_iota(jnp.int32, scores.shape, 1)
    return jnp.where(columns <= rows, scores, masked_score)


def attend(query, pairs, diagonal, carried):
    every, lane_max = [], None
    for index, (keys, _) in enumerate(pairs):
        scores = product_nt(query, keys)
        if diagonal and index == len(pairs) - 1:
            scores = causal(scores)
        lane_max = lane_fold(jnp.maximum, scores, lane_max)
        every.append(scores)
    row_max = jnp.max(lane_max, axis=1, keepdims=True)
    if carried is not None:
        row_max = jnp.maximum(row_max, carried[0])
    lane_sum, mixed = None, None
    for scores, (_, values) in zip(every, pairs):
        probs = jnp.exp2(scores - row_max)
        lane_sum = lane_fold(jnp.add, probs, lane_sum)
        part = product(probs.astype(jnp.bfloat16), values)
        mixed = part if mixed is None else mixed + part
    row_sum = jnp.sum(lane_sum, axis=1, keepdims=True)
    if carried is not None:
        shrink = jnp.exp2(carried[0] - row_max)
        row_sum = carried[1] * shrink + row_sum
        mixed = carried[2] * shrink + mixed
    return row_max, row_sum, mixed


def own_forward_kernel(rows, count, q_ref, k_ref, v_ref, mix_ref, max_ref, sum_ref):
    block = pl.program_id(1)
    for index in range(count):

        @pl.when(block == index)
        def _(index=index):
            pairs = [
                (k_ref[n * rows : (n + 1) * rows, :], v_ref[n * rows : (n + 1) * rows, :])
                for n in range(index + 1)
            ]
            row_max, row_sum, mixed = attend(q_ref[...], pairs, True, None)
            mix_ref[...] = mixed
            max_ref[...] = jnp.broadcast_to(row_max, max_ref.shape)
            sum_ref[...] = jnp.broadcast_to(row_sum, sum_ref.shape)


def own_forward(queries, keys, values, rows=512):
    length, width = queries.shape
    block = pl.BlockSpec((rows, HEAD_DIM), lambda h, i: (i, h))
    whole = pl.BlockSpec((length, HEAD_DIM), lambda h, i: (0, h))
    heads = width // HEAD_DIM
    pairs = heads * length * length // 2
    return pl.pallas_call(
        functools.partial(own_forward_kernel, rows, length // rows),
        grid=(heads, length // rows),
        in_specs=[block, whole, whole],
        out_specs=[block] * 3,
        out_shape=[jax.ShapeDtypeStruct((length, width), jnp.float32)] * 3,
        compiler_params=pltpu.CompilerParams(vmem_limit_bytes=VMEM_BYTES),
        cost_estimate=pl.CostEstimate(
            flops=8 * pairs * HEAD_DIM, transcendentals=pairs, bytes_accessed=18 * length * width
        ),
        name="own_forward",
    )(queries, keys, values)


def memory_specs(heads, rows, count):
    specs = []
    for slot in range(count):
        specs.append(
            pl.BlockSpec((1, rows, HEAD_DIM), lambda h, i, chosen, slot=slot: (chosen[slot], 0, h))
        )
        specs.append(
            pl.BlockSpec(
                (1, rows, HEAD_DIM), lambda h, i, chosen, slot=slot: (chosen[slot], 0, heads + h)
            )
        )
    return specs


def memory_forward_kernel(count, chosen, q_ref, mix_ref, max_ref, sum_ref, *rest):
    blocks = rest[: 2 * count]
    low_ref, out_ref, log_ref = rest[2 * count :]
    carried = (max_ref[:, :1], sum_ref[:, :1], mix_ref[...])

    def finish(row_max, row_sum, mixed):
        out = mixed * (1.0 / row_sum)
        out_ref[...] = out
        low_ref[...] = out.astype(jnp.bfloat16)
        log_ref[...] = jnp.broadcast_to(row_max + jnp.log2(row_sum), log_ref.shape)

    @pl.when(chosen[count] > 0)
    def _():
        pairs = [(blocks[2 * n][0], blocks[2 * n + 1][0]) for n in range(count)]
        finish(*attend(q_ref[...], pairs, False, carried))

    @pl.when(chosen[count] <= 0)
    def _():
        finish(*carried)


def memory_forward(chosen, queries, mixed, row_max, row_sum, memory, rows=512):
    length, width = queries.shape
    heads, count = width // HEAD_DIM, chosen.shape[0] - 1
    block = pl.BlockSpec((rows, HEAD_DIM), lambda h, i, chosen: (i, h))
    pairs = heads * length * count * memory.shape[1]
    return pl.pallas_call(
        functools.partial(memory_forward_kernel, count),
        grid_spec=pltpu.PrefetchScalarGridSpec(
            num_scalar_prefetch=1,
            grid=(heads, length // rows),
            in_specs=[block] * 4 + memory_specs(heads, memory.shape[1], count),
            out_specs=[block] * 3,
        ),
        out_shape=[
            jax.ShapeDtypeStruct((length, width), jnp.bfloat16),
            jax.ShapeDtypeStruct((length, width), jnp.float32),
            jax.ShapeDtypeStruct((length, width), jnp.float32),
        ],
        compiler_params=pltpu.CompilerParams(vmem_limit_bytes=VMEM_BYTES),
        cost_estimate=pl.CostEstimate(
            flops=8 * pairs * HEAD_DIM, transcendentals=pairs, bytes_accessed=36 * length * width
        ),
        name="memory_forward",
    )(chosen, queries, mixed, row_max, row_sum, *[memory] * (2 * count))


def memory_backward_kernel(count, tile, chosen, q_ref, g_ref, out_ref, log_ref, *rest):
    blocks = rest[: 2 * count]
    dq_ref, delta_ref = rest[2 * count :]
    query, upstream = q_ref[...], g_ref[...]
    delta = jnp.sum(upstream.astype(jnp.float32) * out_ref[...], axis=1, keepdims=True)
    delta_ref[...] = jnp.broadcast_to(delta, delta_ref.shape)
    log_total = log_ref[:, :1]

    @pl.when(chosen[count] > 0)
    def _():
        total = jnp.zeros(dq_ref.shape, jnp.float32)
        for n in range(count):
            for start in range(0, blocks[0].shape[1], tile):
                keys = blocks[2 * n][0, start : start + tile, :]
                values = blocks[2 * n + 1][0, start : start + tile, :]
                probs = jnp.exp2(product_nt(query, keys) - log_total)
                dscores = probs * (product_nt(upstream, values) - delta)
                total = total + product(dscores.astype(jnp.bfloat16), keys)
        dq_ref[...] = total

    @pl.when(chosen[count] <= 0)
    def _():
        dq_ref[...] = jnp.zeros(dq_ref.shape, jnp.float32)


def memory_backward(chosen, queries, upstream, out, log_totals, memory, rows=512, tile=512):
    length, width = queries.shape
    heads, count = width // HEAD_DIM, chosen.shape[0] - 1
    block = pl.BlockSpec((rows, HEAD_DIM), lambda h, i, chosen: (i, h))
    pairs = heads * length * count * memory.shape[1]
    return pl.pallas_call(
        functools.partial(memory_backward_kernel, count, math.gcd(tile, memory.shape[1])),
        grid_spec=pltpu.PrefetchScalarGridSpec(
            num_scalar_prefetch=1,
            grid=(heads, length // rows),
            in_specs=[block] * 4 + memory_specs(heads, memory.shape[1], count),
            out_specs=[block] * 2,
        ),
        out_shape=[jax.ShapeDtypeStruct((length, width), jnp.float32)] * 2,
        compiler_params=pltpu.CompilerParams(vmem_limit_bytes=VMEM_BYTES),
        cost_estimate=pl.CostEstimate(
            flops=12 * pairs * HEAD_DIM, transcendentals=pairs, bytes_accessed=36 * length * width
        ),
        name="memory_backward",
    )(chosen, queries, upstream, out, log_totals, *[memory] * (2 * count))


def own_backward_kernel(
    rows, q_ref, k_ref, v_ref, g_ref, log_ref, delta_ref, start_ref, dq_ref, dk_ref, dv_ref, dk, dv
):
    block = pl.program_id(1)

    @pl.when(block == 0)
    def _():
        dk[...] = jnp.zeros_like(dk)
        dv[...] = jnp.zeros_like(dv)

    query, upstream = q_ref[...], g_ref[...]
    log_total, delta = log_ref[:, :1], delta_ref[:, :1]

    def turn(other, total, diagonal):
        span = pl.ds(pl.multiple_of(other * rows, rows), rows)
        keys = k_ref[span, :]
        scores = product_nt(query, keys)
        if diagonal:
            scores = causal(scores)
        probs = jnp.exp2(scores - log_total)
        dscores = (probs * (product_nt(upstream, v_ref[span, :]) - delta)).astype(jnp.bfloat16)
        dv[span, :] += product_tn(probs.astype(jnp.bfloat16), upstream)
        dk[span, :] += product_tn(dscores, query)
        return total + product(dscores, keys)

    total = turn(block, start_ref[...], True)
    total = lax.fori_loop(0, block, lambda other, total: turn(other, total, False), total)
    dq_ref[...] = total * SCORE_SCALE

    @pl.when(block == pl.num_programs(1) - 1)
    def _():
        dk_ref[...] = dk[...] * LN2
        dv_ref[...] = dv[...]


def own_backward(queries, keys, values, upstream, log_totals, delta, start, rows=512):
    length, width = queries.shape
    block = pl.BlockSpec((rows, HEAD_DIM), lambda h, i: (i, h))
    whole = pl.BlockSpec((length, HEAD_DIM), lambda h, i: (0, h))
    heads = width // HEAD_DIM
    pairs = heads * length * length // 2
    return pl.pallas_call(
        functools.partial(own_backward_kernel, rows),
        grid=(heads, length // rows),
        in_specs=[block, whole, whole, block, block, block, block],
        out_specs=[block, whole, whole],
        out_shape=[jax.ShapeDtypeStruct((length, width), jnp.float32)] * 3,
        scratch_shapes=[pltpu.VMEM((length, HEAD_DIM), jnp.float32)] * 2,
        compiler_params=pltpu.CompilerParams(vmem_limit_bytes=VMEM_BYTES),
        cost_estimate=pl.CostEstimate(
            flops=20 * pairs * HEAD_DIM, transcendentals=pairs, bytes_accessed=36 * length * width
        ),
        name="own_backward",
    )(queries, keys, values, upstream, log_totals, delta, start)


def rotate_block(matrix, cosine_table, sine_table, direction):
    row_count, width = matrix.shape
    half_dim = HEAD_DIM // 2
    shaped = matrix.reshape(row_count, width // HEAD_DIM, HEAD_DIM)
    turned = jnp.concatenate([-shaped[..., half_dim:], shaped[..., :half_dim]], axis=-1)
    return (shaped * cosine_table + direction * turned * sine_table).reshape(row_count, width)


def core_groups(seg_size):
    return [[2 * z, 2 * z + 1] for z in range(seg_size // 2)]


def line_groups(seg_size):
    return [[2 * z + core for z in range(seg_size // 2)] for core in range(2)]


def reduce_rows(terms, seg_size, seq_size):
    rows, columns = terms.shape
    split = terms.astype(jnp.bfloat16).reshape(seq_size, 2, rows // (2 * seq_size), columns)
    halves = jnp.swapaxes(split, 0, 1)
    swapped = lax.all_to_all(halves, "seg", 0, 0, axis_index_groups=core_groups(seg_size))
    chip = (swapped[0].astype(jnp.float32) + swapped[1].astype(jnp.float32)).astype(jnp.bfloat16)
    share = lax.psum_scatter(chip, "seq", scatter_dimension=0)
    total = lax.psum(share, "seg", axis_index_groups=line_groups(seg_size))
    both = lax.all_gather(total, "seg", axis=0, axis_index_groups=core_groups(seg_size))
    return both.reshape(rows // seq_size, columns).astype(jnp.float32)


def head_plan(
    seg_size,
    seq_size,
    layer_input,
    output_grad,
    norm1_gain,
    norm2_gain,
    w_qkv,
    w_out,
    w_gate,
    w_up,
    w_down,
    mem_keys,
    mem_values,
    memory_flags,
    sources,
):
    seg_index = lax.axis_index("seg")
    seq_index = lax.axis_index("seq")
    tokens = layer_input.shape[1]
    length = tokens * seq_size
    width = D // seq_size
    flag = lax.dynamic_index_in_dim(memory_flags, seg_index, 0, keepdims=True)
    listed = lax.dynamic_index_in_dim(sources, seg_index, 0, keepdims=False)
    chosen = jnp.concatenate([jnp.reshape(seg_index, (1,)), listed, flag]).astype(jnp.int32)

    mem_rows = mem_keys.shape[1]
    both = jnp.concatenate(
        [mem_keys[0].reshape(mem_rows, seq_size, width), mem_values[0].reshape(mem_rows, seq_size, width)],
        axis=2,
    ).reshape(mem_rows, 2 * D)
    own_memory = lax.all_to_all(both, "seq", 1, 0, tiled=True)
    memory = lax.all_gather(own_memory, "seg", axis=0)

    inputs = layer_input[0].astype(jnp.float32)
    first_norm, first_inverse = norm_forward(inputs, norm1_gain)
    first_low = first_norm.astype(jnp.bfloat16)
    every_low = lax.all_gather(first_low, "seq", axis=0, tiled=True)
    w_heads = lax.dynamic_index_in_dim(
        w_qkv.reshape(D, 3, seq_size, width), seq_index, 2, keepdims=False
    ).reshape(D, 3 * width)
    projected = product(every_low, w_heads)
    cosine_table, sine_table = turn_tables(lax.iota(jnp.int32, length).astype(jnp.float32))
    scale = SCORE_SCALE / LN2
    queries = rotate_block(
        projected[:, :width], cosine_table * scale, sine_table * scale, 1.0
    ).astype(jnp.bfloat16)
    keys = rotate_block(projected[:, width : 2 * width], cosine_table, sine_table, 1.0).astype(
        jnp.bfloat16
    )
    values = projected[:, 2 * width :].astype(jnp.bfloat16)

    mixed, row_max, row_sum = own_forward(queries, keys, values)
    heads_low, heads_out, log_totals = memory_forward(
        chosen, queries, mixed, row_max, row_sum, memory
    )
    attended_low = lax.all_to_all(heads_low, "seq", 0, 1, tiled=True)

    residual = inputs + product(attended_low, w_out)
    second_norm, second_inverse = norm_forward(residual, norm2_gain)
    second_low = second_norm.astype(jnp.bfloat16)
    gate_values = product(second_low, w_gate)
    up_values = product(second_low, w_up)
    sigmoid_gate = jax.nn.sigmoid(gate_values)
    activated = gate_values * sigmoid_gate
    hidden_low = (activated * up_values).astype(jnp.bfloat16)
    output = (residual + product(hidden_low, w_down)).astype(jnp.bfloat16)
    upstream = output_grad[0]
    grad_down = reduce_rows(product_tn(hidden_low, upstream), seg_size, seq_size)
    grad_hidden = product_nt(upstream, w_down)
    grad_gate_low = (
        grad_hidden * up_values * sigmoid_gate * (1.0 + gate_values * (1.0 - sigmoid_gate))
    ).astype(jnp.bfloat16)
    grad_up_low = (grad_hidden * activated).astype(jnp.bfloat16)
    grad_gate = reduce_rows(product_tn(second_low, grad_gate_low), seg_size, seq_size)
    grad_up = reduce_rows(product_tn(second_low, grad_up_low), seg_size, seq_size)
    grad_second = product_nt(grad_gate_low, w_gate) + product_nt(grad_up_low, w_up)
    grad_residual, grad_norm2 = norm_backward(residual, second_inverse, norm2_gain, grad_second)
    grad_residual = grad_residual + upstream.astype(jnp.float32)
    residual_low = grad_residual.astype(jnp.bfloat16)
    grad_out = reduce_rows(product_tn(attended_low, residual_low), seg_size, seq_size)
    grad_attended = product_nt(residual_low, w_out).astype(jnp.bfloat16)
    grad_heads = lax.all_to_all(grad_attended, "seq", 1, 0, tiled=True)

    start, delta = memory_backward(chosen, queries, grad_heads, heads_out, log_totals, memory)
    grad_queries, grad_keys, grad_values = own_backward(
        queries, keys, values, grad_heads, log_totals, delta, start
    )
    grad_projected = jnp.concatenate(
        [
            rotate_block(grad_queries, cosine_table, sine_table, -1.0),
            rotate_block(grad_keys, cosine_table, sine_table, -1.0),
            grad_values,
        ],
        axis=1,
    ).astype(jnp.bfloat16)
    part_first = product_nt(grad_projected, w_heads).astype(jnp.bfloat16)
    grad_first = lax.psum_scatter(part_first, "seq", scatter_dimension=0, tiled=True).astype(
        jnp.float32
    )
    part_qkv = product_tn(every_low, grad_projected).astype(jnp.bfloat16)
    traded = lax.all_to_all(part_qkv.reshape(seq_size, D // seq_size, 3 * width), "seq", 0, 0)
    rows_qkv = jnp.transpose(
        traded.reshape(seq_size, D // seq_size, 3, width), (1, 2, 0, 3)
    ).reshape(D // seq_size, 3 * D)
    grad_qkv = lax.psum(rows_qkv, "seg").astype(jnp.float32)
    grad_inputs, grad_norm1 = norm_backward(inputs, first_inverse, norm1_gain, grad_first)
    input_grad = (grad_inputs + grad_residual)[None]
    gains = jnp.stack([grad_norm1, grad_norm2], axis=0)
    gain_total = lax.psum(gains, ("seg", "seq"))
    gain_rows = lax.dynamic_slice_in_dim(gain_total, seq_index * width, width, 1)
    return (
        output[None],
        input_grad,
        gain_rows[0],
        gain_rows[1],
        grad_qkv,
        grad_out,
        grad_gate,
        grad_up,
        grad_down,
    )


def solution(mesh):
    seq_size = mesh.shape["seq"]
    heads_fit = HEADS % seq_size == 0 and mesh.shape["seg"] % 2 == 0
    plan = functools.partial(head_plan, mesh.shape["seg"], seq_size) if heads_fit else general_plan
    placed = (
        P("seg", "seq", None),
        P("seg", "seq", None),
        P(),
        P(),
        P(),
        P(),
        P(),
        P(),
        P(),
        P("seg", "seq", None),
        P("seg", "seq", None),
        P(),
        P(),
    )
    return jax.shard_map(
        plan,
        mesh=mesh,
        in_specs=placed,
        out_specs=(
            P("seg", "seq", None),
            P("seg", "seq", None),
            P("seq"),
            P("seq"),
            P("seq", None),
            P("seq", None),
            P("seq", None),
            P("seq", None),
            P("seq", None),
        ),
        check_vma=False,
    )
```

```python
import functools
import math

import jax
import jax.numpy as jnp
from jax import lax
from jax.experimental import pallas as pl
from jax.experimental.pallas import tpu as pltpu
from jax.sharding import PartitionSpec as P

D = 1024
HEADS = 8
HEAD_DIM = 128


masked_score = -1e30
epsilon = 1e-06
rotary_base = 10000.0


def product(former, latter):
    return jnp.dot(former, latter, preferred_element_type=jnp.float32)


def product_nt(former, latter):
    return lax.dot_general(
        former, latter, (((1,), (1,)), ((), ())), preferred_element_type=jnp.float32
    )


def product_tn(former, latter):
    return lax.dot_general(
        former, latter, (((0,), (0,)), ((), ())), preferred_element_type=jnp.float32
    )


def norm_forward(values, norm_gain):
    inverse = lax.rsqrt(jnp.mean(values * values, axis=-1, keepdims=True) + epsilon)
    return (values * inverse * norm_gain, inverse)


def norm_backward(values, inverse, norm_gain, upstream):
    weighted = upstream * norm_gain
    inner_mean = jnp.mean(weighted * values, axis=-1, keepdims=True)
    grad_values = inverse * weighted - inverse * inverse * inverse * values * inner_mean
    grad_gain = jnp.sum(upstream * values * inverse, axis=0)
    return (grad_values, grad_gain)


def turn_tables(positions):
    half_dim = HEAD_DIM // 2
    exponent = -2.0 * jnp.arange(half_dim, dtype=jnp.float32) / HEAD_DIM
    angles = positions[:, None] * jnp.power(rotary_base, exponent)[None, :]
    angles = jnp.concatenate([angles, angles], axis=1)
    return (jnp.cos(angles)[:, None, :], jnp.sin(angles)[:, None, :])


def rotate(matrix, cosine_table, sine_table, direction):
    row_count = matrix.shape[0]
    half_dim = HEAD_DIM // 2
    shaped = matrix.reshape(row_count, HEADS, HEAD_DIM)
    turned = jnp.concatenate([-shaped[..., half_dim:], shaped[..., :half_dim]], axis=-1)
    return (shaped * cosine_table + direction * turned * sine_table).reshape(
        row_count, HEADS * HEAD_DIM
    )


def general_plan(
    layer_input,
    output_grad,
    norm1_gain,
    norm2_gain,
    w_qkv,
    w_out,
    w_gate,
    w_up,
    w_down,
    mem_keys,
    mem_values,
    memory_flags,
    sources,
):
    seg_index = lax.axis_index("seg")
    seq_index = lax.axis_index("seq")
    tokens = layer_input.shape[1]
    score_scale = HEAD_DIM ** (-0.5)
    flag_on = lax.dynamic_index_in_dim(memory_flags, seg_index, 0, keepdims=False) > 0
    listed = lax.dynamic_index_in_dim(sources, seg_index, 0, keepdims=False)
    picked = jnp.concatenate([jnp.reshape(seg_index, (1,)), listed])
    every_keys, every_values = (
        lax.all_gather(mem_keys, "seg", axis=0, tiled=True),
        lax.all_gather(mem_values, "seg", axis=0, tiled=True),
    )
    chosen_keys = jnp.take(every_keys, picked, axis=0)
    chosen_values = jnp.take(every_values, picked, axis=0)
    memory_keys, memory_values = (
        lax.all_gather(chosen_keys, "seq", axis=1, tiled=True),
        lax.all_gather(chosen_values, "seq", axis=1, tiled=True),
    )
    memory_key_blocks = memory_keys.reshape(-1, tokens, HEADS, HEAD_DIM)
    memory_value_blocks = memory_values.reshape(-1, tokens, HEADS, HEAD_DIM)
    memory_blocks = memory_key_blocks.shape[0]
    inputs = layer_input[0].astype(jnp.float32)
    first_norm, first_inverse = norm_forward(inputs, norm1_gain)
    first_low = first_norm.astype(jnp.bfloat16)
    projected = product(first_low, w_qkv)
    positions = seq_index * tokens + lax.iota(jnp.int32, tokens)
    cosine_table, sine_table = turn_tables(positions.astype(jnp.float32))
    queries = rotate(projected[:, :D], cosine_table, sine_table, 1.0).astype(jnp.bfloat16)
    own_keys = rotate(projected[:, D : 2 * D], cosine_table, sine_table, 1.0).astype(jnp.bfloat16)
    own_values = projected[:, 2 * D :].astype(jnp.bfloat16)
    all_keys, all_values = (
        lax.all_gather(own_keys, "seq", axis=0, tiled=True),
        lax.all_gather(own_values, "seq", axis=0, tiled=True),
    )
    key_blocks = all_keys.reshape(-1, tokens, HEADS, HEAD_DIM)
    value_blocks = all_values.reshape(-1, tokens, HEADS, HEAD_DIM)
    query_heads = queries.reshape(tokens, HEADS, HEAD_DIM)
    memory_open = jnp.broadcast_to(flag_on, (tokens, tokens))
    own_count = seq_index + 1
    key_offsets = lax.iota(jnp.int32, tokens)

    def own_open(block):
        return (block * tokens + key_offsets)[None, :] <= positions[:, None]

    def block_scores(key_block, open_mask):
        raw = (
            jnp.einsum("qhd,khd->hqk", query_heads, key_block, preferred_element_type=jnp.float32)
            * score_scale
        )
        return jnp.where(open_mask[None], raw, masked_score)

    def sweep(step, carry):

        def memory_turn(block, state):
            return step(
                state,
                block,
                memory_key_blocks[block],
                memory_value_blocks[block],
                memory_open,
                False,
            )

        def own_turn(block, state):
            return step(state, block, key_blocks[block], value_blocks[block], own_open(block), True)

        carry = lax.fori_loop(0, memory_blocks, memory_turn, carry)
        return lax.fori_loop(0, own_count, own_turn, carry)

    def max_step(carry, block, key_block, value_block, open_mask, own):
        row_max, row_sum = carry
        scores = block_scores(key_block, open_mask)
        new_max = jnp.maximum(row_max, jnp.max(scores, axis=2))
        row_sum = row_sum * jnp.exp(row_max - new_max) + jnp.sum(
            jnp.exp(scores - new_max[..., None]), axis=2
        )
        return (new_max, row_sum)

    start_max = jnp.full((HEADS, tokens), masked_score, jnp.float32)
    row_max, row_sum = sweep(max_step, (start_max, jnp.zeros((HEADS, tokens), jnp.float32)))
    log_totals = row_max + jnp.log(row_sum)

    def mix_step(total, block, key_block, value_block, open_mask, own):
        weights_low = jnp.exp(block_scores(key_block, open_mask) - log_totals[..., None]).astype(
            jnp.bfloat16
        )
        return total + jnp.einsum(
            "hqk,khd->qhd", weights_low, value_block, preferred_element_type=jnp.float32
        )

    attended = sweep(mix_step, jnp.zeros((tokens, HEADS, HEAD_DIM), jnp.float32))
    attended_low = attended.reshape(tokens, D).astype(jnp.bfloat16)
    residual = inputs + product(attended_low, w_out)
    second_norm, second_inverse = norm_forward(residual, norm2_gain)
    second_low = second_norm.astype(jnp.bfloat16)
    gate_values = product(second_low, w_gate)
    up_values = product(second_low, w_up)
    sigmoid_gate = jax.nn.sigmoid(gate_values)
    activated = gate_values * sigmoid_gate
    hidden_low = (activated * up_values).astype(jnp.bfloat16)
    output = (residual + product(hidden_low, w_down)).astype(jnp.bfloat16)
    upstream = output_grad[0]
    grad_down = product_tn(hidden_low, upstream)
    grad_hidden = product_nt(upstream, w_down)
    grad_gate_low = (
        grad_hidden * up_values * sigmoid_gate * (1.0 + gate_values * (1.0 - sigmoid_gate))
    ).astype(jnp.bfloat16)
    grad_up_low = (grad_hidden * activated).astype(jnp.bfloat16)
    grad_gate = product_tn(second_low, grad_gate_low)
    grad_up = product_tn(second_low, grad_up_low)
    grad_second = product_nt(grad_gate_low, w_gate) + product_nt(grad_up_low, w_up)
    grad_residual, grad_norm2 = norm_backward(residual, second_inverse, norm2_gain, grad_second)
    grad_residual = grad_residual + upstream.astype(jnp.float32)
    residual_low = grad_residual.astype(jnp.bfloat16)
    grad_out = product_tn(attended_low, residual_low)
    grad_attended = product_nt(residual_low, w_out).astype(jnp.bfloat16)
    grad_heads = grad_attended.reshape(tokens, HEADS, HEAD_DIM)

    def probs_pair(key_block, value_block, open_mask):
        probs = jnp.exp(block_scores(key_block, open_mask) - log_totals[..., None])
        dprobs = jnp.einsum(
            "qhd,khd->hqk", grad_heads, value_block, preferred_element_type=jnp.float32
        )
        return (probs, dprobs)

    def delta_step(total, block, key_block, value_block, open_mask, own):
        probs, dprobs = probs_pair(key_block, value_block, open_mask)
        return total + jnp.sum(probs * dprobs, axis=2)

    delta_rows = sweep(delta_step, jnp.zeros((HEADS, tokens), jnp.float32))

    def grad_step(carry, block, key_block, value_block, open_mask, own):
        grad_query, key_terms, value_terms = carry
        probs, dprobs = probs_pair(key_block, value_block, open_mask)
        dscores = (probs * (dprobs - delta_rows[..., None])).astype(jnp.bfloat16)
        grad_query = grad_query + jnp.einsum(
            "hqk,khd->qhd", dscores, key_block, preferred_element_type=jnp.float32
        )
        if own:
            key_part = (
                jnp.einsum("hqk,qhd->khd", dscores, query_heads, preferred_element_type=jnp.float32)
                * score_scale
            )
            value_part = jnp.einsum(
                "hqk,qhd->khd",
                probs.astype(jnp.bfloat16),
                grad_heads,
                preferred_element_type=jnp.float32,
            )
            key_terms = lax.dynamic_update_index_in_dim(key_terms, key_part, block, 0)
            value_terms = lax.dynamic_update_index_in_dim(value_terms, value_part, block, 0)
        return (grad_query, key_terms, value_terms)

    term_shape = key_blocks.shape
    start_grads = (
        jnp.zeros((tokens, HEADS, HEAD_DIM), jnp.float32),
        jnp.zeros(term_shape, jnp.float32),
        jnp.zeros(term_shape, jnp.float32),
    )
    grad_query, key_terms, value_terms = sweep(grad_step, start_grads)
    grad_queries = (grad_query * score_scale).reshape(tokens, D)
    grad_keys, grad_values = (
        lax.psum_scatter(
            key_terms.astype(jnp.bfloat16), "seq", scatter_dimension=0, tiled=True
        ).astype(jnp.float32),
        lax.psum_scatter(
            value_terms.astype(jnp.bfloat16), "seq", scatter_dimension=0, tiled=True
        ).astype(jnp.float32),
    )
    grad_projected = jnp.concatenate(
        [
            rotate(grad_queries, cosine_table, sine_table, -1.0),
            rotate(grad_keys.reshape(tokens, D), cosine_table, sine_table, -1.0),
            grad_values.reshape(tokens, D),
        ],
        axis=1,
    ).astype(jnp.bfloat16)
    grad_qkv = product_tn(first_low, grad_projected)
    grad_first = product_nt(grad_projected, w_qkv)
    grad_inputs, grad_norm1 = norm_backward(inputs, first_inverse, norm1_gain, grad_first)
    input_grad = (grad_inputs + grad_residual)[None]
    shares = (
        lax.psum_scatter(
            grad_norm1.astype(jnp.bfloat16), "seq", scatter_dimension=0, tiled=True
        ).astype(jnp.float32),
        lax.psum_scatter(
            grad_norm2.astype(jnp.bfloat16), "seq", scatter_dimension=0, tiled=True
        ).astype(jnp.float32),
        lax.psum_scatter(
            grad_qkv.astype(jnp.bfloat16), "seq", scatter_dimension=0, tiled=True
        ).astype(jnp.float32),
        lax.psum_scatter(
            grad_out.astype(jnp.bfloat16), "seq", scatter_dimension=0, tiled=True
        ).astype(jnp.float32),
        lax.psum_scatter(
            grad_gate.astype(jnp.bfloat16), "seq", scatter_dimension=0, tiled=True
        ).astype(jnp.float32),
        lax.psum_scatter(
            grad_up.astype(jnp.bfloat16), "seq", scatter_dimension=0, tiled=True
        ).astype(jnp.float32),
        lax.psum_scatter(
            grad_down.astype(jnp.bfloat16), "seq", scatter_dimension=0, tiled=True
        ).astype(jnp.float32),
    )
    totals = (
        lax.psum(shares[0].astype(jnp.bfloat16), "seg").astype(jnp.float32),
        lax.psum(shares[1].astype(jnp.bfloat16), "seg").astype(jnp.float32),
        lax.psum(shares[2].astype(jnp.bfloat16), "seg").astype(jnp.float32),
        lax.psum(shares[3].astype(jnp.bfloat16), "seg").astype(jnp.float32),
        lax.psum(shares[4].astype(jnp.bfloat16), "seg").astype(jnp.float32),
        lax.psum(shares[5].astype(jnp.bfloat16), "seg").astype(jnp.float32),
        lax.psum(shares[6].astype(jnp.bfloat16), "seg").astype(jnp.float32),
    )
    return (
        output[None],
        input_grad,
        totals[0],
        totals[1],
        totals[2],
        totals[3],
        totals[4],
        totals[5],
        totals[6],
    )


VMEM_BYTES = 60 * 1024 * 1024
LN2 = math.log(2.0)
SCORE_SCALE = HEAD_DIM ** (-0.5)


def lane_fold(op, tile, running):
    for column in range(tile.shape[1] // HEAD_DIM):
        piece = tile[:, column * HEAD_DIM : (column + 1) * HEAD_DIM]
        running = piece if running is None else op(running, piece)
    return running


def causal(scores):
    rows = lax.broadcasted_iota(jnp.int32, scores.shape, 0)
    columns = lax.broadcasted_iota(jnp.int32, scores.shape, 1)
    return jnp.where(columns <= rows, scores, masked_score)


def attend(query, pairs, diagonal, carried):
    every, lane_max = [], None
    for index, (keys, _) in enumerate(pairs):
        scores = product_nt(query, keys)
        if diagonal and index == len(pairs) - 1:
            scores = causal(scores)
        lane_max = lane_fold(jnp.maximum, scores, lane_max)
        every.append(scores)
    row_max = jnp.max(lane_max, axis=1, keepdims=True)
    if carried is not None:
        row_max = jnp.maximum(row_max, carried[0])
    lane_sum, mixed = None, None
    for scores, (_, values) in zip(every, pairs):
        probs = jnp.exp2(scores - row_max)
        lane_sum = lane_fold(jnp.add, probs, lane_sum)
        part = product(probs.astype(jnp.bfloat16), values)
        mixed = part if mixed is None else mixed + part
    row_sum = jnp.sum(lane_sum, axis=1, keepdims=True)
    if carried is not None:
        shrink = jnp.exp2(carried[0] - row_max)
        row_sum = carried[1] * shrink + row_sum
        mixed = carried[2] * shrink + mixed
    return row_max, row_sum, mixed


def own_forward_kernel(rows, count, q_ref, k_ref, v_ref, mix_ref, max_ref, sum_ref):
    block = pl.program_id(1)
    for index in range(count):

        @pl.when(block == index)
        def _(index=index):
            pairs = [
                (k_ref[n * rows : (n + 1) * rows, :], v_ref[n * rows : (n + 1) * rows, :])
                for n in range(index + 1)
            ]
            row_max, row_sum, mixed = attend(q_ref[...], pairs, True, None)
            mix_ref[...] = mixed
            max_ref[...] = jnp.broadcast_to(row_max, max_ref.shape)
            sum_ref[...] = jnp.broadcast_to(row_sum, sum_ref.shape)


def own_forward(queries, keys, values, rows=512):
    length, width = queries.shape
    block = pl.BlockSpec((rows, HEAD_DIM), lambda h, i: (i, h))
    whole = pl.BlockSpec((length, HEAD_DIM), lambda h, i: (0, h))
    heads = width // HEAD_DIM
    pairs = heads * length * length // 2
    return pl.pallas_call(
        functools.partial(own_forward_kernel, rows, length // rows),
        grid=(heads, length // rows),
        in_specs=[block, whole, whole],
        out_specs=[block] * 3,
        out_shape=[jax.ShapeDtypeStruct((length, width), jnp.float32)] * 3,
        compiler_params=pltpu.CompilerParams(vmem_limit_bytes=VMEM_BYTES),
        cost_estimate=pl.CostEstimate(
            flops=8 * pairs * HEAD_DIM, transcendentals=pairs, bytes_accessed=18 * length * width
        ),
        name="own_forward",
    )(queries, keys, values)


def memory_specs(heads, rows, count):
    specs = []
    for slot in range(count):
        specs.append(
            pl.BlockSpec((1, rows, HEAD_DIM), lambda h, i, chosen, slot=slot: (chosen[slot], 0, h))
        )
        specs.append(
            pl.BlockSpec(
                (1, rows, HEAD_DIM), lambda h, i, chosen, slot=slot: (chosen[slot], 0, heads + h)
            )
        )
    return specs


def memory_forward_kernel(count, chosen, q_ref, mix_ref, max_ref, sum_ref, *rest):
    blocks = rest[: 2 * count]
    low_ref, out_ref, log_ref = rest[2 * count :]
    carried = (max_ref[:, :1], sum_ref[:, :1], mix_ref[...])

    def finish(row_max, row_sum, mixed):
        out = mixed * (1.0 / row_sum)
        out_ref[...] = out
        low_ref[...] = out.astype(jnp.bfloat16)
        log_ref[...] = jnp.broadcast_to(row_max + jnp.log2(row_sum), log_ref.shape)

    @pl.when(chosen[count] > 0)
    def _():
        pairs = [(blocks[2 * n][0], blocks[2 * n + 1][0]) for n in range(count)]
        finish(*attend(q_ref[...], pairs, False, carried))

    @pl.when(chosen[count] <= 0)
    def _():
        finish(*carried)


def memory_forward(chosen, queries, mixed, row_max, row_sum, memory, rows=512):
    length, width = queries.shape
    heads, count = width // HEAD_DIM, chosen.shape[0] - 1
    block = pl.BlockSpec((rows, HEAD_DIM), lambda h, i, chosen: (i, h))
    pairs = heads * length * count * memory.shape[1]
    return pl.pallas_call(
        functools.partial(memory_forward_kernel, count),
        grid_spec=pltpu.PrefetchScalarGridSpec(
            num_scalar_prefetch=1,
            grid=(heads, length // rows),
            in_specs=[block] * 4 + memory_specs(heads, memory.shape[1], count),
            out_specs=[block] * 3,
        ),
        out_shape=[
            jax.ShapeDtypeStruct((length, width), jnp.bfloat16),
            jax.ShapeDtypeStruct((length, width), jnp.float32),
            jax.ShapeDtypeStruct((length, width), jnp.float32),
        ],
        compiler_params=pltpu.CompilerParams(vmem_limit_bytes=VMEM_BYTES),
        cost_estimate=pl.CostEstimate(
            flops=8 * pairs * HEAD_DIM, transcendentals=pairs, bytes_accessed=36 * length * width
        ),
        name="memory_forward",
    )(chosen, queries, mixed, row_max, row_sum, *[memory] * (2 * count))


def memory_backward_kernel(count, tile, chosen, q_ref, g_ref, out_ref, log_ref, *rest):
    blocks = rest[: 2 * count]
    dq_ref, delta_ref = rest[2 * count :]
    query, upstream = q_ref[...], g_ref[...]
    delta = jnp.sum(upstream.astype(jnp.float32) * out_ref[...], axis=1, keepdims=True)
    delta_ref[...] = jnp.broadcast_to(delta, delta_ref.shape)
    log_total = log_ref[:, :1]

    @pl.when(chosen[count] > 0)
    def _():
        total = jnp.zeros(dq_ref.shape, jnp.float32)
        for n in range(count):
            for start in range(0, blocks[0].shape[1], tile):
                keys = blocks[2 * n][0, start : start + tile, :]
                values = blocks[2 * n + 1][0, start : start + tile, :]
                probs = jnp.exp2(product_nt(query, keys) - log_total)
                dscores = probs * (product_nt(upstream, values) - delta)
                total = total + product(dscores.astype(jnp.bfloat16), keys)
        dq_ref[...] = total

    @pl.when(chosen[count] <= 0)
    def _():
        dq_ref[...] = jnp.zeros(dq_ref.shape, jnp.float32)


def memory_backward(chosen, queries, upstream, out, log_totals, memory, rows=512, tile=512):
    length, width = queries.shape
    heads, count = width // HEAD_DIM, chosen.shape[0] - 1
    block = pl.BlockSpec((rows, HEAD_DIM), lambda h, i, chosen: (i, h))
    pairs = heads * length * count * memory.shape[1]
    return pl.pallas_call(
        functools.partial(memory_backward_kernel, count, math.gcd(tile, memory.shape[1])),
        grid_spec=pltpu.PrefetchScalarGridSpec(
            num_scalar_prefetch=1,
            grid=(heads, length // rows),
            in_specs=[block] * 4 + memory_specs(heads, memory.shape[1], count),
            out_specs=[block] * 2,
        ),
        out_shape=[jax.ShapeDtypeStruct((length, width), jnp.float32)] * 2,
        compiler_params=pltpu.CompilerParams(vmem_limit_bytes=VMEM_BYTES),
        cost_estimate=pl.CostEstimate(
            flops=12 * pairs * HEAD_DIM, transcendentals=pairs, bytes_accessed=36 * length * width
        ),
        name="memory_backward",
    )(chosen, queries, upstream, out, log_totals, *[memory] * (2 * count))


def own_backward_kernel(
    rows, heads, q_ref, k_ref, v_ref, g_ref, log_ref, delta_ref, start_ref, cos_ref, sin_ref, d_ref, dk, dv
):
    head, block = pl.program_id(0), pl.program_id(1)

    def lanes(part):
        return pl.ds(pl.multiple_of((part * heads + head) * HEAD_DIM, HEAD_DIM), HEAD_DIM)

    @pl.when(block == 0)
    def _():
        dk[...] = jnp.zeros_like(dk)
        dv[...] = jnp.zeros_like(dv)

    query, upstream = q_ref[...], g_ref[...]
    log_total, delta = log_ref[:, :1], delta_ref[:, :1]

    def turn(other, total, diagonal):
        span = pl.ds(pl.multiple_of(other * rows, rows), rows)
        keys = k_ref[span, :]
        scores = product_nt(query, keys)
        if diagonal:
            scores = causal(scores)
        probs = jnp.exp2(scores - log_total)
        dscores = (probs * (product_nt(upstream, v_ref[span, :]) - delta)).astype(jnp.bfloat16)
        dv[span, :] += product_tn(probs.astype(jnp.bfloat16), upstream)
        dk[span, :] += product_tn(dscores, query)
        return total + product(dscores, keys)

    total = turn(block, start_ref[...], True)
    total = lax.fori_loop(0, block, lambda other, total: turn(other, total, False), total)
    mine = pl.ds(pl.multiple_of(block * rows, rows), rows)
    d_ref[mine, lanes(0)] = turn_block(
        total * SCORE_SCALE, cos_ref[mine, :], -sin_ref[mine, :]
    ).astype(jnp.bfloat16)

    @pl.when(block == pl.num_programs(1) - 1)
    def _():
        d_ref[:, lanes(1)] = turn_block(dk[...] * LN2, cos_ref[...], -sin_ref[...]).astype(
            jnp.bfloat16
        )
        d_ref[:, lanes(2)] = dv[...].astype(jnp.bfloat16)


def own_backward(
    queries, keys, values, upstream, log_totals, delta, start, cosine, sine, rows=512
):
    length, width = queries.shape
    block = pl.BlockSpec((rows, HEAD_DIM), lambda h, i: (i, h))
    whole = pl.BlockSpec((length, HEAD_DIM), lambda h, i: (0, h))
    table = pl.BlockSpec((length, HEAD_DIM), lambda h, i: (0, 0))
    heads = width // HEAD_DIM
    pairs = heads * length * length // 2
    return pl.pallas_call(
        functools.partial(own_backward_kernel, rows, heads),
        grid=(heads, length // rows),
        in_specs=[block, whole, whole, block, block, block, block, table, table],
        out_specs=pl.BlockSpec((length, 3 * width), lambda h, i: (0, 0)),
        out_shape=jax.ShapeDtypeStruct((length, 3 * width), jnp.bfloat16),
        scratch_shapes=[pltpu.VMEM((length, HEAD_DIM), jnp.float32)] * 2,
        compiler_params=pltpu.CompilerParams(vmem_limit_bytes=VMEM_BYTES),
        cost_estimate=pl.CostEstimate(
            flops=20 * pairs * HEAD_DIM, transcendentals=pairs, bytes_accessed=36 * length * width
        ),
        name="own_backward",
    )(queries, keys, values, upstream, log_totals, delta, start, cosine, sine)


def turn_block(matrix, cosine, sine):
    return matrix * cosine + pltpu.roll(matrix, HEAD_DIM // 2, 1) * sine


def project_kernel(x_ref, wq_ref, wk_ref, wv_ref, cos_ref, sin_ref, q_ref, k_ref, v_ref):
    cosine, sine = cos_ref[...], sin_ref[...]
    scale = SCORE_SCALE / LN2
    rows = x_ref[...]
    queries, keys = product(rows, wq_ref[...]), product(rows, wk_ref[...])
    for head in range(q_ref.shape[1] // HEAD_DIM):
        lanes = slice(head * HEAD_DIM, (head + 1) * HEAD_DIM)
        q_ref[:, lanes] = turn_block(queries[:, lanes], cosine * scale, sine * scale).astype(
            jnp.bfloat16
        )
        k_ref[:, lanes] = turn_block(keys[:, lanes], cosine, sine).astype(jnp.bfloat16)
    v_ref[...] = product(rows, wv_ref[...]).astype(jnp.bfloat16)


def project(inputs, w_heads, cosine, sine, rows=512):
    length, depth = inputs.shape
    width = w_heads.shape[1] // 3
    table = pl.BlockSpec((rows, HEAD_DIM), lambda i: (i, 0))
    block = pl.BlockSpec((rows, width), lambda i: (i, 0))
    weights = [pl.BlockSpec((depth, width), lambda i, part=part: (0, part)) for part in range(3)]
    return pl.pallas_call(
        project_kernel,
        grid=(length // rows,),
        in_specs=[pl.BlockSpec((rows, depth), lambda i: (i, 0))] + weights + [table] * 2,
        out_specs=[block] * 3,
        out_shape=[jax.ShapeDtypeStruct((length, width), jnp.bfloat16)] * 3,
        compiler_params=pltpu.CompilerParams(vmem_limit_bytes=VMEM_BYTES),
        cost_estimate=pl.CostEstimate(
            flops=6 * length * depth * width, transcendentals=0, bytes_accessed=4 * length * depth
        ),
        name="project",
    )(inputs, w_heads, w_heads, w_heads, cosine, sine)


LINK_RATE = {"core": 300e3, "x": 45e3, "y": 45e3, "z": 45e3}


class Place:
    def __init__(self):
        seg, seq = lax.axis_index("seg"), lax.axis_index("seq")
        self.core, self.z = lax.rem(seg, 2), lax.div(seg, 2)
        self.x, self.y = lax.rem(seq, 2), lax.div(seq, 2)
        odd = lax.rem(self.z, 2)
        self.inner = jnp.logical_or(self.z == 1, self.z == 2)
        self.outer = jnp.logical_not(self.inner)
        self.peer = {
            "core": (seg + 1 - 2 * self.core, seq),
            "x": (seg, seq + 1 - 2 * self.x),
            "y": (seg, seq + 2 - 4 * self.y),
            "xy": (seg, 3 - seq),
            "pair": (seg + 2 - 4 * odd, seq),
            "middle": (seg - 2 + 4 * odd, seq),
        }

    def greet(self, names):
        barrier = pltpu.get_barrier_semaphore()

        def hail(name):
            pl.semaphore_signal(
                barrier, inc=1, device_id=self.peer[name], device_id_type=pl.DeviceIdType.MESH
            )

        for name in names:
            hail(name)

        @pl.when(self.inner)
        def _():
            hail("middle")

        pl.semaphore_wait(barrier, len(names) + self.inner.astype(jnp.int32))


def add_into(total, addend, step=16):
    def turn(index, carry):
        rows = pl.ds(pl.multiple_of(index * step, step), step)
        total[rows, :] = total[rows, :] + addend[rows, :]
        return carry

    lax.fori_loop(0, total.shape[0] // step, turn, 0)


def add_to(result, former, latter, step=16):
    def turn(index, carry):
        rows = pl.ds(pl.multiple_of(index * step, step), step)
        result[rows, :] = former[rows, :] + latter[rows, :]
        return carry

    lax.fori_loop(0, result.shape[0] // step, turn, 0)


class Chunk:
    def __init__(self, term, offset, rows, columns, gather=False):
        self.term, self.offset, self.rows, self.columns = term, offset, rows, columns
        self.gather = gather

    def scratch(self):
        rows, columns, half = self.rows, self.columns, self.columns // 2
        low = jnp.bfloat16
        four = pltpu.VMEM((2, 2, rows, columns), low)
        one = four if self.gather else pltpu.VMEM((rows, columns), low)
        if self.gather:
            middle = [four]
        else:
            middle = [
                pltpu.VMEM((2, rows, half), low),
                pltpu.VMEM((2, rows, half), low),
                pltpu.VMEM((rows, half), low),
                pltpu.VMEM((rows, half), low),
            ]
        return [four, four] + middle + [one] * 3 + [
            pltpu.SemaphoreType.DMA((9,)),
            pltpu.SemaphoreType.DMA((9,)),
            pltpu.SemaphoreType.DMA((3,)),
        ]

    def bind(self, place, source, result, refs):
        self.place, self.source, self.result = place, source, result
        self.mine, self.core_in = refs[0], refs[1]
        self.middle = refs[2:-6]
        self.z_first, self.z_second, self.z_last = refs[-6:-3]
        self.sent, self.received, self.local = refs[-3:]

    def remote(self, slot, source, target, peer):
        return pltpu.make_async_remote_copy(
            src_ref=source,
            dst_ref=target,
            send_sem=self.sent.at[slot],
            recv_sem=self.received.at[slot],
            device_id=self.place.peer[peer],
            device_id_type=pl.DeviceIdType.MESH,
        )

    def core_copy(self):
        rows = pl.ds(self.offset, self.rows)
        return self.remote(
            0, self.source.at[:, :, 1 - self.place.core, rows, :], self.core_in, "core"
        )

    def load(self):
        rows = pl.ds(self.offset, self.rows)
        return pltpu.make_async_copy(
            self.source.at[:, :, self.place.core, rows, :], self.mine, self.local.at[0]
        )

    def halves(self):
        half = self.columns // 2
        return pl.ds(0, half), pl.ds(half, half)

    def wide_copies(self):
        p, (left, right) = self.place, self.halves()
        if self.gather:
            return [
                self.remote(1, self.mine.at[p.y, 1 - p.x], self.middle[0].at[p.y, p.x], "x"),
                self.remote(2, self.mine.at[1 - p.y, p.x], self.middle[0].at[p.y, p.x], "y"),
                self.remote(3, self.mine.at[1 - p.y, 1 - p.x], self.middle[0].at[p.y, p.x], "xy"),
            ]
        return [
            self.remote(1, self.mine.at[:, 1 - p.x, :, left], self.middle[0], "x"),
            self.remote(2, self.mine.at[1 - p.y, :, :, right], self.middle[1], "y"),
        ]

    def narrow_copies(self):
        p, (left, right) = self.place, self.halves()
        return [
            self.remote(3, self.mine.at[1 - p.y, p.x, :, left], self.middle[2], "y"),
            self.remote(4, self.mine.at[p.y, 1 - p.x, :, right], self.middle[3], "x"),
        ]

    def summed(self):
        return self.middle[0] if self.gather else self.mine.at[self.place.y, self.place.x]

    def pair_copy(self):
        return self.remote(5, self.summed(), self.z_first, "pair")

    def middle_copy(self):
        return self.remote(6, self.summed(), self.z_second, "middle")

    def last_copy(self):
        return self.remote(7, self.z_last, self.z_last, "pair")

    def out_copies(self):
        rows = pl.ds(self.offset, self.rows)
        core = self.place.core
        target = self.result.at[:, :, core, rows, :] if self.gather else self.result.at[core, rows, :]
        return (
            self.remote(8, self.z_last, target, "core"),
            pltpu.make_async_copy(self.z_last, target, self.local.at[1]),
        )

    def parts(self, ref):
        if self.gather:
            return [ref.at[a, b] for a in range(2) for b in range(2)]
        return [ref]

    def stage_start(self):
        self.core_copy().start()
        self.load().start()

    def stage_core(self):
        self.core_copy().wait_recv()
        self.load().wait()
        for a in range(2):
            for b in range(2):
                add_into(self.mine.at[a, b], self.core_in.at[a, b])
        for copy in self.wide_copies():
            copy.start()

    def stage_wide(self):
        p, (left, right) = self.place, self.halves()
        if self.gather:
            stay = pltpu.make_async_copy(
                self.mine.at[p.y, p.x], self.middle[0].at[p.y, p.x], self.local.at[2]
            )
            stay.start()
            for copy in self.wide_copies():
                copy.wait_recv()
            stay.wait()
            self.z_start()
            return
        for copy in self.wide_copies():
            copy.wait_recv()
        for a in range(2):
            add_into(self.mine.at[a, p.x, :, left], self.middle[0].at[a])
            add_into(self.mine.at[p.y, a, :, right], self.middle[1].at[a])
        for copy in self.narrow_copies():
            copy.start()

    def stage_narrow(self):
        p, (left, right) = self.place, self.halves()
        for copy in self.narrow_copies():
            copy.wait_recv()
        add_into(self.mine.at[p.y, p.x, :, left], self.middle[2])
        add_into(self.mine.at[p.y, p.x, :, right], self.middle[3])
        self.z_start()

    def z_start(self):
        @pl.when(self.place.outer)
        def _():
            self.pair_copy().start()

    def stage_pair(self):
        @pl.when(self.place.inner)
        def _():
            self.pair_copy().wait_recv()
            for total, addend in zip(self.parts(self.summed()), self.parts(self.z_first)):
                add_into(total, addend)
            self.middle_copy().start()

    def stage_middle(self):
        @pl.when(self.place.inner)
        def _():
            self.middle_copy().wait_recv()
            for total, former, latter in zip(
                self.parts(self.z_last), self.parts(self.summed()), self.parts(self.z_second)
            ):
                add_to(total, former, latter)
            self.last_copy().start()
            for copy in self.out_copies():
                copy.start()

    def stage_last(self):
        @pl.when(self.place.outer)
        def _():
            self.last_copy().wait_recv()
            for copy in self.out_copies():
                copy.start()

    def stage_end(self):
        remote_out, local_out = self.out_copies()
        remote_out.wait()
        local_out.wait()
        self.core_copy().wait_send()
        for copy in self.wide_copies():
            copy.wait_send()
        if not self.gather:
            for copy in self.narrow_copies():
                copy.wait_send()

        @pl.when(self.place.outer)
        def _():
            self.pair_copy().wait_send()

        @pl.when(self.place.inner)
        def _():
            self.middle_copy().wait_send()
            self.last_copy().wait_send()

    def plan(self):
        piece = 2 * self.rows * self.columns
        if self.gather:
            return [
                (self.stage_core, [("x", 1.5 * piece), ("y", 1.5 * piece)]),
                (self.stage_wide, [("z", 4 * piece)]),
                (self.stage_pair, [("z", 4 * piece)]),
                (self.stage_middle, [("z", 4 * piece)]),
                (self.stage_last, [("core", 4 * piece)]),
                (self.stage_end, []),
            ]
        return [
            (self.stage_core, [("x", piece), ("y", piece)]),
            (self.stage_wide, [("x", piece / 2), ("y", piece / 2)]),
            (self.stage_narrow, [("z1", piece)]),
            (self.stage_pair, [("z2", piece)]),
            (self.stage_middle, [("z3", piece)]),
            (self.stage_last, [("core", piece)]),
            (self.stage_end, []),
        ]

    def opening(self):
        return [("core", 8 * self.rows * self.columns)]


class RowChunk:
    def __init__(self, term, offset, rows, columns):
        self.term, self.offset, self.rows, self.columns = term, offset, rows, columns

    def scratch(self):
        rows, columns, half = self.rows, self.columns, self.columns // 2
        low = jnp.bfloat16
        return [
            pltpu.VMEM((2, 2, rows, columns), low),
            pltpu.VMEM((2, rows, half), low),
            pltpu.VMEM((2, rows, half), low),
            pltpu.VMEM((rows, half), low),
            pltpu.VMEM((rows, half), low),
            pltpu.SemaphoreType.DMA((4,)),
            pltpu.SemaphoreType.DMA((4,)),
            pltpu.SemaphoreType.DMA((2,)),
        ]

    def bind(self, place, source, result, refs):
        self.place, self.source, self.result = place, source, result
        self.mine, self.middle = refs[0], refs[1:5]
        self.sent, self.received, self.local = refs[5:]

    remote = Chunk.remote
    halves = Chunk.halves

    def load(self):
        rows = pl.ds(self.offset, self.rows)
        return pltpu.make_async_copy(self.source.at[:, :, rows, :], self.mine, self.local.at[0])

    def wide_copies(self):
        p, (left, right) = self.place, self.halves()
        return [
            self.remote(0, self.mine.at[:, 1 - p.x, :, left], self.middle[0], "x"),
            self.remote(1, self.mine.at[1 - p.y, :, :, right], self.middle[1], "y"),
        ]

    def narrow_copies(self):
        p, (left, right) = self.place, self.halves()
        return [
            self.remote(2, self.mine.at[1 - p.y, p.x, :, left], self.middle[2], "y"),
            self.remote(3, self.mine.at[p.y, 1 - p.x, :, right], self.middle[3], "x"),
        ]

    def out_copy(self):
        p = self.place
        return pltpu.make_async_copy(
            self.mine.at[p.y, p.x], self.result.at[pl.ds(self.offset, self.rows), :], self.local.at[1]
        )

    def stage_start(self):
        self.load().start()

    def stage_load(self):
        self.load().wait()
        for copy in self.wide_copies():
            copy.start()

    def stage_wide(self):
        p, (left, right) = self.place, self.halves()
        for copy in self.wide_copies():
            copy.wait_recv()
        for a in range(2):
            add_into(self.mine.at[a, p.x, :, left], self.middle[0].at[a])
            add_into(self.mine.at[p.y, a, :, right], self.middle[1].at[a])
        for copy in self.narrow_copies():
            copy.start()

    def stage_narrow(self):
        p, (left, right) = self.place, self.halves()
        for copy in self.narrow_copies():
            copy.wait_recv()
        add_into(self.mine.at[p.y, p.x, :, left], self.middle[2])
        add_into(self.mine.at[p.y, p.x, :, right], self.middle[3])
        self.out_copy().start()

    def stage_end(self):
        self.out_copy().wait()
        for copy in self.wide_copies() + self.narrow_copies():
            copy.wait_send()

    def plan(self):
        piece = 2 * self.rows * self.columns
        return [
            (self.stage_load, [("x", piece), ("y", piece)]),
            (self.stage_wide, [("x", piece / 2), ("y", piece / 2)]),
            (self.stage_narrow, [("core", 0.0)]),
            (self.stage_end, []),
        ]

    def opening(self):
        return [("core", 0.0)]


def stage_order(chunks):
    free, ready, order = {}, [], []

    def send(transfers, now):
        ends = [now]
        for link, size in transfers:
            start = max(now, free.get(link, 0.0))
            free[link] = start + size / LINK_RATE.get(link, LINK_RATE["z"])
            ends.append(free[link] + 2.0)
        return max(ends)

    for number, chunk in enumerate(chunks):
        ready.append((send(chunk.opening(), 0.0), number, 0))
    now = 0.0
    while ready:
        ready.sort()
        when, number, index = ready.pop(0)
        now = max(now, when) + 0.3
        stage, transfers = chunks[number].plan()[index]
        order.append((now, stage))
        if index + 1 < len(chunks[number].plan()):
            ready.append((send(transfers, now), number, index + 1))
    return order


def bind_chunks(chunks, place, sources, results, refs):
    used = 0
    for chunk in chunks:
        count = len(chunk.scratch())
        chunk.bind(place, sources[chunk.term], results[chunk.term], refs[used : used + count])
        used += count


def exchange_kernel(chunks, peers, count, *refs):
    sources, results = refs[:count], refs[count : 2 * count]
    place = Place()
    bind_chunks(chunks, place, sources, results, refs[2 * count :])
    place.greet(peers)
    for chunk in chunks:
        chunk.stage_start()
    for _, stage in stage_order(chunks):
        stage()


def exchange(chunks, terms, shapes, collective_id, name):
    anywhere = pl.BlockSpec(memory_space=pl.ANY)
    return pl.pallas_call(
        functools.partial(exchange_kernel, chunks, ("core", "x", "y", "xy", "pair"), len(terms)),
        in_specs=[anywhere] * len(terms),
        out_specs=[anywhere] * len(terms),
        out_shape=[jax.ShapeDtypeStruct(shape, jnp.bfloat16) for shape in shapes],
        scratch_shapes=[ref for chunk in chunks for ref in chunk.scratch()],
        compiler_params=pltpu.CompilerParams(
            collective_id=collective_id, has_side_effects=True, vmem_limit_bytes=VMEM_BYTES
        ),
        name=name,
    )(*terms)


def norm_input_grad(values, inverse, norm_gain, upstream):
    weighted = upstream * norm_gain
    inner_mean = jnp.mean(weighted * values, axis=-1, keepdims=True)
    return inverse * weighted - inverse * inverse * inverse * values * inner_mean


def head_plan(
    seg_size,
    seq_size,
    layer_input,
    output_grad,
    norm1_gain,
    norm2_gain,
    w_qkv,
    w_out,
    w_gate,
    w_up,
    w_down,
    mem_keys,
    mem_values,
    memory_flags,
    sources,
):
    seg_index = lax.axis_index("seg")
    seq_index = lax.axis_index("seq")
    tokens = layer_input.shape[1]
    length = tokens * seq_size
    width = D // seq_size
    flag = lax.dynamic_index_in_dim(memory_flags, seg_index, 0, keepdims=True)
    listed = lax.dynamic_index_in_dim(sources, seg_index, 0, keepdims=False)
    chosen = jnp.concatenate([jnp.reshape(seg_index, (1,)), listed, flag]).astype(jnp.int32)

    mem_rows = mem_keys.shape[1]
    both = jnp.concatenate(
        [mem_keys[0].reshape(mem_rows, seq_size, width), mem_values[0].reshape(mem_rows, seq_size, width)],
        axis=2,
    ).reshape(mem_rows, 2 * D)
    own_memory = lax.all_to_all(both, "seq", 1, 0, tiled=True)
    memory = lax.all_gather(own_memory, "seg", axis=0)

    inputs = layer_input[0].astype(jnp.float32)
    first_norm, first_inverse = norm_forward(inputs, norm1_gain)
    first_low = first_norm.astype(jnp.bfloat16)
    every_low = lax.all_gather(first_low, "seq", axis=0, tiled=True)
    w_heads = lax.dynamic_index_in_dim(
        w_qkv.reshape(D, 3, seq_size, width), seq_index, 2, keepdims=False
    ).reshape(D, 3 * width)
    cosine, sine = turn_tables(lax.iota(jnp.int32, length).astype(jnp.float32))
    cosine, sine = cosine[:, 0, :], sine[:, 0, :]
    first_half = lax.broadcasted_iota(jnp.int32, sine.shape, 1) < HEAD_DIM // 2
    sine = jnp.where(first_half, -sine, sine)
    queries, keys, values = project(every_low, w_heads, cosine, sine)

    mixed, row_max, row_sum = own_forward(queries, keys, values)
    heads_low, heads_out, log_totals = memory_forward(
        chosen, queries, mixed, row_max, row_sum, memory
    )
    attended_low = lax.all_to_all(heads_low, "seq", 0, 1, tiled=True)

    residual = inputs + product(attended_low, w_out)
    second_norm, second_inverse = norm_forward(residual, norm2_gain)
    second_low = second_norm.astype(jnp.bfloat16)
    gate_values = product(second_low, w_gate)
    up_values = product(second_low, w_up)
    sigmoid_gate = jax.nn.sigmoid(gate_values)
    activated = gate_values * sigmoid_gate
    hidden_low = (activated * up_values).astype(jnp.bfloat16)
    output = (residual + product(hidden_low, w_down)).astype(jnp.bfloat16)
    upstream = output_grad[0]
    low = jnp.bfloat16
    term_down = product_tn(hidden_low, upstream).astype(low)
    grad_hidden = product_nt(upstream, w_down)
    grad_gate_low = (
        grad_hidden * up_values * sigmoid_gate * (1.0 + gate_values * (1.0 - sigmoid_gate))
    ).astype(low)
    grad_up_low = (grad_hidden * activated).astype(low)
    term_gate = product_tn(second_low, grad_gate_low).astype(low)
    term_up = product_tn(second_low, grad_up_low).astype(low)
    grad_second = product_nt(grad_gate_low, w_gate) + product_nt(grad_up_low, w_up)
    grad_residual = norm_input_grad(residual, second_inverse, norm2_gain, grad_second)
    grad_residual = grad_residual + upstream.astype(jnp.float32)
    residual_low = grad_residual.astype(low)
    term_out = product_tn(attended_low, residual_low).astype(low)
    grad_attended = product_nt(residual_low, w_out).astype(low)
    grad_heads = lax.all_to_all(grad_attended, "seq", 1, 0, tiled=True)

    start, delta = memory_backward(chosen, queries, grad_heads, heads_out, log_totals, memory)
    grad_projected = own_backward(
        queries, keys, values, grad_heads, log_totals, delta, start, cosine, sine
    )
    terms = [term_down, term_gate, term_up, term_out]
    pieces = [(term.shape[0] // (2 * seq_size), term.shape[1]) for term in terms]
    chunks = []
    for index, (rows, columns) in enumerate(pieces):
        parts = 2 if rows % 32 == 0 and index < 3 else 1
        chunks += [Chunk(index, n * rows // parts, rows // parts, columns) for n in range(parts)]
    sums = exchange(
        chunks,
        [term.reshape((2, 2, 2) + piece) for term, piece in zip(terms, pieces)],
        [(2,) + piece for piece in pieces],
        1,
        "sum_terms",
    )
    grad_down, grad_gate, grad_up, grad_out = [
        total.reshape(2 * piece[0], piece[1]).astype(jnp.float32) for total, piece in zip(sums, pieces)
    ]

    part_first = product_nt(grad_projected, w_heads).astype(low)
    part_qkv = product_tn(every_low, grad_projected).astype(low)
    rows = D // (2 * seq_size)
    qkv_rows, first_rows = exchange(
        [Chunk(0, n * rows // 2, rows // 2, 3 * width, True) for n in range(2)]
        + [RowChunk(1, n * tokens // 4, tokens // 4, D) for n in range(4)],
        [part_qkv.reshape(2, 2, 2, rows, 3 * width), part_first.reshape(2, 2, tokens, D)],
        [(2, 2, 2, rows, 3 * width), (tokens, D)],
        2,
        "sum_first",
    )
    grad_qkv = jnp.transpose(
        qkv_rows.reshape(seq_size, 2 * rows, 3, width), (1, 2, 0, 3)
    ).reshape(2 * rows, 3 * D).astype(jnp.float32)
    grad_inputs = norm_input_grad(
        inputs, first_inverse, norm1_gain, first_rows.astype(jnp.float32)
    )
    input_grad = (grad_inputs + grad_residual)[None]

    def row_block(whole):
        return lax.dynamic_slice_in_dim(whole, seq_index * width, width, 0)

    def gain_rows(weights, grads, gain):
        dots = [
            jnp.sum(row_block(weight).astype(jnp.float32) * grad, axis=1)
            for weight, grad in zip(weights, grads)
        ]
        return sum(dots[1:], dots[0]) / row_block(gain)

    grad_norm1 = gain_rows([w_qkv], [grad_qkv], norm1_gain)
    grad_norm2 = gain_rows([w_gate, w_up], [grad_gate, grad_up], norm2_gain)
    return (
        output[None],
        input_grad,
        grad_norm1,
        grad_norm2,
        grad_qkv,
        grad_out,
        grad_gate,
        grad_up,
        grad_down,
    )


def solution(mesh):
    seq_size = mesh.shape["seq"]
    heads_fit = seq_size == 4 and mesh.shape["seg"] == 8
    plan = functools.partial(head_plan, mesh.shape["seg"], seq_size) if heads_fit else general_plan
    placed = (
        P("seg", "seq", None),
        P("seg", "seq", None),
        P(),
        P(),
        P(),
        P(),
        P(),
        P(),
        P(),
        P("seg", "seq", None),
        P("seg", "seq", None),
        P(),
        P(),
    )
    return jax.shard_map(
        plan,
        mesh=mesh,
        in_specs=placed,
        out_specs=(
            P("seg", "seq", None),
            P("seg", "seq", None),
            P("seq"),
            P("seq"),
            P("seq", None),
            P("seq", None),
            P("seq", None),
            P("seq", None),
            P("seq", None),
        ),
        check_vma=False,
    )
```

```python
import functools
import math

import jax
import jax.numpy as jnp
from jax import lax
from jax.experimental import pallas as pl
from jax.experimental.pallas import tpu as pltpu
from jax.sharding import PartitionSpec as P

D = 1024
HEADS = 8
HEAD_DIM = 128


masked_score = -1e30
epsilon = 1e-06
rotary_base = 10000.0


def product(former, latter):
    return jnp.dot(former, latter, preferred_element_type=jnp.float32)


def product_nt(former, latter):
    return lax.dot_general(
        former, latter, (((1,), (1,)), ((), ())), preferred_element_type=jnp.float32
    )


def product_tn(former, latter):
    return lax.dot_general(
        former, latter, (((0,), (0,)), ((), ())), preferred_element_type=jnp.float32
    )


def norm_forward(values, norm_gain):
    inverse = lax.rsqrt(jnp.mean(values * values, axis=-1, keepdims=True) + epsilon)
    return (values * inverse * norm_gain, inverse)


def norm_backward(values, inverse, norm_gain, upstream):
    weighted = upstream * norm_gain
    inner_mean = jnp.mean(weighted * values, axis=-1, keepdims=True)
    grad_values = inverse * weighted - inverse * inverse * inverse * values * inner_mean
    grad_gain = jnp.sum(upstream * values * inverse, axis=0)
    return (grad_values, grad_gain)


def turn_tables(positions):
    half_dim = HEAD_DIM // 2
    exponent = -2.0 * jnp.arange(half_dim, dtype=jnp.float32) / HEAD_DIM
    angles = positions[:, None] * jnp.power(rotary_base, exponent)[None, :]
    angles = jnp.concatenate([angles, angles], axis=1)
    return (jnp.cos(angles)[:, None, :], jnp.sin(angles)[:, None, :])


def rotate(matrix, cosine_table, sine_table, direction):
    row_count = matrix.shape[0]
    half_dim = HEAD_DIM // 2
    shaped = matrix.reshape(row_count, HEADS, HEAD_DIM)
    turned = jnp.concatenate([-shaped[..., half_dim:], shaped[..., :half_dim]], axis=-1)
    return (shaped * cosine_table + direction * turned * sine_table).reshape(
        row_count, HEADS * HEAD_DIM
    )


def general_plan(
    layer_input,
    output_grad,
    norm1_gain,
    norm2_gain,
    w_qkv,
    w_out,
    w_gate,
    w_up,
    w_down,
    mem_keys,
    mem_values,
    memory_flags,
    sources,
):
    seg_index = lax.axis_index("seg")
    seq_index = lax.axis_index("seq")
    tokens = layer_input.shape[1]
    score_scale = HEAD_DIM ** (-0.5)
    flag_on = lax.dynamic_index_in_dim(memory_flags, seg_index, 0, keepdims=False) > 0
    listed = lax.dynamic_index_in_dim(sources, seg_index, 0, keepdims=False)
    picked = jnp.concatenate([jnp.reshape(seg_index, (1,)), listed])
    every_keys, every_values = (
        lax.all_gather(mem_keys, "seg", axis=0, tiled=True),
        lax.all_gather(mem_values, "seg", axis=0, tiled=True),
    )
    chosen_keys = jnp.take(every_keys, picked, axis=0)
    chosen_values = jnp.take(every_values, picked, axis=0)
    memory_keys, memory_values = (
        lax.all_gather(chosen_keys, "seq", axis=1, tiled=True),
        lax.all_gather(chosen_values, "seq", axis=1, tiled=True),
    )
    memory_key_blocks = memory_keys.reshape(-1, tokens, HEADS, HEAD_DIM)
    memory_value_blocks = memory_values.reshape(-1, tokens, HEADS, HEAD_DIM)
    memory_blocks = memory_key_blocks.shape[0]
    inputs = layer_input[0].astype(jnp.float32)
    first_norm, first_inverse = norm_forward(inputs, norm1_gain)
    first_low = first_norm.astype(jnp.bfloat16)
    projected = product(first_low, w_qkv)
    positions = seq_index * tokens + lax.iota(jnp.int32, tokens)
    cosine_table, sine_table = turn_tables(positions.astype(jnp.float32))
    queries = rotate(projected[:, :D], cosine_table, sine_table, 1.0).astype(jnp.bfloat16)
    own_keys = rotate(projected[:, D : 2 * D], cosine_table, sine_table, 1.0).astype(jnp.bfloat16)
    own_values = projected[:, 2 * D :].astype(jnp.bfloat16)
    all_keys, all_values = (
        lax.all_gather(own_keys, "seq", axis=0, tiled=True),
        lax.all_gather(own_values, "seq", axis=0, tiled=True),
    )
    key_blocks = all_keys.reshape(-1, tokens, HEADS, HEAD_DIM)
    value_blocks = all_values.reshape(-1, tokens, HEADS, HEAD_DIM)
    query_heads = queries.reshape(tokens, HEADS, HEAD_DIM)
    memory_open = jnp.broadcast_to(flag_on, (tokens, tokens))
    own_count = seq_index + 1
    key_offsets = lax.iota(jnp.int32, tokens)

    def own_open(block):
        return (block * tokens + key_offsets)[None, :] <= positions[:, None]

    def block_scores(key_block, open_mask):
        raw = (
            jnp.einsum("qhd,khd->hqk", query_heads, key_block, preferred_element_type=jnp.float32)
            * score_scale
        )
        return jnp.where(open_mask[None], raw, masked_score)

    def sweep(step, carry):

        def memory_turn(block, state):
            return step(
                state,
                block,
                memory_key_blocks[block],
                memory_value_blocks[block],
                memory_open,
                False,
            )

        def own_turn(block, state):
            return step(state, block, key_blocks[block], value_blocks[block], own_open(block), True)

        carry = lax.fori_loop(0, memory_blocks, memory_turn, carry)
        return lax.fori_loop(0, own_count, own_turn, carry)

    def max_step(carry, block, key_block, value_block, open_mask, own):
        row_max, row_sum = carry
        scores = block_scores(key_block, open_mask)
        new_max = jnp.maximum(row_max, jnp.max(scores, axis=2))
        row_sum = row_sum * jnp.exp(row_max - new_max) + jnp.sum(
            jnp.exp(scores - new_max[..., None]), axis=2
        )
        return (new_max, row_sum)

    start_max = jnp.full((HEADS, tokens), masked_score, jnp.float32)
    row_max, row_sum = sweep(max_step, (start_max, jnp.zeros((HEADS, tokens), jnp.float32)))
    log_totals = row_max + jnp.log(row_sum)

    def mix_step(total, block, key_block, value_block, open_mask, own):
        weights_low = jnp.exp(block_scores(key_block, open_mask) - log_totals[..., None]).astype(
            jnp.bfloat16
        )
        return total + jnp.einsum(
            "hqk,khd->qhd", weights_low, value_block, preferred_element_type=jnp.float32
        )

    attended = sweep(mix_step, jnp.zeros((tokens, HEADS, HEAD_DIM), jnp.float32))
    attended_low = attended.reshape(tokens, D).astype(jnp.bfloat16)
    residual = inputs + product(attended_low, w_out)
    second_norm, second_inverse = norm_forward(residual, norm2_gain)
    second_low = second_norm.astype(jnp.bfloat16)
    gate_values = product(second_low, w_gate)
    up_values = product(second_low, w_up)
    sigmoid_gate = jax.nn.sigmoid(gate_values)
    activated = gate_values * sigmoid_gate
    hidden_low = (activated * up_values).astype(jnp.bfloat16)
    output = (residual + product(hidden_low, w_down)).astype(jnp.bfloat16)
    upstream = output_grad[0]
    grad_down = product_tn(hidden_low, upstream)
    grad_hidden = product_nt(upstream, w_down)
    grad_gate_low = (
        grad_hidden * up_values * sigmoid_gate * (1.0 + gate_values * (1.0 - sigmoid_gate))
    ).astype(jnp.bfloat16)
    grad_up_low = (grad_hidden * activated).astype(jnp.bfloat16)
    grad_gate = product_tn(second_low, grad_gate_low)
    grad_up = product_tn(second_low, grad_up_low)
    grad_second = product_nt(grad_gate_low, w_gate) + product_nt(grad_up_low, w_up)
    grad_residual, grad_norm2 = norm_backward(residual, second_inverse, norm2_gain, grad_second)
    grad_residual = grad_residual + upstream.astype(jnp.float32)
    residual_low = grad_residual.astype(jnp.bfloat16)
    grad_out = product_tn(attended_low, residual_low)
    grad_attended = product_nt(residual_low, w_out).astype(jnp.bfloat16)
    grad_heads = grad_attended.reshape(tokens, HEADS, HEAD_DIM)

    def probs_pair(key_block, value_block, open_mask):
        probs = jnp.exp(block_scores(key_block, open_mask) - log_totals[..., None])
        dprobs = jnp.einsum(
            "qhd,khd->hqk", grad_heads, value_block, preferred_element_type=jnp.float32
        )
        return (probs, dprobs)

    def delta_step(total, block, key_block, value_block, open_mask, own):
        probs, dprobs = probs_pair(key_block, value_block, open_mask)
        return total + jnp.sum(probs * dprobs, axis=2)

    delta_rows = sweep(delta_step, jnp.zeros((HEADS, tokens), jnp.float32))

    def grad_step(carry, block, key_block, value_block, open_mask, own):
        grad_query, key_terms, value_terms = carry
        probs, dprobs = probs_pair(key_block, value_block, open_mask)
        dscores = (probs * (dprobs - delta_rows[..., None])).astype(jnp.bfloat16)
        grad_query = grad_query + jnp.einsum(
            "hqk,khd->qhd", dscores, key_block, preferred_element_type=jnp.float32
        )
        if own:
            key_part = (
                jnp.einsum("hqk,qhd->khd", dscores, query_heads, preferred_element_type=jnp.float32)
                * score_scale
            )
            value_part = jnp.einsum(
                "hqk,qhd->khd",
                probs.astype(jnp.bfloat16),
                grad_heads,
                preferred_element_type=jnp.float32,
            )
            key_terms = lax.dynamic_update_index_in_dim(key_terms, key_part, block, 0)
            value_terms = lax.dynamic_update_index_in_dim(value_terms, value_part, block, 0)
        return (grad_query, key_terms, value_terms)

    term_shape = key_blocks.shape
    start_grads = (
        jnp.zeros((tokens, HEADS, HEAD_DIM), jnp.float32),
        jnp.zeros(term_shape, jnp.float32),
        jnp.zeros(term_shape, jnp.float32),
    )
    grad_query, key_terms, value_terms = sweep(grad_step, start_grads)
    grad_queries = (grad_query * score_scale).reshape(tokens, D)
    grad_keys, grad_values = (
        lax.psum_scatter(
            key_terms.astype(jnp.bfloat16), "seq", scatter_dimension=0, tiled=True
        ).astype(jnp.float32),
        lax.psum_scatter(
            value_terms.astype(jnp.bfloat16), "seq", scatter_dimension=0, tiled=True
        ).astype(jnp.float32),
    )
    grad_projected = jnp.concatenate(
        [
            rotate(grad_queries, cosine_table, sine_table, -1.0),
            rotate(grad_keys.reshape(tokens, D), cosine_table, sine_table, -1.0),
            grad_values.reshape(tokens, D),
        ],
        axis=1,
    ).astype(jnp.bfloat16)
    grad_qkv = product_tn(first_low, grad_projected)
    grad_first = product_nt(grad_projected, w_qkv)
    grad_inputs, grad_norm1 = norm_backward(inputs, first_inverse, norm1_gain, grad_first)
    input_grad = (grad_inputs + grad_residual)[None]
    shares = (
        lax.psum_scatter(
            grad_norm1.astype(jnp.bfloat16), "seq", scatter_dimension=0, tiled=True
        ).astype(jnp.float32),
        lax.psum_scatter(
            grad_norm2.astype(jnp.bfloat16), "seq", scatter_dimension=0, tiled=True
        ).astype(jnp.float32),
        lax.psum_scatter(
            grad_qkv.astype(jnp.bfloat16), "seq", scatter_dimension=0, tiled=True
        ).astype(jnp.float32),
        lax.psum_scatter(
            grad_out.astype(jnp.bfloat16), "seq", scatter_dimension=0, tiled=True
        ).astype(jnp.float32),
        lax.psum_scatter(
            grad_gate.astype(jnp.bfloat16), "seq", scatter_dimension=0, tiled=True
        ).astype(jnp.float32),
        lax.psum_scatter(
            grad_up.astype(jnp.bfloat16), "seq", scatter_dimension=0, tiled=True
        ).astype(jnp.float32),
        lax.psum_scatter(
            grad_down.astype(jnp.bfloat16), "seq", scatter_dimension=0, tiled=True
        ).astype(jnp.float32),
    )
    totals = (
        lax.psum(shares[0].astype(jnp.bfloat16), "seg").astype(jnp.float32),
        lax.psum(shares[1].astype(jnp.bfloat16), "seg").astype(jnp.float32),
        lax.psum(shares[2].astype(jnp.bfloat16), "seg").astype(jnp.float32),
        lax.psum(shares[3].astype(jnp.bfloat16), "seg").astype(jnp.float32),
        lax.psum(shares[4].astype(jnp.bfloat16), "seg").astype(jnp.float32),
        lax.psum(shares[5].astype(jnp.bfloat16), "seg").astype(jnp.float32),
        lax.psum(shares[6].astype(jnp.bfloat16), "seg").astype(jnp.float32),
    )
    return (
        output[None],
        input_grad,
        totals[0],
        totals[1],
        totals[2],
        totals[3],
        totals[4],
        totals[5],
        totals[6],
    )


VMEM_BYTES = 60 * 1024 * 1024
LN2 = math.log(2.0)
SCORE_SCALE = HEAD_DIM ** (-0.5)


def lane_fold(op, tile, running):
    for column in range(tile.shape[1] // HEAD_DIM):
        piece = tile[:, column * HEAD_DIM : (column + 1) * HEAD_DIM]
        running = piece if running is None else op(running, piece)
    return running


def causal(scores):
    rows = lax.broadcasted_iota(jnp.int32, scores.shape, 0)
    columns = lax.broadcasted_iota(jnp.int32, scores.shape, 1)
    return jnp.where(columns <= rows, scores, masked_score)


def attend(query, pairs, diagonal, carried):
    every, lane_max = [], None
    for index, (keys, _) in enumerate(pairs):
        scores = product_nt(query, keys)
        if diagonal and index == len(pairs) - 1:
            scores = causal(scores)
        lane_max = lane_fold(jnp.maximum, scores, lane_max)
        every.append(scores)
    row_max = jnp.max(lane_max, axis=1, keepdims=True)
    if carried is not None:
        row_max = jnp.maximum(row_max, carried[0])
    lane_sum, mixed = None, None
    for scores, (_, values) in zip(every, pairs):
        probs = jnp.exp2(scores - row_max)
        lane_sum = lane_fold(jnp.add, probs, lane_sum)
        part = product(probs.astype(jnp.bfloat16), values)
        mixed = part if mixed is None else mixed + part
    row_sum = jnp.sum(lane_sum, axis=1, keepdims=True)
    if carried is not None:
        shrink = jnp.exp2(carried[0] - row_max)
        row_sum = carried[1] * shrink + row_sum
        mixed = carried[2] * shrink + mixed
    return row_max, row_sum, mixed


def memory_specs(heads, rows, count):
    specs = []
    for slot in range(count):
        specs.append(
            pl.BlockSpec((1, rows, HEAD_DIM), lambda h, i, chosen, slot=slot: (chosen[slot], 0, h))
        )
        specs.append(
            pl.BlockSpec(
                (1, rows, HEAD_DIM), lambda h, i, chosen, slot=slot: (chosen[slot], 0, heads + h)
            )
        )
    return specs


def memory_forward_kernel(count, chosen, q_ref, mix_ref, max_ref, sum_ref, *rest):
    blocks = rest[: 2 * count]
    low_ref, out_ref, log_ref = rest[2 * count :]
    carried = (max_ref[:, :1], sum_ref[:, :1], mix_ref[...])

    def finish(row_max, row_sum, mixed):
        out = mixed * (1.0 / row_sum)
        out_ref[...] = out
        low_ref[...] = out.astype(jnp.bfloat16)
        log_ref[...] = jnp.broadcast_to(row_max + jnp.log2(row_sum), log_ref.shape)

    @pl.when(chosen[count] > 0)
    def _():
        pairs = [(blocks[2 * n][0], blocks[2 * n + 1][0]) for n in range(count)]
        finish(*attend(q_ref[...], pairs, False, carried))

    @pl.when(chosen[count] <= 0)
    def _():
        finish(*carried)


def memory_forward(chosen, queries, mixed, row_max, row_sum, memory, rows=512):
    length, width = queries.shape
    heads, count = width // HEAD_DIM, chosen.shape[0] - 1
    block = pl.BlockSpec((rows, HEAD_DIM), lambda h, i, chosen: (i, h))
    pairs = heads * length * count * memory.shape[1]
    return pl.pallas_call(
        functools.partial(memory_forward_kernel, count),
        grid_spec=pltpu.PrefetchScalarGridSpec(
            num_scalar_prefetch=1,
            grid=(heads, length // rows),
            in_specs=[block] * 4 + memory_specs(heads, memory.shape[1], count),
            out_specs=[block] * 3,
        ),
        out_shape=[
            jax.ShapeDtypeStruct((length, width), jnp.bfloat16),
            jax.ShapeDtypeStruct((length, width), jnp.float32),
            jax.ShapeDtypeStruct((length, width), jnp.float32),
        ],
        compiler_params=pltpu.CompilerParams(vmem_limit_bytes=VMEM_BYTES),
        cost_estimate=pl.CostEstimate(
            flops=8 * pairs * HEAD_DIM, transcendentals=pairs, bytes_accessed=36 * length * width
        ),
        name="memory_forward",
    )(chosen, queries, mixed, row_max, row_sum, *[memory] * (2 * count))


def memory_backward_kernel(count, tile, chosen, q_ref, g_ref, out_ref, log_ref, *rest):
    blocks = rest[: 2 * count]
    dq_ref, delta_ref = rest[2 * count :]
    query, upstream = q_ref[...], g_ref[...]
    delta = jnp.sum(upstream.astype(jnp.float32) * out_ref[...], axis=1, keepdims=True)
    delta_ref[...] = jnp.broadcast_to(delta, delta_ref.shape)
    log_total = log_ref[:, :1]

    @pl.when(chosen[count] > 0)
    def _():
        total = jnp.zeros(dq_ref.shape, jnp.float32)
        for n in range(count):
            for start in range(0, blocks[0].shape[1], tile):
                keys = blocks[2 * n][0, start : start + tile, :]
                values = blocks[2 * n + 1][0, start : start + tile, :]
                probs = jnp.exp2(product_nt(query, keys) - log_total)
                dscores = probs * (product_nt(upstream, values) - delta)
                total = total + product(dscores.astype(jnp.bfloat16), keys)
        dq_ref[...] = total

    @pl.when(chosen[count] <= 0)
    def _():
        dq_ref[...] = jnp.zeros(dq_ref.shape, jnp.float32)


def memory_backward(chosen, queries, upstream, out, log_totals, memory, rows=512, tile=512):
    length, width = queries.shape
    heads, count = width // HEAD_DIM, chosen.shape[0] - 1
    block = pl.BlockSpec((rows, HEAD_DIM), lambda h, i, chosen: (i, h))
    pairs = heads * length * count * memory.shape[1]
    return pl.pallas_call(
        functools.partial(memory_backward_kernel, count, math.gcd(tile, memory.shape[1])),
        grid_spec=pltpu.PrefetchScalarGridSpec(
            num_scalar_prefetch=1,
            grid=(heads, length // rows),
            in_specs=[block] * 4 + memory_specs(heads, memory.shape[1], count),
            out_specs=[block] * 2,
        ),
        out_shape=[jax.ShapeDtypeStruct((length, width), jnp.float32)] * 2,
        compiler_params=pltpu.CompilerParams(vmem_limit_bytes=VMEM_BYTES),
        cost_estimate=pl.CostEstimate(
            flops=12 * pairs * HEAD_DIM, transcendentals=pairs, bytes_accessed=36 * length * width
        ),
        name="memory_backward",
    )(chosen, queries, upstream, out, log_totals, *[memory] * (2 * count))


def own_backward_kernel(
    rows, heads, q_ref, k_ref, v_ref, g_ref, log_ref, delta_ref, start_ref, cos_ref, sin_ref, d_ref, dk, dv
):
    head, block = pl.program_id(0), pl.program_id(1)

    def lanes(part):
        return pl.ds(pl.multiple_of((part * heads + head) * HEAD_DIM, HEAD_DIM), HEAD_DIM)

    @pl.when(block == 0)
    def _():
        dk[...] = jnp.zeros_like(dk)
        dv[...] = jnp.zeros_like(dv)

    query, upstream = q_ref[...], g_ref[...]
    log_total, delta = log_ref[:, :1], delta_ref[:, :1]

    def turn(other, total, diagonal):
        span = pl.ds(pl.multiple_of(other * rows, rows), rows)
        keys = k_ref[span, :]
        scores = product_nt(query, keys)
        if diagonal:
            scores = causal(scores)
        probs = jnp.exp2(scores - log_total)
        dscores = (probs * (product_nt(upstream, v_ref[span, :]) - delta)).astype(jnp.bfloat16)
        dv[span, :] += product_tn(probs.astype(jnp.bfloat16), upstream)
        dk[span, :] += product_tn(dscores, query)
        return total + product(dscores, keys)

    total = turn(block, start_ref[...], True)
    total = lax.fori_loop(0, block, lambda other, total: turn(other, total, False), total)
    mine = pl.ds(pl.multiple_of(block * rows, rows), rows)
    d_ref[mine, lanes(0)] = turn_block(
        total * SCORE_SCALE, cos_ref[mine, :], -sin_ref[mine, :]
    ).astype(jnp.bfloat16)

    @pl.when(block == pl.num_programs(1) - 1)
    def _():
        d_ref[:, lanes(1)] = turn_block(dk[...] * LN2, cos_ref[...], -sin_ref[...]).astype(
            jnp.bfloat16
        )
        d_ref[:, lanes(2)] = dv[...].astype(jnp.bfloat16)


def own_backward(
    queries, keys, values, upstream, log_totals, delta, start, cosine, sine, rows=512
):
    length, width = queries.shape
    block = pl.BlockSpec((rows, HEAD_DIM), lambda h, i: (i, h))
    whole = pl.BlockSpec((length, HEAD_DIM), lambda h, i: (0, h))
    table = pl.BlockSpec((length, HEAD_DIM), lambda h, i: (0, 0))
    heads = width // HEAD_DIM
    pairs = heads * length * length // 2
    return pl.pallas_call(
        functools.partial(own_backward_kernel, rows, heads),
        grid=(heads, length // rows),
        in_specs=[block, whole, whole, block, block, block, block, table, table],
        out_specs=pl.BlockSpec((length, 3 * width), lambda h, i: (0, 0)),
        out_shape=jax.ShapeDtypeStruct((length, 3 * width), jnp.bfloat16),
        scratch_shapes=[pltpu.VMEM((length, HEAD_DIM), jnp.float32)] * 2,
        compiler_params=pltpu.CompilerParams(vmem_limit_bytes=VMEM_BYTES),
        cost_estimate=pl.CostEstimate(
            flops=20 * pairs * HEAD_DIM, transcendentals=pairs, bytes_accessed=36 * length * width
        ),
        name="own_backward",
    )(queries, keys, values, upstream, log_totals, delta, start, cosine, sine)


def turn_block(matrix, cosine, sine):
    return matrix * cosine + pltpu.roll(matrix, HEAD_DIM // 2, 1) * sine


LINK_RATE = {"core": 300e3, "x": 45e3, "y": 45e3, "z": 45e3}


class Place:
    def __init__(self):
        seg, seq = lax.axis_index("seg"), lax.axis_index("seq")
        self.core, self.z = lax.rem(seg, 2), lax.div(seg, 2)
        self.x, self.y = lax.rem(seq, 2), lax.div(seq, 2)
        odd = lax.rem(self.z, 2)
        self.inner = jnp.logical_or(self.z == 1, self.z == 2)
        self.outer = jnp.logical_not(self.inner)
        self.peer = {
            "core": (seg + 1 - 2 * self.core, seq),
            "x": (seg, seq + 1 - 2 * self.x),
            "y": (seg, seq + 2 - 4 * self.y),
            "xy": (seg, 3 - seq),
            "pair": (seg + 2 - 4 * odd, seq),
            "middle": (seg - 2 + 4 * odd, seq),
        }

    def greet(self, names):
        barrier = pltpu.get_barrier_semaphore()

        def hail(name):
            pl.semaphore_signal(
                barrier, inc=1, device_id=self.peer[name], device_id_type=pl.DeviceIdType.MESH
            )

        for name in names:
            hail(name)

        @pl.when(self.inner)
        def _():
            hail("middle")

        pl.semaphore_wait(barrier, len(names) + self.inner.astype(jnp.int32))


def add_into(total, addend, step=16):
    def turn(index, carry):
        rows = pl.ds(pl.multiple_of(index * step, step), step)
        total[rows, :] = total[rows, :] + addend[rows, :]
        return carry

    lax.fori_loop(0, total.shape[0] // step, turn, 0)


def add_to(result, former, latter, step=16):
    def turn(index, carry):
        rows = pl.ds(pl.multiple_of(index * step, step), step)
        result[rows, :] = former[rows, :] + latter[rows, :]
        return carry

    lax.fori_loop(0, result.shape[0] // step, turn, 0)


class Chunk:
    def __init__(self, term, offset, rows, columns, gather=False):
        self.term, self.offset, self.rows, self.columns = term, offset, rows, columns
        self.gather = gather

    def scratch(self):
        rows, columns, half = self.rows, self.columns, self.columns // 2
        low = jnp.bfloat16
        four = pltpu.VMEM((2, 2, rows, columns), low)
        one = four if self.gather else pltpu.VMEM((rows, columns), low)
        last = pltpu.VMEM((rows, 4 * columns), low) if self.gather else one
        if self.gather:
            middle = [four]
        else:
            middle = [
                pltpu.VMEM((2, rows, half), low),
                pltpu.VMEM((2, rows, half), low),
                pltpu.VMEM((rows, half), low),
                pltpu.VMEM((rows, half), low),
            ]
        return [four, four] + middle + [one, one, last] + [
            pltpu.SemaphoreType.DMA((9,)),
            pltpu.SemaphoreType.DMA((9,)),
            pltpu.SemaphoreType.DMA((3,)),
        ]

    def bind(self, place, source, result, refs):
        self.place, self.source, self.result = place, source, result
        self.mine, self.core_in = refs[0], refs[1]
        self.middle = refs[2:-6]
        self.z_first, self.z_second, self.z_last = refs[-6:-3]
        self.sent, self.received, self.local = refs[-3:]

    def remote(self, slot, source, target, peer):
        return pltpu.make_async_remote_copy(
            src_ref=source,
            dst_ref=target,
            send_sem=self.sent.at[slot],
            recv_sem=self.received.at[slot],
            device_id=self.place.peer[peer],
            device_id_type=pl.DeviceIdType.MESH,
        )

    def core_copy(self):
        rows = pl.ds(self.offset, self.rows)
        return self.remote(
            0, self.source.at[:, :, 1 - self.place.core, rows, :], self.core_in, "core"
        )

    def load(self):
        rows = pl.ds(self.offset, self.rows)
        return pltpu.make_async_copy(
            self.source.at[:, :, self.place.core, rows, :], self.mine, self.local.at[0]
        )

    def halves(self):
        half = self.columns // 2
        return pl.ds(0, half), pl.ds(half, half)

    def wide_copies(self):
        p, (left, right) = self.place, self.halves()
        if self.gather:
            return [
                self.remote(1, self.mine.at[p.y, 1 - p.x], self.middle[0].at[p.y, p.x], "x"),
                self.remote(2, self.mine.at[1 - p.y, p.x], self.middle[0].at[p.y, p.x], "y"),
                self.remote(3, self.mine.at[1 - p.y, 1 - p.x], self.middle[0].at[p.y, p.x], "xy"),
            ]
        return [
            self.remote(1, self.mine.at[:, 1 - p.x, :, left], self.middle[0], "x"),
            self.remote(2, self.mine.at[1 - p.y, :, :, right], self.middle[1], "y"),
        ]

    def narrow_copies(self):
        p, (left, right) = self.place, self.halves()
        return [
            self.remote(3, self.mine.at[1 - p.y, p.x, :, left], self.middle[2], "y"),
            self.remote(4, self.mine.at[p.y, 1 - p.x, :, right], self.middle[3], "x"),
        ]

    def summed(self):
        return self.middle[0] if self.gather else self.mine.at[self.place.y, self.place.x]

    def pair_copy(self):
        return self.remote(5, self.summed(), self.z_first, "pair")

    def middle_copy(self):
        return self.remote(6, self.summed(), self.z_second, "middle")

    def last_copy(self):
        return self.remote(7, self.z_last, self.z_last, "pair")

    def out_copies(self):
        rows = pl.ds(self.offset, self.rows)
        core = self.place.core
        target = self.result.at[core, rows, :]
        return (
            self.remote(8, self.z_last, target, "core"),
            pltpu.make_async_copy(self.z_last, target, self.local.at[1]),
        )

    def parts(self, ref):
        if self.gather:
            return [ref.at[a, b] for a in range(2) for b in range(2)]
        return [ref]

    def lay_out(self):
        part = self.columns // 3
        for owner in range(4):
            for kind in range(3):
                lanes = pl.ds(kind * part, part)
                former = self.middle[0].at[owner // 2, owner % 2, :, lanes]
                latter = self.z_second.at[owner // 2, owner % 2, :, lanes]
                add_to(self.z_last.at[:, pl.ds((4 * kind + owner) * part, part)], former, latter)

    def stage_start(self):
        self.core_copy().start()
        self.load().start()

    def stage_core(self):
        self.core_copy().wait_recv()
        self.load().wait()
        for a in range(2):
            for b in range(2):
                add_into(self.mine.at[a, b], self.core_in.at[a, b])
        for copy in self.wide_copies():
            copy.start()

    def stage_wide(self):
        p, (left, right) = self.place, self.halves()
        if self.gather:
            stay = pltpu.make_async_copy(
                self.mine.at[p.y, p.x], self.middle[0].at[p.y, p.x], self.local.at[2]
            )
            stay.start()
            for copy in self.wide_copies():
                copy.wait_recv()
            stay.wait()
            self.z_start()
            return
        for copy in self.wide_copies():
            copy.wait_recv()
        for a in range(2):
            add_into(self.mine.at[a, p.x, :, left], self.middle[0].at[a])
            add_into(self.mine.at[p.y, a, :, right], self.middle[1].at[a])
        for copy in self.narrow_copies():
            copy.start()

    def stage_narrow(self):
        p, (left, right) = self.place, self.halves()
        for copy in self.narrow_copies():
            copy.wait_recv()
        add_into(self.mine.at[p.y, p.x, :, left], self.middle[2])
        add_into(self.mine.at[p.y, p.x, :, right], self.middle[3])
        self.z_start()

    def z_start(self):
        @pl.when(self.place.outer)
        def _():
            self.pair_copy().start()

    def stage_pair(self):
        @pl.when(self.place.inner)
        def _():
            self.pair_copy().wait_recv()
            for total, addend in zip(self.parts(self.summed()), self.parts(self.z_first)):
                add_into(total, addend)
            self.middle_copy().start()

    def stage_middle(self):
        @pl.when(self.place.inner)
        def _():
            self.middle_copy().wait_recv()
            if self.gather:
                self.lay_out()
            else:
                add_to(self.z_last, self.summed(), self.z_second)
            self.last_copy().start()
            for copy in self.out_copies():
                copy.start()

    def stage_last(self):
        @pl.when(self.place.outer)
        def _():
            self.last_copy().wait_recv()
            for copy in self.out_copies():
                copy.start()

    def stage_end(self):
        remote_out, local_out = self.out_copies()
        remote_out.wait()
        local_out.wait()
        self.core_copy().wait_send()
        for copy in self.wide_copies():
            copy.wait_send()
        if not self.gather:
            for copy in self.narrow_copies():
                copy.wait_send()

        @pl.when(self.place.outer)
        def _():
            self.pair_copy().wait_send()

        @pl.when(self.place.inner)
        def _():
            self.middle_copy().wait_send()
            self.last_copy().wait_send()

    def plan(self):
        piece = 2 * self.rows * self.columns
        if self.gather:
            return [
                (self.stage_core, [("x", 1.5 * piece), ("y", 1.5 * piece)]),
                (self.stage_wide, [("z", 4 * piece)]),
                (self.stage_pair, [("z", 4 * piece)]),
                (self.stage_middle, [("z", 4 * piece)]),
                (self.stage_last, [("core", 4 * piece)]),
                (self.stage_end, []),
            ]
        return [
            (self.stage_core, [("x", piece), ("y", piece)]),
            (self.stage_wide, [("x", piece / 2), ("y", piece / 2)]),
            (self.stage_narrow, [("z1", piece)]),
            (self.stage_pair, [("z2", piece)]),
            (self.stage_middle, [("z3", piece)]),
            (self.stage_last, [("core", piece)]),
            (self.stage_end, []),
        ]

    def opening(self):
        return [("core", 8 * self.rows * self.columns)]


class RowChunk:
    def __init__(self, term, offset, rows, columns):
        self.term, self.offset, self.rows, self.columns = term, offset, rows, columns

    def scratch(self):
        rows, columns, half = self.rows, self.columns, self.columns // 2
        low = jnp.bfloat16
        return [
            pltpu.VMEM((2, 2, rows, columns), low),
            pltpu.VMEM((2, rows, half), low),
            pltpu.VMEM((2, rows, half), low),
            pltpu.VMEM((rows, half), low),
            pltpu.VMEM((rows, half), low),
            pltpu.SemaphoreType.DMA((4,)),
            pltpu.SemaphoreType.DMA((4,)),
            pltpu.SemaphoreType.DMA((2,)),
        ]

    def bind(self, place, source, result, refs):
        self.place, self.source, self.result = place, source, result
        self.mine, self.middle = refs[0], refs[1:5]
        self.sent, self.received, self.local = refs[5:]

    remote = Chunk.remote
    halves = Chunk.halves

    def load(self):
        rows = pl.ds(self.offset, self.rows)
        return pltpu.make_async_copy(self.source.at[:, :, rows, :], self.mine, self.local.at[0])

    def wide_copies(self):
        p, (left, right) = self.place, self.halves()
        return [
            self.remote(0, self.mine.at[:, 1 - p.x, :, left], self.middle[0], "x"),
            self.remote(1, self.mine.at[1 - p.y, :, :, right], self.middle[1], "y"),
        ]

    def narrow_copies(self):
        p, (left, right) = self.place, self.halves()
        return [
            self.remote(2, self.mine.at[1 - p.y, p.x, :, left], self.middle[2], "y"),
            self.remote(3, self.mine.at[p.y, 1 - p.x, :, right], self.middle[3], "x"),
        ]

    def out_copy(self):
        p = self.place
        return pltpu.make_async_copy(
            self.mine.at[p.y, p.x], self.result.at[pl.ds(self.offset, self.rows), :], self.local.at[1]
        )

    def stage_start(self):
        self.load().start()

    def stage_load(self):
        self.load().wait()
        for copy in self.wide_copies():
            copy.start()

    def stage_wide(self):
        p, (left, right) = self.place, self.halves()
        for copy in self.wide_copies():
            copy.wait_recv()
        for a in range(2):
            add_into(self.mine.at[a, p.x, :, left], self.middle[0].at[a])
            add_into(self.mine.at[p.y, a, :, right], self.middle[1].at[a])
        for copy in self.narrow_copies():
            copy.start()

    def stage_narrow(self):
        p, (left, right) = self.place, self.halves()
        for copy in self.narrow_copies():
            copy.wait_recv()
        add_into(self.mine.at[p.y, p.x, :, left], self.middle[2])
        add_into(self.mine.at[p.y, p.x, :, right], self.middle[3])
        self.out_copy().start()

    def stage_end(self):
        self.out_copy().wait()
        for copy in self.wide_copies() + self.narrow_copies():
            copy.wait_send()

    def plan(self):
        piece = 2 * self.rows * self.columns
        return [
            (self.stage_load, [("x", piece), ("y", piece)]),
            (self.stage_wide, [("x", piece / 2), ("y", piece / 2)]),
            (self.stage_narrow, [("core", 0.0)]),
            (self.stage_end, []),
        ]

    def opening(self):
        return [("core", 0.0)]


def stage_order(chunks):
    free, ready, order = {}, [], []

    def send(transfers, now):
        ends = [now]
        for link, size in transfers:
            start = max(now, free.get(link, 0.0))
            free[link] = start + size / LINK_RATE.get(link, LINK_RATE["z"])
            ends.append(free[link] + 2.0)
        return max(ends)

    for number, chunk in enumerate(chunks):
        ready.append((send(chunk.opening(), 0.0), number, 0))
    now = 0.0
    while ready:
        ready.sort()
        when, number, index = ready.pop(0)
        now = max(now, when) + 0.3
        stage, transfers = chunks[number].plan()[index]
        order.append((now, stage))
        if index + 1 < len(chunks[number].plan()):
            ready.append((send(transfers, now), number, index + 1))
    return order


def bind_chunks(chunks, place, sources, results, refs):
    used = 0
    for chunk in chunks:
        count = len(chunk.scratch())
        chunk.bind(place, sources[chunk.term], results[chunk.term], refs[used : used + count])
        used += count


def exchange_kernel(chunks, peers, count, *refs):
    sources, results = refs[:count], refs[count : 2 * count]
    place = Place()
    bind_chunks(chunks, place, sources, results, refs[2 * count :])
    place.greet(peers)
    for chunk in chunks:
        chunk.stage_start()
    for _, stage in stage_order(chunks):
        stage()


def exchange(chunks, terms, shapes, collective_id, name):
    anywhere = pl.BlockSpec(memory_space=pl.ANY)
    return pl.pallas_call(
        functools.partial(exchange_kernel, chunks, ("core", "x", "y", "xy", "pair"), len(terms)),
        in_specs=[anywhere] * len(terms),
        out_specs=[anywhere] * len(terms),
        out_shape=[jax.ShapeDtypeStruct(shape, jnp.bfloat16) for shape in shapes],
        scratch_shapes=[ref for chunk in chunks for ref in chunk.scratch()],
        compiler_params=pltpu.CompilerParams(
            collective_id=collective_id, has_side_effects=True, vmem_limit_bytes=VMEM_BYTES
        ),
        name=name,
    )(*terms)


class Line:
    def __init__(self, place, seg, slab, memory, runs, refs):
        self.place, self.seg, self.slab, self.memory, self.runs = place, seg, slab, memory, runs
        self.sent, self.received, self.core_sent, self.core_received = refs
        self.rows = slab.shape[0] // runs

    def span(self, run):
        return pl.ds(run * self.rows, self.rows)

    def there(self, way, step):
        return self.place.z >= step if way == 0 else self.place.z + step <= 3

    def goes(self, way, step):
        has = self.there(way, step - 1)
        return jnp.logical_and(has, self.place.z <= 2 if way == 0 else self.place.z >= 1)

    def index(self, way, step):
        return self.seg - 2 * step if way == 0 else self.seg + 2 * step

    def hop(self, way, step, run):
        name = self.index(way, step - 1)
        target = self.memory.at[name, self.span(run), :]
        slot = (way * 3 + step - 1) * self.runs + run
        seg, seq = lax.axis_index("seg"), lax.axis_index("seq")
        return pltpu.make_async_remote_copy(
            src_ref=self.slab.at[self.span(run), :] if step == 1 else target,
            dst_ref=target,
            send_sem=self.sent.at[slot],
            recv_sem=self.received.at[slot],
            device_id=(seg + 2 - 4 * way, seq),
            device_id_type=pl.DeviceIdType.MESH,
        )

    def arrival(self, way, step, run):
        target = self.memory.at[self.index(way, step), self.span(run), :]
        slot = (way * 3 + step - 1) * self.runs + run
        return pltpu.make_async_remote_copy(
            src_ref=target,
            dst_ref=target,
            send_sem=self.sent.at[slot],
            recv_sem=self.received.at[slot],
            device_id=self.place.peer["core"],
            device_id_type=pl.DeviceIdType.MESH,
        )

    def share(self, way, step, run):
        name = self.index(way, step)
        target = self.memory.at[name, self.span(run), :]
        slot = (way * 3 + step) * self.runs + run
        return pltpu.make_async_remote_copy(
            src_ref=self.slab.at[self.span(run), :] if step == 0 else target,
            dst_ref=target,
            send_sem=self.core_sent.at[slot],
            recv_sem=self.core_received.at[slot],
            device_id=self.place.peer["core"],
            device_id_type=pl.DeviceIdType.MESH,
        )

    def start(self):
        for run in range(self.runs):
            for way in range(2):

                @pl.when(self.goes(way, 1))
                def _(way=way, run=run):
                    self.hop(way, 1, run).start()

        for run in range(self.runs):
            self.share(0, 0, run).start()

    def advance(self, step, run):
        for way in range(2):

            @pl.when(self.there(way, step))
            def _(way=way):
                self.arrival(way, step, run).wait_recv()

            if step < 3:

                @pl.when(self.goes(way, step + 1))
                def _(way=way):
                    self.hop(way, step + 1, run).start()

            @pl.when(self.there(way, step))
            def _(way=way):
                self.share(way, step, run).start()

    def finish(self):
        for run in range(self.runs):
            self.share(0, 0, run).wait()
            for way in range(2):
                for step in range(1, 4):

                    @pl.when(self.there(way, step))
                    def _(way=way, step=step, run=run):
                        self.share(way, step, run).wait()

                    @pl.when(self.goes(way, step))
                    def _(way=way, step=step, run=run):
                        self.hop(way, step, run).wait_send()


def front_kernel(
    heads,
    x_ref,
    mem_k_ref,
    mem_v_ref,
    w_ref,
    cos_ref,
    sin_ref,
    every_ref,
    memory_ref,
    q_ref,
    k_ref,
    v_ref,
    mix_ref,
    max_ref,
    sum_ref,
    rows,
    slab,
    trade_sent,
    trade_received,
    rows_sent,
    rows_received,
    line_sent,
    line_received,
    core_sent,
    core_received,
    local,
):
    place = Place()
    seg, seq = lax.axis_index("seg"), lax.axis_index("seq")
    width = heads * HEAD_DIM
    count = mem_k_ref.shape[0]
    tokens, depth = x_ref.shape
    across = {"x": seq + 1 - 2 * place.x, "y": seq + 2 - 4 * place.y, "xy": 3 - seq}

    def remote(source, target, sent, received, slot, peer):
        return pltpu.make_async_remote_copy(
            src_ref=source,
            dst_ref=target,
            send_sem=sent.at[slot],
            recv_sem=received.at[slot],
            device_id=place.peer[peer],
            device_id_type=pl.DeviceIdType.MESH,
        )

    def columns(owner, start=0):
        return pl.ds(pl.multiple_of(start + owner * width, HEAD_DIM), width)

    def seat(owner):
        return pl.ds(pl.multiple_of(owner * count, 16), count)

    trades, arrivals = [], []
    for number, peer in enumerate(("x", "y", "xy")):
        for kind, source in enumerate((mem_k_ref, mem_v_ref)):
            lanes = pl.ds(kind * width, width)
            trades.append(
                remote(
                    source.at[:, columns(across[peer])],
                    slab.at[seat(seq), lanes],
                    trade_sent,
                    trade_received,
                    2 * number + kind,
                    peer,
                )
            )

    def trade_arrivals():
        for copy in trades:
            copy.wait_recv()

    keeps = [
        pltpu.make_async_copy(
            source.at[:, columns(seq)],
            slab.at[seat(seq), pl.ds(kind * width, width)],
            local.at[kind],
        )
        for kind, source in enumerate((mem_k_ref, mem_v_ref))
    ]
    half = depth // 2
    left, right = pl.ds(0, half), pl.ds(half, half)
    load = pltpu.make_async_copy(x_ref, rows.at[seq], local.at[2])
    direct = [
        remote(x_ref.at[:, left], rows.at[seq, :, left], rows_sent, rows_received, 0, "x"),
        remote(x_ref.at[:, right], rows.at[seq, :, right], rows_sent, rows_received, 1, "y"),
        remote(x_ref.at[:, right], rows.at[seq, :, right], rows_sent, rows_received, 2, "x"),
        remote(x_ref.at[:, left], rows.at[seq, :, left], rows_sent, rows_received, 3, "y"),
    ]
    onward = [
        remote(
            rows.at[across["x"], :, left], rows.at[across["x"], :, left], rows_sent, rows_received, 4, "y"
        ),
        remote(
            rows.at[across["y"], :, right], rows.at[across["y"], :, right], rows_sent, rows_received, 5, "x"
        ),
    ]
    line = Line(
        place, seg, slab, memory_ref, 2, (line_sent, line_received, core_sent, core_received)
    )
    keep_slab = pltpu.make_async_copy(slab, memory_ref.at[seg], local.at[3])
    keep_rows = pltpu.make_async_copy(rows, every_ref, local.at[4])

    def project_rows(owner):
        block = rows[owner]
        span = pl.ds(pl.multiple_of(owner * tokens, 16), tokens)
        cosine, sine = cos_ref[span, :], sin_ref[span, :]
        scale = SCORE_SCALE / LN2
        queries = product(block, w_ref[:, :width])
        keys = product(block, w_ref[:, width : 2 * width])
        for head in range(heads):
            lanes = slice(head * HEAD_DIM, (head + 1) * HEAD_DIM)
            q_ref[span, lanes] = turn_block(queries[:, lanes], cosine * scale, sine * scale).astype(
                jnp.bfloat16
            )
            k_ref[span, lanes] = turn_block(keys[:, lanes], cosine, sine).astype(jnp.bfloat16)
        v_ref[span, :] = product(block, w_ref[:, 2 * width :]).astype(jnp.bfloat16)

    def own_rows(block):
        def turn(head, carry):
            lanes = pl.ds(pl.multiple_of(head * HEAD_DIM, HEAD_DIM), HEAD_DIM)
            span = pl.ds(block * tokens, tokens)
            pairs = [
                (k_ref[pl.ds(n * tokens, tokens), lanes], v_ref[pl.ds(n * tokens, tokens), lanes])
                for n in range(block + 1)
            ]
            row_max, row_sum, mixed = attend(q_ref[span, lanes], pairs, True, None)
            mix_ref[span, lanes] = mixed
            max_ref[span, lanes] = jnp.broadcast_to(row_max, mixed.shape)
            sum_ref[span, lanes] = jnp.broadcast_to(row_sum, mixed.shape)
            return carry

        lax.fori_loop(0, heads, turn, 0)

    barrier = pltpu.get_barrier_semaphore()

    def hail(device):
        pl.semaphore_signal(barrier, inc=1, device_id=device, device_id_type=pl.DeviceIdType.MESH)

    for peer in ("x", "y", "xy", "core"):
        hail(place.peer[peer])
    below, above = place.z >= 1, place.z <= 2

    @pl.when(below)
    def _():
        hail((seg - 2, seq))

    @pl.when(above)
    def _():
        hail((seg + 2, seq))

    pl.semaphore_wait(barrier, 4 + below.astype(jnp.int32) + above.astype(jnp.int32))

    for copy in keeps + trades:
        copy.start()
    load.start()
    for copy in direct:
        copy.start()
    load.wait()
    project_rows(seq)
    for copy in keeps:
        copy.wait()
    trade_arrivals()
    line.start()
    keep_slab.start()
    direct[0].wait_recv()
    direct[1].wait_recv()
    for copy in onward:
        copy.start()
    line.advance(1, 0)
    direct[2].wait_recv()
    direct[3].wait_recv()
    project_rows(across["x"])
    line.advance(1, 1)
    project_rows(across["y"])
    for copy in onward:
        copy.wait_recv()
    project_rows(3 - seq)
    keep_rows.start()
    line.advance(2, 0)
    own_rows(0)
    own_rows(1)
    line.advance(2, 1)
    own_rows(2)
    own_rows(3)
    line.advance(3, 0)
    line.advance(3, 1)
    keep_slab.wait()
    keep_rows.wait()
    for copy in trades + direct + onward:
        copy.wait_send()
    line.finish()


def front(first_low, mem_keys, mem_values, w_heads, cosine, sine, seg_size, seq_size, collective_id):
    tokens, depth = first_low.shape
    length = tokens * seq_size
    width = w_heads.shape[1] // 3
    count = mem_keys.shape[0]
    anywhere = pl.BlockSpec(memory_space=pl.ANY)
    inside = pl.BlockSpec(memory_space=pltpu.VMEM)
    low = jnp.bfloat16
    shape = jax.ShapeDtypeStruct
    dma = pltpu.SemaphoreType.DMA
    return pl.pallas_call(
        functools.partial(front_kernel, width // HEAD_DIM),
        in_specs=[anywhere] * 3 + [inside] * 3,
        out_specs=[anywhere] * 2 + [inside] * 6,
        out_shape=[
            shape((seq_size, tokens, depth), low),
            shape((seg_size, count * seq_size, 2 * width), low),
        ]
        + [shape((length, width), low)] * 3
        + [shape((length, width), jnp.float32)] * 3,
        scratch_shapes=[
            pltpu.VMEM((seq_size, tokens, depth), low),
            pltpu.VMEM((count * seq_size, 2 * width), low),
            dma((6,)),
            dma((6,)),
            dma((6,)),
            dma((6,)),
            dma((12,)),
            dma((12,)),
            dma((16,)),
            dma((16,)),
            dma((5,)),
        ],
        compiler_params=pltpu.CompilerParams(
            collective_id=collective_id, has_side_effects=True, vmem_limit_bytes=VMEM_BYTES
        ),
        name="front",
    )(first_low, mem_keys, mem_values, w_heads, cosine, sine)


def norm_input_grad(values, inverse, norm_gain, upstream):
    weighted = upstream * norm_gain
    inner_mean = jnp.mean(weighted * values, axis=-1, keepdims=True)
    return inverse * weighted - inverse * inverse * inverse * values * inner_mean


def head_plan(
    seg_size,
    seq_size,
    layer_input,
    output_grad,
    norm1_gain,
    norm2_gain,
    w_qkv,
    w_out,
    w_gate,
    w_up,
    w_down,
    mem_keys,
    mem_values,
    memory_flags,
    sources,
):
    seg_index = lax.axis_index("seg")
    seq_index = lax.axis_index("seq")
    tokens = layer_input.shape[1]
    length = tokens * seq_size
    width = D // seq_size
    flag = lax.dynamic_index_in_dim(memory_flags, seg_index, 0, keepdims=True)
    listed = lax.dynamic_index_in_dim(sources, seg_index, 0, keepdims=False)
    chosen = jnp.concatenate([jnp.reshape(seg_index, (1,)), listed, flag]).astype(jnp.int32)

    inputs = layer_input[0].astype(jnp.float32)
    first_norm, first_inverse = norm_forward(inputs, norm1_gain)
    first_low = first_norm.astype(jnp.bfloat16)
    w_heads = lax.dynamic_index_in_dim(
        w_qkv.reshape(D, 3, seq_size, width), seq_index, 2, keepdims=False
    ).reshape(D, 3 * width)
    cosine, sine = turn_tables(lax.iota(jnp.int32, length).astype(jnp.float32))
    cosine, sine = cosine[:, 0, :], sine[:, 0, :]
    first_half = lax.broadcasted_iota(jnp.int32, sine.shape, 1) < HEAD_DIM // 2
    sine = jnp.where(first_half, -sine, sine)
    every_low, memory, queries, keys, values, mixed, row_max, row_sum = front(
        first_low, mem_keys[0], mem_values[0], w_heads, cosine, sine, seg_size, seq_size, 3
    )
    every_low = every_low.reshape(length, D)
    heads_low, heads_out, log_totals = memory_forward(
        chosen, queries, mixed, row_max, row_sum, memory
    )
    attended_low = lax.all_to_all(heads_low, "seq", 0, 1, tiled=True)

    residual = inputs + product(attended_low, w_out)
    second_norm, second_inverse = norm_forward(residual, norm2_gain)
    second_low = second_norm.astype(jnp.bfloat16)
    gate_values = product(second_low, w_gate)
    up_values = product(second_low, w_up)
    sigmoid_gate = jax.nn.sigmoid(gate_values)
    activated = gate_values * sigmoid_gate
    hidden_low = (activated * up_values).astype(jnp.bfloat16)
    output = (residual + product(hidden_low, w_down)).astype(jnp.bfloat16)
    upstream = output_grad[0]
    low = jnp.bfloat16
    term_down = product_tn(hidden_low, upstream).astype(low)
    grad_hidden = product_nt(upstream, w_down)
    grad_gate_low = (
        grad_hidden * up_values * sigmoid_gate * (1.0 + gate_values * (1.0 - sigmoid_gate))
    ).astype(low)
    grad_up_low = (grad_hidden * activated).astype(low)
    term_gate = product_tn(second_low, grad_gate_low).astype(low)
    term_up = product_tn(second_low, grad_up_low).astype(low)
    grad_second = product_nt(grad_gate_low, w_gate) + product_nt(grad_up_low, w_up)
    grad_residual = norm_input_grad(residual, second_inverse, norm2_gain, grad_second)
    grad_residual = grad_residual + upstream.astype(jnp.float32)
    residual_low = grad_residual.astype(low)
    term_out = product_tn(attended_low, residual_low).astype(low)
    grad_attended = product_nt(residual_low, w_out).astype(low)
    grad_heads = lax.all_to_all(grad_attended, "seq", 1, 0, tiled=True)

    start, delta = memory_backward(chosen, queries, grad_heads, heads_out, log_totals, memory)
    grad_projected = own_backward(
        queries, keys, values, grad_heads, log_totals, delta, start, cosine, sine
    )
    terms = [term_down, term_gate, term_up, term_out]
    pieces = [(term.shape[0] // (2 * seq_size), term.shape[1]) for term in terms]
    chunks = []
    for index, (rows, columns) in enumerate(pieces):
        parts = 2 if rows % 32 == 0 and index < 3 else 1
        chunks += [Chunk(index, n * rows // parts, rows // parts, columns) for n in range(parts)]
    sums = exchange(
        chunks,
        [term.reshape((2, 2, 2) + piece) for term, piece in zip(terms, pieces)],
        [(2,) + piece for piece in pieces],
        1,
        "sum_terms",
    )
    grad_down, grad_gate, grad_up, grad_out = [
        total.reshape(2 * piece[0], piece[1]).astype(jnp.float32) for total, piece in zip(sums, pieces)
    ]

    part_first = product_nt(grad_projected, w_heads).astype(low)
    part_qkv = product_tn(every_low, grad_projected).astype(low)
    rows = D // (2 * seq_size)
    qkv_rows, first_rows = exchange(
        [Chunk(0, n * rows // 2, rows // 2, 3 * width, True) for n in range(2)]
        + [RowChunk(1, n * tokens // 4, tokens // 4, D) for n in range(4)],
        [part_qkv.reshape(2, 2, 2, rows, 3 * width), part_first.reshape(2, 2, tokens, D)],
        [(2, rows, 3 * D), (tokens, D)],
        2,
        "sum_first",
    )
    grad_qkv = qkv_rows.reshape(2 * rows, 3 * D).astype(jnp.float32)
    grad_inputs = norm_input_grad(
        inputs, first_inverse, norm1_gain, first_rows.astype(jnp.float32)
    )
    input_grad = (grad_inputs + grad_residual)[None]

    def row_block(whole):
        return lax.dynamic_slice_in_dim(whole, seq_index * width, width, 0)

    def gain_rows(weights, grads, gain):
        dots = [
            jnp.sum(row_block(weight).astype(jnp.float32) * grad, axis=1)
            for weight, grad in zip(weights, grads)
        ]
        return sum(dots[1:], dots[0]) / row_block(gain)

    grad_norm1 = gain_rows([w_qkv], [grad_qkv], norm1_gain)
    grad_norm2 = gain_rows([w_gate, w_up], [grad_gate, grad_up], norm2_gain)
    return (
        output[None],
        input_grad,
        grad_norm1,
        grad_norm2,
        grad_qkv,
        grad_out,
        grad_gate,
        grad_up,
        grad_down,
    )


def solution(mesh):
    seq_size = mesh.shape["seq"]
    heads_fit = seq_size == 4 and mesh.shape["seg"] == 8
    plan = functools.partial(head_plan, mesh.shape["seg"], seq_size) if heads_fit else general_plan
    placed = (
        P("seg", "seq", None),
        P("seg", "seq", None),
        P(),
        P(),
        P(),
        P(),
        P(),
        P(),
        P(),
        P("seg", "seq", None),
        P("seg", "seq", None),
        P(),
        P(),
    )
    return jax.shard_map(
        plan,
        mesh=mesh,
        in_specs=placed,
        out_specs=(
            P("seg", "seq", None),
            P("seg", "seq", None),
            P("seq"),
            P("seq"),
            P("seq", None),
            P("seq", None),
            P("seq", None),
            P("seq", None),
            P("seq", None),
        ),
        check_vma=False,
    )
```

```python
import functools
import math

import jax
import jax.numpy as jnp
from jax import lax
from jax.experimental import pallas as pl
from jax.experimental.pallas import tpu as pltpu
from jax.sharding import PartitionSpec as P

D = 1024
HEADS = 8
HEAD_DIM = 128


masked_score = -1e30
epsilon = 1e-06
rotary_base = 10000.0


def product(former, latter):
    return jnp.dot(former, latter, preferred_element_type=jnp.float32)


def product_nt(former, latter):
    return lax.dot_general(
        former, latter, (((1,), (1,)), ((), ())), preferred_element_type=jnp.float32
    )


def product_tn(former, latter):
    return lax.dot_general(
        former, latter, (((0,), (0,)), ((), ())), preferred_element_type=jnp.float32
    )


def norm_forward(values, norm_gain):
    inverse = lax.rsqrt(jnp.mean(values * values, axis=-1, keepdims=True) + epsilon)
    return (values * inverse * norm_gain, inverse)


def norm_backward(values, inverse, norm_gain, upstream):
    weighted = upstream * norm_gain
    inner_mean = jnp.mean(weighted * values, axis=-1, keepdims=True)
    grad_values = inverse * weighted - inverse * inverse * inverse * values * inner_mean
    grad_gain = jnp.sum(upstream * values * inverse, axis=0)
    return (grad_values, grad_gain)


def turn_tables(positions):
    half_dim = HEAD_DIM // 2
    exponent = -2.0 * jnp.arange(half_dim, dtype=jnp.float32) / HEAD_DIM
    angles = positions[:, None] * jnp.power(rotary_base, exponent)[None, :]
    angles = jnp.concatenate([angles, angles], axis=1)
    return (jnp.cos(angles)[:, None, :], jnp.sin(angles)[:, None, :])


def rotate(matrix, cosine_table, sine_table, direction):
    row_count = matrix.shape[0]
    half_dim = HEAD_DIM // 2
    shaped = matrix.reshape(row_count, HEADS, HEAD_DIM)
    turned = jnp.concatenate([-shaped[..., half_dim:], shaped[..., :half_dim]], axis=-1)
    return (shaped * cosine_table + direction * turned * sine_table).reshape(
        row_count, HEADS * HEAD_DIM
    )


def general_plan(
    layer_input,
    output_grad,
    norm1_gain,
    norm2_gain,
    w_qkv,
    w_out,
    w_gate,
    w_up,
    w_down,
    mem_keys,
    mem_values,
    memory_flags,
    sources,
):
    seg_index = lax.axis_index("seg")
    seq_index = lax.axis_index("seq")
    tokens = layer_input.shape[1]
    score_scale = HEAD_DIM ** (-0.5)
    flag_on = lax.dynamic_index_in_dim(memory_flags, seg_index, 0, keepdims=False) > 0
    listed = lax.dynamic_index_in_dim(sources, seg_index, 0, keepdims=False)
    picked = jnp.concatenate([jnp.reshape(seg_index, (1,)), listed])
    every_keys, every_values = (
        lax.all_gather(mem_keys, "seg", axis=0, tiled=True),
        lax.all_gather(mem_values, "seg", axis=0, tiled=True),
    )
    chosen_keys = jnp.take(every_keys, picked, axis=0)
    chosen_values = jnp.take(every_values, picked, axis=0)
    memory_keys, memory_values = (
        lax.all_gather(chosen_keys, "seq", axis=1, tiled=True),
        lax.all_gather(chosen_values, "seq", axis=1, tiled=True),
    )
    memory_key_blocks = memory_keys.reshape(-1, tokens, HEADS, HEAD_DIM)
    memory_value_blocks = memory_values.reshape(-1, tokens, HEADS, HEAD_DIM)
    memory_blocks = memory_key_blocks.shape[0]
    inputs = layer_input[0].astype(jnp.float32)
    first_norm, first_inverse = norm_forward(inputs, norm1_gain)
    first_low = first_norm.astype(jnp.bfloat16)
    projected = product(first_low, w_qkv)
    positions = seq_index * tokens + lax.iota(jnp.int32, tokens)
    cosine_table, sine_table = turn_tables(positions.astype(jnp.float32))
    queries = rotate(projected[:, :D], cosine_table, sine_table, 1.0).astype(jnp.bfloat16)
    own_keys = rotate(projected[:, D : 2 * D], cosine_table, sine_table, 1.0).astype(jnp.bfloat16)
    own_values = projected[:, 2 * D :].astype(jnp.bfloat16)
    all_keys, all_values = (
        lax.all_gather(own_keys, "seq", axis=0, tiled=True),
        lax.all_gather(own_values, "seq", axis=0, tiled=True),
    )
    key_blocks = all_keys.reshape(-1, tokens, HEADS, HEAD_DIM)
    value_blocks = all_values.reshape(-1, tokens, HEADS, HEAD_DIM)
    query_heads = queries.reshape(tokens, HEADS, HEAD_DIM)
    memory_open = jnp.broadcast_to(flag_on, (tokens, tokens))
    own_count = seq_index + 1
    key_offsets = lax.iota(jnp.int32, tokens)

    def own_open(block):
        return (block * tokens + key_offsets)[None, :] <= positions[:, None]

    def block_scores(key_block, open_mask):
        raw = (
            jnp.einsum("qhd,khd->hqk", query_heads, key_block, preferred_element_type=jnp.float32)
            * score_scale
        )
        return jnp.where(open_mask[None], raw, masked_score)

    def sweep(step, carry):

        def memory_turn(block, state):
            return step(
                state,
                block,
                memory_key_blocks[block],
                memory_value_blocks[block],
                memory_open,
                False,
            )

        def own_turn(block, state):
            return step(state, block, key_blocks[block], value_blocks[block], own_open(block), True)

        carry = lax.fori_loop(0, memory_blocks, memory_turn, carry)
        return lax.fori_loop(0, own_count, own_turn, carry)

    def max_step(carry, block, key_block, value_block, open_mask, own):
        row_max, row_sum = carry
        scores = block_scores(key_block, open_mask)
        new_max = jnp.maximum(row_max, jnp.max(scores, axis=2))
        row_sum = row_sum * jnp.exp(row_max - new_max) + jnp.sum(
            jnp.exp(scores - new_max[..., None]), axis=2
        )
        return (new_max, row_sum)

    start_max = jnp.full((HEADS, tokens), masked_score, jnp.float32)
    row_max, row_sum = sweep(max_step, (start_max, jnp.zeros((HEADS, tokens), jnp.float32)))
    log_totals = row_max + jnp.log(row_sum)

    def mix_step(total, block, key_block, value_block, open_mask, own):
        weights_low = jnp.exp(block_scores(key_block, open_mask) - log_totals[..., None]).astype(
            jnp.bfloat16
        )
        return total + jnp.einsum(
            "hqk,khd->qhd", weights_low, value_block, preferred_element_type=jnp.float32
        )

    attended = sweep(mix_step, jnp.zeros((tokens, HEADS, HEAD_DIM), jnp.float32))
    attended_low = attended.reshape(tokens, D).astype(jnp.bfloat16)
    residual = inputs + product(attended_low, w_out)
    second_norm, second_inverse = norm_forward(residual, norm2_gain)
    second_low = second_norm.astype(jnp.bfloat16)
    gate_values = product(second_low, w_gate)
    up_values = product(second_low, w_up)
    sigmoid_gate = jax.nn.sigmoid(gate_values)
    activated = gate_values * sigmoid_gate
    hidden_low = (activated * up_values).astype(jnp.bfloat16)
    output = (residual + product(hidden_low, w_down)).astype(jnp.bfloat16)
    upstream = output_grad[0]
    grad_down = product_tn(hidden_low, upstream)
    grad_hidden = product_nt(upstream, w_down)
    grad_gate_low = (
        grad_hidden * up_values * sigmoid_gate * (1.0 + gate_values * (1.0 - sigmoid_gate))
    ).astype(jnp.bfloat16)
    grad_up_low = (grad_hidden * activated).astype(jnp.bfloat16)
    grad_gate = product_tn(second_low, grad_gate_low)
    grad_up = product_tn(second_low, grad_up_low)
    grad_second = product_nt(grad_gate_low, w_gate) + product_nt(grad_up_low, w_up)
    grad_residual, grad_norm2 = norm_backward(residual, second_inverse, norm2_gain, grad_second)
    grad_residual = grad_residual + upstream.astype(jnp.float32)
    residual_low = grad_residual.astype(jnp.bfloat16)
    grad_out = product_tn(attended_low, residual_low)
    grad_attended = product_nt(residual_low, w_out).astype(jnp.bfloat16)
    grad_heads = grad_attended.reshape(tokens, HEADS, HEAD_DIM)

    def probs_pair(key_block, value_block, open_mask):
        probs = jnp.exp(block_scores(key_block, open_mask) - log_totals[..., None])
        dprobs = jnp.einsum(
            "qhd,khd->hqk", grad_heads, value_block, preferred_element_type=jnp.float32
        )
        return (probs, dprobs)

    def delta_step(total, block, key_block, value_block, open_mask, own):
        probs, dprobs = probs_pair(key_block, value_block, open_mask)
        return total + jnp.sum(probs * dprobs, axis=2)

    delta_rows = sweep(delta_step, jnp.zeros((HEADS, tokens), jnp.float32))

    def grad_step(carry, block, key_block, value_block, open_mask, own):
        grad_query, key_terms, value_terms = carry
        probs, dprobs = probs_pair(key_block, value_block, open_mask)
        dscores = (probs * (dprobs - delta_rows[..., None])).astype(jnp.bfloat16)
        grad_query = grad_query + jnp.einsum(
            "hqk,khd->qhd", dscores, key_block, preferred_element_type=jnp.float32
        )
        if own:
            key_part = (
                jnp.einsum("hqk,qhd->khd", dscores, query_heads, preferred_element_type=jnp.float32)
                * score_scale
            )
            value_part = jnp.einsum(
                "hqk,qhd->khd",
                probs.astype(jnp.bfloat16),
                grad_heads,
                preferred_element_type=jnp.float32,
            )
            key_terms = lax.dynamic_update_index_in_dim(key_terms, key_part, block, 0)
            value_terms = lax.dynamic_update_index_in_dim(value_terms, value_part, block, 0)
        return (grad_query, key_terms, value_terms)

    term_shape = key_blocks.shape
    start_grads = (
        jnp.zeros((tokens, HEADS, HEAD_DIM), jnp.float32),
        jnp.zeros(term_shape, jnp.float32),
        jnp.zeros(term_shape, jnp.float32),
    )
    grad_query, key_terms, value_terms = sweep(grad_step, start_grads)
    grad_queries = (grad_query * score_scale).reshape(tokens, D)
    grad_keys, grad_values = (
        lax.psum_scatter(
            key_terms.astype(jnp.bfloat16), "seq", scatter_dimension=0, tiled=True
        ).astype(jnp.float32),
        lax.psum_scatter(
            value_terms.astype(jnp.bfloat16), "seq", scatter_dimension=0, tiled=True
        ).astype(jnp.float32),
    )
    grad_projected = jnp.concatenate(
        [
            rotate(grad_queries, cosine_table, sine_table, -1.0),
            rotate(grad_keys.reshape(tokens, D), cosine_table, sine_table, -1.0),
            grad_values.reshape(tokens, D),
        ],
        axis=1,
    ).astype(jnp.bfloat16)
    grad_qkv = product_tn(first_low, grad_projected)
    grad_first = product_nt(grad_projected, w_qkv)
    grad_inputs, grad_norm1 = norm_backward(inputs, first_inverse, norm1_gain, grad_first)
    input_grad = (grad_inputs + grad_residual)[None]
    shares = (
        lax.psum_scatter(
            grad_norm1.astype(jnp.bfloat16), "seq", scatter_dimension=0, tiled=True
        ).astype(jnp.float32),
        lax.psum_scatter(
            grad_norm2.astype(jnp.bfloat16), "seq", scatter_dimension=0, tiled=True
        ).astype(jnp.float32),
        lax.psum_scatter(
            grad_qkv.astype(jnp.bfloat16), "seq", scatter_dimension=0, tiled=True
        ).astype(jnp.float32),
        lax.psum_scatter(
            grad_out.astype(jnp.bfloat16), "seq", scatter_dimension=0, tiled=True
        ).astype(jnp.float32),
        lax.psum_scatter(
            grad_gate.astype(jnp.bfloat16), "seq", scatter_dimension=0, tiled=True
        ).astype(jnp.float32),
        lax.psum_scatter(
            grad_up.astype(jnp.bfloat16), "seq", scatter_dimension=0, tiled=True
        ).astype(jnp.float32),
        lax.psum_scatter(
            grad_down.astype(jnp.bfloat16), "seq", scatter_dimension=0, tiled=True
        ).astype(jnp.float32),
    )
    totals = (
        lax.psum(shares[0].astype(jnp.bfloat16), "seg").astype(jnp.float32),
        lax.psum(shares[1].astype(jnp.bfloat16), "seg").astype(jnp.float32),
        lax.psum(shares[2].astype(jnp.bfloat16), "seg").astype(jnp.float32),
        lax.psum(shares[3].astype(jnp.bfloat16), "seg").astype(jnp.float32),
        lax.psum(shares[4].astype(jnp.bfloat16), "seg").astype(jnp.float32),
        lax.psum(shares[5].astype(jnp.bfloat16), "seg").astype(jnp.float32),
        lax.psum(shares[6].astype(jnp.bfloat16), "seg").astype(jnp.float32),
    )
    return (
        output[None],
        input_grad,
        totals[0],
        totals[1],
        totals[2],
        totals[3],
        totals[4],
        totals[5],
        totals[6],
    )


VMEM_BYTES = 60 * 1024 * 1024
VMEM_MOST = 67043328
LN2 = math.log(2.0)
SCORE_SCALE = HEAD_DIM ** (-0.5)


def lane_fold(op, tile, running):
    for column in range(tile.shape[1] // HEAD_DIM):
        piece = tile[:, column * HEAD_DIM : (column + 1) * HEAD_DIM]
        running = piece if running is None else op(running, piece)
    return running


def causal(scores):
    rows = lax.broadcasted_iota(jnp.int32, scores.shape, 0)
    columns = lax.broadcasted_iota(jnp.int32, scores.shape, 1)
    return jnp.where(columns <= rows, scores, masked_score)


def attend(query, pairs, diagonal, carried):
    every, lane_max = [], None
    for index, (keys, _) in enumerate(pairs):
        scores = product_nt(query, keys)
        if diagonal and index == len(pairs) - 1:
            scores = causal(scores)
        lane_max = lane_fold(jnp.maximum, scores, lane_max)
        every.append(scores)
    row_max = jnp.max(lane_max, axis=1, keepdims=True)
    if carried is not None:
        row_max = jnp.maximum(row_max, carried[0])
    lane_sum, mixed = None, None
    for scores, (_, values) in zip(every, pairs):
        probs = jnp.exp2(scores - row_max)
        lane_sum = lane_fold(jnp.add, probs, lane_sum)
        part = product(probs.astype(jnp.bfloat16), values)
        mixed = part if mixed is None else mixed + part
    row_sum = jnp.sum(lane_sum, axis=1, keepdims=True)
    if carried is not None:
        shrink = jnp.exp2(carried[0] - row_max)
        row_sum = carried[1] * shrink + row_sum
        mixed = carried[2] * shrink + mixed
    return row_max, row_sum, mixed


def memory_specs(heads, rows, count):
    specs = []
    for slot in range(count):
        specs.append(
            pl.BlockSpec((1, rows, HEAD_DIM), lambda h, i, chosen, slot=slot: (chosen[slot], 0, h))
        )
        specs.append(
            pl.BlockSpec(
                (1, rows, HEAD_DIM), lambda h, i, chosen, slot=slot: (chosen[slot], 0, heads + h)
            )
        )
    return specs


def memory_forward_kernel(count, chosen, q_ref, mix_ref, max_ref, sum_ref, *rest):
    blocks = rest[: 2 * count]
    low_ref, copy_ref, log_ref = rest[2 * count :]
    head = pl.program_id(0)
    carried = (max_ref[:, :1], sum_ref[:, :1], mix_ref[...])

    def finish(row_max, row_sum, mixed):
        low_ref[...] = (mixed * (1.0 / row_sum)).astype(jnp.bfloat16)
        log_ref[...] = jnp.broadcast_to(row_max + jnp.log2(row_sum), log_ref.shape)

    @pl.when(pl.program_id(1) == 0)
    def _():
        rows = copy_ref.shape[1]
        width = copy_ref.shape[2] // 4
        for n in range(count):
            for run in range(2):
                for kind in range(2):
                    start = pl.multiple_of((2 * run + kind) * width + head * HEAD_DIM, HEAD_DIM)
                    copy_ref[n, :, pl.ds(start, HEAD_DIM)] = blocks[2 * n + kind][
                        0, run * rows : (run + 1) * rows, :
                    ]

    @pl.when(chosen[count] > 0)
    def _():
        pairs = [(blocks[2 * n][0], blocks[2 * n + 1][0]) for n in range(count)]
        finish(*attend(q_ref[...], pairs, False, carried))

    @pl.when(chosen[count] <= 0)
    def _():
        finish(*carried)


def memory_forward(chosen, queries, mixed, row_max, row_sum, memory, rows=512):
    length, width = queries.shape
    heads, count = width // HEAD_DIM, chosen.shape[0] - 1
    block = pl.BlockSpec((rows, HEAD_DIM), lambda h, i, chosen: (i, h))
    pairs = heads * length * count * memory.shape[1]
    return pl.pallas_call(
        functools.partial(memory_forward_kernel, count),
        grid_spec=pltpu.PrefetchScalarGridSpec(
            num_scalar_prefetch=1,
            grid=(heads, length // rows),
            in_specs=[block] * 4 + memory_specs(heads, memory.shape[1], count),
            out_specs=[
                block,
                pl.BlockSpec((count, memory.shape[1] // 2, 4 * width), lambda h, i, chosen: (0, 0, 0)),
                block,
            ],
        ),
        out_shape=[
            jax.ShapeDtypeStruct((length, width), jnp.bfloat16),
            jax.ShapeDtypeStruct((count, memory.shape[1] // 2, 4 * width), jnp.bfloat16),
            jax.ShapeDtypeStruct((length, width), jnp.float32),
        ],
        compiler_params=pltpu.CompilerParams(vmem_limit_bytes=VMEM_BYTES),
        cost_estimate=pl.CostEstimate(
            flops=8 * pairs * HEAD_DIM, transcendentals=pairs, bytes_accessed=36 * length * width
        ),
        name="memory_forward",
    )(chosen, queries, mixed, row_max, row_sum, *[memory] * (2 * count))


def turn_block(matrix, cosine, sine):
    return matrix * cosine + pltpu.roll(matrix, HEAD_DIM // 2, 1) * sine


LINK_RATE = {"core": 300e3, "x": 49e3, "y": 49e3, "z": 49e3}


class Place:
    def __init__(self):
        seg, seq = lax.axis_index("seg"), lax.axis_index("seq")
        self.core, self.z = lax.rem(seg, 2), lax.div(seg, 2)
        self.x, self.y = lax.rem(seq, 2), lax.div(seq, 2)
        odd = lax.rem(self.z, 2)
        self.inner = jnp.logical_or(self.z == 1, self.z == 2)
        self.outer = jnp.logical_not(self.inner)
        self.peer = {
            "core": (seg + 1 - 2 * self.core, seq),
            "x": (seg, seq + 1 - 2 * self.x),
            "y": (seg, seq + 2 - 4 * self.y),
            "xy": (seg, 3 - seq),
            "pair": (seg + 2 - 4 * odd, seq),
            "middle": (seg - 2 + 4 * odd, seq),
        }

    def greet(self, names):
        barrier = pltpu.get_barrier_semaphore()

        def hail(name):
            pl.semaphore_signal(
                barrier, inc=1, device_id=self.peer[name], device_id_type=pl.DeviceIdType.MESH
            )

        for name in names:
            hail(name)

        @pl.when(self.inner)
        def _():
            hail("middle")

        pl.semaphore_wait(barrier, len(names) + self.inner.astype(jnp.int32))


def add_into(total, addend, step=16):
    def turn(index, carry):
        rows = pl.ds(pl.multiple_of(index * step, step), step)
        total[rows, :] = total[rows, :] + addend[rows, :]
        return carry

    lax.fori_loop(0, total.shape[0] // step, turn, 0)


def add_to(result, former, latter, step=16):
    def turn(index, carry):
        rows = pl.ds(pl.multiple_of(index * step, step), step)
        result[rows, :] = former[rows, :] + latter[rows, :]
        return carry

    lax.fori_loop(0, result.shape[0] // step, turn, 0)


class Chunk:
    def __init__(self, term, offset, rows, columns, gather=False):
        self.term, self.offset, self.rows, self.columns = term, offset, rows, columns
        self.gather = gather

    def scratch(self):
        rows, columns, half = self.rows, self.columns, self.columns // 2
        low = jnp.bfloat16
        four = pltpu.VMEM((2, 2, rows, columns), low)
        one = four if self.gather else pltpu.VMEM((rows, columns), low)
        last = pltpu.VMEM((rows, 4 * columns), low) if self.gather else one
        if self.gather:
            middle = [four]
        else:
            middle = [
                pltpu.VMEM((2, rows, half), low),
                pltpu.VMEM((2, rows, half), low),
                pltpu.VMEM((rows, half), low),
                pltpu.VMEM((rows, half), low),
            ]
        ends = [one, one, last] if self.gather else [one, one]
        return [four, four] + middle + ends + [
            pltpu.SemaphoreType.DMA((9,)),
            pltpu.SemaphoreType.DMA((9,)),
            pltpu.SemaphoreType.DMA((3,)),
        ]

    def bind(self, place, source, result, refs):
        self.place, self.source, self.result = place, source, result
        self.mine, self.core_in = refs[0], refs[1]
        ends = 3 if self.gather else 2
        self.middle = refs[2 : -3 - ends]
        self.z_last, self.z_second = refs[-4], refs[-5]
        self.z_first = refs[-6] if self.gather else self.z_last
        self.sent, self.received, self.local = refs[-3:]

    def remote(self, slot, source, target, peer):
        return pltpu.make_async_remote_copy(
            src_ref=source,
            dst_ref=target,
            send_sem=self.sent.at[slot],
            recv_sem=self.received.at[slot],
            device_id=self.place.peer[peer],
            device_id_type=pl.DeviceIdType.MESH,
        )

    def core_copy(self):
        rows = pl.ds(self.offset, self.rows)
        return self.remote(
            0, self.source.at[:, :, 1 - self.place.core, rows, :], self.core_in, "core"
        )

    def load(self):
        rows = pl.ds(self.offset, self.rows)
        return pltpu.make_async_copy(
            self.source.at[:, :, self.place.core, rows, :], self.mine, self.local.at[0]
        )

    def halves(self):
        half = self.columns // 2
        return pl.ds(0, half), pl.ds(half, half)

    def wide_copies(self):
        p, (left, right) = self.place, self.halves()
        if self.gather:
            return [
                self.remote(1, self.mine.at[p.y, 1 - p.x], self.middle[0].at[p.y, p.x], "x"),
                self.remote(2, self.mine.at[1 - p.y, p.x], self.middle[0].at[p.y, p.x], "y"),
                self.remote(3, self.mine.at[1 - p.y, 1 - p.x], self.middle[0].at[p.y, p.x], "xy"),
            ]
        return [
            self.remote(1, self.mine.at[:, 1 - p.x, :, left], self.middle[0], "x"),
            self.remote(2, self.mine.at[1 - p.y, :, :, right], self.middle[1], "y"),
        ]

    def narrow_copies(self):
        p, (left, right) = self.place, self.halves()
        return [
            self.remote(3, self.mine.at[1 - p.y, p.x, :, left], self.middle[2], "y"),
            self.remote(4, self.mine.at[p.y, 1 - p.x, :, right], self.middle[3], "x"),
        ]

    def summed(self):
        return self.middle[0] if self.gather else self.mine.at[self.place.y, self.place.x]

    def pair_copy(self):
        return self.remote(5, self.summed(), self.z_first, "pair")

    def middle_copy(self):
        return self.remote(6, self.summed(), self.z_second, "middle")

    def last_copy(self):
        return self.remote(7, self.z_last, self.z_last, "pair")

    def out_copies(self):
        rows = pl.ds(self.offset, self.rows)
        core = self.place.core
        target = self.result.at[core, rows, :]
        return (
            self.remote(8, self.z_last, target, "core"),
            pltpu.make_async_copy(self.z_last, target, self.local.at[1]),
        )

    def parts(self, ref):
        if self.gather:
            return [ref.at[a, b] for a in range(2) for b in range(2)]
        return [ref]

    def lay_out(self):
        part = self.columns // 3
        for owner in range(4):
            for kind in range(3):
                lanes = pl.ds(kind * part, part)
                former = self.middle[0].at[owner // 2, owner % 2, :, lanes]
                latter = self.z_second.at[owner // 2, owner % 2, :, lanes]
                add_to(self.z_last.at[:, pl.ds((4 * kind + owner) * part, part)], former, latter)

    def stage_start(self):
        self.core_copy().start()
        self.load().start()

    def stage_core(self):
        self.core_copy().wait_recv()
        self.load().wait()
        for a in range(2):
            for b in range(2):
                add_into(self.mine.at[a, b], self.core_in.at[a, b])
        for copy in self.wide_copies():
            copy.start()

    def stage_wide(self):
        p, (left, right) = self.place, self.halves()
        if self.gather:
            stay = pltpu.make_async_copy(
                self.mine.at[p.y, p.x], self.middle[0].at[p.y, p.x], self.local.at[2]
            )
            stay.start()
            for copy in self.wide_copies():
                copy.wait_recv()
            stay.wait()
            self.z_start()
            return
        for copy in self.wide_copies():
            copy.wait_recv()
        for a in range(2):
            add_into(self.mine.at[a, p.x, :, left], self.middle[0].at[a])
            add_into(self.mine.at[p.y, a, :, right], self.middle[1].at[a])
        for copy in self.narrow_copies():
            copy.start()

    def stage_narrow(self):
        p, (left, right) = self.place, self.halves()
        for copy in self.narrow_copies():
            copy.wait_recv()
        add_into(self.mine.at[p.y, p.x, :, left], self.middle[2])
        add_into(self.mine.at[p.y, p.x, :, right], self.middle[3])
        self.z_start()

    def z_start(self):
        @pl.when(self.place.outer)
        def _():
            self.pair_copy().start()

    def stage_pair(self):
        @pl.when(self.place.inner)
        def _():
            self.pair_copy().wait_recv()
            for total, addend in zip(self.parts(self.summed()), self.parts(self.z_first)):
                add_into(total, addend)
            self.middle_copy().start()

    def stage_middle(self):
        @pl.when(self.place.inner)
        def _():
            self.middle_copy().wait_recv()
            if self.gather:
                self.lay_out()
            else:
                add_to(self.z_last, self.summed(), self.z_second)
            self.last_copy().start()
            for copy in self.out_copies():
                copy.start()

    def stage_last(self):
        @pl.when(self.place.outer)
        def _():
            self.last_copy().wait_recv()
            for copy in self.out_copies():
                copy.start()

    def stage_end(self):
        remote_out, local_out = self.out_copies()
        remote_out.wait()
        local_out.wait()
        self.core_copy().wait_send()
        for copy in self.wide_copies():
            copy.wait_send()
        if not self.gather:
            for copy in self.narrow_copies():
                copy.wait_send()

        @pl.when(self.place.outer)
        def _():
            self.pair_copy().wait_send()

        @pl.when(self.place.inner)
        def _():
            self.middle_copy().wait_send()
            self.last_copy().wait_send()

    def plan(self):
        piece = 2 * self.rows * self.columns
        if self.gather:
            return [
                (self.stage_core, [("x", 1.5 * piece), ("y", 1.5 * piece)]),
                (self.stage_wide, [("z", 4 * piece)]),
                (self.stage_pair, [("z", 4 * piece)]),
                (self.stage_middle, [("z", 4 * piece)]),
                (self.stage_last, [("core", 4 * piece)]),
                (self.stage_end, []),
            ]
        return [
            (self.stage_core, [("x", piece), ("y", piece)]),
            (self.stage_wide, [("x", piece / 2), ("y", piece / 2)]),
            (self.stage_narrow, [("z1", piece)]),
            (self.stage_pair, [("z2", piece)]),
            (self.stage_middle, [("z3", piece)]),
            (self.stage_last, [("core", piece)]),
            (self.stage_end, []),
        ]

    def opening(self):
        return [("core", 8 * self.rows * self.columns)]


class RowChunk:
    def __init__(self, term, offset, rows, columns):
        self.term, self.offset, self.rows, self.columns = term, offset, rows, columns

    def scratch(self):
        rows, columns, half = self.rows, self.columns, self.columns // 2
        low = jnp.bfloat16
        return [
            pltpu.VMEM((2, rows, half), low),
            pltpu.VMEM((2, rows, half), low),
            pltpu.VMEM((rows, half), low),
            pltpu.VMEM((rows, half), low),
            pltpu.SemaphoreType.DMA((6,)),
            pltpu.SemaphoreType.DMA((6,)),
            pltpu.SemaphoreType.DMA((1,)),
        ]

    def bind(self, place, source, result, refs):
        self.place, self.result = place, result
        self.blocks = source
        self.middle = refs[:4]
        self.sent, self.received, self.local = refs[4:]

    def mine(self, y, x, lanes):
        return self.blocks.at[2 * y + x, pl.ds(self.offset, self.rows), lanes]

    remote = Chunk.remote
    halves = Chunk.halves

    def wide_copies(self):
        p, (left, right) = self.place, self.halves()
        copies = []
        for a in range(2):
            copies.append(
                self.remote(a, self.mine(a, 1 - p.x, left), self.middle[0].at[a], "x")
            )
            copies.append(
                self.remote(2 + a, self.mine(1 - p.y, a, right), self.middle[1].at[a], "y")
            )
        return copies

    def narrow_copies(self):
        p, (left, right) = self.place, self.halves()
        return [
            self.remote(4, self.mine(1 - p.y, p.x, left), self.middle[2], "y"),
            self.remote(5, self.mine(p.y, 1 - p.x, right), self.middle[3], "x"),
        ]

    def out_copy(self):
        p = self.place
        whole = pl.ds(0, self.columns)
        return pltpu.make_async_copy(
            self.mine(p.y, p.x, whole),
            self.result.at[pl.ds(self.offset, self.rows), :],
            self.local.at[0],
        )

    def stage_start(self):
        for copy in self.wide_copies():
            copy.start()

    def stage_wide(self):
        p, (left, right) = self.place, self.halves()
        for copy in self.wide_copies():
            copy.wait_recv()
        for a in range(2):
            add_into(self.mine(a, p.x, left), self.middle[0].at[a])
            add_into(self.mine(p.y, a, right), self.middle[1].at[a])
        for copy in self.narrow_copies():
            copy.start()

    def stage_narrow(self):
        p, (left, right) = self.place, self.halves()
        for copy in self.narrow_copies():
            copy.wait_recv()
        add_into(self.mine(p.y, p.x, left), self.middle[2])
        add_into(self.mine(p.y, p.x, right), self.middle[3])
        self.out_copy().start()

    def stage_end(self):
        self.out_copy().wait()
        for copy in self.wide_copies() + self.narrow_copies():
            copy.wait_send()

    def plan(self):
        piece = 2 * self.rows * self.columns
        return [
            (self.stage_wide, [("x", piece / 2), ("y", piece / 2)]),
            (self.stage_narrow, [("core", 0.0)]),
            (self.stage_end, []),
        ]

    def opening(self):
        piece = 2 * self.rows * self.columns
        return [("x", piece), ("y", piece)]


class Steps:
    def __init__(self, start):
        self.now, self.free, self.waiting = start, {}, []

    def send(self, transfers):
        ends = [self.now]
        for link, size in transfers:
            start = max(self.now, self.free.get(link, 0.0))
            self.free[link] = start + size / LINK_RATE.get(link, LINK_RATE["z"])
            ends.append(self.free[link] + 2.0)
        return max(ends)

    def open(self, chunks):
        for chunk in chunks:
            self.waiting.append((self.send(chunk.opening()), len(self.waiting), chunk, 0))

    def due(self, everything=False):
        stages = []
        while self.waiting:
            self.waiting.sort(key=lambda entry: entry[:2])
            when, number, chunk, index = self.waiting[0]
            if when > self.now and not everything:
                break
            self.waiting.pop(0)
            self.now = max(self.now, when) + 0.4
            stage, transfers = chunk.plan()[index]
            stages.append(stage)
            if index + 1 < len(chunk.plan()):
                self.waiting.append((self.send(transfers), number, chunk, index + 1))
        return stages

    def spend(self, duration):
        self.now += duration


def back_kernel(
    chunks,
    first_chunks,
    heads,
    flag_ref,
    g_ref,
    q_hbm,
    k_hbm,
    v_hbm,
    memory_hbm,
    every_hbm,
    down_ref,
    gate_ref,
    up_ref,
    out_ref,
    w_ref,
    mix_ref,
    log_ref,
    table_ref,
    sum_down,
    sum_gate,
    sum_up,
    sum_out,
    sum_qkv,
    sum_first,
    q,
    k,
    v,
    upstream,
    shared,
    dk,
    dv,
    total,
    delta,
    part_qkv,
    trade_sent,
    trade_received,
    local,
    *refs,
):
    place = Place()
    seq = lax.axis_index("seq")
    tokens = g_ref.shape[0]
    width = heads * HEAD_DIM
    used = 0
    sources = [down_ref, gate_ref, up_ref, out_ref, part_qkv, shared]
    results = [sum_down, sum_gate, sum_up, sum_out, sum_qkv, sum_first]
    for chunk in chunks + first_chunks:
        count = len(chunk.scratch())
        chunk.bind(place, sources[chunk.term], results[chunk.term], refs[used : used + count])
        used += count

    def owner_at(turn):
        low, high = lax.rem(turn, 2), lax.div(turn, 2)
        x = place.x + low - 2 * place.x * low
        y = place.y + high - 2 * place.y * high
        return 2 * y + x

    def columns(owner):
        return pl.ds(pl.multiple_of(owner * width, HEAD_DIM), width)

    def span(block):
        return pl.ds(pl.multiple_of(block * tokens, tokens), tokens)

    def lanes(head):
        return pl.ds(pl.multiple_of(head * HEAD_DIM, HEAD_DIM), HEAD_DIM)

    across = {"x": seq + 1 - 2 * place.x, "y": seq + 2 - 4 * place.y, "xy": 3 - seq}
    trades = [
        pltpu.make_async_remote_copy(
            src_ref=g_ref.at[:, columns(across[peer])],
            dst_ref=upstream.at[span(seq), :],
            send_sem=trade_sent.at[slot],
            recv_sem=trade_received.at[slot],
            device_id=place.peer[peer],
            device_id_type=pl.DeviceIdType.MESH,
        )
        for slot, peer in enumerate(("x", "y", "xy"))
    ]
    loads = [
        pltpu.make_async_copy(g_ref.at[:, columns(seq)], upstream.at[span(seq), :], local.at[0]),
        pltpu.make_async_copy(q_hbm, q, local.at[1]),
        pltpu.make_async_copy(k_hbm, k, local.at[2]),
        pltpu.make_async_copy(v_hbm, v, local.at[3]),
        pltpu.make_async_copy(memory_hbm, shared, local.at[4]),
    ]
    load_every = pltpu.make_async_copy(every_hbm, shared, local.at[5])

    def tables(rows):
        both = table_ref[rows, :]
        swapped = pltpu.roll(both, HEAD_DIM // 2, 1)
        first = lax.broadcasted_iota(jnp.int32, both.shape, 1) < HEAD_DIM // 2
        return jnp.where(first, both, swapped), jnp.where(first, swapped, -both)

    def turn_back(matrix, rows):
        cosine, sine = tables(rows)
        return turn_block(matrix, cosine, sine).astype(jnp.bfloat16)

    def memory_part(head, block):
        rows, mine = span(block), lanes(head)
        query, grads = q[rows, mine], upstream[rows, mine]
        row_delta = jnp.sum(
            grads.astype(jnp.float32) * mix_ref[rows, mine].astype(jnp.float32), axis=1, keepdims=True
        )
        delta[...] = jnp.broadcast_to(row_delta, delta.shape)
        closed = (1 - flag_ref[0]).astype(jnp.float32) * 1e30
        log_total = log_ref[rows, mine][:, :1] + closed
        result = jnp.zeros(total.shape, jnp.float32)
        for slot in range(shared.shape[0]):
            for run in range(2):

                def tile(kind):
                    start = pl.multiple_of((2 * run + kind) * width + head * HEAD_DIM, HEAD_DIM)
                    return shared[slot, :, pl.ds(start, HEAD_DIM)]

                keys, values = tile(0), tile(1)
                probs = jnp.exp2(product_nt(query, keys) - log_total)
                dscores = probs * (product_nt(grads, values) - row_delta)
                result = result + product(dscores.astype(jnp.bfloat16), keys)
        total[...] = result

    def own_part(head, block):
        rows, mine = span(block), lanes(head)
        query, grads = q[rows, mine], upstream[rows, mine]
        log_total, row_delta = log_ref[rows, mine][:, :1], delta[:, :1]

        def turn(other, result, diagonal):
            keys = k[span(other), mine]
            scores = product_nt(query, keys)
            if diagonal:
                scores = causal(scores)
            probs = jnp.exp2(scores - log_total)
            dscores = (probs * (product_nt(grads, v[span(other), mine]) - row_delta)).astype(
                jnp.bfloat16
            )
            dv[span(other), :] += product_tn(probs.astype(jnp.bfloat16), grads)
            dk[span(other), :] += product_tn(dscores, query)
            return result + product(dscores, keys)

        result = turn(block, total[...], True)
        result = lax.fori_loop(0, block, lambda other, r: turn(other, r, False), result)
        q[rows, mine] = turn_back(result * SCORE_SCALE, rows)

    def close_head(head):
        mine = lanes(head)

        def turn(block, carry):
            rows = span(block)
            k[rows, mine] = turn_back(dk[rows, :] * LN2, rows)
            v[rows, mine] = dv[rows, :].astype(jnp.bfloat16)
            return carry

        lax.fori_loop(0, 4, turn, 0)

    def multiply_qkv(index, carry):
        cut = pl.ds(pl.multiple_of(index * width, HEAD_DIM), width)
        for kind, part in enumerate((q, k, v)):
            term = None
            for block in range(shared.shape[0]):
                product_part = product_tn(shared[block, :, cut], part[block * tokens : (block + 1) * tokens, :])
                term = product_part if term is None else term + product_part
            term = term.astype(jnp.bfloat16)
            half = term.shape[0] // 2
            place_y, place_x = lax.div(index, 2), lax.rem(index, 2)
            for core in range(2):
                part_qkv[place_y, place_x, core, :, kind * width : (kind + 1) * width] = term[
                    core * half : (core + 1) * half, :
                ]
        return carry

    def multiply_first(block, carry):
        rows = span(block)
        result = None
        for kind, part in enumerate((q, k, v)):
            term = product_nt(part[rows, :], w_ref[:, kind * width : (kind + 1) * width])
            result = term if result is None else result + term
        shared[block] = result.astype(jnp.bfloat16)
        return carry

    place.greet(("core", "x", "y", "xy", "pair"))
    for copy in trades + loads:
        copy.start()
    for chunk in chunks:
        chunk.stage_start()
    steps = Steps(3.0)
    steps.free.update(x=11.0, y=11.0)
    steps.open(chunks)
    for copy in loads:
        copy.wait()
    slots = []
    for unit in range(2 * 4 * heads):
        slots.append(steps.due())
        steps.spend(4.3 if unit % 2 == 0 else 3.2)

    def run(stages):
        for stage in stages:
            stage()

    def unit(index, carry):
        head, turn = lax.div(index, 4), lax.rem(index, 4)
        block = owner_at(turn)
        for number in range(4 * heads):
            if slots[2 * number] or number in (1, 2, 3):

                @pl.when(index == number)
                def _(number=number):
                    run(slots[2 * number])
                    if number in (1, 2, 3):
                        trades[number - 1].wait_recv()

        @pl.when(turn == 0)
        def _():
            dk[...] = jnp.zeros_like(dk)
            dv[...] = jnp.zeros_like(dv)

        memory_part(head, block)
        for number in range(4 * heads):
            if slots[2 * number + 1]:

                @pl.when(index == number)
                def _(number=number):
                    run(slots[2 * number + 1])

        own_part(head, block)

        @pl.when(turn == 3)
        def _():
            close_head(head)

        return carry

    lax.fori_loop(0, 4 * heads, unit, 0)
    load_every.start()
    run(steps.due())
    load_every.wait()
    lax.fori_loop(0, 4, multiply_qkv, 0)
    steps.spend(8.0)
    qkv_chunks = [chunk for chunk in first_chunks if chunk.term == 4]
    row_chunks = [chunk for chunk in first_chunks if chunk.term == 5]
    for chunk in qkv_chunks:
        chunk.stage_start()
    steps.open(qkv_chunks)
    run(steps.due())
    lax.fori_loop(0, 4, multiply_first, 0)
    steps.spend(6.0)
    for chunk in row_chunks:
        chunk.stage_start()
    steps.open(row_chunks)
    run(steps.due(True))
    for copy in trades:
        copy.wait_send()


def back(flag, grads, queries, keys, values, memory, every, terms, w_heads, attended, log_totals, table, collective_id):
    tokens, depth = grads.shape
    length, width = queries.shape
    low = jnp.bfloat16
    chunks, shapes = [], []
    for index, term in enumerate(terms):
        rows, columns = term.shape[0] // 8, term.shape[1]
        parts = 2 if rows % 32 == 0 and index < 3 else 1
        chunks += [Chunk(index, n * rows // parts, rows // parts, columns) for n in range(parts)]
        shapes.append((2, rows, columns))
    rows = depth // 8
    first_chunks = [Chunk(4, n * rows // 2, rows // 2, 3 * width, True) for n in range(2)]
    first_chunks += [RowChunk(5, n * tokens // 4, tokens // 4, depth) for n in range(4)]
    shapes += [(2, rows, 12 * width), (tokens, depth)]
    anywhere = pl.BlockSpec(memory_space=pl.ANY)
    inside = pl.BlockSpec(memory_space=pltpu.VMEM)
    scratch = (
        [pltpu.VMEM((length, width), low)] * 4
        + [pltpu.VMEM((4, tokens, depth), low)]
        + [pltpu.VMEM((length, HEAD_DIM), jnp.float32)] * 2
        + [pltpu.VMEM((tokens, HEAD_DIM), jnp.float32)] * 2
        + [pltpu.VMEM((2, 2, 2, rows, 3 * width), low)]
        + [pltpu.SemaphoreType.DMA((3,))] * 2
        + [pltpu.SemaphoreType.DMA((6,))]
    )
    return pl.pallas_call(
        functools.partial(back_kernel, chunks, first_chunks, width // HEAD_DIM),
        in_specs=[pl.BlockSpec(memory_space=pltpu.SMEM)] + [anywhere] * 10 + [inside] * 4,
        out_specs=[anywhere] * len(shapes),
        out_shape=[jax.ShapeDtypeStruct(shape, low) for shape in shapes],
        scratch_shapes=scratch + [ref for chunk in chunks + first_chunks for ref in chunk.scratch()],
        compiler_params=pltpu.CompilerParams(
            collective_id=collective_id, has_side_effects=True, vmem_limit_bytes=VMEM_MOST
        ),
        name="back",
    )(
        flag,
        grads,
        queries,
        keys,
        values,
        memory,
        every,
        *[term.reshape((2, 2, 2, term.shape[0] // 8, term.shape[1])) for term in terms],
        w_heads,
        attended,
        log_totals,
        table,
    )


class Line:
    def __init__(self, place, seg, slab, memory, runs, refs):
        self.place, self.seg, self.slab, self.memory, self.runs = place, seg, slab, memory, runs
        self.sent, self.received, self.core_sent, self.core_received = refs
        self.rows = slab.shape[0] // runs

    def span(self, run):
        return pl.ds(run * self.rows, self.rows)

    def there(self, way, step):
        return self.place.z >= step if way == 0 else self.place.z + step <= 3

    def goes(self, way, step):
        has = self.there(way, step - 1)
        return jnp.logical_and(has, self.place.z <= 2 if way == 0 else self.place.z >= 1)

    def index(self, way, step):
        return self.seg - 2 * step if way == 0 else self.seg + 2 * step

    def hop(self, way, step, run):
        name = self.index(way, step - 1)
        target = self.memory.at[name, self.span(run), :]
        slot = (way * 3 + step - 1) * self.runs + run
        seg, seq = lax.axis_index("seg"), lax.axis_index("seq")
        return pltpu.make_async_remote_copy(
            src_ref=self.slab.at[self.span(run), :] if step == 1 else target,
            dst_ref=target,
            send_sem=self.sent.at[slot],
            recv_sem=self.received.at[slot],
            device_id=(seg + 2 - 4 * way, seq),
            device_id_type=pl.DeviceIdType.MESH,
        )

    def arrival(self, way, step, run):
        target = self.memory.at[self.index(way, step), self.span(run), :]
        slot = (way * 3 + step - 1) * self.runs + run
        return pltpu.make_async_remote_copy(
            src_ref=target,
            dst_ref=target,
            send_sem=self.sent.at[slot],
            recv_sem=self.received.at[slot],
            device_id=self.place.peer["core"],
            device_id_type=pl.DeviceIdType.MESH,
        )

    def share(self, way, step, run):
        name = self.index(way, step)
        target = self.memory.at[name, self.span(run), :]
        slot = (way * 3 + step) * self.runs + run
        return pltpu.make_async_remote_copy(
            src_ref=self.slab.at[self.span(run), :] if step == 0 else target,
            dst_ref=target,
            send_sem=self.core_sent.at[slot],
            recv_sem=self.core_received.at[slot],
            device_id=self.place.peer["core"],
            device_id_type=pl.DeviceIdType.MESH,
        )

    def start(self):
        for run in range(self.runs):
            for way in range(2):

                @pl.when(self.goes(way, 1))
                def _(way=way, run=run):
                    self.hop(way, 1, run).start()

        for run in range(self.runs):
            self.share(0, 0, run).start()

    def advance(self, step, run):
        for way in range(2):

            @pl.when(self.there(way, step))
            def _(way=way):
                self.arrival(way, step, run).wait_recv()

            if step < 3:

                @pl.when(self.goes(way, step + 1))
                def _(way=way):
                    self.hop(way, step + 1, run).start()

            @pl.when(self.there(way, step))
            def _(way=way):
                self.share(way, step, run).start()

    def finish(self):
        for run in range(self.runs):
            self.share(0, 0, run).wait()
            for way in range(2):
                for step in range(1, 4):

                    @pl.when(self.there(way, step))
                    def _(way=way, step=step, run=run):
                        self.share(way, step, run).wait()

                    @pl.when(self.goes(way, step))
                    def _(way=way, step=step, run=run):
                        self.hop(way, step, run).wait_send()


def front_kernel(
    heads,
    x_ref,
    mem_k_ref,
    mem_v_ref,
    w_ref,
    cos_ref,
    sin_ref,
    every_ref,
    memory_ref,
    q_ref,
    k_ref,
    v_ref,
    mix_ref,
    max_ref,
    sum_ref,
    rows,
    slab,
    trade_sent,
    trade_received,
    rows_sent,
    rows_received,
    line_sent,
    line_received,
    core_sent,
    core_received,
    local,
):
    place = Place()
    seg, seq = lax.axis_index("seg"), lax.axis_index("seq")
    width = heads * HEAD_DIM
    count = mem_k_ref.shape[0]
    tokens, depth = x_ref.shape
    across = {"x": seq + 1 - 2 * place.x, "y": seq + 2 - 4 * place.y, "xy": 3 - seq}

    def remote(source, target, sent, received, slot, peer):
        return pltpu.make_async_remote_copy(
            src_ref=source,
            dst_ref=target,
            send_sem=sent.at[slot],
            recv_sem=received.at[slot],
            device_id=place.peer[peer],
            device_id_type=pl.DeviceIdType.MESH,
        )

    def columns(owner, start=0):
        return pl.ds(pl.multiple_of(start + owner * width, HEAD_DIM), width)

    def seat(owner):
        return pl.ds(pl.multiple_of(owner * count, 16), count)

    trades, arrivals = [], []
    for number, peer in enumerate(("x", "y", "xy")):
        for kind, source in enumerate((mem_k_ref, mem_v_ref)):
            lanes = pl.ds(kind * width, width)
            trades.append(
                remote(
                    source.at[:, columns(across[peer])],
                    slab.at[seat(seq), lanes],
                    trade_sent,
                    trade_received,
                    2 * number + kind,
                    peer,
                )
            )

    def trade_arrivals():
        for copy in trades:
            copy.wait_recv()

    keeps = [
        pltpu.make_async_copy(
            source.at[:, columns(seq)],
            slab.at[seat(seq), pl.ds(kind * width, width)],
            local.at[kind],
        )
        for kind, source in enumerate((mem_k_ref, mem_v_ref))
    ]
    half = depth // 2
    left, right = pl.ds(0, half), pl.ds(half, half)
    load = pltpu.make_async_copy(x_ref, rows.at[seq], local.at[2])
    direct = [
        remote(x_ref.at[:, left], rows.at[seq, :, left], rows_sent, rows_received, 0, "x"),
        remote(x_ref.at[:, right], rows.at[seq, :, right], rows_sent, rows_received, 1, "y"),
        remote(x_ref.at[:, right], rows.at[seq, :, right], rows_sent, rows_received, 2, "x"),
        remote(x_ref.at[:, left], rows.at[seq, :, left], rows_sent, rows_received, 3, "y"),
    ]
    onward = [
        remote(
            rows.at[across["x"], :, left], rows.at[across["x"], :, left], rows_sent, rows_received, 4, "y"
        ),
        remote(
            rows.at[across["y"], :, right], rows.at[across["y"], :, right], rows_sent, rows_received, 5, "x"
        ),
    ]
    line = Line(
        place, seg, slab, memory_ref, 2, (line_sent, line_received, core_sent, core_received)
    )
    keep_slab = pltpu.make_async_copy(slab, memory_ref.at[seg], local.at[3])
    keep_rows = pltpu.make_async_copy(rows, every_ref, local.at[4])

    def project_rows(owner):
        block = rows[owner]
        span = pl.ds(pl.multiple_of(owner * tokens, 16), tokens)
        cosine, sine = cos_ref[span, :], sin_ref[span, :]
        scale = SCORE_SCALE / LN2
        queries = product(block, w_ref[:, :width])
        keys = product(block, w_ref[:, width : 2 * width])
        for head in range(heads):
            lanes = slice(head * HEAD_DIM, (head + 1) * HEAD_DIM)
            q_ref[span, lanes] = turn_block(queries[:, lanes], cosine * scale, sine * scale).astype(
                jnp.bfloat16
            )
            k_ref[span, lanes] = turn_block(keys[:, lanes], cosine, sine).astype(jnp.bfloat16)
        v_ref[span, :] = product(block, w_ref[:, 2 * width :]).astype(jnp.bfloat16)

    def own_rows(block):
        def turn(head, carry):
            lanes = pl.ds(pl.multiple_of(head * HEAD_DIM, HEAD_DIM), HEAD_DIM)
            span = pl.ds(block * tokens, tokens)
            pairs = [
                (k_ref[pl.ds(n * tokens, tokens), lanes], v_ref[pl.ds(n * tokens, tokens), lanes])
                for n in range(block + 1)
            ]
            row_max, row_sum, mixed = attend(q_ref[span, lanes], pairs, True, None)
            mix_ref[span, lanes] = mixed
            max_ref[span, lanes] = jnp.broadcast_to(row_max, mixed.shape)
            sum_ref[span, lanes] = jnp.broadcast_to(row_sum, mixed.shape)
            return carry

        lax.fori_loop(0, heads, turn, 0)

    barrier = pltpu.get_barrier_semaphore()

    def hail(device):
        pl.semaphore_signal(barrier, inc=1, device_id=device, device_id_type=pl.DeviceIdType.MESH)

    for peer in ("x", "y", "xy", "core"):
        hail(place.peer[peer])
    below, above = place.z >= 1, place.z <= 2

    @pl.when(below)
    def _():
        hail((seg - 2, seq))

    @pl.when(above)
    def _():
        hail((seg + 2, seq))

    pl.semaphore_wait(barrier, 4 + below.astype(jnp.int32) + above.astype(jnp.int32))

    for copy in keeps + trades:
        copy.start()
    load.start()
    for copy in direct:
        copy.start()
    load.wait()
    project_rows(seq)
    for copy in keeps:
        copy.wait()
    trade_arrivals()
    line.start()
    keep_slab.start()
    direct[0].wait_recv()
    direct[1].wait_recv()
    for copy in onward:
        copy.start()
    line.advance(1, 0)
    direct[2].wait_recv()
    direct[3].wait_recv()
    project_rows(across["x"])
    line.advance(1, 1)
    project_rows(across["y"])
    for copy in onward:
        copy.wait_recv()
    project_rows(3 - seq)
    keep_rows.start()
    line.advance(2, 0)
    own_rows(0)
    own_rows(1)
    line.advance(2, 1)
    own_rows(2)
    own_rows(3)
    line.advance(3, 0)
    line.advance(3, 1)
    keep_slab.wait()
    keep_rows.wait()
    for copy in trades + direct + onward:
        copy.wait_send()
    line.finish()


def front(first_low, mem_keys, mem_values, w_heads, cosine, sine, seg_size, seq_size, collective_id):
    tokens, depth = first_low.shape
    length = tokens * seq_size
    width = w_heads.shape[1] // 3
    count = mem_keys.shape[0]
    anywhere = pl.BlockSpec(memory_space=pl.ANY)
    inside = pl.BlockSpec(memory_space=pltpu.VMEM)
    low = jnp.bfloat16
    shape = jax.ShapeDtypeStruct
    dma = pltpu.SemaphoreType.DMA
    return pl.pallas_call(
        functools.partial(front_kernel, width // HEAD_DIM),
        in_specs=[anywhere] * 3 + [inside] * 3,
        out_specs=[anywhere] * 2 + [inside] * 6,
        out_shape=[
            shape((seq_size, tokens, depth), low),
            shape((seg_size, count * seq_size, 2 * width), low),
        ]
        + [shape((length, width), low)] * 3
        + [shape((length, width), jnp.float32)] * 3,
        scratch_shapes=[
            pltpu.VMEM((seq_size, tokens, depth), low),
            pltpu.VMEM((count * seq_size, 2 * width), low),
            dma((6,)),
            dma((6,)),
            dma((6,)),
            dma((6,)),
            dma((12,)),
            dma((12,)),
            dma((16,)),
            dma((16,)),
            dma((5,)),
        ],
        compiler_params=pltpu.CompilerParams(
            collective_id=collective_id, has_side_effects=True, vmem_limit_bytes=VMEM_BYTES
        ),
        name="front",
    )(first_low, mem_keys, mem_values, w_heads, cosine, sine)


def norm_input_grad(values, inverse, norm_gain, upstream):
    weighted = upstream * norm_gain
    inner_mean = jnp.mean(weighted * values, axis=-1, keepdims=True)
    return inverse * weighted - inverse * inverse * inverse * values * inner_mean


def head_plan(
    seg_size,
    seq_size,
    layer_input,
    output_grad,
    norm1_gain,
    norm2_gain,
    w_qkv,
    w_out,
    w_gate,
    w_up,
    w_down,
    mem_keys,
    mem_values,
    memory_flags,
    sources,
):
    seg_index = lax.axis_index("seg")
    seq_index = lax.axis_index("seq")
    tokens = layer_input.shape[1]
    length = tokens * seq_size
    width = D // seq_size
    flag = lax.dynamic_index_in_dim(memory_flags, seg_index, 0, keepdims=True)
    listed = lax.dynamic_index_in_dim(sources, seg_index, 0, keepdims=False)
    chosen = jnp.concatenate([jnp.reshape(seg_index, (1,)), listed, flag]).astype(jnp.int32)

    inputs = layer_input[0].astype(jnp.float32)
    first_norm, first_inverse = norm_forward(inputs, norm1_gain)
    first_low = first_norm.astype(jnp.bfloat16)
    w_heads = lax.dynamic_index_in_dim(
        w_qkv.reshape(D, 3, seq_size, width), seq_index, 2, keepdims=False
    ).reshape(D, 3 * width)
    cosine, sine = turn_tables(lax.iota(jnp.int32, length).astype(jnp.float32))
    cosine, sine = cosine[:, 0, :], sine[:, 0, :]
    table = jnp.concatenate([cosine[:, : HEAD_DIM // 2], sine[:, : HEAD_DIM // 2]], axis=1)
    first_half = lax.broadcasted_iota(jnp.int32, sine.shape, 1) < HEAD_DIM // 2
    sine = jnp.where(first_half, -sine, sine)
    every_low, memory, queries, keys, values, mixed, row_max, row_sum = front(
        first_low, mem_keys[0], mem_values[0], w_heads, cosine, sine, seg_size, seq_size, 1
    )
    heads_low, chosen_memory, log_totals = memory_forward(
        chosen, queries, mixed, row_max, row_sum, memory
    )
    attended_low = lax.all_to_all(heads_low, "seq", 0, 1, tiled=True)

    residual = inputs + product(attended_low, w_out)
    second_norm, second_inverse = norm_forward(residual, norm2_gain)
    second_low = second_norm.astype(jnp.bfloat16)
    gate_values = product(second_low, w_gate)
    up_values = product(second_low, w_up)
    sigmoid_gate = jax.nn.sigmoid(gate_values)
    activated = gate_values * sigmoid_gate
    hidden_low = (activated * up_values).astype(jnp.bfloat16)
    output = (residual + product(hidden_low, w_down)).astype(jnp.bfloat16)
    upstream = output_grad[0]
    low = jnp.bfloat16
    term_down = product_tn(hidden_low, upstream).astype(low)
    grad_hidden = product_nt(upstream, w_down)
    grad_gate_low = (
        grad_hidden * up_values * sigmoid_gate * (1.0 + gate_values * (1.0 - sigmoid_gate))
    ).astype(low)
    grad_up_low = (grad_hidden * activated).astype(low)
    term_gate = product_tn(second_low, grad_gate_low).astype(low)
    term_up = product_tn(second_low, grad_up_low).astype(low)
    grad_second = product_nt(grad_gate_low, w_gate) + product_nt(grad_up_low, w_up)
    grad_residual = norm_input_grad(residual, second_inverse, norm2_gain, grad_second)
    grad_residual = grad_residual + upstream.astype(jnp.float32)
    residual_low = grad_residual.astype(low)
    term_out = product_tn(attended_low, residual_low).astype(low)
    grad_attended = product_nt(residual_low, w_out).astype(low)
    *sums, qkv_rows, first_rows = back(
        flag.astype(jnp.int32),
        grad_attended,
        queries,
        keys,
        values,
        chosen_memory,
        every_low,
        [term_down, term_gate, term_up, term_out],
        w_heads,
        heads_low,
        log_totals,
        table,
        2,
    )
    grad_down, grad_gate, grad_up, grad_out = [
        total.reshape(2 * total.shape[1], total.shape[2]).astype(jnp.float32) for total in sums
    ]
    grad_qkv = qkv_rows.reshape(width, 3 * D).astype(jnp.float32)
    grad_inputs = norm_input_grad(
        inputs, first_inverse, norm1_gain, first_rows.astype(jnp.float32)
    )
    input_grad = (grad_inputs + grad_residual)[None]

    def row_block(whole):
        return lax.dynamic_slice_in_dim(whole, seq_index * width, width, 0)

    def gain_rows(weights, grads, gain):
        dots = [
            jnp.sum(row_block(weight).astype(jnp.float32) * grad, axis=1)
            for weight, grad in zip(weights, grads)
        ]
        return sum(dots[1:], dots[0]) / row_block(gain)

    grad_norm1 = gain_rows([w_qkv], [grad_qkv], norm1_gain)
    grad_norm2 = gain_rows([w_gate, w_up], [grad_gate, grad_up], norm2_gain)
    return (
        output[None],
        input_grad,
        grad_norm1,
        grad_norm2,
        grad_qkv,
        grad_out,
        grad_gate,
        grad_up,
        grad_down,
    )


def solution(mesh):
    seq_size = mesh.shape["seq"]
    heads_fit = seq_size == 4 and mesh.shape["seg"] == 8
    plan = functools.partial(head_plan, mesh.shape["seg"], seq_size) if heads_fit else general_plan
    placed = (
        P("seg", "seq", None),
        P("seg", "seq", None),
        P(),
        P(),
        P(),
        P(),
        P(),
        P(),
        P(),
        P("seg", "seq", None),
        P("seg", "seq", None),
        P(),
        P(),
    )
    return jax.shard_map(
        plan,
        mesh=mesh,
        in_specs=placed,
        out_specs=(
            P("seg", "seq", None),
            P("seg", "seq", None),
            P("seq"),
            P("seq"),
            P("seq", None),
            P("seq", None),
            P("seq", None),
            P("seq", None),
            P("seq", None),
        ),
        check_vma=False,
    )
```

```python
import functools
import math

import jax
import jax.numpy as jnp
import numpy as np
from jax import lax
from jax.experimental import pallas as pl
from jax.experimental.pallas import tpu as pltpu
from jax.sharding import PartitionSpec as P

D = 1024
HEADS = 8
HEAD_DIM = 128


masked_score = -1e30
epsilon = 1e-06
rotary_base = 10000.0


def product(former, latter):
    return jnp.dot(former, latter, preferred_element_type=jnp.float32)


def product_nt(former, latter):
    return lax.dot_general(
        former, latter, (((1,), (1,)), ((), ())), preferred_element_type=jnp.float32
    )


def product_tn(former, latter):
    return lax.dot_general(
        former, latter, (((0,), (0,)), ((), ())), preferred_element_type=jnp.float32
    )


def norm_forward(values, norm_gain):
    inverse = lax.rsqrt(jnp.mean(values * values, axis=-1, keepdims=True) + epsilon)
    return (values * inverse * norm_gain, inverse)


def norm_backward(values, inverse, norm_gain, upstream):
    weighted = upstream * norm_gain
    inner_mean = jnp.mean(weighted * values, axis=-1, keepdims=True)
    grad_values = inverse * weighted - inverse * inverse * inverse * values * inner_mean
    grad_gain = jnp.sum(upstream * values * inverse, axis=0)
    return (grad_values, grad_gain)


def turn_tables(positions):
    half_dim = HEAD_DIM // 2
    exponent = -2.0 * jnp.arange(half_dim, dtype=jnp.float32) / HEAD_DIM
    angles = positions[:, None] * jnp.power(rotary_base, exponent)[None, :]
    angles = jnp.concatenate([angles, angles], axis=1)
    return (jnp.cos(angles)[:, None, :], jnp.sin(angles)[:, None, :])


def rotate(matrix, cosine_table, sine_table, direction):
    row_count = matrix.shape[0]
    half_dim = HEAD_DIM // 2
    shaped = matrix.reshape(row_count, HEADS, HEAD_DIM)
    turned = jnp.concatenate([-shaped[..., half_dim:], shaped[..., :half_dim]], axis=-1)
    return (shaped * cosine_table + direction * turned * sine_table).reshape(
        row_count, HEADS * HEAD_DIM
    )


def general_plan(
    layer_input,
    output_grad,
    norm1_gain,
    norm2_gain,
    w_qkv,
    w_out,
    w_gate,
    w_up,
    w_down,
    mem_keys,
    mem_values,
    memory_flags,
    sources,
):
    seg_index = lax.axis_index("seg")
    seq_index = lax.axis_index("seq")
    tokens = layer_input.shape[1]
    score_scale = HEAD_DIM ** (-0.5)
    flag_on = lax.dynamic_index_in_dim(memory_flags, seg_index, 0, keepdims=False) > 0
    listed = lax.dynamic_index_in_dim(sources, seg_index, 0, keepdims=False)
    picked = jnp.concatenate([jnp.reshape(seg_index, (1,)), listed])
    every_keys, every_values = (
        lax.all_gather(mem_keys, "seg", axis=0, tiled=True),
        lax.all_gather(mem_values, "seg", axis=0, tiled=True),
    )
    chosen_keys = jnp.take(every_keys, picked, axis=0)
    chosen_values = jnp.take(every_values, picked, axis=0)
    memory_keys, memory_values = (
        lax.all_gather(chosen_keys, "seq", axis=1, tiled=True),
        lax.all_gather(chosen_values, "seq", axis=1, tiled=True),
    )
    memory_key_blocks = memory_keys.reshape(-1, tokens, HEADS, HEAD_DIM)
    memory_value_blocks = memory_values.reshape(-1, tokens, HEADS, HEAD_DIM)
    memory_blocks = memory_key_blocks.shape[0]
    inputs = layer_input[0].astype(jnp.float32)
    first_norm, first_inverse = norm_forward(inputs, norm1_gain)
    first_low = first_norm.astype(jnp.bfloat16)
    projected = product(first_low, w_qkv)
    positions = seq_index * tokens + lax.iota(jnp.int32, tokens)
    cosine_table, sine_table = turn_tables(positions.astype(jnp.float32))
    queries = rotate(projected[:, :D], cosine_table, sine_table, 1.0).astype(jnp.bfloat16)
    own_keys = rotate(projected[:, D : 2 * D], cosine_table, sine_table, 1.0).astype(jnp.bfloat16)
    own_values = projected[:, 2 * D :].astype(jnp.bfloat16)
    all_keys, all_values = (
        lax.all_gather(own_keys, "seq", axis=0, tiled=True),
        lax.all_gather(own_values, "seq", axis=0, tiled=True),
    )
    key_blocks = all_keys.reshape(-1, tokens, HEADS, HEAD_DIM)
    value_blocks = all_values.reshape(-1, tokens, HEADS, HEAD_DIM)
    query_heads = queries.reshape(tokens, HEADS, HEAD_DIM)
    memory_open = jnp.broadcast_to(flag_on, (tokens, tokens))
    own_count = seq_index + 1
    key_offsets = lax.iota(jnp.int32, tokens)

    def own_open(block):
        return (block * tokens + key_offsets)[None, :] <= positions[:, None]

    def block_scores(key_block, open_mask):
        raw = (
            jnp.einsum("qhd,khd->hqk", query_heads, key_block, preferred_element_type=jnp.float32)
            * score_scale
        )
        return jnp.where(open_mask[None], raw, masked_score)

    def sweep(step, carry):

        def memory_turn(block, state):
            return step(
                state,
                block,
                memory_key_blocks[block],
                memory_value_blocks[block],
                memory_open,
                False,
            )

        def own_turn(block, state):
            return step(state, block, key_blocks[block], value_blocks[block], own_open(block), True)

        carry = lax.fori_loop(0, memory_blocks, memory_turn, carry)
        return lax.fori_loop(0, own_count, own_turn, carry)

    def max_step(carry, block, key_block, value_block, open_mask, own):
        row_max, row_sum = carry
        scores = block_scores(key_block, open_mask)
        new_max = jnp.maximum(row_max, jnp.max(scores, axis=2))
        row_sum = row_sum * jnp.exp(row_max - new_max) + jnp.sum(
            jnp.exp(scores - new_max[..., None]), axis=2
        )
        return (new_max, row_sum)

    start_max = jnp.full((HEADS, tokens), masked_score, jnp.float32)
    row_max, row_sum = sweep(max_step, (start_max, jnp.zeros((HEADS, tokens), jnp.float32)))
    log_totals = row_max + jnp.log(row_sum)

    def mix_step(total, block, key_block, value_block, open_mask, own):
        weights_low = jnp.exp(block_scores(key_block, open_mask) - log_totals[..., None]).astype(
            jnp.bfloat16
        )
        return total + jnp.einsum(
            "hqk,khd->qhd", weights_low, value_block, preferred_element_type=jnp.float32
        )

    attended = sweep(mix_step, jnp.zeros((tokens, HEADS, HEAD_DIM), jnp.float32))
    attended_low = attended.reshape(tokens, D).astype(jnp.bfloat16)
    residual = inputs + product(attended_low, w_out)
    second_norm, second_inverse = norm_forward(residual, norm2_gain)
    second_low = second_norm.astype(jnp.bfloat16)
    gate_values = product(second_low, w_gate)
    up_values = product(second_low, w_up)
    sigmoid_gate = jax.nn.sigmoid(gate_values)
    activated = gate_values * sigmoid_gate
    hidden_low = (activated * up_values).astype(jnp.bfloat16)
    output = (residual + product(hidden_low, w_down)).astype(jnp.bfloat16)
    upstream = output_grad[0]
    grad_down = product_tn(hidden_low, upstream)
    grad_hidden = product_nt(upstream, w_down)
    grad_gate_low = (
        grad_hidden * up_values * sigmoid_gate * (1.0 + gate_values * (1.0 - sigmoid_gate))
    ).astype(jnp.bfloat16)
    grad_up_low = (grad_hidden * activated).astype(jnp.bfloat16)
    grad_gate = product_tn(second_low, grad_gate_low)
    grad_up = product_tn(second_low, grad_up_low)
    grad_second = product_nt(grad_gate_low, w_gate) + product_nt(grad_up_low, w_up)
    grad_residual, grad_norm2 = norm_backward(residual, second_inverse, norm2_gain, grad_second)
    grad_residual = grad_residual + upstream.astype(jnp.float32)
    residual_low = grad_residual.astype(jnp.bfloat16)
    grad_out = product_tn(attended_low, residual_low)
    grad_attended = product_nt(residual_low, w_out).astype(jnp.bfloat16)
    grad_heads = grad_attended.reshape(tokens, HEADS, HEAD_DIM)

    def probs_pair(key_block, value_block, open_mask):
        probs = jnp.exp(block_scores(key_block, open_mask) - log_totals[..., None])
        dprobs = jnp.einsum(
            "qhd,khd->hqk", grad_heads, value_block, preferred_element_type=jnp.float32
        )
        return (probs, dprobs)

    def delta_step(total, block, key_block, value_block, open_mask, own):
        probs, dprobs = probs_pair(key_block, value_block, open_mask)
        return total + jnp.sum(probs * dprobs, axis=2)

    delta_rows = sweep(delta_step, jnp.zeros((HEADS, tokens), jnp.float32))

    def grad_step(carry, block, key_block, value_block, open_mask, own):
        grad_query, key_terms, value_terms = carry
        probs, dprobs = probs_pair(key_block, value_block, open_mask)
        dscores = (probs * (dprobs - delta_rows[..., None])).astype(jnp.bfloat16)
        grad_query = grad_query + jnp.einsum(
            "hqk,khd->qhd", dscores, key_block, preferred_element_type=jnp.float32
        )
        if own:
            key_part = (
                jnp.einsum("hqk,qhd->khd", dscores, query_heads, preferred_element_type=jnp.float32)
                * score_scale
            )
            value_part = jnp.einsum(
                "hqk,qhd->khd",
                probs.astype(jnp.bfloat16),
                grad_heads,
                preferred_element_type=jnp.float32,
            )
            key_terms = lax.dynamic_update_index_in_dim(key_terms, key_part, block, 0)
            value_terms = lax.dynamic_update_index_in_dim(value_terms, value_part, block, 0)
        return (grad_query, key_terms, value_terms)

    term_shape = key_blocks.shape
    start_grads = (
        jnp.zeros((tokens, HEADS, HEAD_DIM), jnp.float32),
        jnp.zeros(term_shape, jnp.float32),
        jnp.zeros(term_shape, jnp.float32),
    )
    grad_query, key_terms, value_terms = sweep(grad_step, start_grads)
    grad_queries = (grad_query * score_scale).reshape(tokens, D)
    grad_keys, grad_values = (
        lax.psum_scatter(
            key_terms.astype(jnp.bfloat16), "seq", scatter_dimension=0, tiled=True
        ).astype(jnp.float32),
        lax.psum_scatter(
            value_terms.astype(jnp.bfloat16), "seq", scatter_dimension=0, tiled=True
        ).astype(jnp.float32),
    )
    grad_projected = jnp.concatenate(
        [
            rotate(grad_queries, cosine_table, sine_table, -1.0),
            rotate(grad_keys.reshape(tokens, D), cosine_table, sine_table, -1.0),
            grad_values.reshape(tokens, D),
        ],
        axis=1,
    ).astype(jnp.bfloat16)
    grad_qkv = product_tn(first_low, grad_projected)
    grad_first = product_nt(grad_projected, w_qkv)
    grad_inputs, grad_norm1 = norm_backward(inputs, first_inverse, norm1_gain, grad_first)
    input_grad = (grad_inputs + grad_residual)[None]
    shares = (
        lax.psum_scatter(
            grad_norm1.astype(jnp.bfloat16), "seq", scatter_dimension=0, tiled=True
        ).astype(jnp.float32),
        lax.psum_scatter(
            grad_norm2.astype(jnp.bfloat16), "seq", scatter_dimension=0, tiled=True
        ).astype(jnp.float32),
        lax.psum_scatter(
            grad_qkv.astype(jnp.bfloat16), "seq", scatter_dimension=0, tiled=True
        ).astype(jnp.float32),
        lax.psum_scatter(
            grad_out.astype(jnp.bfloat16), "seq", scatter_dimension=0, tiled=True
        ).astype(jnp.float32),
        lax.psum_scatter(
            grad_gate.astype(jnp.bfloat16), "seq", scatter_dimension=0, tiled=True
        ).astype(jnp.float32),
        lax.psum_scatter(
            grad_up.astype(jnp.bfloat16), "seq", scatter_dimension=0, tiled=True
        ).astype(jnp.float32),
        lax.psum_scatter(
            grad_down.astype(jnp.bfloat16), "seq", scatter_dimension=0, tiled=True
        ).astype(jnp.float32),
    )
    totals = (
        lax.psum(shares[0].astype(jnp.bfloat16), "seg").astype(jnp.float32),
        lax.psum(shares[1].astype(jnp.bfloat16), "seg").astype(jnp.float32),
        lax.psum(shares[2].astype(jnp.bfloat16), "seg").astype(jnp.float32),
        lax.psum(shares[3].astype(jnp.bfloat16), "seg").astype(jnp.float32),
        lax.psum(shares[4].astype(jnp.bfloat16), "seg").astype(jnp.float32),
        lax.psum(shares[5].astype(jnp.bfloat16), "seg").astype(jnp.float32),
        lax.psum(shares[6].astype(jnp.bfloat16), "seg").astype(jnp.float32),
    )
    return (
        output[None],
        input_grad,
        totals[0],
        totals[1],
        totals[2],
        totals[3],
        totals[4],
        totals[5],
        totals[6],
    )


VMEM_BYTES = 60 * 1024 * 1024
VMEM_MOST = 67043328
LN2 = math.log(2.0)
SCORE_SCALE = HEAD_DIM ** (-0.5)


def lane_fold(op, tile, running):
    for column in range(tile.shape[1] // HEAD_DIM):
        piece = tile[:, column * HEAD_DIM : (column + 1) * HEAD_DIM]
        running = piece if running is None else op(running, piece)
    return running


def causal(scores):
    rows = lax.broadcasted_iota(jnp.int32, scores.shape, 0)
    columns = lax.broadcasted_iota(jnp.int32, scores.shape, 1)
    return jnp.where(columns <= rows, scores, masked_score)


def attend(query, pairs, diagonal, carried, closed=0.0):
    every, lane_max = [], None
    for index, (keys, _) in enumerate(pairs):
        scores = product_nt(query, keys)
        if diagonal and index == len(pairs) - 1:
            scores = causal(scores)
        lane_max = lane_fold(jnp.maximum, scores, lane_max)
        every.append(scores)
    row_max = jnp.max(lane_max, axis=1, keepdims=True) - closed
    if carried is not None:
        row_max = jnp.maximum(row_max, carried[0])
    shift = row_max + closed
    lane_sum, mixed = None, None
    for scores, (_, values) in zip(every, pairs):
        probs = jnp.exp2(scores - shift)
        lane_sum = lane_fold(jnp.add, probs, lane_sum)
        part = product(probs.astype(jnp.bfloat16), values)
        mixed = part if mixed is None else mixed + part
    row_sum = jnp.sum(lane_sum, axis=1, keepdims=True)
    if carried is not None:
        shrink = jnp.exp2(carried[0] - row_max)
        row_sum = carried[1] * shrink + row_sum
        mixed = carried[2] * shrink + mixed
    return row_max, row_sum, mixed


def turn_block(matrix, cosine, sine):
    return matrix * cosine + pltpu.roll(matrix, HEAD_DIM // 2, 1) * sine


def turn_factors(both):
    swapped = pltpu.roll(both, HEAD_DIM // 2, 1)
    first = lax.broadcasted_iota(jnp.int32, both.shape, 1) < HEAD_DIM // 2
    return jnp.where(first, both, swapped), jnp.where(first, swapped, -both)


def turn_table(length, step=64):
    frequency = rotary_base ** (-2.0 * np.arange(HEAD_DIM // 2) / HEAD_DIM)
    coarse = np.arange(length // step)[:, None] * step * frequency
    fine = np.arange(step)[:, None] * frequency

    def pair(former, latter):
        return jnp.asarray(np.concatenate([former, latter], axis=1), jnp.float32)

    table = (
        pair(np.cos(coarse), np.sin(coarse))[:, None, :] * pair(np.cos(fine), np.cos(fine))[None]
        + pair(-np.sin(coarse), np.cos(coarse))[:, None, :] * pair(np.sin(fine), np.sin(fine))[None]
    )
    return table.reshape(length, HEAD_DIM)


LINK_RATE = {"core": 300e3, "x": 49e3, "y": 49e3, "z": 49e3}


class Place:
    def __init__(self):
        seg, seq = lax.axis_index("seg"), lax.axis_index("seq")
        self.core, self.z = lax.rem(seg, 2), lax.div(seg, 2)
        self.x, self.y = lax.rem(seq, 2), lax.div(seq, 2)
        odd = lax.rem(self.z, 2)
        self.inner = jnp.logical_or(self.z == 1, self.z == 2)
        self.outer = jnp.logical_not(self.inner)
        self.peer = {
            "core": (seg + 1 - 2 * self.core, seq),
            "x": (seg, seq + 1 - 2 * self.x),
            "y": (seg, seq + 2 - 4 * self.y),
            "xy": (seg, 3 - seq),
            "pair": (seg + 2 - 4 * odd, seq),
            "middle": (seg - 2 + 4 * odd, seq),
        }

    def greet(self, names):
        barrier = pltpu.get_barrier_semaphore()

        def hail(name):
            pl.semaphore_signal(
                barrier, inc=1, device_id=self.peer[name], device_id_type=pl.DeviceIdType.MESH
            )

        for name in names:
            hail(name)

        @pl.when(self.inner)
        def _():
            hail("middle")

        pl.semaphore_wait(barrier, len(names) + self.inner.astype(jnp.int32))


def add_into(total, addend, step=16):
    def turn(index, carry):
        rows = pl.ds(pl.multiple_of(index * step, step), step)
        total[rows, :] = total[rows, :] + addend[rows, :]
        return carry

    lax.fori_loop(0, total.shape[0] // step, turn, 0)


def add_to(result, former, latter, step=16):
    def turn(index, carry):
        rows = pl.ds(pl.multiple_of(index * step, step), step)
        result[rows, :] = former[rows, :] + latter[rows, :]
        return carry

    lax.fori_loop(0, result.shape[0] // step, turn, 0)


def weight_copies(whole, part, seq, semaphores, first):
    width = part.shape[1] // 3
    depth = whole.shape[1] // 3
    return [
        pltpu.make_async_copy(
            whole.at[:, pl.ds(pl.multiple_of(kind * depth + seq * width, HEAD_DIM), width)],
            part.at[:, pl.ds(kind * width, width)],
            semaphores.at[first + kind],
        )
        for kind in range(3)
    ]


class Chunk:
    def __init__(self, term, offset, rows, columns, gather=False):
        self.term, self.offset, self.rows, self.columns = term, offset, rows, columns
        self.gather = gather

    def scratch(self):
        rows, columns, half = self.rows, self.columns, self.columns // 2
        low = jnp.bfloat16
        four = pltpu.VMEM((2, 2, rows, columns), low)
        one = four if self.gather else pltpu.VMEM((rows, columns), low)
        last = pltpu.VMEM((rows, 4 * columns), low) if self.gather else one
        if self.gather:
            middle = [four]
        else:
            middle = [
                pltpu.VMEM((2, rows, half), low),
                pltpu.VMEM((2, rows, half), low),
                pltpu.VMEM((rows, half), low),
                pltpu.VMEM((rows, half), low),
            ]
        ends = [one, one, last] if self.gather else [one, one]
        return [four, four] + middle + ends + [
            pltpu.SemaphoreType.DMA((9,)),
            pltpu.SemaphoreType.DMA((9,)),
            pltpu.SemaphoreType.DMA((3,)),
        ]

    def bind(self, place, source, result, refs):
        self.place, self.source, self.result = place, source, result
        self.mine, self.core_in = refs[0], refs[1]
        ends = 3 if self.gather else 2
        self.middle = refs[2 : -3 - ends]
        self.z_last, self.z_second = refs[-4], refs[-5]
        self.z_first = refs[-6] if self.gather else self.z_last
        self.sent, self.received, self.local = refs[-3:]

    def remote(self, slot, source, target, peer):
        return pltpu.make_async_remote_copy(
            src_ref=source,
            dst_ref=target,
            send_sem=self.sent.at[slot],
            recv_sem=self.received.at[slot],
            device_id=self.place.peer[peer],
            device_id_type=pl.DeviceIdType.MESH,
        )

    def core_copy(self):
        rows = pl.ds(self.offset, self.rows)
        return self.remote(
            0, self.source.at[:, :, 1 - self.place.core, rows, :], self.core_in, "core"
        )

    def load(self):
        rows = pl.ds(self.offset, self.rows)
        return pltpu.make_async_copy(
            self.source.at[:, :, self.place.core, rows, :], self.mine, self.local.at[0]
        )

    def halves(self):
        half = self.columns // 2
        return pl.ds(0, half), pl.ds(half, half)

    def wide_copies(self):
        p, (left, right) = self.place, self.halves()
        if self.gather:
            return [
                self.remote(1, self.mine.at[p.y, 1 - p.x], self.middle[0].at[p.y, p.x], "x"),
                self.remote(2, self.mine.at[1 - p.y, p.x], self.middle[0].at[p.y, p.x], "y"),
                self.remote(3, self.mine.at[1 - p.y, 1 - p.x], self.middle[0].at[p.y, p.x], "xy"),
            ]
        return [
            self.remote(1, self.mine.at[:, 1 - p.x, :, left], self.middle[0], "x"),
            self.remote(2, self.mine.at[1 - p.y, :, :, right], self.middle[1], "y"),
        ]

    def narrow_copies(self):
        p, (left, right) = self.place, self.halves()
        return [
            self.remote(3, self.mine.at[1 - p.y, p.x, :, left], self.middle[2], "y"),
            self.remote(4, self.mine.at[p.y, 1 - p.x, :, right], self.middle[3], "x"),
        ]

    def summed(self):
        return self.middle[0] if self.gather else self.mine.at[self.place.y, self.place.x]

    def pair_copy(self):
        return self.remote(5, self.summed(), self.z_first, "pair")

    def middle_copy(self):
        return self.remote(6, self.summed(), self.z_second, "middle")

    def last_copy(self):
        return self.remote(7, self.z_last, self.z_last, "pair")

    def out_copies(self):
        rows = pl.ds(self.offset, self.rows)
        core = self.place.core
        target = self.result.at[core, rows, :]
        return (
            self.remote(8, self.z_last, target, "core"),
            pltpu.make_async_copy(self.z_last, target, self.local.at[1]),
        )

    def parts(self, ref):
        if self.gather:
            return [ref.at[a, b] for a in range(2) for b in range(2)]
        return [ref]

    def lay_out(self):
        part = self.columns // 3
        for owner in range(4):
            for kind in range(3):
                lanes = pl.ds(kind * part, part)
                former = self.middle[0].at[owner // 2, owner % 2, :, lanes]
                latter = self.z_second.at[owner // 2, owner % 2, :, lanes]
                add_to(self.z_last.at[:, pl.ds((4 * kind + owner) * part, part)], former, latter)

    def stage_start(self):
        self.core_copy().start()
        self.load().start()

    def stage_core(self):
        self.core_copy().wait_recv()
        self.load().wait()
        for a in range(2):
            for b in range(2):
                add_into(self.mine.at[a, b], self.core_in.at[a, b])
        for copy in self.wide_copies():
            copy.start()

    def stage_wide(self):
        p, (left, right) = self.place, self.halves()
        if self.gather:
            stay = pltpu.make_async_copy(
                self.mine.at[p.y, p.x], self.middle[0].at[p.y, p.x], self.local.at[2]
            )
            stay.start()
            for copy in self.wide_copies():
                copy.wait_recv()
            stay.wait()
            self.z_start()
            return
        for copy in self.wide_copies():
            copy.wait_recv()
        for a in range(2):
            add_into(self.mine.at[a, p.x, :, left], self.middle[0].at[a])
            add_into(self.mine.at[p.y, a, :, right], self.middle[1].at[a])
        for copy in self.narrow_copies():
            copy.start()

    def stage_narrow(self):
        p, (left, right) = self.place, self.halves()
        for copy in self.narrow_copies():
            copy.wait_recv()
        add_into(self.mine.at[p.y, p.x, :, left], self.middle[2])
        add_into(self.mine.at[p.y, p.x, :, right], self.middle[3])
        self.z_start()

    def z_start(self):
        @pl.when(self.place.outer)
        def _():
            self.pair_copy().start()

    def stage_pair(self):
        @pl.when(self.place.inner)
        def _():
            self.pair_copy().wait_recv()
            for total, addend in zip(self.parts(self.summed()), self.parts(self.z_first)):
                add_into(total, addend)
            self.middle_copy().start()

    def stage_middle(self):
        @pl.when(self.place.inner)
        def _():
            self.middle_copy().wait_recv()
            if self.gather:
                self.lay_out()
            else:
                add_to(self.z_last, self.summed(), self.z_second)
            self.last_copy().start()
            for copy in self.out_copies():
                copy.start()

    def stage_last(self):
        @pl.when(self.place.outer)
        def _():
            self.last_copy().wait_recv()
            for copy in self.out_copies():
                copy.start()

    def stage_end(self):
        remote_out, local_out = self.out_copies()
        remote_out.wait()
        local_out.wait()
        self.core_copy().wait_send()
        for copy in self.wide_copies():
            copy.wait_send()
        if not self.gather:
            for copy in self.narrow_copies():
                copy.wait_send()

        @pl.when(self.place.outer)
        def _():
            self.pair_copy().wait_send()

        @pl.when(self.place.inner)
        def _():
            self.middle_copy().wait_send()
            self.last_copy().wait_send()

    def plan(self):
        piece = 2 * self.rows * self.columns
        if self.gather:
            return [
                (self.stage_core, [("x", 1.5 * piece), ("y", 1.5 * piece)]),
                (self.stage_wide, [("z", 4 * piece)]),
                (self.stage_pair, [("z", 4 * piece)]),
                (self.stage_middle, [("z", 4 * piece)]),
                (self.stage_last, [("core", 4 * piece)]),
                (self.stage_end, []),
            ]
        return [
            (self.stage_core, [("x", piece), ("y", piece)]),
            (self.stage_wide, [("x", piece / 2), ("y", piece / 2)]),
            (self.stage_narrow, [("z1", piece)]),
            (self.stage_pair, [("z2", piece)]),
            (self.stage_middle, [("z3", piece)]),
            (self.stage_last, [("core", piece)]),
            (self.stage_end, []),
        ]

    def opening(self):
        return [("core", 8 * self.rows * self.columns)]


class RowChunk:
    def __init__(self, term, offset, rows, columns):
        self.term, self.offset, self.rows, self.columns = term, offset, rows, columns

    def scratch(self):
        rows, columns, half = self.rows, self.columns, self.columns // 2
        low = jnp.bfloat16
        return [
            pltpu.VMEM((2, rows, half), low),
            pltpu.VMEM((2, rows, half), low),
            pltpu.VMEM((rows, half), low),
            pltpu.VMEM((rows, half), low),
            pltpu.SemaphoreType.DMA((6,)),
            pltpu.SemaphoreType.DMA((6,)),
            pltpu.SemaphoreType.DMA((1,)),
        ]

    def bind(self, place, source, result, refs):
        self.place, self.result = place, result
        self.blocks = source
        self.middle = refs[:4]
        self.sent, self.received, self.local = refs[4:]

    def mine(self, y, x, lanes):
        return self.blocks.at[2 * y + x, pl.ds(self.offset, self.rows), lanes]

    remote = Chunk.remote
    halves = Chunk.halves

    def wide_copies(self):
        p, (left, right) = self.place, self.halves()
        copies = []
        for a in range(2):
            copies.append(
                self.remote(a, self.mine(a, 1 - p.x, left), self.middle[0].at[a], "x")
            )
            copies.append(
                self.remote(2 + a, self.mine(1 - p.y, a, right), self.middle[1].at[a], "y")
            )
        return copies

    def narrow_copies(self):
        p, (left, right) = self.place, self.halves()
        return [
            self.remote(4, self.mine(1 - p.y, p.x, left), self.middle[2], "y"),
            self.remote(5, self.mine(p.y, 1 - p.x, right), self.middle[3], "x"),
        ]

    def out_copy(self):
        p = self.place
        whole = pl.ds(0, self.columns)
        return pltpu.make_async_copy(
            self.mine(p.y, p.x, whole),
            self.result.at[pl.ds(self.offset, self.rows), :],
            self.local.at[0],
        )

    def stage_start(self):
        for copy in self.wide_copies():
            copy.start()

    def stage_wide(self):
        p, (left, right) = self.place, self.halves()
        for copy in self.wide_copies():
            copy.wait_recv()
        for a in range(2):
            add_into(self.mine(a, p.x, left), self.middle[0].at[a])
            add_into(self.mine(p.y, a, right), self.middle[1].at[a])
        for copy in self.narrow_copies():
            copy.start()

    def stage_narrow(self):
        p, (left, right) = self.place, self.halves()
        for copy in self.narrow_copies():
            copy.wait_recv()
        add_into(self.mine(p.y, p.x, left), self.middle[2])
        add_into(self.mine(p.y, p.x, right), self.middle[3])
        self.out_copy().start()

    def stage_end(self):
        self.out_copy().wait()
        for copy in self.wide_copies() + self.narrow_copies():
            copy.wait_send()

    def plan(self):
        piece = 2 * self.rows * self.columns
        return [
            (self.stage_wide, [("x", piece / 2), ("y", piece / 2)]),
            (self.stage_narrow, [("core", 0.0)]),
            (self.stage_end, []),
        ]

    def opening(self):
        piece = 2 * self.rows * self.columns
        return [("x", piece), ("y", piece)]


class Steps:
    def __init__(self, start):
        self.now, self.free, self.waiting = start, {}, []

    def send(self, transfers):
        ends = [self.now]
        for link, size in transfers:
            start = max(self.now, self.free.get(link, 0.0))
            self.free[link] = start + size / LINK_RATE.get(link, LINK_RATE["z"])
            ends.append(self.free[link] + 2.0)
        return max(ends)

    def open(self, chunks):
        for chunk in chunks:
            self.waiting.append((self.send(chunk.opening()), len(self.waiting), chunk, 0))

    def due(self, everything=False):
        stages = []
        while self.waiting:
            self.waiting.sort(key=lambda entry: entry[:2])
            when, number, chunk, index = self.waiting[0]
            if when > self.now and not everything:
                break
            self.waiting.pop(0)
            self.now = max(self.now, when) + 0.4
            stage, transfers = chunk.plan()[index]
            stages.append(stage)
            if index + 1 < len(chunk.plan()):
                self.waiting.append((self.send(transfers), number, chunk, index + 1))
        return stages

    def spend(self, duration):
        self.now += duration


def back_kernel(
    chunks,
    first_chunks,
    heads,
    flag_ref,
    g_ref,
    q_hbm,
    k_hbm,
    v_hbm,
    memory_hbm,
    every_hbm,
    down_ref,
    gate_ref,
    up_ref,
    out_ref,
    w_hbm,
    mix_ref,
    log_ref,
    table_ref,
    sum_down,
    sum_gate,
    sum_up,
    sum_out,
    sum_qkv,
    sum_first,
    w_ref,
    q,
    k,
    v,
    upstream,
    shared,
    dk,
    dv,
    total,
    delta,
    part_qkv,
    trade_sent,
    trade_received,
    local,
    *refs,
):
    place = Place()
    seq = lax.axis_index("seq")
    tokens = g_ref.shape[0]
    width = heads * HEAD_DIM
    used = 0
    sources = [down_ref, gate_ref, up_ref, out_ref, part_qkv, shared]
    results = [sum_down, sum_gate, sum_up, sum_out, sum_qkv, sum_first]
    for chunk in chunks + first_chunks:
        count = len(chunk.scratch())
        chunk.bind(place, sources[chunk.term], results[chunk.term], refs[used : used + count])
        used += count

    def owner_at(turn):
        low, high = lax.rem(turn, 2), lax.div(turn, 2)
        x = place.x + low - 2 * place.x * low
        y = place.y + high - 2 * place.y * high
        return 2 * y + x

    def columns(owner):
        return pl.ds(pl.multiple_of(owner * width, HEAD_DIM), width)

    def span(block):
        return pl.ds(pl.multiple_of(block * tokens, tokens), tokens)

    def lanes(head):
        return pl.ds(pl.multiple_of(head * HEAD_DIM, HEAD_DIM), HEAD_DIM)

    across = {"x": seq + 1 - 2 * place.x, "y": seq + 2 - 4 * place.y, "xy": 3 - seq}
    trades = [
        pltpu.make_async_remote_copy(
            src_ref=g_ref.at[:, columns(across[peer])],
            dst_ref=upstream.at[span(seq), :],
            send_sem=trade_sent.at[slot],
            recv_sem=trade_received.at[slot],
            device_id=place.peer[peer],
            device_id_type=pl.DeviceIdType.MESH,
        )
        for slot, peer in enumerate(("x", "y", "xy"))
    ]
    loads = [
        pltpu.make_async_copy(g_ref.at[:, columns(seq)], upstream.at[span(seq), :], local.at[0]),
        pltpu.make_async_copy(q_hbm, q, local.at[1]),
        pltpu.make_async_copy(k_hbm, k, local.at[2]),
        pltpu.make_async_copy(v_hbm, v, local.at[3]),
        pltpu.make_async_copy(memory_hbm, shared, local.at[4]),
    ] + weight_copies(w_hbm, w_ref, seq, local, 6)
    load_every = pltpu.make_async_copy(every_hbm, shared, local.at[5])

    def turn_back(matrix, rows):
        cosine, sine = turn_factors(table_ref[rows, :])
        return turn_block(matrix, cosine, sine).astype(jnp.bfloat16)

    def memory_part(head, block):
        rows, mine = span(block), lanes(head)
        query, grads = q[rows, mine], upstream[rows, mine]
        row_delta = jnp.sum(
            grads.astype(jnp.float32) * mix_ref[rows, mine].astype(jnp.float32), axis=1, keepdims=True
        )
        delta[...] = jnp.broadcast_to(row_delta, delta.shape)
        closed = (1 - flag_ref[lax.axis_index("seg")]).astype(jnp.float32) * 1e30
        log_total = log_ref[rows, mine][:, :1] + closed
        result = jnp.zeros(total.shape, jnp.float32)
        for slot in range(shared.shape[0]):
            for run in range(2):

                def tile(kind):
                    start = pl.multiple_of((2 * run + kind) * width + head * HEAD_DIM, HEAD_DIM)
                    return shared[slot, :, pl.ds(start, HEAD_DIM)]

                keys, values = tile(0), tile(1)
                probs = jnp.exp2(product_nt(query, keys) - log_total)
                dscores = probs * (product_nt(grads, values) - row_delta)
                result = result + product(dscores.astype(jnp.bfloat16), keys)
        total[...] = result

    def own_part(head, block):
        rows, mine = span(block), lanes(head)
        query, grads = q[rows, mine], upstream[rows, mine]
        log_total, row_delta = log_ref[rows, mine][:, :1], delta[:, :1]

        def turn(other, result, diagonal):
            keys = k[span(other), mine]
            scores = product_nt(query, keys)
            if diagonal:
                scores = causal(scores)
            probs = jnp.exp2(scores - log_total)
            dscores = (probs * (product_nt(grads, v[span(other), mine]) - row_delta)).astype(
                jnp.bfloat16
            )
            dv[span(other), :] += product_tn(probs.astype(jnp.bfloat16), grads)
            dk[span(other), :] += product_tn(dscores, query)
            return result + product(dscores, keys)

        result = turn(block, total[...], True)
        result = lax.fori_loop(0, block, lambda other, r: turn(other, r, False), result)
        q[rows, mine] = turn_back(result * SCORE_SCALE, rows)

    def close_head(head):
        mine = lanes(head)

        def turn(block, carry):
            rows = span(block)
            k[rows, mine] = turn_back(dk[rows, :] * LN2, rows)
            v[rows, mine] = dv[rows, :].astype(jnp.bfloat16)
            return carry

        lax.fori_loop(0, 4, turn, 0)

    def multiply_qkv(index, carry):
        cut = pl.ds(pl.multiple_of(index * width, HEAD_DIM), width)
        for kind, part in enumerate((q, k, v)):
            term = None
            for block in range(shared.shape[0]):
                product_part = product_tn(shared[block, :, cut], part[block * tokens : (block + 1) * tokens, :])
                term = product_part if term is None else term + product_part
            term = term.astype(jnp.bfloat16)
            half = term.shape[0] // 2
            place_y, place_x = lax.div(index, 2), lax.rem(index, 2)
            for core in range(2):
                part_qkv[place_y, place_x, core, :, kind * width : (kind + 1) * width] = term[
                    core * half : (core + 1) * half, :
                ]
        return carry

    def multiply_first(block, carry):
        rows = span(block)
        result = None
        for kind, part in enumerate((q, k, v)):
            term = product_nt(part[rows, :], w_ref[:, kind * width : (kind + 1) * width])
            result = term if result is None else result + term
        shared[block] = result.astype(jnp.bfloat16)
        return carry

    place.greet(("core", "x", "y", "xy", "pair"))
    for copy in trades + loads:
        copy.start()
    for chunk in chunks:
        chunk.stage_start()
    steps = Steps(3.0)
    steps.free.update(x=11.0, y=11.0)
    steps.open(chunks)
    for copy in loads:
        copy.wait()
    slots = []
    for unit in range(2 * 4 * heads):
        slots.append(steps.due())
        steps.spend(4.3 if unit % 2 == 0 else 3.2)

    def run(stages):
        for stage in stages:
            stage()

    def unit(index, carry):
        head, turn = lax.div(index, 4), lax.rem(index, 4)
        block = owner_at(turn)
        for number in range(4 * heads):
            if slots[2 * number] or number in (1, 2, 3):

                @pl.when(index == number)
                def _(number=number):
                    run(slots[2 * number])
                    if number in (1, 2, 3):
                        trades[number - 1].wait_recv()

        @pl.when(turn == 0)
        def _():
            dk[...] = jnp.zeros_like(dk)
            dv[...] = jnp.zeros_like(dv)

        memory_part(head, block)
        for number in range(4 * heads):
            if slots[2 * number + 1]:

                @pl.when(index == number)
                def _(number=number):
                    run(slots[2 * number + 1])

        own_part(head, block)

        @pl.when(turn == 3)
        def _():
            close_head(head)

        return carry

    lax.fori_loop(0, 4 * heads, unit, 0)
    load_every.start()
    run(steps.due())
    load_every.wait()
    lax.fori_loop(0, 4, multiply_qkv, 0)
    steps.spend(8.0)
    qkv_chunks = [chunk for chunk in first_chunks if chunk.term == 4]
    row_chunks = [chunk for chunk in first_chunks if chunk.term == 5]
    for chunk in qkv_chunks:
        chunk.stage_start()
    steps.open(qkv_chunks)
    run(steps.due())
    lax.fori_loop(0, 4, multiply_first, 0)
    steps.spend(6.0)
    for chunk in row_chunks:
        chunk.stage_start()
    steps.open(row_chunks)
    run(steps.due(True))
    for copy in trades:
        copy.wait_send()


def back(
    flags, grads, queries, keys, values, memory, every, terms, w_qkv, attended, log_totals, table, collective_id
):
    tokens, depth = grads.shape
    length, width = queries.shape
    low = jnp.bfloat16
    chunks, shapes = [], []
    for index, term in enumerate(terms):
        rows, columns = term.shape[0] // 8, term.shape[1]
        parts = 2 if rows % 32 == 0 and index < 3 else 1
        chunks += [Chunk(index, n * rows // parts, rows // parts, columns) for n in range(parts)]
        shapes.append((2, rows, columns))
    rows = depth // 8
    first_chunks = [Chunk(4, n * rows // 2, rows // 2, 3 * width, True) for n in range(2)]
    first_chunks += [RowChunk(5, n * tokens // 4, tokens // 4, depth) for n in range(4)]
    shapes += [(2, rows, 12 * width), (tokens, depth)]
    anywhere = pl.BlockSpec(memory_space=pl.ANY)
    inside = pl.BlockSpec(memory_space=pltpu.VMEM)
    scratch = (
        [pltpu.VMEM((depth, 3 * width), low)]
        + [pltpu.VMEM((length, width), low)] * 4
        + [pltpu.VMEM((4, tokens, depth), low)]
        + [pltpu.VMEM((length, HEAD_DIM), jnp.float32)] * 2
        + [pltpu.VMEM((tokens, HEAD_DIM), jnp.float32)] * 2
        + [pltpu.VMEM((2, 2, 2, rows, 3 * width), low)]
        + [pltpu.SemaphoreType.DMA((3,))] * 2
        + [pltpu.SemaphoreType.DMA((9,))]
    )
    return pl.pallas_call(
        functools.partial(back_kernel, chunks, first_chunks, width // HEAD_DIM),
        in_specs=[pl.BlockSpec(memory_space=pltpu.SMEM)] + [anywhere] * 11 + [inside] * 3,
        out_specs=[anywhere] * len(shapes),
        out_shape=[jax.ShapeDtypeStruct(shape, low) for shape in shapes],
        scratch_shapes=scratch + [ref for chunk in chunks + first_chunks for ref in chunk.scratch()],
        compiler_params=pltpu.CompilerParams(
            collective_id=collective_id, has_side_effects=True, vmem_limit_bytes=VMEM_MOST
        ),
        name="back",
    )(
        flags,
        grads,
        queries,
        keys,
        values,
        memory,
        every,
        *[term.reshape((2, 2, 2, term.shape[0] // 8, term.shape[1])) for term in terms],
        w_qkv,
        attended,
        log_totals,
        table,
    )


class Line:
    def __init__(self, place, seg, memory, spans, refs):
        self.place, self.seg, self.memory, self.spans = place, seg, memory, spans
        self.runs = len(spans)
        self.sent, self.received, self.core_sent, self.core_received = refs

    def span(self, run):
        return self.spans[run]

    def there(self, way, step):
        return self.place.z >= step if way == 0 else self.place.z + step <= 3

    def goes(self, way, step):
        has = self.there(way, step - 1)
        return jnp.logical_and(has, self.place.z <= 2 if way == 0 else self.place.z >= 1)

    def index(self, way, step):
        return self.seg - 2 * step if way == 0 else self.seg + 2 * step

    def hop(self, way, step, run):
        name = self.index(way, step - 1)
        target = self.memory.at[name, self.span(run), :]
        slot = (way * 3 + step - 1) * self.runs + run
        seg, seq = lax.axis_index("seg"), lax.axis_index("seq")
        return pltpu.make_async_remote_copy(
            src_ref=target,
            dst_ref=target,
            send_sem=self.sent.at[slot],
            recv_sem=self.received.at[slot],
            device_id=(seg + 2 - 4 * way, seq),
            device_id_type=pl.DeviceIdType.MESH,
        )

    def arrival(self, way, step, run):
        target = self.memory.at[self.index(way, step), self.span(run), :]
        slot = (way * 3 + step - 1) * self.runs + run
        return pltpu.make_async_remote_copy(
            src_ref=target,
            dst_ref=target,
            send_sem=self.sent.at[slot],
            recv_sem=self.received.at[slot],
            device_id=self.place.peer["core"],
            device_id_type=pl.DeviceIdType.MESH,
        )

    def share(self, way, step, run):
        name = self.index(way, step)
        target = self.memory.at[name, self.span(run), :]
        slot = (way * 3 + step) * self.runs + run
        return pltpu.make_async_remote_copy(
            src_ref=target,
            dst_ref=target,
            send_sem=self.core_sent.at[slot],
            recv_sem=self.core_received.at[slot],
            device_id=self.place.peer["core"],
            device_id_type=pl.DeviceIdType.MESH,
        )

    def start(self, run):
        for way in range(2):

            @pl.when(self.goes(way, 1))
            def _(way=way):
                self.hop(way, 1, run).start()

        self.share(0, 0, run).start()

    def advance(self, step, run):
        for way in range(2):

            @pl.when(self.there(way, step))
            def _(way=way):
                self.arrival(way, step, run).wait_recv()

            if step < 3:

                @pl.when(self.goes(way, step + 1))
                def _(way=way):
                    self.hop(way, step + 1, run).start()

            @pl.when(self.there(way, step))
            def _(way=way):
                self.share(way, step, run).start()

    def finish(self):
        for run in range(self.runs):
            self.share(0, 0, run).wait()
            for way in range(2):
                for step in range(1, 4):

                    @pl.when(self.there(way, step))
                    def _(way=way, step=step, run=run):
                        self.share(way, step, run).wait()

                    @pl.when(self.goes(way, step))
                    def _(way=way, step=step, run=run):
                        self.hop(way, step, run).wait_send()


def front_kernel(
    heads,
    flag_ref,
    source_ref,
    x_ref,
    mem_k_ref,
    mem_v_ref,
    w_hbm,
    table_ref,
    every_ref,
    chosen_ref,
    attended_ref,
    q_ref,
    k_ref,
    v_ref,
    low_ref,
    log_ref,
    w_ref,
    rows,
    memory,
    listed,
    mix_ref,
    max_ref,
    sum_ref,
    trade_sent,
    trade_received,
    rows_sent,
    rows_received,
    line_sent,
    line_received,
    core_sent,
    core_received,
    back_sent,
    back_received,
    local,
):
    place = Place()
    seg, seq = lax.axis_index("seg"), lax.axis_index("seq")
    width = heads * HEAD_DIM
    count = mem_k_ref.shape[0]
    tokens, depth = x_ref.shape
    across = {"x": seq + 1 - 2 * place.x, "y": seq + 2 - 4 * place.y, "xy": 3 - seq}

    def remote(source, target, sent, received, slot, peer):
        return pltpu.make_async_remote_copy(
            src_ref=source,
            dst_ref=target,
            send_sem=sent.at[slot],
            recv_sem=received.at[slot],
            device_id=place.peer[peer],
            device_id_type=pl.DeviceIdType.MESH,
        )

    def columns(owner, start=0):
        return pl.ds(pl.multiple_of(start + owner * width, HEAD_DIM), width)

    def seat(owner):
        return pl.ds(pl.multiple_of(owner * count, 16), count)

    def owner_at(turn):
        low, high = lax.rem(turn, 2), lax.div(turn, 2)
        x = place.x + low - 2 * place.x * low
        y = place.y + high - 2 * place.y * high
        return 2 * y + x

    def block_rows(block):
        return pl.ds(pl.multiple_of(block * tokens, 16), tokens)

    peers = ("x", "y", "xy")
    trades = []
    for number, peer in enumerate(peers):
        for kind, source in enumerate((mem_k_ref, mem_v_ref)):
            lanes = pl.ds(kind * width, width)
            trades.append(
                remote(
                    source.at[:, columns(across[peer])],
                    memory.at[seg, seat(seq), lanes],
                    trade_sent,
                    trade_received,
                    2 * number + kind,
                    peer,
                )
            )
    keeps = [
        pltpu.make_async_copy(
            source.at[:, columns(seq)],
            memory.at[seg, seat(seq), pl.ds(kind * width, width)],
            local.at[kind],
        )
        for kind, source in enumerate((mem_k_ref, mem_v_ref))
    ]
    half = depth // 2
    left, right = pl.ds(0, half), pl.ds(half, half)
    load = pltpu.make_async_copy(x_ref, rows.at[seq], local.at[2])
    loads = weight_copies(w_hbm, w_ref, seq, local, 3)
    direct = [
        remote(x_ref.at[:, left], rows.at[seq, :, left], rows_sent, rows_received, 0, "x"),
        remote(x_ref.at[:, right], rows.at[seq, :, right], rows_sent, rows_received, 1, "y"),
        remote(x_ref.at[:, right], rows.at[seq, :, right], rows_sent, rows_received, 2, "x"),
        remote(x_ref.at[:, left], rows.at[seq, :, left], rows_sent, rows_received, 3, "y"),
    ]
    onward = [
        remote(
            rows.at[across["x"], :, left], rows.at[across["x"], :, left], rows_sent, rows_received, 4, "y"
        ),
        remote(
            rows.at[across["y"], :, right], rows.at[across["y"], :, right], rows_sent, rows_received, 5, "x"
        ),
    ]
    line = Line(
        place,
        seg,
        memory,
        [seat(owner) for owner in (seq, across["x"], across["y"], across["xy"])],
        (line_sent, line_received, core_sent, core_received),
    )
    keep_rows = pltpu.make_async_copy(rows, every_ref, local.at[6])
    run_rows = memory.shape[1] // 2
    keep_chosen = []
    for run in range(2):
        span, lanes = pl.ds(run * run_rows, run_rows), pl.ds(2 * run * width, 2 * width)
        keep_chosen.append(
            pltpu.make_async_copy(memory.at[seg, span, :], chosen_ref.at[0, :, lanes], local.at[7 + run])
        )
        keep_chosen.append(
            pltpu.make_async_copy(
                listed.at[:, span, :],
                chosen_ref.at[pl.ds(1, listed.shape[0]), :, lanes],
                local.at[9 + run],
            )
        )
    returns = [
        remote(
            low_ref.at[block_rows(across[peer]), :],
            attended_ref.at[:, columns(seq)],
            back_sent,
            back_received,
            slot,
            peer,
        )
        for slot, peer in enumerate(peers)
    ]
    keep_attended = pltpu.make_async_copy(
        low_ref.at[block_rows(seq), :], attended_ref.at[:, columns(seq)], local.at[11]
    )

    def project_rows(owner):
        block = rows[owner]
        span = block_rows(owner)
        cosine, sine = turn_factors(table_ref[span, :])
        scale = SCORE_SCALE / LN2
        queries = product(block, w_ref[:, :width])
        keys = product(block, w_ref[:, width : 2 * width])
        for head in range(heads):
            lanes = slice(head * HEAD_DIM, (head + 1) * HEAD_DIM)
            q_ref[span, lanes] = turn_block(
                queries[:, lanes], cosine * scale, sine * (-scale)
            ).astype(jnp.bfloat16)
            k_ref[span, lanes] = turn_block(keys[:, lanes], cosine, -sine).astype(jnp.bfloat16)
        v_ref[span, :] = product(block, w_ref[:, 2 * width :]).astype(jnp.bfloat16)

    def head_lanes(head, start=0):
        return pl.ds(pl.multiple_of(start + head * HEAD_DIM, HEAD_DIM), HEAD_DIM)

    def keep(span, lanes, row_max, row_sum, mixed):
        mix_ref[span, lanes] = mixed
        max_ref[span, lanes] = jnp.broadcast_to(row_max, mixed.shape)
        sum_ref[span, lanes] = jnp.broadcast_to(row_sum, mixed.shape)

    def own_rows(block):
        def turn(head, carry):
            lanes = head_lanes(head)
            span = pl.ds(block * tokens, tokens)
            pairs = [
                (k_ref[pl.ds(n * tokens, tokens), lanes], v_ref[pl.ds(n * tokens, tokens), lanes])
                for n in range(block + 1)
            ]
            keep(span, lanes, *attend(q_ref[span, lanes], pairs, True, None))
            return carry

        lax.fori_loop(0, heads, turn, 0)

    closed = (1 - flag_ref[seg]).astype(jnp.float32) * 1e30

    def carried(span, lanes):
        return max_ref[span, lanes][:, :1], sum_ref[span, lanes][:, :1], mix_ref[span, lanes]

    def own_memory(first, last):
        def turn(index, carry):
            head = lax.rem(index, heads)
            lanes, span = head_lanes(head), block_rows(lax.div(index, heads))
            pair = (memory[seg, :, lanes], memory[seg, :, head_lanes(head, width)])
            keep(span, lanes, *attend(q_ref[span, lanes], [pair], False, carried(span, lanes), closed))
            return carry

        lax.fori_loop(first * heads, last * heads, turn, 0)

    barrier = pltpu.get_barrier_semaphore()

    def hail(device):
        pl.semaphore_signal(barrier, inc=1, device_id=device, device_id_type=pl.DeviceIdType.MESH)

    for copy in keeps + [load] + loads:
        copy.start()
    for peer in ("x", "y", "xy", "core"):
        hail(place.peer[peer])
    below, above = place.z >= 1, place.z <= 2

    @pl.when(below)
    def _():
        hail((seg - 2, seq))

    @pl.when(above)
    def _():
        hail((seg + 2, seq))

    pl.semaphore_wait(barrier, 4 + below.astype(jnp.int32) + above.astype(jnp.int32))

    for copy in trades + direct:
        copy.start()
    for copy in keeps:
        copy.wait()
    line.start(0)
    load.wait()
    for copy in loads:
        copy.wait()
    project_rows(seq)
    for number in range(3):
        for kind in range(2):
            trades[2 * number + kind].wait_recv()
        line.start(number + 1)
        line.advance(1, number)
    direct[0].wait_recv()
    direct[1].wait_recv()
    for copy in onward:
        copy.start()
    line.advance(1, 3)
    line.advance(2, 0)
    direct[2].wait_recv()
    direct[3].wait_recv()
    project_rows(across["x"])
    line.advance(2, 1)
    project_rows(across["y"])
    line.advance(2, 2)
    for copy in onward:
        copy.wait_recv()
    project_rows(3 - seq)
    keep_rows.start()
    line.advance(2, 3)
    own_rows(0)
    own_rows(1)
    line.advance(3, 0)
    own_rows(2)
    line.advance(3, 1)
    own_rows(3)
    line.advance(3, 2)
    own_memory(0, 2)
    line.advance(3, 3)
    own_memory(2, 4)
    line.finish()
    for n in range(listed.shape[0]):
        listed[n] = memory[source_ref[seg, n]]

    def unit(index, carry):
        turn, head = lax.div(index, heads), lax.rem(index, heads)

        @pl.when(index == heads // 2)
        def _():
            for copy in keep_chosen:
                copy.start()

        for number in range(3):

            @pl.when(index == heads * (3 - number))
            def _(number=number):
                returns[number].start()

        lanes, span = head_lanes(head), block_rows(owner_at(3 - turn))
        pairs = [
            (listed[n, :, lanes], listed[n, :, head_lanes(head, width)])
            for n in range(listed.shape[0])
        ]
        row_max, row_sum, mixed = attend(
            q_ref[span, lanes], pairs, False, carried(span, lanes), closed
        )
        low_ref[span, lanes] = (mixed * (1.0 / row_sum)).astype(jnp.bfloat16)
        log_ref[span, lanes] = jnp.broadcast_to(row_max + jnp.log2(row_sum), mixed.shape)
        return carry

    lax.fori_loop(0, 4 * heads, unit, 0)
    keep_attended.start()
    for copy in returns:
        copy.wait()
    for copy in keep_chosen + [keep_rows, keep_attended]:
        copy.wait()
    for copy in trades + direct + onward:
        copy.wait_send()


def front(
    flags, sources, first_low, mem_keys, mem_values, w_qkv, table, seg_size, seq_size, collective_id
):
    tokens, depth = first_low.shape
    length = tokens * seq_size
    width = depth // seq_size
    count = mem_keys.shape[0] * seq_size
    slots = sources.shape[1]
    anywhere = pl.BlockSpec(memory_space=pl.ANY)
    inside = pl.BlockSpec(memory_space=pltpu.VMEM)
    scalars = pl.BlockSpec(memory_space=pltpu.SMEM)
    low = jnp.bfloat16
    shape = jax.ShapeDtypeStruct
    dma = pltpu.SemaphoreType.DMA
    return pl.pallas_call(
        functools.partial(front_kernel, width // HEAD_DIM),
        in_specs=[scalars] * 2 + [anywhere] * 4 + [inside],
        out_specs=[anywhere] * 3 + [inside] * 5,
        out_shape=[
            shape((seq_size, tokens, depth), low),
            shape((slots + 1, count // 2, 4 * width), low),
            shape((tokens, depth), low),
        ]
        + [shape((length, width), low)] * 4
        + [shape((length, width), jnp.float32)],
        scratch_shapes=[
            pltpu.VMEM((depth, 3 * width), low),
            pltpu.VMEM((seq_size, tokens, depth), low),
            pltpu.VMEM((seg_size, count, 2 * width), low),
            pltpu.VMEM((slots, count, 2 * width), low),
        ]
        + [pltpu.VMEM((length, width), jnp.float32)] * 3
        + [dma((6,))] * 4
        + [dma((24,))] * 2
        + [dma((28,))] * 2
        + [dma((3,))] * 2
        + [dma((12,))],
        compiler_params=pltpu.CompilerParams(
            collective_id=collective_id, has_side_effects=True, vmem_limit_bytes=VMEM_BYTES
        ),
        name="front",
    )(flags, sources, first_low, mem_keys, mem_values, w_qkv, table)


def norm_input_grad(values, inverse, norm_gain, upstream):
    weighted = upstream * norm_gain
    inner_mean = jnp.mean(weighted * values, axis=-1, keepdims=True)
    return inverse * weighted - inverse * inverse * inverse * values * inner_mean


def head_plan(
    seg_size,
    seq_size,
    layer_input,
    output_grad,
    norm1_gain,
    norm2_gain,
    w_qkv,
    w_out,
    w_gate,
    w_up,
    w_down,
    mem_keys,
    mem_values,
    memory_flags,
    sources,
):
    seq_index = lax.axis_index("seq")
    tokens = layer_input.shape[1]
    length = tokens * seq_size
    width = D // seq_size
    inputs = layer_input[0].astype(jnp.float32)
    first_norm, first_inverse = norm_forward(inputs, norm1_gain)
    first_low = first_norm.astype(jnp.bfloat16)
    table = turn_table(length)
    every_low, chosen_memory, attended_low, queries, keys, values, heads_low, log_totals = front(
        memory_flags, sources, first_low, mem_keys[0], mem_values[0], w_qkv, table, seg_size, seq_size, 1
    )

    residual = inputs + product(attended_low, w_out)
    second_norm, second_inverse = norm_forward(residual, norm2_gain)
    second_low = second_norm.astype(jnp.bfloat16)
    gate_values = product(second_low, w_gate)
    up_values = product(second_low, w_up)
    sigmoid_gate = jax.nn.sigmoid(gate_values)
    activated = gate_values * sigmoid_gate
    hidden_low = (activated * up_values).astype(jnp.bfloat16)
    output = (residual + product(hidden_low, w_down)).astype(jnp.bfloat16)
    upstream = output_grad[0]
    low = jnp.bfloat16
    term_down = product_tn(hidden_low, upstream).astype(low)
    grad_hidden = product_nt(upstream, w_down)
    grad_gate_low = (
        grad_hidden * up_values * sigmoid_gate * (1.0 + gate_values * (1.0 - sigmoid_gate))
    ).astype(low)
    grad_up_low = (grad_hidden * activated).astype(low)
    term_gate = product_tn(second_low, grad_gate_low).astype(low)
    term_up = product_tn(second_low, grad_up_low).astype(low)
    grad_second = product_nt(grad_gate_low, w_gate) + product_nt(grad_up_low, w_up)
    grad_residual = norm_input_grad(residual, second_inverse, norm2_gain, grad_second)
    grad_residual = grad_residual + upstream.astype(jnp.float32)
    residual_low = grad_residual.astype(low)
    term_out = product_tn(attended_low, residual_low).astype(low)
    grad_attended = product_nt(residual_low, w_out).astype(low)
    *sums, qkv_rows, first_rows = back(
        memory_flags,
        grad_attended,
        queries,
        keys,
        values,
        chosen_memory,
        every_low,
        [term_down, term_gate, term_up, term_out],
        w_qkv,
        heads_low,
        log_totals,
        table,
        2,
    )
    grad_down, grad_gate, grad_up, grad_out = [
        total.reshape(2 * total.shape[1], total.shape[2]).astype(jnp.float32) for total in sums
    ]
    grad_qkv = qkv_rows.reshape(width, 3 * D).astype(jnp.float32)
    grad_inputs = norm_input_grad(
        inputs, first_inverse, norm1_gain, first_rows.astype(jnp.float32)
    )
    input_grad = (grad_inputs + grad_residual)[None]

    def row_block(whole):
        return lax.dynamic_slice_in_dim(whole, seq_index * width, width, 0)

    def gain_rows(weights, grads, gain):
        dots = [
            jnp.sum(row_block(weight).astype(jnp.float32) * grad, axis=1)
            for weight, grad in zip(weights, grads)
        ]
        return sum(dots[1:], dots[0]) / row_block(gain)

    grad_norm1 = gain_rows([w_qkv], [grad_qkv], norm1_gain)
    grad_norm2 = gain_rows([w_gate, w_up], [grad_gate, grad_up], norm2_gain)
    return (
        output[None],
        input_grad,
        grad_norm1,
        grad_norm2,
        grad_qkv,
        grad_out,
        grad_gate,
        grad_up,
        grad_down,
    )


def solution(mesh):
    seq_size = mesh.shape["seq"]
    heads_fit = seq_size == 4 and mesh.shape["seg"] == 8
    plan = functools.partial(head_plan, mesh.shape["seg"], seq_size) if heads_fit else general_plan
    placed = (
        P("seg", "seq", None),
        P("seg", "seq", None),
        P(),
        P(),
        P(),
        P(),
        P(),
        P(),
        P(),
        P("seg", "seq", None),
        P("seg", "seq", None),
        P(),
        P(),
    )
    return jax.shard_map(
        plan,
        mesh=mesh,
        in_specs=placed,
        out_specs=(
            P("seg", "seq", None),
            P("seg", "seq", None),
            P("seq"),
            P("seq"),
            P("seq", None),
            P("seq", None),
            P("seq", None),
            P("seq", None),
            P("seq", None),
        ),
        check_vma=False,
    )
```

```python
import functools
import math

import jax
import jax.numpy as jnp
import numpy as np
from jax import lax
from jax.experimental import pallas as pl
from jax.experimental.pallas import tpu as pltpu
from jax.sharding import PartitionSpec as P

D = 1024
HEADS = 8
HEAD_DIM = 128


masked_score = -1e30
epsilon = 1e-06
rotary_base = 10000.0


def product(former, latter):
    return jnp.dot(former, latter, preferred_element_type=jnp.float32)


def product_nt(former, latter):
    return lax.dot_general(
        former, latter, (((1,), (1,)), ((), ())), preferred_element_type=jnp.float32
    )


def product_tn(former, latter):
    return lax.dot_general(
        former, latter, (((0,), (0,)), ((), ())), preferred_element_type=jnp.float32
    )


def norm_forward(values, norm_gain):
    inverse = lax.rsqrt(jnp.mean(values * values, axis=-1, keepdims=True) + epsilon)
    return (values * inverse * norm_gain, inverse)


def norm_backward(values, inverse, norm_gain, upstream):
    weighted = upstream * norm_gain
    inner_mean = jnp.mean(weighted * values, axis=-1, keepdims=True)
    grad_values = inverse * weighted - inverse * inverse * inverse * values * inner_mean
    grad_gain = jnp.sum(upstream * values * inverse, axis=0)
    return (grad_values, grad_gain)


def turn_tables(positions):
    half_dim = HEAD_DIM // 2
    exponent = -2.0 * jnp.arange(half_dim, dtype=jnp.float32) / HEAD_DIM
    angles = positions[:, None] * jnp.power(rotary_base, exponent)[None, :]
    angles = jnp.concatenate([angles, angles], axis=1)
    return (jnp.cos(angles)[:, None, :], jnp.sin(angles)[:, None, :])


def rotate(matrix, cosine_table, sine_table, direction):
    row_count = matrix.shape[0]
    half_dim = HEAD_DIM // 2
    shaped = matrix.reshape(row_count, HEADS, HEAD_DIM)
    turned = jnp.concatenate([-shaped[..., half_dim:], shaped[..., :half_dim]], axis=-1)
    return (shaped * cosine_table + direction * turned * sine_table).reshape(
        row_count, HEADS * HEAD_DIM
    )


def general_plan(
    layer_input,
    output_grad,
    norm1_gain,
    norm2_gain,
    w_qkv,
    w_out,
    w_gate,
    w_up,
    w_down,
    mem_keys,
    mem_values,
    memory_flags,
    sources,
):
    seg_index = lax.axis_index("seg")
    seq_index = lax.axis_index("seq")
    tokens = layer_input.shape[1]
    score_scale = HEAD_DIM ** (-0.5)
    flag_on = lax.dynamic_index_in_dim(memory_flags, seg_index, 0, keepdims=False) > 0
    listed = lax.dynamic_index_in_dim(sources, seg_index, 0, keepdims=False)
    picked = jnp.concatenate([jnp.reshape(seg_index, (1,)), listed])
    every_keys, every_values = (
        lax.all_gather(mem_keys, "seg", axis=0, tiled=True),
        lax.all_gather(mem_values, "seg", axis=0, tiled=True),
    )
    chosen_keys = jnp.take(every_keys, picked, axis=0)
    chosen_values = jnp.take(every_values, picked, axis=0)
    memory_keys, memory_values = (
        lax.all_gather(chosen_keys, "seq", axis=1, tiled=True),
        lax.all_gather(chosen_values, "seq", axis=1, tiled=True),
    )
    memory_key_blocks = memory_keys.reshape(-1, tokens, HEADS, HEAD_DIM)
    memory_value_blocks = memory_values.reshape(-1, tokens, HEADS, HEAD_DIM)
    memory_blocks = memory_key_blocks.shape[0]
    inputs = layer_input[0].astype(jnp.float32)
    first_norm, first_inverse = norm_forward(inputs, norm1_gain)
    first_low = first_norm.astype(jnp.bfloat16)
    projected = product(first_low, w_qkv)
    positions = seq_index * tokens + lax.iota(jnp.int32, tokens)
    cosine_table, sine_table = turn_tables(positions.astype(jnp.float32))
    queries = rotate(projected[:, :D], cosine_table, sine_table, 1.0).astype(jnp.bfloat16)
    own_keys = rotate(projected[:, D : 2 * D], cosine_table, sine_table, 1.0).astype(jnp.bfloat16)
    own_values = projected[:, 2 * D :].astype(jnp.bfloat16)
    all_keys, all_values = (
        lax.all_gather(own_keys, "seq", axis=0, tiled=True),
        lax.all_gather(own_values, "seq", axis=0, tiled=True),
    )
    key_blocks = all_keys.reshape(-1, tokens, HEADS, HEAD_DIM)
    value_blocks = all_values.reshape(-1, tokens, HEADS, HEAD_DIM)
    query_heads = queries.reshape(tokens, HEADS, HEAD_DIM)
    memory_open = jnp.broadcast_to(flag_on, (tokens, tokens))
    own_count = seq_index + 1
    key_offsets = lax.iota(jnp.int32, tokens)

    def own_open(block):
        return (block * tokens + key_offsets)[None, :] <= positions[:, None]

    def block_scores(key_block, open_mask):
        raw = (
            jnp.einsum("qhd,khd->hqk", query_heads, key_block, preferred_element_type=jnp.float32)
            * score_scale
        )
        return jnp.where(open_mask[None], raw, masked_score)

    def sweep(step, carry):

        def memory_turn(block, state):
            return step(
                state,
                block,
                memory_key_blocks[block],
                memory_value_blocks[block],
                memory_open,
                False,
            )

        def own_turn(block, state):
            return step(state, block, key_blocks[block], value_blocks[block], own_open(block), True)

        carry = lax.fori_loop(0, memory_blocks, memory_turn, carry)
        return lax.fori_loop(0, own_count, own_turn, carry)

    def max_step(carry, block, key_block, value_block, open_mask, own):
        row_max, row_sum = carry
        scores = block_scores(key_block, open_mask)
        new_max = jnp.maximum(row_max, jnp.max(scores, axis=2))
        row_sum = row_sum * jnp.exp(row_max - new_max) + jnp.sum(
            jnp.exp(scores - new_max[..., None]), axis=2
        )
        return (new_max, row_sum)

    start_max = jnp.full((HEADS, tokens), masked_score, jnp.float32)
    row_max, row_sum = sweep(max_step, (start_max, jnp.zeros((HEADS, tokens), jnp.float32)))
    log_totals = row_max + jnp.log(row_sum)

    def mix_step(total, block, key_block, value_block, open_mask, own):
        weights_low = jnp.exp(block_scores(key_block, open_mask) - log_totals[..., None]).astype(
            jnp.bfloat16
        )
        return total + jnp.einsum(
            "hqk,khd->qhd", weights_low, value_block, preferred_element_type=jnp.float32
        )

    attended = sweep(mix_step, jnp.zeros((tokens, HEADS, HEAD_DIM), jnp.float32))
    attended_low = attended.reshape(tokens, D).astype(jnp.bfloat16)
    residual = inputs + product(attended_low, w_out)
    second_norm, second_inverse = norm_forward(residual, norm2_gain)
    second_low = second_norm.astype(jnp.bfloat16)
    gate_values = product(second_low, w_gate)
    up_values = product(second_low, w_up)
    sigmoid_gate = jax.nn.sigmoid(gate_values)
    activated = gate_values * sigmoid_gate
    hidden_low = (activated * up_values).astype(jnp.bfloat16)
    output = (residual + product(hidden_low, w_down)).astype(jnp.bfloat16)
    upstream = output_grad[0]
    grad_down = product_tn(hidden_low, upstream)
    grad_hidden = product_nt(upstream, w_down)
    grad_gate_low = (
        grad_hidden * up_values * sigmoid_gate * (1.0 + gate_values * (1.0 - sigmoid_gate))
    ).astype(jnp.bfloat16)
    grad_up_low = (grad_hidden * activated).astype(jnp.bfloat16)
    grad_gate = product_tn(second_low, grad_gate_low)
    grad_up = product_tn(second_low, grad_up_low)
    grad_second = product_nt(grad_gate_low, w_gate) + product_nt(grad_up_low, w_up)
    grad_residual, grad_norm2 = norm_backward(residual, second_inverse, norm2_gain, grad_second)
    grad_residual = grad_residual + upstream.astype(jnp.float32)
    residual_low = grad_residual.astype(jnp.bfloat16)
    grad_out = product_tn(attended_low, residual_low)
    grad_attended = product_nt(residual_low, w_out).astype(jnp.bfloat16)
    grad_heads = grad_attended.reshape(tokens, HEADS, HEAD_DIM)

    def probs_pair(key_block, value_block, open_mask):
        probs = jnp.exp(block_scores(key_block, open_mask) - log_totals[..., None])
        dprobs = jnp.einsum(
            "qhd,khd->hqk", grad_heads, value_block, preferred_element_type=jnp.float32
        )
        return (probs, dprobs)

    def delta_step(total, block, key_block, value_block, open_mask, own):
        probs, dprobs = probs_pair(key_block, value_block, open_mask)
        return total + jnp.sum(probs * dprobs, axis=2)

    delta_rows = sweep(delta_step, jnp.zeros((HEADS, tokens), jnp.float32))

    def grad_step(carry, block, key_block, value_block, open_mask, own):
        grad_query, key_terms, value_terms = carry
        probs, dprobs = probs_pair(key_block, value_block, open_mask)
        dscores = (probs * (dprobs - delta_rows[..., None])).astype(jnp.bfloat16)
        grad_query = grad_query + jnp.einsum(
            "hqk,khd->qhd", dscores, key_block, preferred_element_type=jnp.float32
        )
        if own:
            key_part = (
                jnp.einsum("hqk,qhd->khd", dscores, query_heads, preferred_element_type=jnp.float32)
                * score_scale
            )
            value_part = jnp.einsum(
                "hqk,qhd->khd",
                probs.astype(jnp.bfloat16),
                grad_heads,
                preferred_element_type=jnp.float32,
            )
            key_terms = lax.dynamic_update_index_in_dim(key_terms, key_part, block, 0)
            value_terms = lax.dynamic_update_index_in_dim(value_terms, value_part, block, 0)
        return (grad_query, key_terms, value_terms)

    term_shape = key_blocks.shape
    start_grads = (
        jnp.zeros((tokens, HEADS, HEAD_DIM), jnp.float32),
        jnp.zeros(term_shape, jnp.float32),
        jnp.zeros(term_shape, jnp.float32),
    )
    grad_query, key_terms, value_terms = sweep(grad_step, start_grads)
    grad_queries = (grad_query * score_scale).reshape(tokens, D)
    grad_keys, grad_values = (
        lax.psum_scatter(
            key_terms.astype(jnp.bfloat16), "seq", scatter_dimension=0, tiled=True
        ).astype(jnp.float32),
        lax.psum_scatter(
            value_terms.astype(jnp.bfloat16), "seq", scatter_dimension=0, tiled=True
        ).astype(jnp.float32),
    )
    grad_projected = jnp.concatenate(
        [
            rotate(grad_queries, cosine_table, sine_table, -1.0),
            rotate(grad_keys.reshape(tokens, D), cosine_table, sine_table, -1.0),
            grad_values.reshape(tokens, D),
        ],
        axis=1,
    ).astype(jnp.bfloat16)
    grad_qkv = product_tn(first_low, grad_projected)
    grad_first = product_nt(grad_projected, w_qkv)
    grad_inputs, grad_norm1 = norm_backward(inputs, first_inverse, norm1_gain, grad_first)
    input_grad = (grad_inputs + grad_residual)[None]
    shares = (
        lax.psum_scatter(
            grad_norm1.astype(jnp.bfloat16), "seq", scatter_dimension=0, tiled=True
        ).astype(jnp.float32),
        lax.psum_scatter(
            grad_norm2.astype(jnp.bfloat16), "seq", scatter_dimension=0, tiled=True
        ).astype(jnp.float32),
        lax.psum_scatter(
            grad_qkv.astype(jnp.bfloat16), "seq", scatter_dimension=0, tiled=True
        ).astype(jnp.float32),
        lax.psum_scatter(
            grad_out.astype(jnp.bfloat16), "seq", scatter_dimension=0, tiled=True
        ).astype(jnp.float32),
        lax.psum_scatter(
            grad_gate.astype(jnp.bfloat16), "seq", scatter_dimension=0, tiled=True
        ).astype(jnp.float32),
        lax.psum_scatter(
            grad_up.astype(jnp.bfloat16), "seq", scatter_dimension=0, tiled=True
        ).astype(jnp.float32),
        lax.psum_scatter(
            grad_down.astype(jnp.bfloat16), "seq", scatter_dimension=0, tiled=True
        ).astype(jnp.float32),
    )
    totals = (
        lax.psum(shares[0].astype(jnp.bfloat16), "seg").astype(jnp.float32),
        lax.psum(shares[1].astype(jnp.bfloat16), "seg").astype(jnp.float32),
        lax.psum(shares[2].astype(jnp.bfloat16), "seg").astype(jnp.float32),
        lax.psum(shares[3].astype(jnp.bfloat16), "seg").astype(jnp.float32),
        lax.psum(shares[4].astype(jnp.bfloat16), "seg").astype(jnp.float32),
        lax.psum(shares[5].astype(jnp.bfloat16), "seg").astype(jnp.float32),
        lax.psum(shares[6].astype(jnp.bfloat16), "seg").astype(jnp.float32),
    )
    return (
        output[None],
        input_grad,
        totals[0],
        totals[1],
        totals[2],
        totals[3],
        totals[4],
        totals[5],
        totals[6],
    )


VMEM_BYTES = 60 * 1024 * 1024
VMEM_MOST = 67043328
LN2 = math.log(2.0)
SCORE_SCALE = HEAD_DIM ** (-0.5)


def lane_fold(op, tile, running):
    for column in range(tile.shape[1] // HEAD_DIM):
        piece = tile[:, column * HEAD_DIM : (column + 1) * HEAD_DIM]
        running = piece if running is None else op(running, piece)
    return running


def causal(scores):
    rows = lax.broadcasted_iota(jnp.int32, scores.shape, 0)
    columns = lax.broadcasted_iota(jnp.int32, scores.shape, 1)
    return jnp.where(columns <= rows, scores, masked_score)


def attend(query, pairs, diagonal, carried, closed=0.0):
    every, lane_max = [], None
    for index, (keys, _) in enumerate(pairs):
        scores = product_nt(query, keys)
        if diagonal and index == len(pairs) - 1:
            scores = causal(scores)
        lane_max = lane_fold(jnp.maximum, scores, lane_max)
        every.append(scores)
    row_max = jnp.max(lane_max, axis=1, keepdims=True) - closed
    if carried is not None:
        row_max = jnp.maximum(row_max, carried[0])
    shift = row_max + closed
    lane_sum, mixed = None, None
    for scores, (_, values) in zip(every, pairs):
        probs = jnp.exp2(scores - shift)
        lane_sum = lane_fold(jnp.add, probs, lane_sum)
        part = product(probs.astype(jnp.bfloat16), values)
        mixed = part if mixed is None else mixed + part
    row_sum = jnp.sum(lane_sum, axis=1, keepdims=True)
    if carried is not None:
        shrink = jnp.exp2(carried[0] - row_max)
        row_sum = carried[1] * shrink + row_sum
        mixed = carried[2] * shrink + mixed
    return row_max, row_sum, mixed


def turn_block(matrix, cosine, sine):
    return matrix * cosine + pltpu.roll(matrix, HEAD_DIM // 2, 1) * sine


def turn_factors(both):
    swapped = pltpu.roll(both, HEAD_DIM // 2, 1)
    first = lax.broadcasted_iota(jnp.int32, both.shape, 1) < HEAD_DIM // 2
    return jnp.where(first, both, swapped), jnp.where(first, swapped, -both)


def turn_table(length, step=64):
    frequency = rotary_base ** (-2.0 * np.arange(HEAD_DIM // 2) / HEAD_DIM)
    coarse = np.arange(length // step)[:, None] * step * frequency
    fine = np.arange(step)[:, None] * frequency

    def pair(former, latter):
        return jnp.asarray(np.concatenate([former, latter], axis=1), jnp.float32)

    table = (
        pair(np.cos(coarse), np.sin(coarse))[:, None, :] * pair(np.cos(fine), np.cos(fine))[None]
        + pair(-np.sin(coarse), np.cos(coarse))[:, None, :] * pair(np.sin(fine), np.sin(fine))[None]
    )
    return table.reshape(length, HEAD_DIM)


LINK_RATE = {"core": 300e3, "x": 49e3, "y": 49e3, "z": 49e3}


class Place:
    def __init__(self):
        seg, seq = lax.axis_index("seg"), lax.axis_index("seq")
        self.core, self.z = lax.rem(seg, 2), lax.div(seg, 2)
        self.x, self.y = lax.rem(seq, 2), lax.div(seq, 2)
        odd = lax.rem(self.z, 2)
        self.inner = jnp.logical_or(self.z == 1, self.z == 2)
        self.outer = jnp.logical_not(self.inner)
        self.peer = {
            "core": (seg + 1 - 2 * self.core, seq),
            "x": (seg, seq + 1 - 2 * self.x),
            "y": (seg, seq + 2 - 4 * self.y),
            "xy": (seg, 3 - seq),
            "pair": (seg + 2 - 4 * odd, seq),
            "middle": (seg - 2 + 4 * odd, seq),
        }

    def greet(self, names):
        barrier = pltpu.get_barrier_semaphore()

        def hail(name):
            pl.semaphore_signal(
                barrier, inc=1, device_id=self.peer[name], device_id_type=pl.DeviceIdType.MESH
            )

        for name in names:
            hail(name)

        @pl.when(self.inner)
        def _():
            hail("middle")

        pl.semaphore_wait(barrier, len(names) + self.inner.astype(jnp.int32))


def add_into(total, addend, step=16):
    def turn(index, carry):
        rows = pl.ds(pl.multiple_of(index * step, step), step)
        total[rows, :] = total[rows, :] + addend[rows, :]
        return carry

    lax.fori_loop(0, total.shape[0] // step, turn, 0)


def add_to(result, former, latter, step=16):
    def turn(index, carry):
        rows = pl.ds(pl.multiple_of(index * step, step), step)
        result[rows, :] = former[rows, :] + latter[rows, :]
        return carry

    lax.fori_loop(0, result.shape[0] // step, turn, 0)


def weight_copies(whole, part, seq, semaphores, first):
    width = part.shape[1] // 3
    depth = whole.shape[1] // 3
    return [
        pltpu.make_async_copy(
            whole.at[:, pl.ds(pl.multiple_of(kind * depth + seq * width, HEAD_DIM), width)],
            part.at[:, pl.ds(kind * width, width)],
            semaphores.at[first + kind],
        )
        for kind in range(3)
    ]


class Chunk:
    def __init__(self, term, offset, rows, columns, gather=False):
        self.term, self.offset, self.rows, self.columns = term, offset, rows, columns
        self.gather = gather

    def scratch(self):
        rows, columns, half = self.rows, self.columns, self.columns // 2
        low = jnp.bfloat16
        four = pltpu.VMEM((2, 2, rows, columns), low)
        one = four if self.gather else pltpu.VMEM((rows, columns), low)
        last = pltpu.VMEM((rows, 4 * columns), low) if self.gather else one
        if self.gather:
            middle = [four]
        else:
            middle = [
                pltpu.VMEM((2, rows, half), low),
                pltpu.VMEM((2, rows, half), low),
                pltpu.VMEM((rows, half), low),
                pltpu.VMEM((rows, half), low),
            ]
        ends = [one, one, last] if self.gather else [one, one]
        return [four, four] + middle + ends + [
            pltpu.SemaphoreType.DMA((9,)),
            pltpu.SemaphoreType.DMA((9,)),
            pltpu.SemaphoreType.DMA((3,)),
        ]

    def bind(self, place, source, result, refs):
        self.place, self.source, self.result = place, source, result
        self.mine, self.core_in = refs[0], refs[1]
        ends = 3 if self.gather else 2
        self.middle = refs[2 : -3 - ends]
        self.z_last, self.z_second = refs[-4], refs[-5]
        self.z_first = refs[-6] if self.gather else self.z_last
        self.sent, self.received, self.local = refs[-3:]

    def remote(self, slot, source, target, peer):
        return pltpu.make_async_remote_copy(
            src_ref=source,
            dst_ref=target,
            send_sem=self.sent.at[slot],
            recv_sem=self.received.at[slot],
            device_id=self.place.peer[peer],
            device_id_type=pl.DeviceIdType.MESH,
        )

    def core_copy(self):
        rows = pl.ds(self.offset, self.rows)
        return self.remote(
            0, self.source.at[:, :, 1 - self.place.core, rows, :], self.core_in, "core"
        )

    def load(self):
        rows = pl.ds(self.offset, self.rows)
        return pltpu.make_async_copy(
            self.source.at[:, :, self.place.core, rows, :], self.mine, self.local.at[0]
        )

    def halves(self):
        half = self.columns // 2
        return pl.ds(0, half), pl.ds(half, half)

    def wide_copies(self):
        p, (left, right) = self.place, self.halves()
        if self.gather:
            return [
                self.remote(1, self.mine.at[p.y, 1 - p.x], self.middle[0].at[p.y, p.x], "x"),
                self.remote(2, self.mine.at[1 - p.y, p.x], self.middle[0].at[p.y, p.x], "y"),
                self.remote(3, self.mine.at[1 - p.y, 1 - p.x], self.middle[0].at[p.y, p.x], "xy"),
            ]
        return [
            self.remote(1, self.mine.at[:, 1 - p.x, :, left], self.middle[0], "x"),
            self.remote(2, self.mine.at[1 - p.y, :, :, right], self.middle[1], "y"),
        ]

    def narrow_copies(self):
        p, (left, right) = self.place, self.halves()
        return [
            self.remote(3, self.mine.at[1 - p.y, p.x, :, left], self.middle[2], "y"),
            self.remote(4, self.mine.at[p.y, 1 - p.x, :, right], self.middle[3], "x"),
        ]

    def summed(self):
        return self.middle[0] if self.gather else self.mine.at[self.place.y, self.place.x]

    def pair_copy(self):
        return self.remote(5, self.summed(), self.z_first, "pair")

    def middle_copy(self):
        return self.remote(6, self.summed(), self.z_second, "middle")

    def last_copy(self):
        return self.remote(7, self.z_last, self.z_last, "pair")

    def out_copies(self):
        rows = pl.ds(self.offset, self.rows)
        core = self.place.core
        target = self.result.at[core, rows, :]
        return (
            self.remote(8, self.z_last, target, "core"),
            pltpu.make_async_copy(self.z_last, target, self.local.at[1]),
        )

    def parts(self, ref):
        if self.gather:
            return [ref.at[a, b] for a in range(2) for b in range(2)]
        return [ref]

    def lay_out(self):
        part = self.columns // 3
        for owner in range(4):
            for kind in range(3):
                lanes = pl.ds(kind * part, part)
                former = self.middle[0].at[owner // 2, owner % 2, :, lanes]
                latter = self.z_second.at[owner // 2, owner % 2, :, lanes]
                add_to(self.z_last.at[:, pl.ds((4 * kind + owner) * part, part)], former, latter)

    def stage_start(self):
        self.core_copy().start()
        self.load().start()

    def stage_core(self):
        self.core_copy().wait_recv()
        self.load().wait()
        for a in range(2):
            for b in range(2):
                add_into(self.mine.at[a, b], self.core_in.at[a, b])
        for copy in self.wide_copies():
            copy.start()

    def stage_wide(self):
        p, (left, right) = self.place, self.halves()
        if self.gather:
            stay = pltpu.make_async_copy(
                self.mine.at[p.y, p.x], self.middle[0].at[p.y, p.x], self.local.at[2]
            )
            stay.start()
            for copy in self.wide_copies():
                copy.wait_recv()
            stay.wait()
            self.z_start()
            return
        for copy in self.wide_copies():
            copy.wait_recv()
        for a in range(2):
            add_into(self.mine.at[a, p.x, :, left], self.middle[0].at[a])
            add_into(self.mine.at[p.y, a, :, right], self.middle[1].at[a])
        for copy in self.narrow_copies():
            copy.start()

    def stage_narrow(self):
        p, (left, right) = self.place, self.halves()
        for copy in self.narrow_copies():
            copy.wait_recv()
        add_into(self.mine.at[p.y, p.x, :, left], self.middle[2])
        add_into(self.mine.at[p.y, p.x, :, right], self.middle[3])
        self.z_start()

    def z_start(self):
        @pl.when(self.place.outer)
        def _():
            self.pair_copy().start()

    def stage_pair(self):
        @pl.when(self.place.inner)
        def _():
            self.pair_copy().wait_recv()
            for total, addend in zip(self.parts(self.summed()), self.parts(self.z_first)):
                add_into(total, addend)
            self.middle_copy().start()

    def stage_middle(self):
        @pl.when(self.place.inner)
        def _():
            self.middle_copy().wait_recv()
            if self.gather:
                self.lay_out()
            else:
                add_to(self.z_last, self.summed(), self.z_second)
            self.last_copy().start()
            for copy in self.out_copies():
                copy.start()

    def stage_last(self):
        @pl.when(self.place.outer)
        def _():
            self.last_copy().wait_recv()
            for copy in self.out_copies():
                copy.start()

    def stage_end(self):
        remote_out, local_out = self.out_copies()
        remote_out.wait()
        local_out.wait()
        self.core_copy().wait_send()
        for copy in self.wide_copies():
            copy.wait_send()
        if not self.gather:
            for copy in self.narrow_copies():
                copy.wait_send()

        @pl.when(self.place.outer)
        def _():
            self.pair_copy().wait_send()

        @pl.when(self.place.inner)
        def _():
            self.middle_copy().wait_send()
            self.last_copy().wait_send()

    def plan(self):
        piece = 2 * self.rows * self.columns
        if self.gather:
            return [
                (self.stage_core, [("x", 1.5 * piece), ("y", 1.5 * piece)]),
                (self.stage_wide, [("z", 4 * piece)]),
                (self.stage_pair, [("z", 4 * piece)]),
                (self.stage_middle, [("z", 4 * piece)]),
                (self.stage_last, [("core", 4 * piece)]),
                (self.stage_end, []),
            ]
        return [
            (self.stage_core, [("x", piece), ("y", piece)]),
            (self.stage_wide, [("x", piece / 2), ("y", piece / 2)]),
            (self.stage_narrow, [("z1", piece)]),
            (self.stage_pair, [("z2", piece)]),
            (self.stage_middle, [("z3", piece)]),
            (self.stage_last, [("core", piece)]),
            (self.stage_end, []),
        ]

    def opening(self):
        return [("core", 8 * self.rows * self.columns)]


class RowChunk:
    def __init__(self, term, offset, rows, columns):
        self.term, self.offset, self.rows, self.columns = term, offset, rows, columns

    def scratch(self):
        rows, columns, half = self.rows, self.columns, self.columns // 2
        low = jnp.bfloat16
        return [
            pltpu.VMEM((2, rows, half), low),
            pltpu.VMEM((2, rows, half), low),
            pltpu.VMEM((rows, half), low),
            pltpu.VMEM((rows, half), low),
            pltpu.SemaphoreType.DMA((6,)),
            pltpu.SemaphoreType.DMA((6,)),
            pltpu.SemaphoreType.DMA((1,)),
        ]

    def bind(self, place, source, result, refs):
        self.place, self.result = place, result
        self.blocks = source
        self.middle = refs[:4]
        self.sent, self.received, self.local = refs[4:]

    def mine(self, y, x, lanes):
        return self.blocks.at[2 * y + x, pl.ds(self.offset, self.rows), lanes]

    remote = Chunk.remote
    halves = Chunk.halves

    def wide_copies(self):
        p, (left, right) = self.place, self.halves()
        copies = []
        for a in range(2):
            copies.append(
                self.remote(a, self.mine(a, 1 - p.x, left), self.middle[0].at[a], "x")
            )
            copies.append(
                self.remote(2 + a, self.mine(1 - p.y, a, right), self.middle[1].at[a], "y")
            )
        return copies

    def narrow_copies(self):
        p, (left, right) = self.place, self.halves()
        return [
            self.remote(4, self.mine(1 - p.y, p.x, left), self.middle[2], "y"),
            self.remote(5, self.mine(p.y, 1 - p.x, right), self.middle[3], "x"),
        ]

    def out_copy(self):
        p = self.place
        whole = pl.ds(0, self.columns)
        return pltpu.make_async_copy(
            self.mine(p.y, p.x, whole),
            self.result.at[pl.ds(self.offset, self.rows), :],
            self.local.at[0],
        )

    def stage_start(self):
        for copy in self.wide_copies():
            copy.start()

    def stage_wide(self):
        p, (left, right) = self.place, self.halves()
        for copy in self.wide_copies():
            copy.wait_recv()
        for a in range(2):
            add_into(self.mine(a, p.x, left), self.middle[0].at[a])
            add_into(self.mine(p.y, a, right), self.middle[1].at[a])
        for copy in self.narrow_copies():
            copy.start()

    def stage_narrow(self):
        p, (left, right) = self.place, self.halves()
        for copy in self.narrow_copies():
            copy.wait_recv()
        add_into(self.mine(p.y, p.x, left), self.middle[2])
        add_into(self.mine(p.y, p.x, right), self.middle[3])
        self.out_copy().start()

    def stage_end(self):
        self.out_copy().wait()
        for copy in self.wide_copies() + self.narrow_copies():
            copy.wait_send()

    def plan(self):
        piece = 2 * self.rows * self.columns
        return [
            (self.stage_wide, [("x", piece / 2), ("y", piece / 2)]),
            (self.stage_narrow, [("core", 0.0)]),
            (self.stage_end, []),
        ]

    def opening(self):
        piece = 2 * self.rows * self.columns
        return [("x", piece), ("y", piece)]


class Steps:
    def __init__(self, start):
        self.now, self.free, self.waiting = start, {}, []

    def send(self, transfers):
        ends = [self.now]
        for link, size in transfers:
            start = max(self.now, self.free.get(link, 0.0))
            self.free[link] = start + size / LINK_RATE.get(link, LINK_RATE["z"])
            ends.append(self.free[link] + 2.0)
        return max(ends)

    def open(self, chunks):
        for chunk in chunks:
            self.waiting.append((self.send(chunk.opening()), len(self.waiting), chunk, 0))

    def due(self, everything=False):
        stages = []
        while self.waiting:
            self.waiting.sort(key=lambda entry: entry[:2])
            when, number, chunk, index = self.waiting[0]
            if when > self.now and not everything:
                break
            self.waiting.pop(0)
            self.now = max(self.now, when) + 0.4
            stage, transfers = chunk.plan()[index]
            stages.append(stage)
            if index + 1 < len(chunk.plan()):
                self.waiting.append((self.send(transfers), number, chunk, index + 1))
        return stages

    def spend(self, duration):
        self.now += duration


def back_kernel(
    chunks,
    first_chunks,
    heads,
    flag_ref,
    g_ref,
    q_hbm,
    k_hbm,
    v_hbm,
    memory_hbm,
    every_hbm,
    down_ref,
    gate_ref,
    up_ref,
    out_ref,
    w_hbm,
    mix_ref,
    log_ref,
    table_ref,
    sum_down,
    sum_gate,
    sum_up,
    sum_out,
    sum_qkv,
    sum_first,
    w_ref,
    q,
    k,
    v,
    upstream,
    shared,
    dk,
    dv,
    total,
    delta,
    part_qkv,
    trade_sent,
    trade_received,
    local,
    *refs,
):
    place = Place()
    seq = lax.axis_index("seq")
    tokens = g_ref.shape[0]
    width = heads * HEAD_DIM
    used = 0
    sources = [down_ref, gate_ref, up_ref, out_ref, part_qkv, shared]
    results = [sum_down, sum_gate, sum_up, sum_out, sum_qkv, sum_first]
    for chunk in chunks + first_chunks:
        count = len(chunk.scratch())
        chunk.bind(place, sources[chunk.term], results[chunk.term], refs[used : used + count])
        used += count

    def owner_at(turn):
        low, high = lax.rem(turn, 2), lax.div(turn, 2)
        x = place.x + low - 2 * place.x * low
        y = place.y + high - 2 * place.y * high
        return 2 * y + x

    def columns(owner):
        return pl.ds(pl.multiple_of(owner * width, HEAD_DIM), width)

    def span(block):
        return pl.ds(pl.multiple_of(block * tokens, tokens), tokens)

    def lanes(head):
        return pl.ds(pl.multiple_of(head * HEAD_DIM, HEAD_DIM), HEAD_DIM)

    across = {"x": seq + 1 - 2 * place.x, "y": seq + 2 - 4 * place.y, "xy": 3 - seq}
    trades = [
        pltpu.make_async_remote_copy(
            src_ref=g_ref.at[:, columns(across[peer])],
            dst_ref=upstream.at[span(seq), :],
            send_sem=trade_sent.at[slot],
            recv_sem=trade_received.at[slot],
            device_id=place.peer[peer],
            device_id_type=pl.DeviceIdType.MESH,
        )
        for slot, peer in enumerate(("x", "y", "xy"))
    ]
    loads = [
        pltpu.make_async_copy(g_ref.at[:, columns(seq)], upstream.at[span(seq), :], local.at[0]),
        pltpu.make_async_copy(q_hbm, q, local.at[1]),
        pltpu.make_async_copy(k_hbm, k, local.at[2]),
        pltpu.make_async_copy(v_hbm, v, local.at[3]),
        pltpu.make_async_copy(memory_hbm, shared, local.at[4]),
    ] + weight_copies(w_hbm, w_ref, seq, local, 6)
    load_every = pltpu.make_async_copy(every_hbm, shared, local.at[5])

    def turn_back(matrix, rows):
        cosine, sine = turn_factors(table_ref[rows, :])
        return turn_block(matrix, cosine, sine).astype(jnp.bfloat16)

    def memory_part(head, block):
        rows, mine = span(block), lanes(head)
        query, grads = q[rows, mine], upstream[rows, mine]
        row_delta = jnp.sum(
            grads.astype(jnp.float32) * mix_ref[rows, mine].astype(jnp.float32), axis=1, keepdims=True
        )
        delta[...] = jnp.broadcast_to(row_delta, delta.shape)
        closed = (1 - flag_ref[lax.axis_index("seg")]).astype(jnp.float32) * 1e30
        log_total = log_ref[rows, mine][:, :1] + closed
        result = jnp.zeros(total.shape, jnp.float32)
        for slot in range(shared.shape[0]):
            for run in range(2):

                def tile(kind):
                    start = pl.multiple_of((2 * run + kind) * width + head * HEAD_DIM, HEAD_DIM)
                    return shared[slot, :, pl.ds(start, HEAD_DIM)]

                keys, values = tile(0), tile(1)
                probs = jnp.exp2(product_nt(query, keys) - log_total)
                dscores = probs * (product_nt(grads, values) - row_delta)
                result = result + product(dscores.astype(jnp.bfloat16), keys)
        total[...] = result

    def own_part(head, block):
        rows, mine = span(block), lanes(head)
        query, grads = q[rows, mine], upstream[rows, mine]
        log_total, row_delta = log_ref[rows, mine][:, :1], delta[:, :1]

        def turn(other, result, diagonal):
            keys = k[span(other), mine]
            scores = product_nt(query, keys)
            if diagonal:
                scores = causal(scores)
            probs = jnp.exp2(scores - log_total)
            dscores = (probs * (product_nt(grads, v[span(other), mine]) - row_delta)).astype(
                jnp.bfloat16
            )
            dv[span(other), :] += product_tn(probs.astype(jnp.bfloat16), grads)
            dk[span(other), :] += product_tn(dscores, query)
            return result + product(dscores, keys)

        result = turn(block, total[...], True)
        result = lax.fori_loop(0, block, lambda other, r: turn(other, r, False), result)
        q[rows, mine] = turn_back(result * SCORE_SCALE, rows)

    def close_head(head):
        mine = lanes(head)

        def turn(block, carry):
            rows = span(block)
            k[rows, mine] = turn_back(dk[rows, :] * LN2, rows)
            v[rows, mine] = dv[rows, :].astype(jnp.bfloat16)
            return carry

        lax.fori_loop(0, 4, turn, 0)

    def multiply_qkv(index, carry):
        cut = pl.ds(pl.multiple_of(index * width, HEAD_DIM), width)
        for kind, part in enumerate((q, k, v)):
            term = None
            for block in range(shared.shape[0]):
                product_part = product_tn(shared[block, :, cut], part[block * tokens : (block + 1) * tokens, :])
                term = product_part if term is None else term + product_part
            term = term.astype(jnp.bfloat16)
            half = term.shape[0] // 2
            place_y, place_x = lax.div(index, 2), lax.rem(index, 2)
            for core in range(2):
                part_qkv[place_y, place_x, core, :, kind * width : (kind + 1) * width] = term[
                    core * half : (core + 1) * half, :
                ]
        return carry

    def multiply_first(block, carry):
        rows = span(block)
        result = None
        for kind, part in enumerate((q, k, v)):
            term = product_nt(part[rows, :], w_ref[:, kind * width : (kind + 1) * width])
            result = term if result is None else result + term
        shared[block] = result.astype(jnp.bfloat16)
        return carry

    place.greet(("core", "x", "y", "xy", "pair"))
    for copy in trades + loads:
        copy.start()
    for chunk in chunks:
        chunk.stage_start()
    steps = Steps(3.0)
    steps.free.update(x=11.0, y=11.0)
    steps.open(chunks)
    for copy in loads:
        copy.wait()
    slots = []
    for unit in range(2 * 4 * heads):
        slots.append(steps.due())
        steps.spend(4.3 if unit % 2 == 0 else 3.2)

    def run(stages):
        for stage in stages:
            stage()

    def unit(index, carry):
        head, turn = lax.div(index, 4), lax.rem(index, 4)
        block = owner_at(turn)
        for number in range(4 * heads):
            if slots[2 * number] or number in (1, 2, 3):

                @pl.when(index == number)
                def _(number=number):
                    run(slots[2 * number])
                    if number in (1, 2, 3):
                        trades[number - 1].wait_recv()

        @pl.when(turn == 0)
        def _():
            dk[...] = jnp.zeros_like(dk)
            dv[...] = jnp.zeros_like(dv)

        memory_part(head, block)
        for number in range(4 * heads):
            if slots[2 * number + 1]:

                @pl.when(index == number)
                def _(number=number):
                    run(slots[2 * number + 1])

        own_part(head, block)

        @pl.when(turn == 3)
        def _():
            close_head(head)

        return carry

    lax.fori_loop(0, 4 * heads, unit, 0)
    load_every.start()
    run(steps.due())
    load_every.wait()
    lax.fori_loop(0, 4, multiply_qkv, 0)
    steps.spend(8.0)
    qkv_chunks = [chunk for chunk in first_chunks if chunk.term == 4]
    row_chunks = [chunk for chunk in first_chunks if chunk.term == 5]
    for chunk in qkv_chunks:
        chunk.stage_start()
    steps.open(qkv_chunks)
    run(steps.due())
    lax.fori_loop(0, 4, multiply_first, 0)
    steps.spend(6.0)
    for chunk in row_chunks:
        chunk.stage_start()
    steps.open(row_chunks)
    run(steps.due(True))
    for copy in trades:
        copy.wait_send()


def back(
    flags, grads, queries, keys, values, memory, every, terms, w_qkv, attended, log_totals, table, collective_id
):
    tokens, depth = grads.shape
    length, width = queries.shape
    low = jnp.bfloat16
    chunks, shapes = [], []
    for index, term in enumerate(terms):
        rows, columns = term.shape[0] // 8, term.shape[1]
        parts = 2 if rows % 32 == 0 and index < 3 else 1
        chunks += [Chunk(index, n * rows // parts, rows // parts, columns) for n in range(parts)]
        shapes.append((2, rows, columns))
    rows = depth // 8
    first_chunks = [Chunk(4, n * rows // 2, rows // 2, 3 * width, True) for n in range(2)]
    first_chunks += [RowChunk(5, n * tokens // 4, tokens // 4, depth) for n in range(4)]
    shapes += [(2, rows, 12 * width), (tokens, depth)]
    anywhere = pl.BlockSpec(memory_space=pl.ANY)
    inside = pl.BlockSpec(memory_space=pltpu.VMEM)
    scratch = (
        [pltpu.VMEM((depth, 3 * width), low)]
        + [pltpu.VMEM((length, width), low)] * 4
        + [pltpu.VMEM((4, tokens, depth), low)]
        + [pltpu.VMEM((length, HEAD_DIM), jnp.float32)] * 2
        + [pltpu.VMEM((tokens, HEAD_DIM), jnp.float32)] * 2
        + [pltpu.VMEM((2, 2, 2, rows, 3 * width), low)]
        + [pltpu.SemaphoreType.DMA((3,))] * 2
        + [pltpu.SemaphoreType.DMA((9,))]
    )
    return pl.pallas_call(
        functools.partial(back_kernel, chunks, first_chunks, width // HEAD_DIM),
        in_specs=[pl.BlockSpec(memory_space=pltpu.SMEM)] + [anywhere] * 11 + [inside] * 3,
        out_specs=[anywhere] * len(shapes),
        out_shape=[jax.ShapeDtypeStruct(shape, low) for shape in shapes],
        scratch_shapes=scratch + [ref for chunk in chunks + first_chunks for ref in chunk.scratch()],
        compiler_params=pltpu.CompilerParams(
            collective_id=collective_id, has_side_effects=True, vmem_limit_bytes=VMEM_MOST
        ),
        name="back",
    )(
        flags,
        grads,
        queries,
        keys,
        values,
        memory,
        every,
        *[term.reshape((2, 2, 2, term.shape[0] // 8, term.shape[1])) for term in terms],
        w_qkv,
        attended,
        log_totals,
        table,
    )


class Line:
    def __init__(self, place, seg, memory, spans, refs):
        self.place, self.seg, self.memory, self.spans = place, seg, memory, spans
        self.runs = len(spans)
        self.sent, self.received, self.core_sent, self.core_received = refs

    def span(self, run):
        return self.spans[run]

    def there(self, way, step):
        return self.place.z >= step if way == 0 else self.place.z + step <= 3

    def goes(self, way, step):
        has = self.there(way, step - 1)
        return jnp.logical_and(has, self.place.z <= 2 if way == 0 else self.place.z >= 1)

    def index(self, way, step):
        return self.seg - 2 * step if way == 0 else self.seg + 2 * step

    def hop(self, way, step, run):
        name = self.index(way, step - 1)
        target = self.memory.at[name, self.span(run), :]
        slot = (way * 3 + step - 1) * self.runs + run
        seg, seq = lax.axis_index("seg"), lax.axis_index("seq")
        return pltpu.make_async_remote_copy(
            src_ref=target,
            dst_ref=target,
            send_sem=self.sent.at[slot],
            recv_sem=self.received.at[slot],
            device_id=(seg + 2 - 4 * way, seq),
            device_id_type=pl.DeviceIdType.MESH,
        )

    def arrival(self, way, step, run):
        target = self.memory.at[self.index(way, step), self.span(run), :]
        slot = (way * 3 + step - 1) * self.runs + run
        return pltpu.make_async_remote_copy(
            src_ref=target,
            dst_ref=target,
            send_sem=self.sent.at[slot],
            recv_sem=self.received.at[slot],
            device_id=self.place.peer["core"],
            device_id_type=pl.DeviceIdType.MESH,
        )

    def share(self, way, step, run):
        name = self.index(way, step)
        target = self.memory.at[name, self.span(run), :]
        slot = (way * 3 + step) * self.runs + run
        return pltpu.make_async_remote_copy(
            src_ref=target,
            dst_ref=target,
            send_sem=self.core_sent.at[slot],
            recv_sem=self.core_received.at[slot],
            device_id=self.place.peer["core"],
            device_id_type=pl.DeviceIdType.MESH,
        )

    def start(self, run):
        for way in range(2):

            @pl.when(self.goes(way, 1))
            def _(way=way):
                self.hop(way, 1, run).start()

        self.share(0, 0, run).start()

    def advance(self, step, run):
        for way in range(2):

            @pl.when(self.there(way, step))
            def _(way=way):
                self.arrival(way, step, run).wait_recv()

            if step < 3:

                @pl.when(self.goes(way, step + 1))
                def _(way=way):
                    self.hop(way, step + 1, run).start()

            @pl.when(self.there(way, step))
            def _(way=way):
                self.share(way, step, run).start()

    def finish(self):
        for run in range(self.runs):
            self.share(0, 0, run).wait()
            for way in range(2):
                for step in range(1, 4):

                    @pl.when(self.there(way, step))
                    def _(way=way, step=step, run=run):
                        self.share(way, step, run).wait()

                    @pl.when(self.goes(way, step))
                    def _(way=way, step=step, run=run):
                        self.hop(way, step, run).wait_send()


def front_kernel(
    heads,
    flag_ref,
    source_ref,
    x_ref,
    mem_k_ref,
    mem_v_ref,
    w_hbm,
    table_ref,
    every_ref,
    chosen_ref,
    attended_ref,
    q_ref,
    k_ref,
    v_ref,
    low_ref,
    log_ref,
    w_ref,
    rows,
    memory,
    listed,
    mix_ref,
    max_ref,
    sum_ref,
    trade_sent,
    trade_received,
    rows_sent,
    rows_received,
    line_sent,
    line_received,
    core_sent,
    core_received,
    back_sent,
    back_received,
    local,
):
    place = Place()
    seg, seq = lax.axis_index("seg"), lax.axis_index("seq")
    width = heads * HEAD_DIM
    count = mem_k_ref.shape[0]
    tokens, depth = x_ref.shape
    across = {"x": seq + 1 - 2 * place.x, "y": seq + 2 - 4 * place.y, "xy": 3 - seq}

    def remote(source, target, sent, received, slot, peer):
        return pltpu.make_async_remote_copy(
            src_ref=source,
            dst_ref=target,
            send_sem=sent.at[slot],
            recv_sem=received.at[slot],
            device_id=place.peer[peer],
            device_id_type=pl.DeviceIdType.MESH,
        )

    def columns(owner, start=0):
        return pl.ds(pl.multiple_of(start + owner * width, HEAD_DIM), width)

    def seat(owner):
        return pl.ds(pl.multiple_of(owner * count, 16), count)

    def owner_at(turn):
        low, high = lax.rem(turn, 2), lax.div(turn, 2)
        x = place.x + low - 2 * place.x * low
        y = place.y + high - 2 * place.y * high
        return 2 * y + x

    def block_rows(block):
        return pl.ds(pl.multiple_of(block * tokens, 16), tokens)

    peers = ("x", "y", "xy")
    trades = []
    for number, peer in enumerate(peers):
        for kind, source in enumerate((mem_k_ref, mem_v_ref)):
            lanes = pl.ds(kind * width, width)
            trades.append(
                remote(
                    source.at[:, columns(across[peer])],
                    memory.at[seg, seat(seq), lanes],
                    trade_sent,
                    trade_received,
                    2 * number + kind,
                    peer,
                )
            )
    keeps = [
        pltpu.make_async_copy(
            source.at[:, columns(seq)],
            memory.at[seg, seat(seq), pl.ds(kind * width, width)],
            local.at[kind],
        )
        for kind, source in enumerate((mem_k_ref, mem_v_ref))
    ]
    half = depth // 2
    left, right = pl.ds(0, half), pl.ds(half, half)
    load = pltpu.make_async_copy(x_ref, rows.at[seq], local.at[2])
    loads = weight_copies(w_hbm, w_ref, seq, local, 3)
    direct = [
        remote(x_ref.at[:, left], rows.at[seq, :, left], rows_sent, rows_received, 0, "x"),
        remote(x_ref.at[:, right], rows.at[seq, :, right], rows_sent, rows_received, 1, "y"),
        remote(x_ref.at[:, right], rows.at[seq, :, right], rows_sent, rows_received, 2, "x"),
        remote(x_ref.at[:, left], rows.at[seq, :, left], rows_sent, rows_received, 3, "y"),
    ]
    onward = [
        remote(
            rows.at[across["x"], :, left], rows.at[across["x"], :, left], rows_sent, rows_received, 4, "y"
        ),
        remote(
            rows.at[across["y"], :, right], rows.at[across["y"], :, right], rows_sent, rows_received, 5, "x"
        ),
    ]
    line = Line(
        place,
        seg,
        memory,
        [seat(owner) for owner in (seq, across["x"], across["y"], across["xy"])],
        (line_sent, line_received, core_sent, core_received),
    )
    keep_rows = pltpu.make_async_copy(rows, every_ref, local.at[6])
    run_rows = memory.shape[1] // 2
    keep_chosen = []
    for run in range(2):
        span, lanes = pl.ds(run * run_rows, run_rows), pl.ds(2 * run * width, 2 * width)
        keep_chosen.append(
            pltpu.make_async_copy(memory.at[seg, span, :], chosen_ref.at[0, :, lanes], local.at[7 + run])
        )
        keep_chosen.append(
            pltpu.make_async_copy(
                listed.at[:, span, :],
                chosen_ref.at[pl.ds(1, listed.shape[0]), :, lanes],
                local.at[9 + run],
            )
        )
    returns = [
        remote(
            low_ref.at[block_rows(across[peer]), :],
            attended_ref.at[:, columns(seq)],
            back_sent,
            back_received,
            slot,
            peer,
        )
        for slot, peer in enumerate(peers)
    ]
    keep_attended = pltpu.make_async_copy(
        low_ref.at[block_rows(seq), :], attended_ref.at[:, columns(seq)], local.at[11]
    )

    def project_rows(owner):
        block = rows[owner]
        span = block_rows(owner)
        cosine, sine = turn_factors(table_ref[span, :])
        scale = SCORE_SCALE / LN2
        queries = product(block, w_ref[:, :width])
        keys = product(block, w_ref[:, width : 2 * width])
        for head in range(heads):
            lanes = slice(head * HEAD_DIM, (head + 1) * HEAD_DIM)
            q_ref[span, lanes] = turn_block(
                queries[:, lanes], cosine * scale, sine * (-scale)
            ).astype(jnp.bfloat16)
            k_ref[span, lanes] = turn_block(keys[:, lanes], cosine, -sine).astype(jnp.bfloat16)
        v_ref[span, :] = product(block, w_ref[:, 2 * width :]).astype(jnp.bfloat16)

    def head_lanes(head, start=0):
        return pl.ds(pl.multiple_of(start + head * HEAD_DIM, HEAD_DIM), HEAD_DIM)

    def keep(span, lanes, row_max, row_sum, mixed):
        mix_ref[span, lanes] = mixed
        max_ref[span, lanes] = jnp.broadcast_to(row_max, mixed.shape)
        sum_ref[span, lanes] = jnp.broadcast_to(row_sum, mixed.shape)

    def own_rows(block):
        def turn(head, carry):
            lanes = head_lanes(head)
            span = pl.ds(block * tokens, tokens)
            pairs = [
                (k_ref[pl.ds(n * tokens, tokens), lanes], v_ref[pl.ds(n * tokens, tokens), lanes])
                for n in range(block + 1)
            ]
            keep(span, lanes, *attend(q_ref[span, lanes], pairs, True, None))
            return carry

        lax.fori_loop(0, heads, turn, 0)

    closed = (1 - flag_ref[seg]).astype(jnp.float32) * 1e30

    def carried(span, lanes):
        return max_ref[span, lanes][:, :1], sum_ref[span, lanes][:, :1], mix_ref[span, lanes]

    def own_memory(first, last):
        def turn(index, carry):
            head = lax.rem(index, heads)
            lanes, span = head_lanes(head), block_rows(lax.div(index, heads))
            pair = (memory[seg, :, lanes], memory[seg, :, head_lanes(head, width)])
            keep(span, lanes, *attend(q_ref[span, lanes], [pair], False, carried(span, lanes), closed))
            return carry

        lax.fori_loop(first * heads, last * heads, turn, 0)

    barrier = pltpu.get_barrier_semaphore()

    def hail(device):
        pl.semaphore_signal(barrier, inc=1, device_id=device, device_id_type=pl.DeviceIdType.MESH)

    for copy in keeps + [load] + loads:
        copy.start()
    for peer in ("x", "y", "xy", "core"):
        hail(place.peer[peer])
    below, above = place.z >= 1, place.z <= 2

    @pl.when(below)
    def _():
        hail((seg - 2, seq))

    @pl.when(above)
    def _():
        hail((seg + 2, seq))

    pl.semaphore_wait(barrier, 4 + below.astype(jnp.int32) + above.astype(jnp.int32))

    for copy in trades + direct:
        copy.start()
    for copy in keeps:
        copy.wait()
    line.start(0)
    load.wait()
    for copy in loads:
        copy.wait()
    project_rows(seq)
    for number in range(3):
        for kind in range(2):
            trades[2 * number + kind].wait_recv()
        line.start(number + 1)
        line.advance(1, number)
    direct[0].wait_recv()
    direct[1].wait_recv()
    for copy in onward:
        copy.start()
    line.advance(1, 3)
    line.advance(2, 0)
    direct[2].wait_recv()
    direct[3].wait_recv()
    project_rows(across["x"])
    line.advance(2, 1)
    project_rows(across["y"])
    line.advance(2, 2)
    for copy in onward:
        copy.wait_recv()
    project_rows(3 - seq)
    keep_rows.start()
    line.advance(2, 3)
    own_rows(0)
    own_rows(1)
    line.advance(3, 0)
    own_rows(2)
    line.advance(3, 1)
    own_rows(3)
    line.advance(3, 2)
    own_memory(0, 2)
    line.advance(3, 3)
    own_memory(2, 4)
    line.finish()
    for n in range(listed.shape[0]):
        listed[n] = memory[source_ref[seg, n]]

    def unit(index, carry):
        turn, head = lax.div(index, heads), lax.rem(index, heads)

        @pl.when(index == heads // 2)
        def _():
            for copy in keep_chosen:
                copy.start()

        for number in range(3):

            @pl.when(index == heads * (3 - number))
            def _(number=number):
                returns[number].start()

        lanes, span = head_lanes(head), block_rows(owner_at(3 - turn))
        pairs = [
            (listed[n, :, lanes], listed[n, :, head_lanes(head, width)])
            for n in range(listed.shape[0])
        ]
        row_max, row_sum, mixed = attend(
            q_ref[span, lanes], pairs, False, carried(span, lanes), closed
        )
        low_ref[span, lanes] = (mixed * (1.0 / row_sum)).astype(jnp.bfloat16)
        log_ref[span, lanes] = jnp.broadcast_to(row_max + jnp.log2(row_sum), mixed.shape)
        return carry

    lax.fori_loop(0, 4 * heads, unit, 0)
    keep_attended.start()
    for copy in returns:
        copy.wait()
    for copy in keep_chosen + [keep_rows, keep_attended]:
        copy.wait()
    for copy in trades + direct + onward:
        copy.wait_send()


def front(
    flags, sources, first_low, mem_keys, mem_values, w_qkv, table, seg_size, seq_size, collective_id
):
    tokens, depth = first_low.shape
    length = tokens * seq_size
    width = depth // seq_size
    count = mem_keys.shape[0] * seq_size
    slots = sources.shape[1]
    anywhere = pl.BlockSpec(memory_space=pl.ANY)
    inside = pl.BlockSpec(memory_space=pltpu.VMEM)
    scalars = pl.BlockSpec(memory_space=pltpu.SMEM)
    low = jnp.bfloat16
    shape = jax.ShapeDtypeStruct
    dma = pltpu.SemaphoreType.DMA
    return pl.pallas_call(
        functools.partial(front_kernel, width // HEAD_DIM),
        in_specs=[scalars] * 2 + [anywhere] * 4 + [inside],
        out_specs=[anywhere] * 3 + [inside] * 5,
        out_shape=[
            shape((seq_size, tokens, depth), low),
            shape((slots + 1, count // 2, 4 * width), low),
            shape((tokens, depth), low),
        ]
        + [shape((length, width), low)] * 4
        + [shape((length, width), jnp.float32)],
        scratch_shapes=[
            pltpu.VMEM((depth, 3 * width), low),
            pltpu.VMEM((seq_size, tokens, depth), low),
            pltpu.VMEM((seg_size, count, 2 * width), low),
            pltpu.VMEM((slots, count, 2 * width), low),
        ]
        + [pltpu.VMEM((length, width), jnp.float32)] * 3
        + [dma((6,))] * 4
        + [dma((24,))] * 2
        + [dma((28,))] * 2
        + [dma((3,))] * 2
        + [dma((12,))],
        compiler_params=pltpu.CompilerParams(
            collective_id=collective_id, has_side_effects=True, vmem_limit_bytes=VMEM_BYTES
        ),
        name="front",
    )(flags, sources, first_low, mem_keys, mem_values, w_qkv, table)


def norm_input_grad(values, inverse, norm_gain, upstream):
    weighted = upstream * norm_gain
    inner_mean = jnp.mean(weighted * values, axis=-1, keepdims=True)
    return inverse * weighted - inverse * inverse * inverse * values * inner_mean


def dense_kernel(
    x_ref,
    g_ref,
    attended_ref,
    out_ref,
    gain_ref,
    gate_ref,
    up_ref,
    down_ref,
    output_ref,
    grad_ref,
    grad_attended_ref,
    term_down,
    term_gate,
    term_up,
    term_out,
    residual_ref,
    second,
    second_t,
    total,
    grad_second,
):
    index = pl.program_id(0)
    low = jnp.bfloat16

    @pl.when(index == 0)
    def _():
        residual = x_ref[...].astype(jnp.float32) + product(attended_ref[...], out_ref[...])
        residual_ref[...] = residual
        second_low = norm_forward(residual, gain_ref[...])[0].astype(low)
        second[...] = second_low
        second_t[...] = second_low.T

    gate, up = product(second[...], gate_ref[...]), product(second[...], up_ref[...])
    grad_hidden = product_nt(g_ref[...], down_ref[...])
    sigmoid_gate = jax.nn.sigmoid(gate)
    activated = gate * sigmoid_gate
    hidden = (activated * up).astype(low)
    grad_gate = (grad_hidden * up * sigmoid_gate * (1.0 + gate * (1.0 - sigmoid_gate))).astype(low)
    grad_up = (grad_hidden * activated).astype(low)
    term_down[...] = product_tn(hidden, g_ref[...]).astype(low)
    term_gate[...] = product(second_t[...], grad_gate).astype(low)
    term_up[...] = product(second_t[...], grad_up).astype(low)
    part = product(hidden, down_ref[...])
    grad_part = product_nt(grad_gate, gate_ref[...]) + product_nt(grad_up, up_ref[...])

    @pl.when(index == 0)
    def _():
        total[...] = part
        grad_second[...] = grad_part

    @pl.when(index > 0)
    def _():
        total[...] += part
        grad_second[...] += grad_part

    @pl.when(index == pl.num_programs(0) - 1)
    def _():
        residual = residual_ref[...]
        output_ref[...] = (residual + total[...]).astype(low)
        inverse = lax.rsqrt(jnp.mean(residual * residual, axis=-1, keepdims=True) + epsilon)
        grad = norm_input_grad(residual, inverse, gain_ref[...], grad_second[...])
        grad = grad + g_ref[...].astype(jnp.float32)
        grad_ref[...] = grad
        grad_low = grad.astype(low)
        term_out[...] = product_tn(attended_ref[...], grad_low).astype(low)
        grad_attended_ref[...] = product_nt(grad_low, out_ref[...]).astype(low)


def dense(x, grads, attended, w_out, gain, w_gate, w_up, w_down, tile=256):
    tokens, depth = x.shape
    hidden = w_gate.shape[1]
    tile = math.gcd(tile, hidden)
    low = jnp.bfloat16
    shape = jax.ShapeDtypeStruct

    def whole(rows, columns):
        return pl.BlockSpec((rows, columns), lambda j: (0, 0))

    across = pl.BlockSpec((depth, tile), lambda j: (0, j))
    down = pl.BlockSpec((tile, depth), lambda j: (j, 0))
    activation = whole(tokens, depth)
    return pl.pallas_call(
        dense_kernel,
        grid=(hidden // tile,),
        in_specs=[activation] * 3 + [whole(depth, depth), whole(1, depth), across, across, down],
        out_specs=[activation] * 3 + [down, across, across, whole(depth, depth)],
        out_shape=[
            shape((tokens, depth), low),
            shape((tokens, depth), jnp.float32),
            shape((tokens, depth), low),
            shape((hidden, depth), low),
            shape((depth, hidden), low),
            shape((depth, hidden), low),
            shape((depth, depth), low),
        ],
        scratch_shapes=[
            pltpu.VMEM((tokens, depth), jnp.float32),
            pltpu.VMEM((tokens, depth), low),
            pltpu.VMEM((depth, tokens), low),
            pltpu.VMEM((tokens, depth), jnp.float32),
            pltpu.VMEM((tokens, depth), jnp.float32),
        ],
        compiler_params=pltpu.CompilerParams(vmem_limit_bytes=VMEM_BYTES),
        cost_estimate=pl.CostEstimate(
            flops=16 * tokens * depth * hidden + 6 * tokens * depth * depth,
            transcendentals=tokens * hidden,
            bytes_accessed=12 * depth * hidden + 20 * tokens * depth,
        ),
        name="dense",
    )(x, grads, attended, w_out, gain, w_gate, w_up, w_down)


def head_plan(
    seg_size,
    seq_size,
    layer_input,
    output_grad,
    norm1_gain,
    norm2_gain,
    w_qkv,
    w_out,
    w_gate,
    w_up,
    w_down,
    mem_keys,
    mem_values,
    memory_flags,
    sources,
):
    seq_index = lax.axis_index("seq")
    tokens = layer_input.shape[1]
    length = tokens * seq_size
    width = D // seq_size
    inputs = layer_input[0].astype(jnp.float32)
    first_norm, first_inverse = norm_forward(inputs, norm1_gain)
    first_low = first_norm.astype(jnp.bfloat16)
    table = turn_table(length)
    every_low, chosen_memory, attended_low, queries, keys, values, heads_low, log_totals = front(
        memory_flags, sources, first_low, mem_keys[0], mem_values[0], w_qkv, table, seg_size, seq_size, 1
    )

    output, grad_residual, grad_attended, term_down, term_gate, term_up, term_out = dense(
        layer_input[0], output_grad[0], attended_low, w_out, norm2_gain[None], w_gate, w_up, w_down
    )
    *sums, qkv_rows, first_rows = back(
        memory_flags,
        grad_attended,
        queries,
        keys,
        values,
        chosen_memory,
        every_low,
        [term_down, term_gate, term_up, term_out],
        w_qkv,
        heads_low,
        log_totals,
        table,
        2,
    )
    grad_down, grad_gate, grad_up, grad_out = [
        total.reshape(2 * total.shape[1], total.shape[2]).astype(jnp.float32) for total in sums
    ]
    grad_qkv = qkv_rows.reshape(width, 3 * D).astype(jnp.float32)
    grad_inputs = norm_input_grad(
        inputs, first_inverse, norm1_gain, first_rows.astype(jnp.float32)
    )
    input_grad = (grad_inputs + grad_residual)[None]

    def row_block(whole):
        return lax.dynamic_slice_in_dim(whole, seq_index * width, width, 0)

    def gain_rows(weights, grads, gain):
        dots = [
            jnp.sum(row_block(weight).astype(jnp.float32) * grad, axis=1)
            for weight, grad in zip(weights, grads)
        ]
        return sum(dots[1:], dots[0]) / row_block(gain)

    grad_norm1 = gain_rows([w_qkv], [grad_qkv], norm1_gain)
    grad_norm2 = gain_rows([w_gate, w_up], [grad_gate, grad_up], norm2_gain)
    return (
        output[None],
        input_grad,
        grad_norm1,
        grad_norm2,
        grad_qkv,
        grad_out,
        grad_gate,
        grad_up,
        grad_down,
    )


def solution(mesh):
    seq_size = mesh.shape["seq"]
    heads_fit = seq_size == 4 and mesh.shape["seg"] == 8
    plan = functools.partial(head_plan, mesh.shape["seg"], seq_size) if heads_fit else general_plan
    placed = (
        P("seg", "seq", None),
        P("seg", "seq", None),
        P(),
        P(),
        P(),
        P(),
        P(),
        P(),
        P(),
        P("seg", "seq", None),
        P("seg", "seq", None),
        P(),
        P(),
    )
    return jax.shard_map(
        plan,
        mesh=mesh,
        in_specs=placed,
        out_specs=(
            P("seg", "seq", None),
            P("seg", "seq", None),
            P("seq"),
            P("seq"),
            P("seq", None),
            P("seq", None),
            P("seq", None),
            P("seq", None),
            P("seq", None),
        ),
        check_vma=False,
    )
```

```python
import functools
import math

import jax
import jax.numpy as jnp
import numpy as np
from jax import lax
from jax.experimental import pallas as pl
from jax.experimental.pallas import tpu as pltpu
from jax.sharding import PartitionSpec as P

D = 1024
HEADS = 8
HEAD_DIM = 128


masked_score = -1e30
epsilon = 1e-06
rotary_base = 10000.0


def product(former, latter):
    return jnp.dot(former, latter, preferred_element_type=jnp.float32)


def product_nt(former, latter):
    return lax.dot_general(
        former, latter, (((1,), (1,)), ((), ())), preferred_element_type=jnp.float32
    )


def product_tn(former, latter):
    return lax.dot_general(
        former, latter, (((0,), (0,)), ((), ())), preferred_element_type=jnp.float32
    )


def norm_forward(values, norm_gain):
    inverse = lax.rsqrt(jnp.mean(values * values, axis=-1, keepdims=True) + epsilon)
    return (values * inverse * norm_gain, inverse)


def norm_backward(values, inverse, norm_gain, upstream):
    weighted = upstream * norm_gain
    inner_mean = jnp.mean(weighted * values, axis=-1, keepdims=True)
    grad_values = inverse * weighted - inverse * inverse * inverse * values * inner_mean
    grad_gain = jnp.sum(upstream * values * inverse, axis=0)
    return (grad_values, grad_gain)


def turn_tables(positions):
    half_dim = HEAD_DIM // 2
    exponent = -2.0 * jnp.arange(half_dim, dtype=jnp.float32) / HEAD_DIM
    angles = positions[:, None] * jnp.power(rotary_base, exponent)[None, :]
    angles = jnp.concatenate([angles, angles], axis=1)
    return (jnp.cos(angles)[:, None, :], jnp.sin(angles)[:, None, :])


def rotate(matrix, cosine_table, sine_table, direction):
    row_count = matrix.shape[0]
    half_dim = HEAD_DIM // 2
    shaped = matrix.reshape(row_count, HEADS, HEAD_DIM)
    turned = jnp.concatenate([-shaped[..., half_dim:], shaped[..., :half_dim]], axis=-1)
    return (shaped * cosine_table + direction * turned * sine_table).reshape(
        row_count, HEADS * HEAD_DIM
    )


def general_plan(
    layer_input,
    output_grad,
    norm1_gain,
    norm2_gain,
    w_qkv,
    w_out,
    w_gate,
    w_up,
    w_down,
    mem_keys,
    mem_values,
    memory_flags,
    sources,
):
    seg_index = lax.axis_index("seg")
    seq_index = lax.axis_index("seq")
    tokens = layer_input.shape[1]
    score_scale = HEAD_DIM ** (-0.5)
    flag_on = lax.dynamic_index_in_dim(memory_flags, seg_index, 0, keepdims=False) > 0
    listed = lax.dynamic_index_in_dim(sources, seg_index, 0, keepdims=False)
    picked = jnp.concatenate([jnp.reshape(seg_index, (1,)), listed])
    every_keys, every_values = (
        lax.all_gather(mem_keys, "seg", axis=0, tiled=True),
        lax.all_gather(mem_values, "seg", axis=0, tiled=True),
    )
    chosen_keys = jnp.take(every_keys, picked, axis=0)
    chosen_values = jnp.take(every_values, picked, axis=0)
    memory_keys, memory_values = (
        lax.all_gather(chosen_keys, "seq", axis=1, tiled=True),
        lax.all_gather(chosen_values, "seq", axis=1, tiled=True),
    )
    memory_key_blocks = memory_keys.reshape(-1, tokens, HEADS, HEAD_DIM)
    memory_value_blocks = memory_values.reshape(-1, tokens, HEADS, HEAD_DIM)
    memory_blocks = memory_key_blocks.shape[0]
    inputs = layer_input[0].astype(jnp.float32)
    first_norm, first_inverse = norm_forward(inputs, norm1_gain)
    first_low = first_norm.astype(jnp.bfloat16)
    projected = product(first_low, w_qkv)
    positions = seq_index * tokens + lax.iota(jnp.int32, tokens)
    cosine_table, sine_table = turn_tables(positions.astype(jnp.float32))
    queries = rotate(projected[:, :D], cosine_table, sine_table, 1.0).astype(jnp.bfloat16)
    own_keys = rotate(projected[:, D : 2 * D], cosine_table, sine_table, 1.0).astype(jnp.bfloat16)
    own_values = projected[:, 2 * D :].astype(jnp.bfloat16)
    all_keys, all_values = (
        lax.all_gather(own_keys, "seq", axis=0, tiled=True),
        lax.all_gather(own_values, "seq", axis=0, tiled=True),
    )
    key_blocks = all_keys.reshape(-1, tokens, HEADS, HEAD_DIM)
    value_blocks = all_values.reshape(-1, tokens, HEADS, HEAD_DIM)
    query_heads = queries.reshape(tokens, HEADS, HEAD_DIM)
    memory_open = jnp.broadcast_to(flag_on, (tokens, tokens))
    own_count = seq_index + 1
    key_offsets = lax.iota(jnp.int32, tokens)

    def own_open(block):
        return (block * tokens + key_offsets)[None, :] <= positions[:, None]

    def block_scores(key_block, open_mask):
        raw = (
            jnp.einsum("qhd,khd->hqk", query_heads, key_block, preferred_element_type=jnp.float32)
            * score_scale
        )
        return jnp.where(open_mask[None], raw, masked_score)

    def sweep(step, carry):

        def memory_turn(block, state):
            return step(
                state,
                block,
                memory_key_blocks[block],
                memory_value_blocks[block],
                memory_open,
                False,
            )

        def own_turn(block, state):
            return step(state, block, key_blocks[block], value_blocks[block], own_open(block), True)

        carry = lax.fori_loop(0, memory_blocks, memory_turn, carry)
        return lax.fori_loop(0, own_count, own_turn, carry)

    def max_step(carry, block, key_block, value_block, open_mask, own):
        row_max, row_sum = carry
        scores = block_scores(key_block, open_mask)
        new_max = jnp.maximum(row_max, jnp.max(scores, axis=2))
        row_sum = row_sum * jnp.exp(row_max - new_max) + jnp.sum(
            jnp.exp(scores - new_max[..., None]), axis=2
        )
        return (new_max, row_sum)

    start_max = jnp.full((HEADS, tokens), masked_score, jnp.float32)
    row_max, row_sum = sweep(max_step, (start_max, jnp.zeros((HEADS, tokens), jnp.float32)))
    log_totals = row_max + jnp.log(row_sum)

    def mix_step(total, block, key_block, value_block, open_mask, own):
        weights_low = jnp.exp(block_scores(key_block, open_mask) - log_totals[..., None]).astype(
            jnp.bfloat16
        )
        return total + jnp.einsum(
            "hqk,khd->qhd", weights_low, value_block, preferred_element_type=jnp.float32
        )

    attended = sweep(mix_step, jnp.zeros((tokens, HEADS, HEAD_DIM), jnp.float32))
    attended_low = attended.reshape(tokens, D).astype(jnp.bfloat16)
    residual = inputs + product(attended_low, w_out)
    second_norm, second_inverse = norm_forward(residual, norm2_gain)
    second_low = second_norm.astype(jnp.bfloat16)
    gate_values = product(second_low, w_gate)
    up_values = product(second_low, w_up)
    sigmoid_gate = jax.nn.sigmoid(gate_values)
    activated = gate_values * sigmoid_gate
    hidden_low = (activated * up_values).astype(jnp.bfloat16)
    output = (residual + product(hidden_low, w_down)).astype(jnp.bfloat16)
    upstream = output_grad[0]
    grad_down = product_tn(hidden_low, upstream)
    grad_hidden = product_nt(upstream, w_down)
    grad_gate_low = (
        grad_hidden * up_values * sigmoid_gate * (1.0 + gate_values * (1.0 - sigmoid_gate))
    ).astype(jnp.bfloat16)
    grad_up_low = (grad_hidden * activated).astype(jnp.bfloat16)
    grad_gate = product_tn(second_low, grad_gate_low)
    grad_up = product_tn(second_low, grad_up_low)
    grad_second = product_nt(grad_gate_low, w_gate) + product_nt(grad_up_low, w_up)
    grad_residual, grad_norm2 = norm_backward(residual, second_inverse, norm2_gain, grad_second)
    grad_residual = grad_residual + upstream.astype(jnp.float32)
    residual_low = grad_residual.astype(jnp.bfloat16)
    grad_out = product_tn(attended_low, residual_low)
    grad_attended = product_nt(residual_low, w_out).astype(jnp.bfloat16)
    grad_heads = grad_attended.reshape(tokens, HEADS, HEAD_DIM)

    def probs_pair(key_block, value_block, open_mask):
        probs = jnp.exp(block_scores(key_block, open_mask) - log_totals[..., None])
        dprobs = jnp.einsum(
            "qhd,khd->hqk", grad_heads, value_block, preferred_element_type=jnp.float32
        )
        return (probs, dprobs)

    def delta_step(total, block, key_block, value_block, open_mask, own):
        probs, dprobs = probs_pair(key_block, value_block, open_mask)
        return total + jnp.sum(probs * dprobs, axis=2)

    delta_rows = sweep(delta_step, jnp.zeros((HEADS, tokens), jnp.float32))

    def grad_step(carry, block, key_block, value_block, open_mask, own):
        grad_query, key_terms, value_terms = carry
        probs, dprobs = probs_pair(key_block, value_block, open_mask)
        dscores = (probs * (dprobs - delta_rows[..., None])).astype(jnp.bfloat16)
        grad_query = grad_query + jnp.einsum(
            "hqk,khd->qhd", dscores, key_block, preferred_element_type=jnp.float32
        )
        if own:
            key_part = (
                jnp.einsum("hqk,qhd->khd", dscores, query_heads, preferred_element_type=jnp.float32)
                * score_scale
            )
            value_part = jnp.einsum(
                "hqk,qhd->khd",
                probs.astype(jnp.bfloat16),
                grad_heads,
                preferred_element_type=jnp.float32,
            )
            key_terms = lax.dynamic_update_index_in_dim(key_terms, key_part, block, 0)
            value_terms = lax.dynamic_update_index_in_dim(value_terms, value_part, block, 0)
        return (grad_query, key_terms, value_terms)

    term_shape = key_blocks.shape
    start_grads = (
        jnp.zeros((tokens, HEADS, HEAD_DIM), jnp.float32),
        jnp.zeros(term_shape, jnp.float32),
        jnp.zeros(term_shape, jnp.float32),
    )
    grad_query, key_terms, value_terms = sweep(grad_step, start_grads)
    grad_queries = (grad_query * score_scale).reshape(tokens, D)
    grad_keys, grad_values = (
        lax.psum_scatter(
            key_terms.astype(jnp.bfloat16), "seq", scatter_dimension=0, tiled=True
        ).astype(jnp.float32),
        lax.psum_scatter(
            value_terms.astype(jnp.bfloat16), "seq", scatter_dimension=0, tiled=True
        ).astype(jnp.float32),
    )
    grad_projected = jnp.concatenate(
        [
            rotate(grad_queries, cosine_table, sine_table, -1.0),
            rotate(grad_keys.reshape(tokens, D), cosine_table, sine_table, -1.0),
            grad_values.reshape(tokens, D),
        ],
        axis=1,
    ).astype(jnp.bfloat16)
    grad_qkv = product_tn(first_low, grad_projected)
    grad_first = product_nt(grad_projected, w_qkv)
    grad_inputs, grad_norm1 = norm_backward(inputs, first_inverse, norm1_gain, grad_first)
    input_grad = (grad_inputs + grad_residual)[None]
    shares = (
        lax.psum_scatter(
            grad_norm1.astype(jnp.bfloat16), "seq", scatter_dimension=0, tiled=True
        ).astype(jnp.float32),
        lax.psum_scatter(
            grad_norm2.astype(jnp.bfloat16), "seq", scatter_dimension=0, tiled=True
        ).astype(jnp.float32),
        lax.psum_scatter(
            grad_qkv.astype(jnp.bfloat16), "seq", scatter_dimension=0, tiled=True
        ).astype(jnp.float32),
        lax.psum_scatter(
            grad_out.astype(jnp.bfloat16), "seq", scatter_dimension=0, tiled=True
        ).astype(jnp.float32),
        lax.psum_scatter(
            grad_gate.astype(jnp.bfloat16), "seq", scatter_dimension=0, tiled=True
        ).astype(jnp.float32),
        lax.psum_scatter(
            grad_up.astype(jnp.bfloat16), "seq", scatter_dimension=0, tiled=True
        ).astype(jnp.float32),
        lax.psum_scatter(
            grad_down.astype(jnp.bfloat16), "seq", scatter_dimension=0, tiled=True
        ).astype(jnp.float32),
    )
    totals = (
        lax.psum(shares[0].astype(jnp.bfloat16), "seg").astype(jnp.float32),
        lax.psum(shares[1].astype(jnp.bfloat16), "seg").astype(jnp.float32),
        lax.psum(shares[2].astype(jnp.bfloat16), "seg").astype(jnp.float32),
        lax.psum(shares[3].astype(jnp.bfloat16), "seg").astype(jnp.float32),
        lax.psum(shares[4].astype(jnp.bfloat16), "seg").astype(jnp.float32),
        lax.psum(shares[5].astype(jnp.bfloat16), "seg").astype(jnp.float32),
        lax.psum(shares[6].astype(jnp.bfloat16), "seg").astype(jnp.float32),
    )
    return (
        output[None],
        input_grad,
        totals[0],
        totals[1],
        totals[2],
        totals[3],
        totals[4],
        totals[5],
        totals[6],
    )


VMEM_BYTES = 60 * 1024 * 1024
VMEM_MOST = 67043328
LN2 = math.log(2.0)
SCORE_SCALE = HEAD_DIM ** (-0.5)


def lane_fold(op, tile, running):
    for column in range(tile.shape[1] // HEAD_DIM):
        piece = tile[:, column * HEAD_DIM : (column + 1) * HEAD_DIM]
        running = piece if running is None else op(running, piece)
    return running


def causal(scores):
    rows = lax.broadcasted_iota(jnp.int32, scores.shape, 0)
    columns = lax.broadcasted_iota(jnp.int32, scores.shape, 1)
    return jnp.where(columns <= rows, scores, masked_score)


def attend(query, pairs, diagonal, carried, closed=0.0):
    every, lane_max = [], None
    for index, (keys, _) in enumerate(pairs):
        scores = product_nt(query, keys)
        if diagonal and index == len(pairs) - 1:
            scores = causal(scores)
        lane_max = lane_fold(jnp.maximum, scores, lane_max)
        every.append(scores)
    row_max = jnp.max(lane_max, axis=1, keepdims=True) - closed
    if carried is not None:
        row_max = jnp.maximum(row_max, carried[0])
    shift = row_max + closed
    lane_sum, mixed = None, None
    for scores, (_, values) in zip(every, pairs):
        probs = jnp.exp2(scores - shift)
        lane_sum = lane_fold(jnp.add, probs, lane_sum)
        part = product(probs.astype(jnp.bfloat16), values)
        mixed = part if mixed is None else mixed + part
    row_sum = jnp.sum(lane_sum, axis=1, keepdims=True)
    if carried is not None:
        shrink = jnp.exp2(carried[0] - row_max)
        row_sum = carried[1] * shrink + row_sum
        mixed = carried[2] * shrink + mixed
    return row_max, row_sum, mixed


def turn_block(matrix, cosine, sine):
    return matrix * cosine + pltpu.roll(matrix, HEAD_DIM // 2, 1) * sine


def turn_factors(both):
    swapped = pltpu.roll(both, HEAD_DIM // 2, 1)
    first = lax.broadcasted_iota(jnp.int32, both.shape, 1) < HEAD_DIM // 2
    return jnp.where(first, both, swapped), jnp.where(first, swapped, -both)


def turn_table(length, step=64):
    frequency = rotary_base ** (-2.0 * np.arange(HEAD_DIM // 2) / HEAD_DIM)
    coarse = np.arange(length // step)[:, None] * step * frequency
    fine = np.arange(step)[:, None] * frequency

    def pair(former, latter):
        return jnp.asarray(np.concatenate([former, latter], axis=1), jnp.float32)

    table = (
        pair(np.cos(coarse), np.sin(coarse))[:, None, :] * pair(np.cos(fine), np.cos(fine))[None]
        + pair(-np.sin(coarse), np.cos(coarse))[:, None, :] * pair(np.sin(fine), np.sin(fine))[None]
    )
    return table.reshape(length, HEAD_DIM)


LINK_RATE = {"core": 300e3, "x": 49e3, "y": 49e3, "z": 49e3}


class Place:
    def __init__(self):
        seg, seq = lax.axis_index("seg"), lax.axis_index("seq")
        self.core, self.z = lax.rem(seg, 2), lax.div(seg, 2)
        self.x, self.y = lax.rem(seq, 2), lax.div(seq, 2)
        odd = lax.rem(self.z, 2)
        self.inner = jnp.logical_or(self.z == 1, self.z == 2)
        self.outer = jnp.logical_not(self.inner)
        self.peer = {
            "core": (seg + 1 - 2 * self.core, seq),
            "x": (seg, seq + 1 - 2 * self.x),
            "y": (seg, seq + 2 - 4 * self.y),
            "xy": (seg, 3 - seq),
            "pair": (seg + 2 - 4 * odd, seq),
            "middle": (seg - 2 + 4 * odd, seq),
        }

    def greet(self, names):
        barrier = pltpu.get_barrier_semaphore()

        def hail(name):
            pl.semaphore_signal(
                barrier, inc=1, device_id=self.peer[name], device_id_type=pl.DeviceIdType.MESH
            )

        for name in names:
            hail(name)

        @pl.when(self.inner)
        def _():
            hail("middle")

        pl.semaphore_wait(barrier, len(names) + self.inner.astype(jnp.int32))


def add_into(total, addend, step=16):
    def turn(index, carry):
        rows = pl.ds(pl.multiple_of(index * step, step), step)
        total[rows, :] = total[rows, :] + addend[rows, :]
        return carry

    lax.fori_loop(0, total.shape[0] // step, turn, 0)


def add_to(result, former, latter, step=16):
    def turn(index, carry):
        rows = pl.ds(pl.multiple_of(index * step, step), step)
        result[rows, :] = former[rows, :] + latter[rows, :]
        return carry

    lax.fori_loop(0, result.shape[0] // step, turn, 0)


def weight_copies(whole, part, seq, semaphores, first):
    width = part.shape[1] // 3
    depth = whole.shape[1] // 3
    return [
        pltpu.make_async_copy(
            whole.at[:, pl.ds(pl.multiple_of(kind * depth + seq * width, HEAD_DIM), width)],
            part.at[:, pl.ds(kind * width, width)],
            semaphores.at[first + kind],
        )
        for kind in range(3)
    ]


class Chunk:
    def __init__(self, term, offset, rows, columns, gather=False):
        self.term, self.offset, self.rows, self.columns = term, offset, rows, columns
        self.gather = gather

    def scratch(self):
        rows, columns, half = self.rows, self.columns, self.columns // 2
        low = jnp.bfloat16
        four = pltpu.VMEM((2, 2, rows, columns), low)
        one = four if self.gather else pltpu.VMEM((rows, columns), low)
        last = pltpu.VMEM((rows, 4 * columns), low) if self.gather else one
        if self.gather:
            middle = [four]
        else:
            middle = [
                pltpu.VMEM((2, rows, half), low),
                pltpu.VMEM((2, rows, half), low),
                pltpu.VMEM((rows, half), low),
                pltpu.VMEM((rows, half), low),
            ]
        ends = [one, one, last] if self.gather else [one, one]
        return [four, four] + middle + ends + [
            pltpu.SemaphoreType.DMA((9,)),
            pltpu.SemaphoreType.DMA((9,)),
            pltpu.SemaphoreType.DMA((3,)),
        ]

    def bind(self, place, source, result, refs):
        self.place, self.source, self.result = place, source, result
        self.mine, self.core_in = refs[0], refs[1]
        ends = 3 if self.gather else 2
        self.middle = refs[2 : -3 - ends]
        self.z_last, self.z_second = refs[-4], refs[-5]
        self.z_first = refs[-6] if self.gather else self.z_last
        self.sent, self.received, self.local = refs[-3:]

    def remote(self, slot, source, target, peer):
        return pltpu.make_async_remote_copy(
            src_ref=source,
            dst_ref=target,
            send_sem=self.sent.at[slot],
            recv_sem=self.received.at[slot],
            device_id=self.place.peer[peer],
            device_id_type=pl.DeviceIdType.MESH,
        )

    def core_copy(self):
        rows = pl.ds(self.offset, self.rows)
        return self.remote(
            0, self.source.at[:, :, 1 - self.place.core, rows, :], self.core_in, "core"
        )

    def load(self):
        rows = pl.ds(self.offset, self.rows)
        return pltpu.make_async_copy(
            self.source.at[:, :, self.place.core, rows, :], self.mine, self.local.at[0]
        )

    def halves(self):
        half = self.columns // 2
        return pl.ds(0, half), pl.ds(half, half)

    def wide_copies(self):
        p, (left, right) = self.place, self.halves()
        if self.gather:
            return [
                self.remote(1, self.mine.at[p.y, 1 - p.x], self.middle[0].at[p.y, p.x], "x"),
                self.remote(2, self.mine.at[1 - p.y, p.x], self.middle[0].at[p.y, p.x], "y"),
                self.remote(3, self.mine.at[1 - p.y, 1 - p.x], self.middle[0].at[p.y, p.x], "xy"),
            ]
        return [
            self.remote(1, self.mine.at[:, 1 - p.x, :, left], self.middle[0], "x"),
            self.remote(2, self.mine.at[1 - p.y, :, :, right], self.middle[1], "y"),
        ]

    def narrow_copies(self):
        p, (left, right) = self.place, self.halves()
        return [
            self.remote(3, self.mine.at[1 - p.y, p.x, :, left], self.middle[2], "y"),
            self.remote(4, self.mine.at[p.y, 1 - p.x, :, right], self.middle[3], "x"),
        ]

    def summed(self):
        return self.middle[0] if self.gather else self.mine.at[self.place.y, self.place.x]

    def pair_copy(self):
        return self.remote(5, self.summed(), self.z_first, "pair")

    def middle_copy(self):
        return self.remote(6, self.summed(), self.z_second, "middle")

    def last_copy(self):
        return self.remote(7, self.z_last, self.z_last, "pair")

    def out_copies(self):
        rows = pl.ds(self.offset, self.rows)
        core = self.place.core
        target = self.result.at[core, rows, :]
        return (
            self.remote(8, self.z_last, target, "core"),
            pltpu.make_async_copy(self.z_last, target, self.local.at[1]),
        )

    def parts(self, ref):
        if self.gather:
            return [ref.at[a, b] for a in range(2) for b in range(2)]
        return [ref]

    def lay_out(self):
        part = self.columns // 3
        for owner in range(4):
            for kind in range(3):
                lanes = pl.ds(kind * part, part)
                former = self.middle[0].at[owner // 2, owner % 2, :, lanes]
                latter = self.z_second.at[owner // 2, owner % 2, :, lanes]
                add_to(self.z_last.at[:, pl.ds((4 * kind + owner) * part, part)], former, latter)

    def stage_start(self):
        self.core_copy().start()
        self.load().start()

    def stage_core(self):
        self.core_copy().wait_recv()
        self.load().wait()
        for a in range(2):
            for b in range(2):
                add_into(self.mine.at[a, b], self.core_in.at[a, b])
        for copy in self.wide_copies():
            copy.start()

    def stage_wide(self):
        p, (left, right) = self.place, self.halves()
        if self.gather:
            stay = pltpu.make_async_copy(
                self.mine.at[p.y, p.x], self.middle[0].at[p.y, p.x], self.local.at[2]
            )
            stay.start()
            for copy in self.wide_copies():
                copy.wait_recv()
            stay.wait()
            self.z_start()
            return
        for copy in self.wide_copies():
            copy.wait_recv()
        for a in range(2):
            add_into(self.mine.at[a, p.x, :, left], self.middle[0].at[a])
            add_into(self.mine.at[p.y, a, :, right], self.middle[1].at[a])
        for copy in self.narrow_copies():
            copy.start()

    def stage_narrow(self):
        p, (left, right) = self.place, self.halves()
        for copy in self.narrow_copies():
            copy.wait_recv()
        add_into(self.mine.at[p.y, p.x, :, left], self.middle[2])
        add_into(self.mine.at[p.y, p.x, :, right], self.middle[3])
        self.z_start()

    def z_start(self):
        @pl.when(self.place.outer)
        def _():
            self.pair_copy().start()

    def stage_pair(self):
        @pl.when(self.place.inner)
        def _():
            self.pair_copy().wait_recv()
            for total, addend in zip(self.parts(self.summed()), self.parts(self.z_first)):
                add_into(total, addend)
            self.middle_copy().start()

    def stage_middle(self):
        @pl.when(self.place.inner)
        def _():
            self.middle_copy().wait_recv()
            if self.gather:
                self.lay_out()
            else:
                add_to(self.z_last, self.summed(), self.z_second)
            self.last_copy().start()
            for copy in self.out_copies():
                copy.start()

    def stage_last(self):
        @pl.when(self.place.outer)
        def _():
            self.last_copy().wait_recv()
            for copy in self.out_copies():
                copy.start()

    def stage_end(self):
        remote_out, local_out = self.out_copies()
        remote_out.wait()
        local_out.wait()
        self.core_copy().wait_send()
        for copy in self.wide_copies():
            copy.wait_send()
        if not self.gather:
            for copy in self.narrow_copies():
                copy.wait_send()

        @pl.when(self.place.outer)
        def _():
            self.pair_copy().wait_send()

        @pl.when(self.place.inner)
        def _():
            self.middle_copy().wait_send()
            self.last_copy().wait_send()

    def plan(self):
        piece = 2 * self.rows * self.columns
        if self.gather:
            return [
                (self.stage_core, [("x", 1.5 * piece), ("y", 1.5 * piece)]),
                (self.stage_wide, [("z", 4 * piece)]),
                (self.stage_pair, [("z", 4 * piece)]),
                (self.stage_middle, [("z", 4 * piece)]),
                (self.stage_last, [("core", 4 * piece)]),
                (self.stage_end, []),
            ]
        return [
            (self.stage_core, [("x", piece), ("y", piece)]),
            (self.stage_wide, [("x", piece / 2), ("y", piece / 2)]),
            (self.stage_narrow, [("z1", piece)]),
            (self.stage_pair, [("z2", piece)]),
            (self.stage_middle, [("z3", piece)]),
            (self.stage_last, [("core", piece)]),
            (self.stage_end, []),
        ]

    def opening(self):
        return [("core", 8 * self.rows * self.columns)]


class Steps:
    def __init__(self, start):
        self.now, self.free, self.waiting = start, {}, []

    def send(self, transfers):
        ends = [self.now]
        for link, size in transfers:
            start = max(self.now, self.free.get(link, 0.0))
            self.free[link] = start + size / LINK_RATE.get(link, LINK_RATE["z"])
            ends.append(self.free[link] + 2.0)
        return max(ends)

    def open(self, chunks):
        for chunk in chunks:
            self.waiting.append((self.send(chunk.opening()), len(self.waiting), chunk, 0))

    def due(self, everything=False):
        stages = []
        while self.waiting:
            self.waiting.sort(key=lambda entry: entry[:2])
            when, number, chunk, index = self.waiting[0]
            if when > self.now and not everything:
                break
            self.waiting.pop(0)
            self.now = max(self.now, when) + 0.4
            stage, transfers = chunk.plan()[index]
            stages.append(stage)
            if index + 1 < len(chunk.plan()):
                self.waiting.append((self.send(transfers), number, chunk, index + 1))
        return stages

    def spend(self, duration):
        self.now += duration


def back_kernel(
    chunks,
    qkv_chunks,
    heads,
    flag_ref,
    g_ref,
    q_hbm,
    k_hbm,
    v_hbm,
    memory_hbm,
    every_hbm,
    down_ref,
    gate_ref,
    up_ref,
    out_ref,
    mix_ref,
    log_ref,
    table_ref,
    *refs,
):
    results, rows_ref, refs = refs[: 4 + heads], refs[4 + heads], refs[5 + heads :]
    q, k, v, upstream, shared, every, dk, dv, total, delta, part_qkv = refs[:11]
    trade_sent, trade_received, rows_sent, rows_received, local = refs[11:16]
    refs = refs[16:]
    place = Place()
    seq = lax.axis_index("seq")
    tokens = g_ref.shape[0]
    width = heads * HEAD_DIM
    depth = g_ref.shape[1]
    used = 0
    sources = [down_ref, gate_ref, up_ref, out_ref] + [part_qkv.at[head] for head in range(heads)]
    for chunk in chunks + [chunk for group in qkv_chunks for chunk in group]:
        count = len(chunk.scratch())
        chunk.bind(place, sources[chunk.term], results[chunk.term], refs[used : used + count])
        used += count

    def owner_at(turn):
        low, high = lax.rem(turn, 2), lax.div(turn, 2)
        x = place.x + low - 2 * place.x * low
        y = place.y + high - 2 * place.y * high
        return 2 * y + x

    def columns(owner):
        return pl.ds(pl.multiple_of(owner * width, HEAD_DIM), width)

    def span(block):
        return pl.ds(pl.multiple_of(block * tokens, tokens), tokens)

    def lanes(head):
        return pl.ds(pl.multiple_of(head * HEAD_DIM, HEAD_DIM), HEAD_DIM)

    across = {"x": seq + 1 - 2 * place.x, "y": seq + 2 - 4 * place.y, "xy": 3 - seq}
    peers = ("x", "y", "xy")

    def finished(head, kind, peer):
        part = (q, k, v)[kind]
        mine = pl.ds(head * HEAD_DIM, HEAD_DIM)
        start = pl.multiple_of(kind * depth + seq * width + head * HEAD_DIM, HEAD_DIM)
        target = rows_ref.at[:, pl.ds(start, HEAD_DIM)]
        number = 3 * head + kind
        if peer is None:
            return pltpu.make_async_copy(part.at[span(seq), mine], target, local.at[6 + number])
        slot = 3 * number + peers.index(peer)
        return pltpu.make_async_remote_copy(
            src_ref=part.at[span(across[peer]), mine],
            dst_ref=target,
            send_sem=rows_sent.at[slot],
            recv_sem=rows_received.at[slot],
            device_id=place.peer[peer],
            device_id_type=pl.DeviceIdType.MESH,
        )

    trades = [
        pltpu.make_async_remote_copy(
            src_ref=g_ref.at[:, columns(across[peer])],
            dst_ref=upstream.at[span(seq), :],
            send_sem=trade_sent.at[slot],
            recv_sem=trade_received.at[slot],
            device_id=place.peer[peer],
            device_id_type=pl.DeviceIdType.MESH,
        )
        for slot, peer in enumerate(peers)
    ]
    loads = [
        pltpu.make_async_copy(g_ref.at[:, columns(seq)], upstream.at[span(seq), :], local.at[0]),
        pltpu.make_async_copy(q_hbm, q, local.at[1]),
        pltpu.make_async_copy(k_hbm, k, local.at[2]),
        pltpu.make_async_copy(v_hbm, v, local.at[3]),
        pltpu.make_async_copy(memory_hbm, shared, local.at[4]),
    ]
    load_every = pltpu.make_async_copy(every_hbm, every, local.at[5])

    def turn_back(matrix, rows):
        cosine, sine = turn_factors(table_ref[rows, :])
        return turn_block(matrix, cosine, sine).astype(jnp.bfloat16)

    def memory_part(head, block):
        rows, mine = span(block), lanes(head)
        query, grads = q[rows, mine], upstream[rows, mine]
        row_delta = jnp.sum(
            grads.astype(jnp.float32) * mix_ref[rows, mine].astype(jnp.float32), axis=1, keepdims=True
        )
        delta[...] = jnp.broadcast_to(row_delta, delta.shape)
        closed = (1 - flag_ref[lax.axis_index("seg")]).astype(jnp.float32) * 1e30
        log_total = log_ref[rows, mine][:, :1] + closed
        result = jnp.zeros(total.shape, jnp.float32)
        for slot in range(shared.shape[0]):
            for run in range(2):

                def tile(kind):
                    start = pl.multiple_of((2 * run + kind) * width + head * HEAD_DIM, HEAD_DIM)
                    return shared[slot, :, pl.ds(start, HEAD_DIM)]

                keys, values = tile(0), tile(1)
                probs = jnp.exp2(product_nt(query, keys) - log_total)
                dscores = probs * (product_nt(grads, values) - row_delta)
                result = result + product(dscores.astype(jnp.bfloat16), keys)
        total[...] = result

    def own_part(head, block):
        rows, mine = span(block), lanes(head)
        query, grads = q[rows, mine], upstream[rows, mine]
        log_total, row_delta = log_ref[rows, mine][:, :1], delta[:, :1]

        def turn(other, result, diagonal):
            keys = k[span(other), mine]
            scores = product_nt(query, keys)
            if diagonal:
                scores = causal(scores)
            probs = jnp.exp2(scores - log_total)
            dscores = (probs * (product_nt(grads, v[span(other), mine]) - row_delta)).astype(
                jnp.bfloat16
            )
            dv[span(other), :] += product_tn(probs.astype(jnp.bfloat16), grads)
            dk[span(other), :] += product_tn(dscores, query)
            return result + product(dscores, keys)

        result = turn(block, total[...], True)
        result = lax.fori_loop(0, block, lambda other, r: turn(other, r, False), result)
        q[rows, mine] = turn_back(result * SCORE_SCALE, rows)

    def close_head(head):
        mine = lanes(head)

        def turn(block, carry):
            rows = span(block)
            k[rows, mine] = turn_back(dk[rows, :] * LN2, rows)
            v[rows, mine] = dv[rows, :].astype(jnp.bfloat16)
            return carry

        lax.fori_loop(0, 4, turn, 0)

    def multiply_qkv(head):
        mine = slice(head * HEAD_DIM, (head + 1) * HEAD_DIM)

        def turn(index, carry):
            cut = pl.ds(pl.multiple_of(index * width, HEAD_DIM), width)
            term = None
            for block in range(every.shape[0]):
                rows = slice(block * tokens, (block + 1) * tokens)
                parts = jnp.concatenate([part[rows, mine] for part in (q, k, v)], axis=1)
                product_part = product_tn(every[block, :, cut], parts)
                term = product_part if term is None else term + product_part
            term = term.astype(jnp.bfloat16)
            half = term.shape[0] // 2
            place_y, place_x = lax.div(index, 2), lax.rem(index, 2)
            for core in range(2):
                part_qkv[head, place_y, place_x, core] = term[core * half : (core + 1) * half, :]
            return carry

        lax.fori_loop(0, 4, turn, 0)

    def send_unit(number):
        head, turn = number // 4, number % 4
        finished(head, 0, ((None,) + peers)[turn]).start()
        if turn == 3:
            for kind in (1, 2):
                for peer in peers + (None,):
                    finished(head, kind, peer).start()
            if head == 0:
                load_every.wait()
            multiply_qkv(head)
            for chunk in qkv_chunks[head]:
                chunk.stage_start()

    place.greet(("core", "x", "y", "xy", "pair"))
    for copy in trades + loads + [load_every]:
        copy.start()
    for chunk in chunks:
        chunk.stage_start()
    steps = Steps(3.0)
    steps.free.update(x=11.0, y=11.0)
    steps.open(chunks)
    for copy in loads:
        copy.wait()
    slots = []
    piece = 2 * tokens * HEAD_DIM

    def close(head):
        steps.send([("x", 4 * piece), ("y", 4 * piece)])
        steps.spend(5.0)
        steps.open(qkv_chunks[head])

    for unit in range(2 * 4 * heads):
        if unit > 0 and unit % 8 == 0:
            close(unit // 8 - 1)
        slots.append(steps.due())
        steps.spend(4.3 if unit % 2 == 0 else 3.2)

    def run(stages):
        for stage in stages:
            stage()

    def unit(index, carry):
        head, turn = lax.div(index, 4), lax.rem(index, 4)
        block = owner_at(turn)
        for number in range(4 * heads):
            if slots[2 * number] or number > 0:

                @pl.when(index == number)
                def _(number=number):
                    if number > 0:
                        send_unit(number - 1)
                    run(slots[2 * number])
                    if number in (1, 2, 3):
                        trades[number - 1].wait_recv()

        @pl.when(turn == 0)
        def _():
            dk[...] = jnp.zeros_like(dk)
            dv[...] = jnp.zeros_like(dv)

        memory_part(head, block)
        for number in range(4 * heads):
            if slots[2 * number + 1]:

                @pl.when(index == number)
                def _(number=number):
                    run(slots[2 * number + 1])

        own_part(head, block)

        @pl.when(turn == 3)
        def _():
            close_head(head)

        return carry

    lax.fori_loop(0, 4 * heads, unit, 0)
    send_unit(4 * heads - 1)
    close(heads - 1)
    run(steps.due(True))
    for copy in trades:
        copy.wait_send()
    for head in range(heads):
        for kind in range(3):
            for peer in peers + (None,):
                finished(head, kind, peer).wait()


def back(flags, grads, queries, keys, values, memory, every, terms, attended, log_totals, table, collective_id):
    tokens, depth = grads.shape
    length, width = queries.shape
    heads = width // HEAD_DIM
    low = jnp.bfloat16
    chunks, shapes = [], []
    for index, term in enumerate(terms):
        rows, columns = term.shape[0] // 8, term.shape[1]
        parts = 2 if rows % 32 == 0 and index < 3 else 1
        chunks += [Chunk(index, n * rows // parts, rows // parts, columns) for n in range(parts)]
        shapes.append((2, rows, columns))
    rows, columns = depth // 8, 3 * HEAD_DIM
    qkv_chunks = [
        [Chunk(4 + head, n * rows // 2, rows // 2, columns, True) for n in range(2)]
        for head in range(heads)
    ]
    shapes += [(2, rows, 4 * columns)] * heads + [(tokens, 3 * depth)]
    anywhere = pl.BlockSpec(memory_space=pl.ANY)
    inside = pl.BlockSpec(memory_space=pltpu.VMEM)
    dma = pltpu.SemaphoreType.DMA
    scratch = (
        [pltpu.VMEM((length, width), low)] * 4
        + [pltpu.VMEM((4, tokens, depth), low)] * 2
        + [pltpu.VMEM((length, HEAD_DIM), jnp.float32)] * 2
        + [pltpu.VMEM((tokens, HEAD_DIM), jnp.float32)] * 2
        + [pltpu.VMEM((heads, 2, 2, 2, rows, columns), low)]
        + [dma((3,))] * 2
        + [dma((9 * heads,))] * 2
        + [dma((6 + 3 * heads,))]
    )
    every_chunk = chunks + [chunk for group in qkv_chunks for chunk in group]
    return pl.pallas_call(
        functools.partial(back_kernel, chunks, qkv_chunks, heads),
        in_specs=[pl.BlockSpec(memory_space=pltpu.SMEM)] + [anywhere] * 10 + [inside] * 3,
        out_specs=[anywhere] * len(shapes),
        out_shape=[jax.ShapeDtypeStruct(shape, low) for shape in shapes],
        scratch_shapes=scratch + [ref for chunk in every_chunk for ref in chunk.scratch()],
        compiler_params=pltpu.CompilerParams(
            collective_id=collective_id, has_side_effects=True, vmem_limit_bytes=VMEM_MOST
        ),
        name="back",
    )(
        flags,
        grads,
        queries,
        keys,
        values,
        memory,
        every,
        *[term.reshape((2, 2, 2, term.shape[0] // 8, term.shape[1])) for term in terms],
        attended,
        log_totals,
        table,
    )


class Line:
    def __init__(self, place, seg, memory, spans, refs):
        self.place, self.seg, self.memory, self.spans = place, seg, memory, spans
        self.runs = len(spans)
        self.sent, self.received, self.core_sent, self.core_received = refs

    def span(self, run):
        return self.spans[run]

    def there(self, way, step):
        return self.place.z >= step if way == 0 else self.place.z + step <= 3

    def goes(self, way, step):
        has = self.there(way, step - 1)
        return jnp.logical_and(has, self.place.z <= 2 if way == 0 else self.place.z >= 1)

    def index(self, way, step):
        return self.seg - 2 * step if way == 0 else self.seg + 2 * step

    def hop(self, way, step, run):
        name = self.index(way, step - 1)
        target = self.memory.at[name, self.span(run), :]
        slot = (way * 3 + step - 1) * self.runs + run
        seg, seq = lax.axis_index("seg"), lax.axis_index("seq")
        return pltpu.make_async_remote_copy(
            src_ref=target,
            dst_ref=target,
            send_sem=self.sent.at[slot],
            recv_sem=self.received.at[slot],
            device_id=(seg + 2 - 4 * way, seq),
            device_id_type=pl.DeviceIdType.MESH,
        )

    def arrival(self, way, step, run):
        target = self.memory.at[self.index(way, step), self.span(run), :]
        slot = (way * 3 + step - 1) * self.runs + run
        return pltpu.make_async_remote_copy(
            src_ref=target,
            dst_ref=target,
            send_sem=self.sent.at[slot],
            recv_sem=self.received.at[slot],
            device_id=self.place.peer["core"],
            device_id_type=pl.DeviceIdType.MESH,
        )

    def share(self, way, step, run):
        name = self.index(way, step)
        target = self.memory.at[name, self.span(run), :]
        slot = (way * 3 + step) * self.runs + run
        return pltpu.make_async_remote_copy(
            src_ref=target,
            dst_ref=target,
            send_sem=self.core_sent.at[slot],
            recv_sem=self.core_received.at[slot],
            device_id=self.place.peer["core"],
            device_id_type=pl.DeviceIdType.MESH,
        )

    def start(self, run):
        for way in range(2):

            @pl.when(self.goes(way, 1))
            def _(way=way):
                self.hop(way, 1, run).start()

        self.share(0, 0, run).start()

    def advance(self, step, run):
        for way in range(2):

            @pl.when(self.there(way, step))
            def _(way=way):
                self.arrival(way, step, run).wait_recv()

            if step < 3:

                @pl.when(self.goes(way, step + 1))
                def _(way=way):
                    self.hop(way, step + 1, run).start()

            @pl.when(self.there(way, step))
            def _(way=way):
                self.share(way, step, run).start()

    def finish(self):
        for run in range(self.runs):
            self.share(0, 0, run).wait()
            for way in range(2):
                for step in range(1, 4):

                    @pl.when(self.there(way, step))
                    def _(way=way, step=step, run=run):
                        self.share(way, step, run).wait()

                    @pl.when(self.goes(way, step))
                    def _(way=way, step=step, run=run):
                        self.hop(way, step, run).wait_send()


def front_kernel(
    heads,
    flag_ref,
    source_ref,
    x_ref,
    mem_k_ref,
    mem_v_ref,
    w_hbm,
    table_ref,
    every_ref,
    chosen_ref,
    attended_ref,
    q_ref,
    k_ref,
    v_ref,
    low_ref,
    log_ref,
    w_ref,
    rows,
    memory,
    listed,
    mix_ref,
    max_ref,
    sum_ref,
    trade_sent,
    trade_received,
    rows_sent,
    rows_received,
    line_sent,
    line_received,
    core_sent,
    core_received,
    back_sent,
    back_received,
    local,
):
    place = Place()
    seg, seq = lax.axis_index("seg"), lax.axis_index("seq")
    width = heads * HEAD_DIM
    count = mem_k_ref.shape[0]
    tokens, depth = x_ref.shape
    across = {"x": seq + 1 - 2 * place.x, "y": seq + 2 - 4 * place.y, "xy": 3 - seq}

    def remote(source, target, sent, received, slot, peer):
        return pltpu.make_async_remote_copy(
            src_ref=source,
            dst_ref=target,
            send_sem=sent.at[slot],
            recv_sem=received.at[slot],
            device_id=place.peer[peer],
            device_id_type=pl.DeviceIdType.MESH,
        )

    def columns(owner, start=0):
        return pl.ds(pl.multiple_of(start + owner * width, HEAD_DIM), width)

    def seat(owner):
        return pl.ds(pl.multiple_of(owner * count, 16), count)

    def owner_at(turn):
        low, high = lax.rem(turn, 2), lax.div(turn, 2)
        x = place.x + low - 2 * place.x * low
        y = place.y + high - 2 * place.y * high
        return 2 * y + x

    def block_rows(block):
        return pl.ds(pl.multiple_of(block * tokens, 16), tokens)

    peers = ("x", "y", "xy")
    trades = []
    for number, peer in enumerate(peers):
        for kind, source in enumerate((mem_k_ref, mem_v_ref)):
            lanes = pl.ds(kind * width, width)
            trades.append(
                remote(
                    source.at[:, columns(across[peer])],
                    memory.at[seg, seat(seq), lanes],
                    trade_sent,
                    trade_received,
                    2 * number + kind,
                    peer,
                )
            )
    keeps = [
        pltpu.make_async_copy(
            source.at[:, columns(seq)],
            memory.at[seg, seat(seq), pl.ds(kind * width, width)],
            local.at[kind],
        )
        for kind, source in enumerate((mem_k_ref, mem_v_ref))
    ]
    half = depth // 2
    left, right = pl.ds(0, half), pl.ds(half, half)
    load = pltpu.make_async_copy(x_ref, rows.at[seq], local.at[2])
    loads = weight_copies(w_hbm, w_ref, seq, local, 3)
    direct = [
        remote(x_ref.at[:, left], rows.at[seq, :, left], rows_sent, rows_received, 0, "x"),
        remote(x_ref.at[:, right], rows.at[seq, :, right], rows_sent, rows_received, 1, "y"),
        remote(x_ref.at[:, right], rows.at[seq, :, right], rows_sent, rows_received, 2, "x"),
        remote(x_ref.at[:, left], rows.at[seq, :, left], rows_sent, rows_received, 3, "y"),
    ]
    onward = [
        remote(
            rows.at[across["x"], :, left], rows.at[across["x"], :, left], rows_sent, rows_received, 4, "y"
        ),
        remote(
            rows.at[across["y"], :, right], rows.at[across["y"], :, right], rows_sent, rows_received, 5, "x"
        ),
    ]
    line = Line(
        place,
        seg,
        memory,
        [seat(owner) for owner in (seq, across["x"], across["y"], across["xy"])],
        (line_sent, line_received, core_sent, core_received),
    )
    keep_rows = pltpu.make_async_copy(rows, every_ref, local.at[6])
    run_rows = memory.shape[1] // 2
    keep_chosen = []
    for run in range(2):
        span, lanes = pl.ds(run * run_rows, run_rows), pl.ds(2 * run * width, 2 * width)
        keep_chosen.append(
            pltpu.make_async_copy(memory.at[seg, span, :], chosen_ref.at[0, :, lanes], local.at[7 + run])
        )
        keep_chosen.append(
            pltpu.make_async_copy(
                listed.at[:, span, :],
                chosen_ref.at[pl.ds(1, listed.shape[0]), :, lanes],
                local.at[9 + run],
            )
        )
    returns = [
        remote(
            low_ref.at[block_rows(across[peer]), :],
            attended_ref.at[:, columns(seq)],
            back_sent,
            back_received,
            slot,
            peer,
        )
        for slot, peer in enumerate(peers)
    ]
    keep_attended = pltpu.make_async_copy(
        low_ref.at[block_rows(seq), :], attended_ref.at[:, columns(seq)], local.at[11]
    )

    def project_rows(owner):
        block = rows[owner]
        span = block_rows(owner)
        cosine, sine = turn_factors(table_ref[span, :])
        scale = SCORE_SCALE / LN2
        queries = product(block, w_ref[:, :width])
        keys = product(block, w_ref[:, width : 2 * width])
        for head in range(heads):
            lanes = slice(head * HEAD_DIM, (head + 1) * HEAD_DIM)
            q_ref[span, lanes] = turn_block(
                queries[:, lanes], cosine * scale, sine * (-scale)
            ).astype(jnp.bfloat16)
            k_ref[span, lanes] = turn_block(keys[:, lanes], cosine, -sine).astype(jnp.bfloat16)
        v_ref[span, :] = product(block, w_ref[:, 2 * width :]).astype(jnp.bfloat16)

    def head_lanes(head, start=0):
        return pl.ds(pl.multiple_of(start + head * HEAD_DIM, HEAD_DIM), HEAD_DIM)

    def keep(span, lanes, row_max, row_sum, mixed):
        mix_ref[span, lanes] = mixed
        max_ref[span, lanes] = jnp.broadcast_to(row_max, mixed.shape)
        sum_ref[span, lanes] = jnp.broadcast_to(row_sum, mixed.shape)

    def own_rows(block):
        def turn(head, carry):
            lanes = head_lanes(head)
            span = pl.ds(block * tokens, tokens)
            pairs = [
                (k_ref[pl.ds(n * tokens, tokens), lanes], v_ref[pl.ds(n * tokens, tokens), lanes])
                for n in range(block + 1)
            ]
            keep(span, lanes, *attend(q_ref[span, lanes], pairs, True, None))
            return carry

        lax.fori_loop(0, heads, turn, 0)

    closed = (1 - flag_ref[seg]).astype(jnp.float32) * 1e30

    def carried(span, lanes):
        return max_ref[span, lanes][:, :1], sum_ref[span, lanes][:, :1], mix_ref[span, lanes]

    def own_memory(first, last):
        def turn(index, carry):
            head = lax.rem(index, heads)
            lanes, span = head_lanes(head), block_rows(lax.div(index, heads))
            pair = (memory[seg, :, lanes], memory[seg, :, head_lanes(head, width)])
            keep(span, lanes, *attend(q_ref[span, lanes], [pair], False, carried(span, lanes), closed))
            return carry

        lax.fori_loop(first * heads, last * heads, turn, 0)

    barrier = pltpu.get_barrier_semaphore()

    def hail(device):
        pl.semaphore_signal(barrier, inc=1, device_id=device, device_id_type=pl.DeviceIdType.MESH)

    for copy in keeps + [load] + loads:
        copy.start()
    for peer in ("x", "y", "xy", "core"):
        hail(place.peer[peer])
    below, above = place.z >= 1, place.z <= 2

    @pl.when(below)
    def _():
        hail((seg - 2, seq))

    @pl.when(above)
    def _():
        hail((seg + 2, seq))

    pl.semaphore_wait(barrier, 4 + below.astype(jnp.int32) + above.astype(jnp.int32))

    for copy in trades + direct:
        copy.start()
    for copy in keeps:
        copy.wait()
    line.start(0)
    load.wait()
    for copy in loads:
        copy.wait()
    project_rows(seq)
    for number in range(3):
        for kind in range(2):
            trades[2 * number + kind].wait_recv()
        line.start(number + 1)
        line.advance(1, number)
    direct[0].wait_recv()
    direct[1].wait_recv()
    for copy in onward:
        copy.start()
    line.advance(1, 3)
    line.advance(2, 0)
    direct[2].wait_recv()
    direct[3].wait_recv()
    project_rows(across["x"])
    line.advance(2, 1)
    project_rows(across["y"])
    line.advance(2, 2)
    for copy in onward:
        copy.wait_recv()
    project_rows(3 - seq)
    keep_rows.start()
    line.advance(2, 3)
    own_rows(0)
    own_rows(1)
    line.advance(3, 0)
    own_rows(2)
    line.advance(3, 1)
    own_rows(3)
    line.advance(3, 2)
    own_memory(0, 2)
    line.advance(3, 3)
    own_memory(2, 4)
    line.finish()
    for n in range(listed.shape[0]):
        listed[n] = memory[source_ref[seg, n]]

    def unit(index, carry):
        turn, head = lax.div(index, heads), lax.rem(index, heads)

        @pl.when(index == heads // 2)
        def _():
            for copy in keep_chosen:
                copy.start()

        for number in range(3):

            @pl.when(index == heads * (3 - number))
            def _(number=number):
                returns[number].start()

        lanes, span = head_lanes(head), block_rows(owner_at(3 - turn))
        pairs = [
            (listed[n, :, lanes], listed[n, :, head_lanes(head, width)])
            for n in range(listed.shape[0])
        ]
        row_max, row_sum, mixed = attend(
            q_ref[span, lanes], pairs, False, carried(span, lanes), closed
        )
        low_ref[span, lanes] = (mixed * (1.0 / row_sum)).astype(jnp.bfloat16)
        log_ref[span, lanes] = jnp.broadcast_to(row_max + jnp.log2(row_sum), mixed.shape)
        return carry

    lax.fori_loop(0, 4 * heads, unit, 0)
    keep_attended.start()
    for copy in returns:
        copy.wait()
    for copy in keep_chosen + [keep_rows, keep_attended]:
        copy.wait()
    for copy in trades + direct + onward:
        copy.wait_send()


def front(
    flags, sources, first_low, mem_keys, mem_values, w_qkv, table, seg_size, seq_size, collective_id
):
    tokens, depth = first_low.shape
    length = tokens * seq_size
    width = depth // seq_size
    count = mem_keys.shape[0] * seq_size
    slots = sources.shape[1]
    anywhere = pl.BlockSpec(memory_space=pl.ANY)
    inside = pl.BlockSpec(memory_space=pltpu.VMEM)
    scalars = pl.BlockSpec(memory_space=pltpu.SMEM)
    low = jnp.bfloat16
    shape = jax.ShapeDtypeStruct
    dma = pltpu.SemaphoreType.DMA
    return pl.pallas_call(
        functools.partial(front_kernel, width // HEAD_DIM),
        in_specs=[scalars] * 2 + [anywhere] * 4 + [inside],
        out_specs=[anywhere] * 3 + [inside] * 5,
        out_shape=[
            shape((seq_size, tokens, depth), low),
            shape((slots + 1, count // 2, 4 * width), low),
            shape((tokens, depth), low),
        ]
        + [shape((length, width), low)] * 4
        + [shape((length, width), jnp.float32)],
        scratch_shapes=[
            pltpu.VMEM((depth, 3 * width), low),
            pltpu.VMEM((seq_size, tokens, depth), low),
            pltpu.VMEM((seg_size, count, 2 * width), low),
            pltpu.VMEM((slots, count, 2 * width), low),
        ]
        + [pltpu.VMEM((length, width), jnp.float32)] * 3
        + [dma((6,))] * 4
        + [dma((24,))] * 2
        + [dma((28,))] * 2
        + [dma((3,))] * 2
        + [dma((12,))],
        compiler_params=pltpu.CompilerParams(
            collective_id=collective_id, has_side_effects=True, vmem_limit_bytes=VMEM_BYTES
        ),
        name="front",
    )(flags, sources, first_low, mem_keys, mem_values, w_qkv, table)


def norm_input_grad(values, inverse, norm_gain, upstream):
    weighted = upstream * norm_gain
    inner_mean = jnp.mean(weighted * values, axis=-1, keepdims=True)
    return inverse * weighted - inverse * inverse * inverse * values * inner_mean


def dense_kernel(
    x_ref,
    g_ref,
    attended_ref,
    out_ref,
    gain_ref,
    gate_ref,
    up_ref,
    down_ref,
    output_ref,
    grad_ref,
    grad_attended_ref,
    term_down,
    term_gate,
    term_up,
    term_out,
    residual_ref,
    second,
    second_t,
    total,
    grad_second,
):
    index = pl.program_id(0)
    low = jnp.bfloat16

    @pl.when(index == 0)
    def _():
        residual = x_ref[...].astype(jnp.float32) + product(attended_ref[...], out_ref[...])
        residual_ref[...] = residual
        second_low = norm_forward(residual, gain_ref[...])[0].astype(low)
        second[...] = second_low
        second_t[...] = second_low.T

    gate, up = product(second[...], gate_ref[...]), product(second[...], up_ref[...])
    grad_hidden = product_nt(g_ref[...], down_ref[...])
    sigmoid_gate = jax.nn.sigmoid(gate)
    activated = gate * sigmoid_gate
    hidden = (activated * up).astype(low)
    grad_gate = (grad_hidden * up * sigmoid_gate * (1.0 + gate * (1.0 - sigmoid_gate))).astype(low)
    grad_up = (grad_hidden * activated).astype(low)
    term_down[...] = product_tn(hidden, g_ref[...]).astype(low)
    term_gate[...] = product(second_t[...], grad_gate).astype(low)
    term_up[...] = product(second_t[...], grad_up).astype(low)
    part = product(hidden, down_ref[...])
    grad_part = product_nt(grad_gate, gate_ref[...]) + product_nt(grad_up, up_ref[...])

    @pl.when(index == 0)
    def _():
        total[...] = part
        grad_second[...] = grad_part

    @pl.when(index > 0)
    def _():
        total[...] += part
        grad_second[...] += grad_part

    @pl.when(index == pl.num_programs(0) - 1)
    def _():
        residual = residual_ref[...]
        output_ref[...] = (residual + total[...]).astype(low)
        inverse = lax.rsqrt(jnp.mean(residual * residual, axis=-1, keepdims=True) + epsilon)
        grad = norm_input_grad(residual, inverse, gain_ref[...], grad_second[...])
        grad = grad + g_ref[...].astype(jnp.float32)
        grad_ref[...] = grad
        grad_low = grad.astype(low)
        term_out[...] = product_tn(attended_ref[...], grad_low).astype(low)
        grad_attended_ref[...] = product_nt(grad_low, out_ref[...]).astype(low)


def dense(x, grads, attended, w_out, gain, w_gate, w_up, w_down, tile=256):
    tokens, depth = x.shape
    hidden = w_gate.shape[1]
    tile = math.gcd(tile, hidden)
    low = jnp.bfloat16
    shape = jax.ShapeDtypeStruct

    def whole(rows, columns):
        return pl.BlockSpec((rows, columns), lambda j: (0, 0))

    across = pl.BlockSpec((depth, tile), lambda j: (0, j))
    down = pl.BlockSpec((tile, depth), lambda j: (j, 0))
    activation = whole(tokens, depth)
    return pl.pallas_call(
        dense_kernel,
        grid=(hidden // tile,),
        in_specs=[activation] * 3 + [whole(depth, depth), whole(1, depth), across, across, down],
        out_specs=[activation] * 3 + [down, across, across, whole(depth, depth)],
        out_shape=[
            shape((tokens, depth), low),
            shape((tokens, depth), jnp.float32),
            shape((tokens, depth), low),
            shape((hidden, depth), low),
            shape((depth, hidden), low),
            shape((depth, hidden), low),
            shape((depth, depth), low),
        ],
        scratch_shapes=[
            pltpu.VMEM((tokens, depth), jnp.float32),
            pltpu.VMEM((tokens, depth), low),
            pltpu.VMEM((depth, tokens), low),
            pltpu.VMEM((tokens, depth), jnp.float32),
            pltpu.VMEM((tokens, depth), jnp.float32),
        ],
        compiler_params=pltpu.CompilerParams(vmem_limit_bytes=VMEM_BYTES),
        cost_estimate=pl.CostEstimate(
            flops=16 * tokens * depth * hidden + 6 * tokens * depth * depth,
            transcendentals=tokens * hidden,
            bytes_accessed=12 * depth * hidden + 20 * tokens * depth,
        ),
        name="dense",
    )(x, grads, attended, w_out, gain, w_gate, w_up, w_down)


def tail_kernel(
    heads,
    down_hbm,
    gate_hbm,
    up_hbm,
    out_hbm,
    *refs,
):
    qkv_hbm, refs = refs[:heads], refs[heads:]
    turned_hbm, x_hbm, grad_hbm, w_hbm, w_gate_hbm, w_up_hbm, gain1_ref, gain2_ref = refs[:8]
    input_out, norm1_ref, norm2_ref, qkv_out, out_out, gate_out, up_out, down_out = refs[8:16]
    down, gate, up, out = refs[16:20]
    qkv, refs = refs[20 : 20 + heads], refs[20 + heads :]
    turned, x, grad, w, w_gate, w_up = refs[:6]
    input_wide, qkv_wide, out_wide, gate_wide, up_wide, down_wide, dots1, dots2, loaded, stored = refs[6:]
    seq = lax.axis_index("seq")
    count = gate.shape[0]
    block = pl.ds(pl.multiple_of(seq * count, count), count)
    pairs = [
        (gate_hbm, gate),
        (w_gate_hbm.at[block, :], w_gate),
        (up_hbm, up),
        (w_up_hbm.at[block, :], w_up),
        (down_hbm, down),
        (out_hbm, out),
        (turned_hbm, turned),
        (w_hbm, w),
        *zip(qkv_hbm, qkv),
        (x_hbm, x),
        (grad_hbm, grad),
    ]
    loads = [
        pltpu.make_async_copy(source, target, loaded.at[n]) for n, (source, target) in enumerate(pairs)
    ]
    wides = [gate_wide, up_wide, down_wide, out_wide, qkv_wide, input_wide]
    outs = [gate_out, up_out, down_out, out_out, qkv_out, input_out]
    stores = [
        pltpu.make_async_copy(source, target, stored.at[n])
        for n, (source, target) in enumerate(zip(wides, outs))
    ]
    for copy in loads:
        copy.start()

    def by_rows(count, step, body):
        def turn(index, carry):
            body(pl.ds(pl.multiple_of(index * step, step), step))
            return carry

        lax.fori_loop(0, count // step, turn, 0)

    def widen(former, latter):
        def body(rows):
            latter[rows, :] = former[rows, :].astype(jnp.float32)

        by_rows(former.shape[0], 16, body)

    def dot_rows(values, weights):
        return lane_fold(jnp.add, values * weights.astype(jnp.float32), None)

    def gate_body(rows):
        values = gate[rows, :].astype(jnp.float32)
        gate_wide[rows, :] = values
        dots2[rows, :] = dot_rows(values, w_gate[rows, :])

    def up_body(rows):
        values = up[rows, :].astype(jnp.float32)
        up_wide[rows, :] = values
        dots2[rows, :] += dot_rows(values, w_up[rows, :])

    def qkv_body(rows):
        running = None
        weights = pl.ds(pl.multiple_of(seq * count + rows.start, 16), rows.size)
        for number in range(qkv[0].shape[1] // HEAD_DIM):
            for head in range(heads):
                start = (number * heads + head) * HEAD_DIM
                lanes = slice(start, start + HEAD_DIM)
                values = qkv[head][rows, number * HEAD_DIM : (number + 1) * HEAD_DIM].astype(jnp.float32)
                qkv_wide[rows, lanes] = values
                term = values * w[weights, lanes].astype(jnp.float32)
                running = term if running is None else running + term
        dots1[rows, :] = running

    def gain_grads(dots, gain_ref):
        columns = jnp.broadcast_to(jnp.sum(dots[...], axis=1, keepdims=True), dots.shape)
        return columns.T[:1, :] / gain_ref[:, block]

    def wait(*numbers):
        for number in numbers:
            loads[number].wait()

    wait(0, 1)
    by_rows(count, 16, gate_body)
    stores[0].start()
    wait(2, 3)
    by_rows(count, 16, up_body)
    stores[1].start()
    norm2_ref[...] = gain_grads(dots2, gain2_ref)
    wait(4)
    widen(down, down_wide)
    stores[2].start()
    wait(5)
    widen(out, out_wide)
    stores[3].start()
    wait(6, 7)

    def first_columns(index, carry):
        cut = pl.ds(pl.multiple_of(index * count, count), count)
        input_wide[:, cut] = product_nt(turned[...], w[cut, :])
        return carry

    lax.fori_loop(0, w.shape[0] // count, first_columns, 0)
    wait(*range(8, 8 + heads))
    by_rows(count, 16, qkv_body)
    stores[4].start()
    norm1_ref[...] = gain_grads(dots1, gain1_ref)
    wait(8 + heads, 9 + heads)

    def input_body(rows):
        values = x[rows, :].astype(jnp.float32)
        inverse = lax.rsqrt(jnp.mean(values * values, axis=-1, keepdims=True) + epsilon)
        input_wide[rows, :] = grad[rows, :] + norm_input_grad(
            values, inverse, gain1_ref[...], input_wide[rows, :]
        )

    by_rows(x.shape[0], 32, input_body)
    stores[5].start()
    for copy in stores:
        copy.wait()


def tail(sums, turned, x, grad, w_qkv, w_gate, w_up, gain1, gain2):
    down, gate, up, out, *qkv = sums
    tokens, depth = x.shape
    count = gate.shape[0]
    low, wide = jnp.bfloat16, jnp.float32
    anywhere = pl.BlockSpec(memory_space=pl.ANY)
    inside = pl.BlockSpec(memory_space=pltpu.VMEM)
    shapes = [(tokens, depth), (count, w_qkv.shape[1]), out.shape, gate.shape, up.shape, down.shape]
    results = [shapes[0], (1, count), (1, count)] + shapes[1:]
    return pl.pallas_call(
        functools.partial(tail_kernel, len(qkv)),
        in_specs=[anywhere] * (10 + len(qkv)) + [inside] * 2,
        out_specs=[anywhere] + [inside] * 2 + [anywhere] * 5,
        out_shape=[jax.ShapeDtypeStruct(shape, wide) for shape in results],
        scratch_shapes=[pltpu.VMEM(total.shape, low) for total in sums]
        + [
            pltpu.VMEM(turned.shape, low),
            pltpu.VMEM(x.shape, low),
            pltpu.VMEM(x.shape, wide),
            pltpu.VMEM(w_qkv.shape, low),
            pltpu.VMEM(gate.shape, low),
            pltpu.VMEM(up.shape, low),
        ]
        + [pltpu.VMEM(shape, wide) for shape in shapes]
        + [pltpu.VMEM((count, HEAD_DIM), wide)] * 2
        + [pltpu.SemaphoreType.DMA((10 + len(qkv),)), pltpu.SemaphoreType.DMA((6,))],
        compiler_params=pltpu.CompilerParams(vmem_limit_bytes=VMEM_BYTES),
        name="tail",
    )(*sums, turned, x, grad, w_qkv, w_gate, w_up, gain1, gain2)


def head_plan(
    seg_size,
    seq_size,
    layer_input,
    output_grad,
    norm1_gain,
    norm2_gain,
    w_qkv,
    w_out,
    w_gate,
    w_up,
    w_down,
    mem_keys,
    mem_values,
    memory_flags,
    sources,
):
    seq_index = lax.axis_index("seq")
    tokens = layer_input.shape[1]
    length = tokens * seq_size
    width = D // seq_size
    inputs = layer_input[0].astype(jnp.float32)
    first_norm, first_inverse = norm_forward(inputs, norm1_gain)
    first_low = first_norm.astype(jnp.bfloat16)
    table = turn_table(length)
    every_low, chosen_memory, attended_low, queries, keys, values, heads_low, log_totals = front(
        memory_flags, sources, first_low, mem_keys[0], mem_values[0], w_qkv, table, seg_size, seq_size, 1
    )

    output, grad_residual, grad_attended, term_down, term_gate, term_up, term_out = dense(
        layer_input[0], output_grad[0], attended_low, w_out, norm2_gain[None], w_gate, w_up, w_down
    )
    *sums, turned = back(
        memory_flags,
        grad_attended,
        queries,
        keys,
        values,
        chosen_memory,
        every_low,
        [term_down, term_gate, term_up, term_out],
        heads_low,
        log_totals,
        table,
        2,
    )
    sums = [total.reshape(2 * total.shape[1], total.shape[2]) for total in sums]
    input_grad, grad_norm1, grad_norm2, grad_qkv, grad_out, grad_gate, grad_up, grad_down = tail(
        sums, turned, layer_input[0], grad_residual, w_qkv, w_gate, w_up, norm1_gain[None], norm2_gain[None]
    )
    return (
        output[None],
        input_grad[None],
        grad_norm1[0],
        grad_norm2[0],
        grad_qkv,
        grad_out,
        grad_gate,
        grad_up,
        grad_down,
    )


def solution(mesh):
    seq_size = mesh.shape["seq"]
    heads_fit = seq_size == 4 and mesh.shape["seg"] == 8
    plan = functools.partial(head_plan, mesh.shape["seg"], seq_size) if heads_fit else general_plan
    placed = (
        P("seg", "seq", None),
        P("seg", "seq", None),
        P(),
        P(),
        P(),
        P(),
        P(),
        P(),
        P(),
        P("seg", "seq", None),
        P("seg", "seq", None),
        P(),
        P(),
    )
    return jax.shard_map(
        plan,
        mesh=mesh,
        in_specs=placed,
        out_specs=(
            P("seg", "seq", None),
            P("seg", "seq", None),
            P("seq"),
            P("seq"),
            P("seq", None),
            P("seq", None),
            P("seq", None),
            P("seq", None),
            P("seq", None),
        ),
        check_vma=False,
    )
```

```python
import functools
import math

import jax
import jax.numpy as jnp
import numpy as np
from jax import lax
from jax.experimental import pallas as pl
from jax.experimental.pallas import tpu as pltpu
from jax.sharding import PartitionSpec as P

D = 1024
HEADS = 8
HEAD_DIM = 128


masked_score = -1e30
epsilon = 1e-06
rotary_base = 10000.0


def product(former, latter):
    return jnp.dot(former, latter, preferred_element_type=jnp.float32)


def product_nt(former, latter):
    return lax.dot_general(
        former, latter, (((1,), (1,)), ((), ())), preferred_element_type=jnp.float32
    )


def product_tn(former, latter):
    return lax.dot_general(
        former, latter, (((0,), (0,)), ((), ())), preferred_element_type=jnp.float32
    )


def norm_forward(values, norm_gain):
    inverse = lax.rsqrt(jnp.mean(values * values, axis=-1, keepdims=True) + epsilon)
    return (values * inverse * norm_gain, inverse)


def norm_backward(values, inverse, norm_gain, upstream):
    weighted = upstream * norm_gain
    inner_mean = jnp.mean(weighted * values, axis=-1, keepdims=True)
    grad_values = inverse * weighted - inverse * inverse * inverse * values * inner_mean
    grad_gain = jnp.sum(upstream * values * inverse, axis=0)
    return (grad_values, grad_gain)


def turn_tables(positions):
    half_dim = HEAD_DIM // 2
    exponent = -2.0 * jnp.arange(half_dim, dtype=jnp.float32) / HEAD_DIM
    angles = positions[:, None] * jnp.power(rotary_base, exponent)[None, :]
    angles = jnp.concatenate([angles, angles], axis=1)
    return (jnp.cos(angles)[:, None, :], jnp.sin(angles)[:, None, :])


def rotate(matrix, cosine_table, sine_table, direction):
    row_count = matrix.shape[0]
    half_dim = HEAD_DIM // 2
    shaped = matrix.reshape(row_count, HEADS, HEAD_DIM)
    turned = jnp.concatenate([-shaped[..., half_dim:], shaped[..., :half_dim]], axis=-1)
    return (shaped * cosine_table + direction * turned * sine_table).reshape(
        row_count, HEADS * HEAD_DIM
    )


def general_plan(
    layer_input,
    output_grad,
    norm1_gain,
    norm2_gain,
    w_qkv,
    w_out,
    w_gate,
    w_up,
    w_down,
    mem_keys,
    mem_values,
    memory_flags,
    sources,
):
    seg_index = lax.axis_index("seg")
    seq_index = lax.axis_index("seq")
    tokens = layer_input.shape[1]
    score_scale = HEAD_DIM ** (-0.5)
    flag_on = lax.dynamic_index_in_dim(memory_flags, seg_index, 0, keepdims=False) > 0
    listed = lax.dynamic_index_in_dim(sources, seg_index, 0, keepdims=False)
    picked = jnp.concatenate([jnp.reshape(seg_index, (1,)), listed])
    every_keys, every_values = (
        lax.all_gather(mem_keys, "seg", axis=0, tiled=True),
        lax.all_gather(mem_values, "seg", axis=0, tiled=True),
    )
    chosen_keys = jnp.take(every_keys, picked, axis=0)
    chosen_values = jnp.take(every_values, picked, axis=0)
    memory_keys, memory_values = (
        lax.all_gather(chosen_keys, "seq", axis=1, tiled=True),
        lax.all_gather(chosen_values, "seq", axis=1, tiled=True),
    )
    memory_key_blocks = memory_keys.reshape(-1, tokens, HEADS, HEAD_DIM)
    memory_value_blocks = memory_values.reshape(-1, tokens, HEADS, HEAD_DIM)
    memory_blocks = memory_key_blocks.shape[0]
    inputs = layer_input[0].astype(jnp.float32)
    first_norm, first_inverse = norm_forward(inputs, norm1_gain)
    first_low = first_norm.astype(jnp.bfloat16)
    projected = product(first_low, w_qkv)
    positions = seq_index * tokens + lax.iota(jnp.int32, tokens)
    cosine_table, sine_table = turn_tables(positions.astype(jnp.float32))
    queries = rotate(projected[:, :D], cosine_table, sine_table, 1.0).astype(jnp.bfloat16)
    own_keys = rotate(projected[:, D : 2 * D], cosine_table, sine_table, 1.0).astype(jnp.bfloat16)
    own_values = projected[:, 2 * D :].astype(jnp.bfloat16)
    all_keys, all_values = (
        lax.all_gather(own_keys, "seq", axis=0, tiled=True),
        lax.all_gather(own_values, "seq", axis=0, tiled=True),
    )
    key_blocks = all_keys.reshape(-1, tokens, HEADS, HEAD_DIM)
    value_blocks = all_values.reshape(-1, tokens, HEADS, HEAD_DIM)
    query_heads = queries.reshape(tokens, HEADS, HEAD_DIM)
    memory_open = jnp.broadcast_to(flag_on, (tokens, tokens))
    own_count = seq_index + 1
    key_offsets = lax.iota(jnp.int32, tokens)

    def own_open(block):
        return (block * tokens + key_offsets)[None, :] <= positions[:, None]

    def block_scores(key_block, open_mask):
        raw = (
            jnp.einsum("qhd,khd->hqk", query_heads, key_block, preferred_element_type=jnp.float32)
            * score_scale
        )
        return jnp.where(open_mask[None], raw, masked_score)

    def sweep(step, carry):

        def memory_turn(block, state):
            return step(
                state,
                block,
                memory_key_blocks[block],
                memory_value_blocks[block],
                memory_open,
                False,
            )

        def own_turn(block, state):
            return step(state, block, key_blocks[block], value_blocks[block], own_open(block), True)

        carry = lax.fori_loop(0, memory_blocks, memory_turn, carry)
        return lax.fori_loop(0, own_count, own_turn, carry)

    def max_step(carry, block, key_block, value_block, open_mask, own):
        row_max, row_sum = carry
        scores = block_scores(key_block, open_mask)
        new_max = jnp.maximum(row_max, jnp.max(scores, axis=2))
        row_sum = row_sum * jnp.exp(row_max - new_max) + jnp.sum(
            jnp.exp(scores - new_max[..., None]), axis=2
        )
        return (new_max, row_sum)

    start_max = jnp.full((HEADS, tokens), masked_score, jnp.float32)
    row_max, row_sum = sweep(max_step, (start_max, jnp.zeros((HEADS, tokens), jnp.float32)))
    log_totals = row_max + jnp.log(row_sum)

    def mix_step(total, block, key_block, value_block, open_mask, own):
        weights_low = jnp.exp(block_scores(key_block, open_mask) - log_totals[..., None]).astype(
            jnp.bfloat16
        )
        return total + jnp.einsum(
            "hqk,khd->qhd", weights_low, value_block, preferred_element_type=jnp.float32
        )

    attended = sweep(mix_step, jnp.zeros((tokens, HEADS, HEAD_DIM), jnp.float32))
    attended_low = attended.reshape(tokens, D).astype(jnp.bfloat16)
    residual = inputs + product(attended_low, w_out)
    second_norm, second_inverse = norm_forward(residual, norm2_gain)
    second_low = second_norm.astype(jnp.bfloat16)
    gate_values = product(second_low, w_gate)
    up_values = product(second_low, w_up)
    sigmoid_gate = jax.nn.sigmoid(gate_values)
    activated = gate_values * sigmoid_gate
    hidden_low = (activated * up_values).astype(jnp.bfloat16)
    output = (residual + product(hidden_low, w_down)).astype(jnp.bfloat16)
    upstream = output_grad[0]
    grad_down = product_tn(hidden_low, upstream)
    grad_hidden = product_nt(upstream, w_down)
    grad_gate_low = (
        grad_hidden * up_values * sigmoid_gate * (1.0 + gate_values * (1.0 - sigmoid_gate))
    ).astype(jnp.bfloat16)
    grad_up_low = (grad_hidden * activated).astype(jnp.bfloat16)
    grad_gate = product_tn(second_low, grad_gate_low)
    grad_up = product_tn(second_low, grad_up_low)
    grad_second = product_nt(grad_gate_low, w_gate) + product_nt(grad_up_low, w_up)
    grad_residual, grad_norm2 = norm_backward(residual, second_inverse, norm2_gain, grad_second)
    grad_residual = grad_residual + upstream.astype(jnp.float32)
    residual_low = grad_residual.astype(jnp.bfloat16)
    grad_out = product_tn(attended_low, residual_low)
    grad_attended = product_nt(residual_low, w_out).astype(jnp.bfloat16)
    grad_heads = grad_attended.reshape(tokens, HEADS, HEAD_DIM)

    def probs_pair(key_block, value_block, open_mask):
        probs = jnp.exp(block_scores(key_block, open_mask) - log_totals[..., None])
        dprobs = jnp.einsum(
            "qhd,khd->hqk", grad_heads, value_block, preferred_element_type=jnp.float32
        )
        return (probs, dprobs)

    def delta_step(total, block, key_block, value_block, open_mask, own):
        probs, dprobs = probs_pair(key_block, value_block, open_mask)
        return total + jnp.sum(probs * dprobs, axis=2)

    delta_rows = sweep(delta_step, jnp.zeros((HEADS, tokens), jnp.float32))

    def grad_step(carry, block, key_block, value_block, open_mask, own):
        grad_query, key_terms, value_terms = carry
        probs, dprobs = probs_pair(key_block, value_block, open_mask)
        dscores = (probs * (dprobs - delta_rows[..., None])).astype(jnp.bfloat16)
        grad_query = grad_query + jnp.einsum(
            "hqk,khd->qhd", dscores, key_block, preferred_element_type=jnp.float32
        )
        if own:
            key_part = (
                jnp.einsum("hqk,qhd->khd", dscores, query_heads, preferred_element_type=jnp.float32)
                * score_scale
            )
            value_part = jnp.einsum(
                "hqk,qhd->khd",
                probs.astype(jnp.bfloat16),
                grad_heads,
                preferred_element_type=jnp.float32,
            )
            key_terms = lax.dynamic_update_index_in_dim(key_terms, key_part, block, 0)
            value_terms = lax.dynamic_update_index_in_dim(value_terms, value_part, block, 0)
        return (grad_query, key_terms, value_terms)

    term_shape = key_blocks.shape
    start_grads = (
        jnp.zeros((tokens, HEADS, HEAD_DIM), jnp.float32),
        jnp.zeros(term_shape, jnp.float32),
        jnp.zeros(term_shape, jnp.float32),
    )
    grad_query, key_terms, value_terms = sweep(grad_step, start_grads)
    grad_queries = (grad_query * score_scale).reshape(tokens, D)
    grad_keys, grad_values = (
        lax.psum_scatter(
            key_terms.astype(jnp.bfloat16), "seq", scatter_dimension=0, tiled=True
        ).astype(jnp.float32),
        lax.psum_scatter(
            value_terms.astype(jnp.bfloat16), "seq", scatter_dimension=0, tiled=True
        ).astype(jnp.float32),
    )
    grad_projected = jnp.concatenate(
        [
            rotate(grad_queries, cosine_table, sine_table, -1.0),
            rotate(grad_keys.reshape(tokens, D), cosine_table, sine_table, -1.0),
            grad_values.reshape(tokens, D),
        ],
        axis=1,
    ).astype(jnp.bfloat16)
    grad_qkv = product_tn(first_low, grad_projected)
    grad_first = product_nt(grad_projected, w_qkv)
    grad_inputs, grad_norm1 = norm_backward(inputs, first_inverse, norm1_gain, grad_first)
    input_grad = (grad_inputs + grad_residual)[None]
    shares = (
        lax.psum_scatter(
            grad_norm1.astype(jnp.bfloat16), "seq", scatter_dimension=0, tiled=True
        ).astype(jnp.float32),
        lax.psum_scatter(
            grad_norm2.astype(jnp.bfloat16), "seq", scatter_dimension=0, tiled=True
        ).astype(jnp.float32),
        lax.psum_scatter(
            grad_qkv.astype(jnp.bfloat16), "seq", scatter_dimension=0, tiled=True
        ).astype(jnp.float32),
        lax.psum_scatter(
            grad_out.astype(jnp.bfloat16), "seq", scatter_dimension=0, tiled=True
        ).astype(jnp.float32),
        lax.psum_scatter(
            grad_gate.astype(jnp.bfloat16), "seq", scatter_dimension=0, tiled=True
        ).astype(jnp.float32),
        lax.psum_scatter(
            grad_up.astype(jnp.bfloat16), "seq", scatter_dimension=0, tiled=True
        ).astype(jnp.float32),
        lax.psum_scatter(
            grad_down.astype(jnp.bfloat16), "seq", scatter_dimension=0, tiled=True
        ).astype(jnp.float32),
    )
    totals = (
        lax.psum(shares[0].astype(jnp.bfloat16), "seg").astype(jnp.float32),
        lax.psum(shares[1].astype(jnp.bfloat16), "seg").astype(jnp.float32),
        lax.psum(shares[2].astype(jnp.bfloat16), "seg").astype(jnp.float32),
        lax.psum(shares[3].astype(jnp.bfloat16), "seg").astype(jnp.float32),
        lax.psum(shares[4].astype(jnp.bfloat16), "seg").astype(jnp.float32),
        lax.psum(shares[5].astype(jnp.bfloat16), "seg").astype(jnp.float32),
        lax.psum(shares[6].astype(jnp.bfloat16), "seg").astype(jnp.float32),
    )
    return (
        output[None],
        input_grad,
        totals[0],
        totals[1],
        totals[2],
        totals[3],
        totals[4],
        totals[5],
        totals[6],
    )


VMEM_BYTES = 60 * 1024 * 1024
VMEM_MOST = 67043328
LN2 = math.log(2.0)
SCORE_SCALE = HEAD_DIM ** (-0.5)


def lane_fold(op, tile, running):
    for column in range(tile.shape[1] // HEAD_DIM):
        piece = tile[:, column * HEAD_DIM : (column + 1) * HEAD_DIM]
        running = piece if running is None else op(running, piece)
    return running


def causal(scores):
    rows = lax.broadcasted_iota(jnp.int32, scores.shape, 0)
    columns = lax.broadcasted_iota(jnp.int32, scores.shape, 1)
    return jnp.where(columns <= rows, scores, masked_score)


def attend(query, pairs, diagonal, carried, closed=0.0):
    every, lane_max = [], None
    for index, (keys, _) in enumerate(pairs):
        scores = product_nt(query, keys)
        if diagonal and index == len(pairs) - 1:
            scores = causal(scores)
        lane_max = lane_fold(jnp.maximum, scores, lane_max)
        every.append(scores)
    row_max = jnp.max(lane_max, axis=1, keepdims=True) - closed
    if carried is not None:
        row_max = jnp.maximum(row_max, carried[0])
    shift = row_max + closed
    lane_sum, mixed = None, None
    for scores, (_, values) in zip(every, pairs):
        probs = jnp.exp2(scores - shift)
        lane_sum = lane_fold(jnp.add, probs, lane_sum)
        part = product(probs.astype(jnp.bfloat16), values)
        mixed = part if mixed is None else mixed + part
    row_sum = jnp.sum(lane_sum, axis=1, keepdims=True)
    if carried is not None:
        shrink = jnp.exp2(carried[0] - row_max)
        row_sum = carried[1] * shrink + row_sum
        mixed = carried[2] * shrink + mixed
    return row_max, row_sum, mixed


def turn_block(matrix, cosine, sine):
    return matrix * cosine + pltpu.roll(matrix, HEAD_DIM // 2, 1) * sine


def turn_factors(both):
    swapped = pltpu.roll(both, HEAD_DIM // 2, 1)
    first = lax.broadcasted_iota(jnp.int32, both.shape, 1) < HEAD_DIM // 2
    return jnp.where(first, both, swapped), jnp.where(first, swapped, -both)


def turn_table(length, step=64):
    frequency = rotary_base ** (-2.0 * np.arange(HEAD_DIM // 2) / HEAD_DIM)
    coarse = np.arange(length // step)[:, None] * step * frequency
    fine = np.arange(step)[:, None] * frequency

    def pair(former, latter):
        return jnp.asarray(np.concatenate([former, latter], axis=1), jnp.float32)

    table = (
        pair(np.cos(coarse), np.sin(coarse))[:, None, :] * pair(np.cos(fine), np.cos(fine))[None]
        + pair(-np.sin(coarse), np.cos(coarse))[:, None, :] * pair(np.sin(fine), np.sin(fine))[None]
    )
    return table.reshape(length, HEAD_DIM)


LINK_RATE = {"core": 300e3, "x": 49e3, "y": 49e3, "z": 49e3}


class Place:
    def __init__(self):
        seg, seq = lax.axis_index("seg"), lax.axis_index("seq")
        self.core, self.z = lax.rem(seg, 2), lax.div(seg, 2)
        self.x, self.y = lax.rem(seq, 2), lax.div(seq, 2)
        odd = lax.rem(self.z, 2)
        self.inner = jnp.logical_or(self.z == 1, self.z == 2)
        self.outer = jnp.logical_not(self.inner)
        self.peer = {
            "core": (seg + 1 - 2 * self.core, seq),
            "x": (seg, seq + 1 - 2 * self.x),
            "y": (seg, seq + 2 - 4 * self.y),
            "xy": (seg, 3 - seq),
            "pair": (seg + 2 - 4 * odd, seq),
            "middle": (seg - 2 + 4 * odd, seq),
        }

    def greet(self, names):
        barrier = pltpu.get_barrier_semaphore()

        def hail(name):
            pl.semaphore_signal(
                barrier, inc=1, device_id=self.peer[name], device_id_type=pl.DeviceIdType.MESH
            )

        for name in names:
            hail(name)

        @pl.when(self.inner)
        def _():
            hail("middle")

        pl.semaphore_wait(barrier, len(names) + self.inner.astype(jnp.int32))


def add_into(total, addend, step=16):
    def turn(index, carry):
        rows = pl.ds(pl.multiple_of(index * step, step), step)
        total[rows, :] = total[rows, :] + addend[rows, :]
        return carry

    lax.fori_loop(0, total.shape[0] // step, turn, 0)


def add_to(result, former, latter, step=16):
    def turn(index, carry):
        rows = pl.ds(pl.multiple_of(index * step, step), step)
        result[rows, :] = former[rows, :] + latter[rows, :]
        return carry

    lax.fori_loop(0, result.shape[0] // step, turn, 0)


def weight_copies(whole, part, seq, semaphores, first):
    width = part.shape[1] // 3
    depth = whole.shape[1] // 3
    return [
        pltpu.make_async_copy(
            whole.at[:, pl.ds(pl.multiple_of(kind * depth + seq * width, HEAD_DIM), width)],
            part.at[:, pl.ds(kind * width, width)],
            semaphores.at[first + kind],
        )
        for kind in range(3)
    ]


class Chunk:
    def __init__(self, term, offset, rows, columns, gather=False):
        self.term, self.offset, self.rows, self.columns = term, offset, rows, columns
        self.gather = gather

    def scratch(self):
        rows, columns, half = self.rows, self.columns, self.columns // 2
        low = jnp.bfloat16
        four = pltpu.VMEM((2, 2, rows, columns), low)
        one = four if self.gather else pltpu.VMEM((rows, columns), low)
        last = pltpu.VMEM((rows, 4 * columns), low) if self.gather else one
        if self.gather:
            middle = [four]
        else:
            middle = [
                pltpu.VMEM((2, rows, half), low),
                pltpu.VMEM((2, rows, half), low),
                pltpu.VMEM((rows, half), low),
                pltpu.VMEM((rows, half), low),
            ]
        ends = [one, one, last] if self.gather else [one, one]
        return [four, four] + middle + ends + [
            pltpu.SemaphoreType.DMA((9,)),
            pltpu.SemaphoreType.DMA((9,)),
            pltpu.SemaphoreType.DMA((3,)),
        ]

    def bind(self, place, source, result, refs):
        self.place, self.source, self.result = place, source, result
        self.mine, self.core_in = refs[0], refs[1]
        ends = 3 if self.gather else 2
        self.middle = refs[2 : -3 - ends]
        self.z_last, self.z_second = refs[-4], refs[-5]
        self.z_first = refs[-6] if self.gather else self.z_last
        self.sent, self.received, self.local = refs[-3:]

    def remote(self, slot, source, target, peer):
        return pltpu.make_async_remote_copy(
            src_ref=source,
            dst_ref=target,
            send_sem=self.sent.at[slot],
            recv_sem=self.received.at[slot],
            device_id=self.place.peer[peer],
            device_id_type=pl.DeviceIdType.MESH,
        )

    def core_copy(self):
        rows = pl.ds(self.offset, self.rows)
        return self.remote(
            0, self.source.at[:, :, 1 - self.place.core, rows, :], self.core_in, "core"
        )

    def load(self):
        rows = pl.ds(self.offset, self.rows)
        return pltpu.make_async_copy(
            self.source.at[:, :, self.place.core, rows, :], self.mine, self.local.at[0]
        )

    def halves(self):
        half = self.columns // 2
        return pl.ds(0, half), pl.ds(half, half)

    def wide_copies(self):
        p, (left, right) = self.place, self.halves()
        if self.gather:
            return [
                self.remote(1, self.mine.at[p.y, 1 - p.x], self.middle[0].at[p.y, p.x], "x"),
                self.remote(2, self.mine.at[1 - p.y, p.x], self.middle[0].at[p.y, p.x], "y"),
                self.remote(3, self.mine.at[1 - p.y, 1 - p.x], self.middle[0].at[p.y, p.x], "xy"),
            ]
        return [
            self.remote(1, self.mine.at[:, 1 - p.x, :, left], self.middle[0], "x"),
            self.remote(2, self.mine.at[1 - p.y, :, :, right], self.middle[1], "y"),
        ]

    def narrow_copies(self):
        p, (left, right) = self.place, self.halves()
        return [
            self.remote(3, self.mine.at[1 - p.y, p.x, :, left], self.middle[2], "y"),
            self.remote(4, self.mine.at[p.y, 1 - p.x, :, right], self.middle[3], "x"),
        ]

    def summed(self):
        return self.middle[0] if self.gather else self.mine.at[self.place.y, self.place.x]

    def pair_copy(self):
        return self.remote(5, self.summed(), self.z_first, "pair")

    def middle_copy(self):
        return self.remote(6, self.summed(), self.z_second, "middle")

    def last_copy(self):
        return self.remote(7, self.z_last, self.z_last, "pair")

    def out_copies(self):
        rows = pl.ds(self.offset, self.rows)
        core = self.place.core
        target = self.result.at[core, rows, :]
        return (
            self.remote(8, self.z_last, target, "core"),
            pltpu.make_async_copy(self.z_last, target, self.local.at[1]),
        )

    def parts(self, ref):
        if self.gather:
            return [ref.at[a, b] for a in range(2) for b in range(2)]
        return [ref]

    def lay_out(self):
        part = self.columns // 3
        for owner in range(4):
            for kind in range(3):
                lanes = pl.ds(kind * part, part)
                former = self.middle[0].at[owner // 2, owner % 2, :, lanes]
                latter = self.z_second.at[owner // 2, owner % 2, :, lanes]
                add_to(self.z_last.at[:, pl.ds((4 * kind + owner) * part, part)], former, latter)

    def stage_start(self):
        self.core_copy().start()
        self.load().start()

    def stage_core(self):
        self.core_copy().wait_recv()
        self.load().wait()
        for a in range(2):
            for b in range(2):
                add_into(self.mine.at[a, b], self.core_in.at[a, b])
        for copy in self.wide_copies():
            copy.start()

    def stage_wide(self):
        p, (left, right) = self.place, self.halves()
        if self.gather:
            stay = pltpu.make_async_copy(
                self.mine.at[p.y, p.x], self.middle[0].at[p.y, p.x], self.local.at[2]
            )
            stay.start()
            for copy in self.wide_copies():
                copy.wait_recv()
            stay.wait()
            self.z_start()
            return
        for copy in self.wide_copies():
            copy.wait_recv()
        for a in range(2):
            add_into(self.mine.at[a, p.x, :, left], self.middle[0].at[a])
            add_into(self.mine.at[p.y, a, :, right], self.middle[1].at[a])
        for copy in self.narrow_copies():
            copy.start()

    def stage_narrow(self):
        p, (left, right) = self.place, self.halves()
        for copy in self.narrow_copies():
            copy.wait_recv()
        add_into(self.mine.at[p.y, p.x, :, left], self.middle[2])
        add_into(self.mine.at[p.y, p.x, :, right], self.middle[3])
        self.z_start()

    def z_start(self):
        @pl.when(self.place.outer)
        def _():
            self.pair_copy().start()

    def stage_pair(self):
        @pl.when(self.place.inner)
        def _():
            self.pair_copy().wait_recv()
            for total, addend in zip(self.parts(self.summed()), self.parts(self.z_first)):
                add_into(total, addend)
            self.middle_copy().start()

    def stage_middle(self):
        @pl.when(self.place.inner)
        def _():
            self.middle_copy().wait_recv()
            if self.gather:
                self.lay_out()
            else:
                add_to(self.z_last, self.summed(), self.z_second)
            self.last_copy().start()
            for copy in self.out_copies():
                copy.start()

    def stage_last(self):
        @pl.when(self.place.outer)
        def _():
            self.last_copy().wait_recv()
            for copy in self.out_copies():
                copy.start()

    def stage_end(self):
        remote_out, local_out = self.out_copies()
        remote_out.wait()
        local_out.wait()
        self.core_copy().wait_send()
        for copy in self.wide_copies():
            copy.wait_send()
        if not self.gather:
            for copy in self.narrow_copies():
                copy.wait_send()

        @pl.when(self.place.outer)
        def _():
            self.pair_copy().wait_send()

        @pl.when(self.place.inner)
        def _():
            self.middle_copy().wait_send()
            self.last_copy().wait_send()

    def plan(self):
        piece = 2 * self.rows * self.columns
        if self.gather:
            return [
                (self.stage_core, [("x", 1.5 * piece), ("y", 1.5 * piece)]),
                (self.stage_wide, [("z", 4 * piece)]),
                (self.stage_pair, [("z", 4 * piece)]),
                (self.stage_middle, [("z", 4 * piece)]),
                (self.stage_last, [("core", 4 * piece)]),
                (self.stage_end, []),
            ]
        return [
            (self.stage_core, [("x", piece), ("y", piece)]),
            (self.stage_wide, [("x", piece / 2), ("y", piece / 2)]),
            (self.stage_narrow, [("z1", piece)]),
            (self.stage_pair, [("z2", piece)]),
            (self.stage_middle, [("z3", piece)]),
            (self.stage_last, [("core", piece)]),
            (self.stage_end, []),
        ]

    def opening(self):
        return [("core", 8 * self.rows * self.columns)]


class RowChunk:
    def __init__(self, term, offset, rows, columns):
        self.term, self.offset, self.rows, self.columns = term, offset, rows, columns

    def scratch(self):
        rows, columns, half = self.rows, self.columns, self.columns // 2
        low = jnp.bfloat16
        return [
            pltpu.VMEM((2, rows, half), low),
            pltpu.VMEM((2, rows, half), low),
            pltpu.VMEM((rows, half), low),
            pltpu.VMEM((rows, half), low),
            pltpu.SemaphoreType.DMA((6,)),
            pltpu.SemaphoreType.DMA((6,)),
            pltpu.SemaphoreType.DMA((1,)),
        ]

    def bind(self, place, source, result, refs):
        self.place, self.result = place, result
        self.blocks = source
        self.middle = refs[:4]
        self.sent, self.received, self.local = refs[4:]

    def mine(self, y, x, lanes):
        return self.blocks.at[2 * y + x, pl.ds(self.offset, self.rows), lanes]

    remote = Chunk.remote
    halves = Chunk.halves

    def wide_copies(self):
        p, (left, right) = self.place, self.halves()
        copies = []
        for a in range(2):
            copies.append(
                self.remote(a, self.mine(a, 1 - p.x, left), self.middle[0].at[a], "x")
            )
            copies.append(
                self.remote(2 + a, self.mine(1 - p.y, a, right), self.middle[1].at[a], "y")
            )
        return copies

    def narrow_copies(self):
        p, (left, right) = self.place, self.halves()
        return [
            self.remote(4, self.mine(1 - p.y, p.x, left), self.middle[2], "y"),
            self.remote(5, self.mine(p.y, 1 - p.x, right), self.middle[3], "x"),
        ]

    def out_copy(self):
        p = self.place
        whole = pl.ds(0, self.columns)
        return pltpu.make_async_copy(
            self.mine(p.y, p.x, whole),
            self.result.at[pl.ds(self.offset, self.rows), :],
            self.local.at[0],
        )

    def stage_start(self):
        for copy in self.wide_copies():
            copy.start()

    def stage_wide(self):
        p, (left, right) = self.place, self.halves()
        for copy in self.wide_copies():
            copy.wait_recv()
        for a in range(2):
            add_into(self.mine(a, p.x, left), self.middle[0].at[a])
            add_into(self.mine(p.y, a, right), self.middle[1].at[a])
        for copy in self.narrow_copies():
            copy.start()

    def stage_narrow(self):
        p, (left, right) = self.place, self.halves()
        for copy in self.narrow_copies():
            copy.wait_recv()
        add_into(self.mine(p.y, p.x, left), self.middle[2])
        add_into(self.mine(p.y, p.x, right), self.middle[3])
        self.out_copy().start()

    def stage_end(self):
        self.out_copy().wait()
        for copy in self.wide_copies() + self.narrow_copies():
            copy.wait_send()

    def plan(self):
        piece = 2 * self.rows * self.columns
        return [
            (self.stage_wide, [("x", piece / 2), ("y", piece / 2)]),
            (self.stage_narrow, [("core", 0.0)]),
            (self.stage_end, []),
        ]

    def opening(self):
        piece = 2 * self.rows * self.columns
        return [("x", piece), ("y", piece)]


class Steps:
    def __init__(self, start):
        self.now, self.free, self.waiting = start, {}, []

    def send(self, transfers):
        ends = [self.now]
        for link, size in transfers:
            start = max(self.now, self.free.get(link, 0.0))
            self.free[link] = start + size / LINK_RATE.get(link, LINK_RATE["z"])
            ends.append(self.free[link] + 2.0)
        return max(ends)

    def open(self, chunks):
        for chunk in chunks:
            self.waiting.append((self.send(chunk.opening()), len(self.waiting), chunk, 0))

    def due(self, everything=False):
        stages = []
        while self.waiting:
            self.waiting.sort(key=lambda entry: entry[:2])
            when, number, chunk, index = self.waiting[0]
            if when > self.now and not everything:
                break
            self.waiting.pop(0)
            self.now = max(self.now, when) + 0.4
            stage, transfers = chunk.plan()[index]
            stages.append(stage)
            if index + 1 < len(chunk.plan()):
                self.waiting.append((self.send(transfers), number, chunk, index + 1))
        return stages

    def spend(self, duration):
        self.now += duration


def back_kernel(
    chunks,
    first_chunks,
    heads,
    flag_ref,
    g_ref,
    q_hbm,
    k_hbm,
    v_hbm,
    memory_hbm,
    every_hbm,
    down_ref,
    gate_ref,
    up_ref,
    out_ref,
    w_hbm,
    mix_ref,
    log_ref,
    table_ref,
    sum_down,
    sum_gate,
    sum_up,
    sum_out,
    sum_qkv,
    sum_first,
    w_ref,
    q,
    k,
    v,
    upstream,
    shared,
    dk,
    dv,
    total,
    delta,
    part_qkv,
    trade_sent,
    trade_received,
    local,
    *refs,
):
    place = Place()
    seq = lax.axis_index("seq")
    tokens = g_ref.shape[0]
    width = heads * HEAD_DIM
    used = 0
    sources = [down_ref, gate_ref, up_ref, out_ref, part_qkv, shared]
    results = [sum_down, sum_gate, sum_up, sum_out, sum_qkv, sum_first]
    for chunk in chunks + first_chunks:
        count = len(chunk.scratch())
        chunk.bind(place, sources[chunk.term], results[chunk.term], refs[used : used + count])
        used += count

    def owner_at(turn):
        low, high = lax.rem(turn, 2), lax.div(turn, 2)
        x = place.x + low - 2 * place.x * low
        y = place.y + high - 2 * place.y * high
        return 2 * y + x

    def columns(owner):
        return pl.ds(pl.multiple_of(owner * width, HEAD_DIM), width)

    def span(block):
        return pl.ds(pl.multiple_of(block * tokens, tokens), tokens)

    def lanes(head):
        return pl.ds(pl.multiple_of(head * HEAD_DIM, HEAD_DIM), HEAD_DIM)

    across = {"x": seq + 1 - 2 * place.x, "y": seq + 2 - 4 * place.y, "xy": 3 - seq}
    trades = [
        pltpu.make_async_remote_copy(
            src_ref=g_ref.at[:, columns(across[peer])],
            dst_ref=upstream.at[span(seq), :],
            send_sem=trade_sent.at[slot],
            recv_sem=trade_received.at[slot],
            device_id=place.peer[peer],
            device_id_type=pl.DeviceIdType.MESH,
        )
        for slot, peer in enumerate(("x", "y", "xy"))
    ]
    loads = [
        pltpu.make_async_copy(g_ref.at[:, columns(seq)], upstream.at[span(seq), :], local.at[0]),
        pltpu.make_async_copy(q_hbm, q, local.at[1]),
        pltpu.make_async_copy(k_hbm, k, local.at[2]),
        pltpu.make_async_copy(v_hbm, v, local.at[3]),
        pltpu.make_async_copy(memory_hbm, shared, local.at[4]),
    ] + weight_copies(w_hbm, w_ref, seq, local, 6)
    load_every = pltpu.make_async_copy(every_hbm, shared, local.at[5])

    def turn_back(matrix, rows):
        cosine, sine = turn_factors(table_ref[rows, :])
        return turn_block(matrix, cosine, sine).astype(jnp.bfloat16)

    def memory_part(head, block):
        rows, mine = span(block), lanes(head)
        query, grads = q[rows, mine], upstream[rows, mine]
        row_delta = jnp.sum(
            grads.astype(jnp.float32) * mix_ref[rows, mine].astype(jnp.float32), axis=1, keepdims=True
        )
        delta[...] = jnp.broadcast_to(row_delta, delta.shape)
        closed = (1 - flag_ref[lax.axis_index("seg")]).astype(jnp.float32) * 1e30
        log_total = log_ref[rows, mine][:, :1] + closed
        result = jnp.zeros(total.shape, jnp.float32)
        for slot in range(shared.shape[0]):
            for run in range(2):

                def tile(kind):
                    start = pl.multiple_of((2 * run + kind) * width + head * HEAD_DIM, HEAD_DIM)
                    return shared[slot, :, pl.ds(start, HEAD_DIM)]

                keys, values = tile(0), tile(1)
                probs = jnp.exp2(product_nt(query, keys) - log_total)
                dscores = probs * (product_nt(grads, values) - row_delta)
                result = result + product(dscores.astype(jnp.bfloat16), keys)
        total[...] = result

    def own_part(head, block):
        rows, mine = span(block), lanes(head)
        query, grads = q[rows, mine], upstream[rows, mine]
        log_total, row_delta = log_ref[rows, mine][:, :1], delta[:, :1]

        def turn(other, result, diagonal):
            keys = k[span(other), mine]
            scores = product_nt(query, keys)
            if diagonal:
                scores = causal(scores)
            probs = jnp.exp2(scores - log_total)
            dscores = (probs * (product_nt(grads, v[span(other), mine]) - row_delta)).astype(
                jnp.bfloat16
            )
            dv[span(other), :] += product_tn(probs.astype(jnp.bfloat16), grads)
            dk[span(other), :] += product_tn(dscores, query)
            return result + product(dscores, keys)

        result = turn(block, total[...], True)
        result = lax.fori_loop(0, block, lambda other, r: turn(other, r, False), result)
        q[rows, mine] = turn_back(result * SCORE_SCALE, rows)

    def close_head(head):
        mine = lanes(head)

        def turn(block, carry):
            rows = span(block)
            k[rows, mine] = turn_back(dk[rows, :] * LN2, rows)
            v[rows, mine] = dv[rows, :].astype(jnp.bfloat16)
            return carry

        lax.fori_loop(0, 4, turn, 0)

    def multiply_qkv(index, carry):
        cut = pl.ds(pl.multiple_of(index * width, HEAD_DIM), width)
        for kind, part in enumerate((q, k, v)):
            term = None
            for block in range(shared.shape[0]):
                product_part = product_tn(shared[block, :, cut], part[block * tokens : (block + 1) * tokens, :])
                term = product_part if term is None else term + product_part
            term = term.astype(jnp.bfloat16)
            half = term.shape[0] // 2
            place_y, place_x = lax.div(index, 2), lax.rem(index, 2)
            for core in range(2):
                part_qkv[place_y, place_x, core, :, kind * width : (kind + 1) * width] = term[
                    core * half : (core + 1) * half, :
                ]
        return carry

    def multiply_first(block, carry):
        rows = span(block)
        result = None
        for kind, part in enumerate((q, k, v)):
            term = product_nt(part[rows, :], w_ref[:, kind * width : (kind + 1) * width])
            result = term if result is None else result + term
        shared[block] = result.astype(jnp.bfloat16)
        return carry

    place.greet(("core", "x", "y", "xy", "pair"))
    for copy in trades + loads:
        copy.start()
    for chunk in chunks:
        chunk.stage_start()
    steps = Steps(3.0)
    steps.free.update(x=11.0, y=11.0)
    steps.open(chunks)
    for copy in loads:
        copy.wait()
    slots = []
    for unit in range(2 * 4 * heads):
        slots.append(steps.due())
        steps.spend(4.3 if unit % 2 == 0 else 3.2)

    def run(stages):
        for stage in stages:
            stage()

    def unit(index, carry):
        head, turn = lax.div(index, 4), lax.rem(index, 4)
        block = owner_at(turn)
        for number in range(4 * heads):
            if slots[2 * number] or number in (1, 2, 3):

                @pl.when(index == number)
                def _(number=number):
                    run(slots[2 * number])
                    if number in (1, 2, 3):
                        trades[number - 1].wait_recv()

        @pl.when(turn == 0)
        def _():
            dk[...] = jnp.zeros_like(dk)
            dv[...] = jnp.zeros_like(dv)

        memory_part(head, block)
        for number in range(4 * heads):
            if slots[2 * number + 1]:

                @pl.when(index == number)
                def _(number=number):
                    run(slots[2 * number + 1])

        own_part(head, block)

        @pl.when(turn == 3)
        def _():
            close_head(head)

        return carry

    lax.fori_loop(0, 4 * heads, unit, 0)
    load_every.start()
    run(steps.due())
    load_every.wait()
    lax.fori_loop(0, 4, multiply_qkv, 0)
    steps.spend(8.0)
    qkv_chunks = [chunk for chunk in first_chunks if chunk.term == 4]
    row_chunks = [chunk for chunk in first_chunks if chunk.term == 5]
    for chunk in qkv_chunks:
        chunk.stage_start()
    steps.open(qkv_chunks)
    run(steps.due())
    lax.fori_loop(0, 4, multiply_first, 0)
    steps.spend(6.0)
    for chunk in row_chunks:
        chunk.stage_start()
    steps.open(row_chunks)
    run(steps.due(True))
    for copy in trades:
        copy.wait_send()


def back(
    flags, grads, queries, keys, values, memory, every, terms, w_qkv, attended, log_totals, table, collective_id
):
    tokens, depth = grads.shape
    length, width = queries.shape
    low = jnp.bfloat16
    chunks, shapes = [], []
    for index, term in enumerate(terms):
        rows, columns = term.shape[0] // 8, term.shape[1]
        parts = 2 if rows % 32 == 0 and index < 3 else 1
        chunks += [Chunk(index, n * rows // parts, rows // parts, columns) for n in range(parts)]
        shapes.append((2, rows, columns))
    rows = depth // 8
    first_chunks = [Chunk(4, n * rows // 2, rows // 2, 3 * width, True) for n in range(2)]
    first_chunks += [RowChunk(5, n * tokens // 4, tokens // 4, depth) for n in range(4)]
    shapes += [(2, rows, 12 * width), (tokens, depth)]
    anywhere = pl.BlockSpec(memory_space=pl.ANY)
    inside = pl.BlockSpec(memory_space=pltpu.VMEM)
    scratch = (
        [pltpu.VMEM((depth, 3 * width), low)]
        + [pltpu.VMEM((length, width), low)] * 4
        + [pltpu.VMEM((4, tokens, depth), low)]
        + [pltpu.VMEM((length, HEAD_DIM), jnp.float32)] * 2
        + [pltpu.VMEM((tokens, HEAD_DIM), jnp.float32)] * 2
        + [pltpu.VMEM((2, 2, 2, rows, 3 * width), low)]
        + [pltpu.SemaphoreType.DMA((3,))] * 2
        + [pltpu.SemaphoreType.DMA((9,))]
    )
    return pl.pallas_call(
        functools.partial(back_kernel, chunks, first_chunks, width // HEAD_DIM),
        in_specs=[pl.BlockSpec(memory_space=pltpu.SMEM)] + [anywhere] * 11 + [inside] * 3,
        out_specs=[anywhere] * len(shapes),
        out_shape=[jax.ShapeDtypeStruct(shape, low) for shape in shapes],
        scratch_shapes=scratch + [ref for chunk in chunks + first_chunks for ref in chunk.scratch()],
        compiler_params=pltpu.CompilerParams(
            collective_id=collective_id, has_side_effects=True, vmem_limit_bytes=VMEM_MOST
        ),
        name="back",
    )(
        flags,
        grads,
        queries,
        keys,
        values,
        memory,
        every,
        *[term.reshape((2, 2, 2, term.shape[0] // 8, term.shape[1])) for term in terms],
        w_qkv,
        attended,
        log_totals,
        table,
    )


class Line:
    def __init__(self, place, seg, memory, spans, refs):
        self.place, self.seg, self.memory, self.spans = place, seg, memory, spans
        self.runs = len(spans)
        self.sent, self.received, self.core_sent, self.core_received = refs

    def span(self, run):
        return self.spans[run]

    def there(self, way, step):
        return self.place.z >= step if way == 0 else self.place.z + step <= 3

    def goes(self, way, step):
        has = self.there(way, step - 1)
        return jnp.logical_and(has, self.place.z <= 2 if way == 0 else self.place.z >= 1)

    def index(self, way, step):
        return self.seg - 2 * step if way == 0 else self.seg + 2 * step

    def hop(self, way, step, run):
        name = self.index(way, step - 1)
        target = self.memory.at[name, self.span(run), :]
        slot = (way * 3 + step - 1) * self.runs + run
        seg, seq = lax.axis_index("seg"), lax.axis_index("seq")
        return pltpu.make_async_remote_copy(
            src_ref=target,
            dst_ref=target,
            send_sem=self.sent.at[slot],
            recv_sem=self.received.at[slot],
            device_id=(seg + 2 - 4 * way, seq),
            device_id_type=pl.DeviceIdType.MESH,
        )

    def arrival(self, way, step, run):
        target = self.memory.at[self.index(way, step), self.span(run), :]
        slot = (way * 3 + step - 1) * self.runs + run
        return pltpu.make_async_remote_copy(
            src_ref=target,
            dst_ref=target,
            send_sem=self.sent.at[slot],
            recv_sem=self.received.at[slot],
            device_id=self.place.peer["core"],
            device_id_type=pl.DeviceIdType.MESH,
        )

    def share(self, way, step, run):
        name = self.index(way, step)
        target = self.memory.at[name, self.span(run), :]
        slot = (way * 3 + step) * self.runs + run
        return pltpu.make_async_remote_copy(
            src_ref=target,
            dst_ref=target,
            send_sem=self.core_sent.at[slot],
            recv_sem=self.core_received.at[slot],
            device_id=self.place.peer["core"],
            device_id_type=pl.DeviceIdType.MESH,
        )

    def start(self, run):
        for way in range(2):

            @pl.when(self.goes(way, 1))
            def _(way=way):
                self.hop(way, 1, run).start()

        self.share(0, 0, run).start()

    def advance(self, step, run):
        for way in range(2):

            @pl.when(self.there(way, step))
            def _(way=way):
                self.arrival(way, step, run).wait_recv()

            if step < 3:

                @pl.when(self.goes(way, step + 1))
                def _(way=way):
                    self.hop(way, step + 1, run).start()

            @pl.when(self.there(way, step))
            def _(way=way):
                self.share(way, step, run).start()

    def finish(self):
        for run in range(self.runs):
            self.share(0, 0, run).wait()
            for way in range(2):
                for step in range(1, 4):

                    @pl.when(self.there(way, step))
                    def _(way=way, step=step, run=run):
                        self.share(way, step, run).wait()

                    @pl.when(self.goes(way, step))
                    def _(way=way, step=step, run=run):
                        self.hop(way, step, run).wait_send()


def front_kernel(
    heads,
    flag_ref,
    source_ref,
    x_ref,
    mem_k_ref,
    mem_v_ref,
    w_hbm,
    table_ref,
    every_ref,
    chosen_ref,
    attended_ref,
    q_ref,
    k_ref,
    v_ref,
    low_ref,
    log_ref,
    w_ref,
    rows,
    memory,
    listed,
    mix_ref,
    max_ref,
    sum_ref,
    trade_sent,
    trade_received,
    rows_sent,
    rows_received,
    line_sent,
    line_received,
    core_sent,
    core_received,
    back_sent,
    back_received,
    local,
):
    place = Place()
    seg, seq = lax.axis_index("seg"), lax.axis_index("seq")
    width = heads * HEAD_DIM
    count = mem_k_ref.shape[0]
    tokens, depth = x_ref.shape
    across = {"x": seq + 1 - 2 * place.x, "y": seq + 2 - 4 * place.y, "xy": 3 - seq}

    def remote(source, target, sent, received, slot, peer):
        return pltpu.make_async_remote_copy(
            src_ref=source,
            dst_ref=target,
            send_sem=sent.at[slot],
            recv_sem=received.at[slot],
            device_id=place.peer[peer],
            device_id_type=pl.DeviceIdType.MESH,
        )

    def columns(owner, start=0):
        return pl.ds(pl.multiple_of(start + owner * width, HEAD_DIM), width)

    def seat(owner):
        return pl.ds(pl.multiple_of(owner * count, 16), count)

    def owner_at(turn):
        low, high = lax.rem(turn, 2), lax.div(turn, 2)
        x = place.x + low - 2 * place.x * low
        y = place.y + high - 2 * place.y * high
        return 2 * y + x

    def block_rows(block):
        return pl.ds(pl.multiple_of(block * tokens, 16), tokens)

    peers = ("x", "y", "xy")
    trades = []
    for number, peer in enumerate(peers):
        for kind, source in enumerate((mem_k_ref, mem_v_ref)):
            lanes = pl.ds(kind * width, width)
            trades.append(
                remote(
                    source.at[:, columns(across[peer])],
                    memory.at[seg, seat(seq), lanes],
                    trade_sent,
                    trade_received,
                    2 * number + kind,
                    peer,
                )
            )
    keeps = [
        pltpu.make_async_copy(
            source.at[:, columns(seq)],
            memory.at[seg, seat(seq), pl.ds(kind * width, width)],
            local.at[kind],
        )
        for kind, source in enumerate((mem_k_ref, mem_v_ref))
    ]
    half = depth // 2
    left, right = pl.ds(0, half), pl.ds(half, half)
    load = pltpu.make_async_copy(x_ref, rows.at[seq], local.at[2])
    loads = weight_copies(w_hbm, w_ref, seq, local, 3)
    direct = [
        remote(x_ref.at[:, left], rows.at[seq, :, left], rows_sent, rows_received, 0, "x"),
        remote(x_ref.at[:, right], rows.at[seq, :, right], rows_sent, rows_received, 1, "y"),
        remote(x_ref.at[:, right], rows.at[seq, :, right], rows_sent, rows_received, 2, "x"),
        remote(x_ref.at[:, left], rows.at[seq, :, left], rows_sent, rows_received, 3, "y"),
    ]
    onward = [
        remote(
            rows.at[across["x"], :, left], rows.at[across["x"], :, left], rows_sent, rows_received, 4, "y"
        ),
        remote(
            rows.at[across["y"], :, right], rows.at[across["y"], :, right], rows_sent, rows_received, 5, "x"
        ),
    ]
    line = Line(
        place,
        seg,
        memory,
        [seat(owner) for owner in (seq, across["x"], across["y"], across["xy"])],
        (line_sent, line_received, core_sent, core_received),
    )
    keep_rows = pltpu.make_async_copy(rows, every_ref, local.at[6])
    run_rows = memory.shape[1] // 2
    keep_chosen = []
    for run in range(2):
        span, lanes = pl.ds(run * run_rows, run_rows), pl.ds(2 * run * width, 2 * width)
        keep_chosen.append(
            pltpu.make_async_copy(memory.at[seg, span, :], chosen_ref.at[0, :, lanes], local.at[7 + run])
        )
        keep_chosen.append(
            pltpu.make_async_copy(
                listed.at[:, span, :],
                chosen_ref.at[pl.ds(1, listed.shape[0]), :, lanes],
                local.at[9 + run],
            )
        )
    returns = [
        remote(
            low_ref.at[block_rows(across[peer]), :],
            attended_ref.at[:, columns(seq)],
            back_sent,
            back_received,
            slot,
            peer,
        )
        for slot, peer in enumerate(peers)
    ]
    keep_attended = pltpu.make_async_copy(
        low_ref.at[block_rows(seq), :], attended_ref.at[:, columns(seq)], local.at[11]
    )

    def project_rows(owner):
        block = rows[owner]
        span = block_rows(owner)
        cosine, sine = turn_factors(table_ref[span, :])
        scale = SCORE_SCALE / LN2
        queries = product(block, w_ref[:, :width])
        keys = product(block, w_ref[:, width : 2 * width])
        for head in range(heads):
            lanes = slice(head * HEAD_DIM, (head + 1) * HEAD_DIM)
            q_ref[span, lanes] = turn_block(
                queries[:, lanes], cosine * scale, sine * (-scale)
            ).astype(jnp.bfloat16)
            k_ref[span, lanes] = turn_block(keys[:, lanes], cosine, -sine).astype(jnp.bfloat16)
        v_ref[span, :] = product(block, w_ref[:, 2 * width :]).astype(jnp.bfloat16)

    def head_lanes(head, start=0):
        return pl.ds(pl.multiple_of(start + head * HEAD_DIM, HEAD_DIM), HEAD_DIM)

    def keep(span, lanes, row_max, row_sum, mixed):
        mix_ref[span, lanes] = mixed
        max_ref[span, lanes] = jnp.broadcast_to(row_max, mixed.shape)
        sum_ref[span, lanes] = jnp.broadcast_to(row_sum, mixed.shape)

    def own_rows(block):
        def turn(head, carry):
            lanes = head_lanes(head)
            span = pl.ds(block * tokens, tokens)
            pairs = [
                (k_ref[pl.ds(n * tokens, tokens), lanes], v_ref[pl.ds(n * tokens, tokens), lanes])
                for n in range(block + 1)
            ]
            keep(span, lanes, *attend(q_ref[span, lanes], pairs, True, None))
            return carry

        lax.fori_loop(0, heads, turn, 0)

    closed = (1 - flag_ref[seg]).astype(jnp.float32) * 1e30

    def carried(span, lanes):
        return max_ref[span, lanes][:, :1], sum_ref[span, lanes][:, :1], mix_ref[span, lanes]

    def own_memory(first, last):
        def turn(index, carry):
            head = lax.rem(index, heads)
            lanes, span = head_lanes(head), block_rows(lax.div(index, heads))
            pair = (memory[seg, :, lanes], memory[seg, :, head_lanes(head, width)])
            keep(span, lanes, *attend(q_ref[span, lanes], [pair], False, carried(span, lanes), closed))
            return carry

        lax.fori_loop(first * heads, last * heads, turn, 0)

    barrier = pltpu.get_barrier_semaphore()

    def hail(device):
        pl.semaphore_signal(barrier, inc=1, device_id=device, device_id_type=pl.DeviceIdType.MESH)

    for copy in keeps + [load] + loads:
        copy.start()
    for peer in ("x", "y", "xy", "core"):
        hail(place.peer[peer])
    below, above = place.z >= 1, place.z <= 2

    @pl.when(below)
    def _():
        hail((seg - 2, seq))

    @pl.when(above)
    def _():
        hail((seg + 2, seq))

    pl.semaphore_wait(barrier, 4 + below.astype(jnp.int32) + above.astype(jnp.int32))

    for copy in trades + direct:
        copy.start()
    for copy in keeps:
        copy.wait()
    line.start(0)
    load.wait()
    for copy in loads:
        copy.wait()
    project_rows(seq)
    for number in range(3):
        for kind in range(2):
            trades[2 * number + kind].wait_recv()
        line.start(number + 1)
        line.advance(1, number)
    direct[0].wait_recv()
    direct[1].wait_recv()
    for copy in onward:
        copy.start()
    line.advance(1, 3)
    line.advance(2, 0)
    direct[2].wait_recv()
    direct[3].wait_recv()
    project_rows(across["x"])
    line.advance(2, 1)
    project_rows(across["y"])
    line.advance(2, 2)
    for copy in onward:
        copy.wait_recv()
    project_rows(3 - seq)
    keep_rows.start()
    line.advance(2, 3)
    own_rows(0)
    own_rows(1)
    line.advance(3, 0)
    own_rows(2)
    line.advance(3, 1)
    own_rows(3)
    line.advance(3, 2)
    own_memory(0, 2)
    line.advance(3, 3)
    own_memory(2, 4)
    line.finish()
    for n in range(listed.shape[0]):
        listed[n] = memory[source_ref[seg, n]]

    def unit(index, carry):
        turn, head = lax.div(index, heads), lax.rem(index, heads)

        @pl.when(index == heads // 2)
        def _():
            for copy in keep_chosen:
                copy.start()

        for number in range(3):

            @pl.when(index == heads * (3 - number))
            def _(number=number):
                returns[number].start()

        lanes, span = head_lanes(head), block_rows(owner_at(3 - turn))
        pairs = [
            (listed[n, :, lanes], listed[n, :, head_lanes(head, width)])
            for n in range(listed.shape[0])
        ]
        row_max, row_sum, mixed = attend(
            q_ref[span, lanes], pairs, False, carried(span, lanes), closed
        )
        low_ref[span, lanes] = (mixed * (1.0 / row_sum)).astype(jnp.bfloat16)
        log_ref[span, lanes] = jnp.broadcast_to(row_max + jnp.log2(row_sum), mixed.shape)
        return carry

    lax.fori_loop(0, 4 * heads, unit, 0)
    keep_attended.start()
    for copy in returns:
        copy.wait()
    for copy in keep_chosen + [keep_rows, keep_attended]:
        copy.wait()
    for copy in trades + direct + onward:
        copy.wait_send()


def front(
    flags, sources, first_low, mem_keys, mem_values, w_qkv, table, seg_size, seq_size, collective_id
):
    tokens, depth = first_low.shape
    length = tokens * seq_size
    width = depth // seq_size
    count = mem_keys.shape[0] * seq_size
    slots = sources.shape[1]
    anywhere = pl.BlockSpec(memory_space=pl.ANY)
    inside = pl.BlockSpec(memory_space=pltpu.VMEM)
    scalars = pl.BlockSpec(memory_space=pltpu.SMEM)
    low = jnp.bfloat16
    shape = jax.ShapeDtypeStruct
    dma = pltpu.SemaphoreType.DMA
    return pl.pallas_call(
        functools.partial(front_kernel, width // HEAD_DIM),
        in_specs=[scalars] * 2 + [anywhere] * 4 + [inside],
        out_specs=[anywhere] * 3 + [inside] * 5,
        out_shape=[
            shape((seq_size, tokens, depth), low),
            shape((slots + 1, count // 2, 4 * width), low),
            shape((tokens, depth), low),
        ]
        + [shape((length, width), low)] * 4
        + [shape((length, width), jnp.float32)],
        scratch_shapes=[
            pltpu.VMEM((depth, 3 * width), low),
            pltpu.VMEM((seq_size, tokens, depth), low),
            pltpu.VMEM((seg_size, count, 2 * width), low),
            pltpu.VMEM((slots, count, 2 * width), low),
        ]
        + [pltpu.VMEM((length, width), jnp.float32)] * 3
        + [dma((6,))] * 4
        + [dma((24,))] * 2
        + [dma((28,))] * 2
        + [dma((3,))] * 2
        + [dma((12,))],
        compiler_params=pltpu.CompilerParams(
            collective_id=collective_id, has_side_effects=True, vmem_limit_bytes=VMEM_BYTES
        ),
        name="front",
    )(flags, sources, first_low, mem_keys, mem_values, w_qkv, table)


def norm_input_grad(values, inverse, norm_gain, upstream):
    weighted = upstream * norm_gain
    inner_mean = jnp.mean(weighted * values, axis=-1, keepdims=True)
    return inverse * weighted - inverse * inverse * inverse * values * inner_mean


def dense_kernel(
    x_ref,
    g_ref,
    attended_ref,
    out_ref,
    gain_ref,
    gate_ref,
    up_ref,
    down_ref,
    output_ref,
    grad_ref,
    grad_attended_ref,
    term_down,
    term_gate,
    term_up,
    term_out,
    residual_ref,
    second,
    second_t,
    total,
    grad_second,
):
    index = pl.program_id(0)
    low = jnp.bfloat16

    @pl.when(index == 0)
    def _():
        residual = x_ref[...].astype(jnp.float32) + product(attended_ref[...], out_ref[...])
        residual_ref[...] = residual
        second_low = norm_forward(residual, gain_ref[...])[0].astype(low)
        second[...] = second_low
        second_t[...] = second_low.T

    gate, up = product(second[...], gate_ref[...]), product(second[...], up_ref[...])
    grad_hidden = product_nt(g_ref[...], down_ref[...])
    sigmoid_gate = jax.nn.sigmoid(gate)
    activated = gate * sigmoid_gate
    hidden = (activated * up).astype(low)
    grad_gate = (grad_hidden * up * sigmoid_gate * (1.0 + gate * (1.0 - sigmoid_gate))).astype(low)
    grad_up = (grad_hidden * activated).astype(low)
    term_down[...] = product_tn(hidden, g_ref[...]).astype(low)
    term_gate[...] = product(second_t[...], grad_gate).astype(low)
    term_up[...] = product(second_t[...], grad_up).astype(low)
    part = product(hidden, down_ref[...])
    grad_part = product_nt(grad_gate, gate_ref[...]) + product_nt(grad_up, up_ref[...])

    @pl.when(index == 0)
    def _():
        total[...] = part
        grad_second[...] = grad_part

    @pl.when(index > 0)
    def _():
        total[...] += part
        grad_second[...] += grad_part

    @pl.when(index == pl.num_programs(0) - 1)
    def _():
        residual = residual_ref[...]
        output_ref[...] = (residual + total[...]).astype(low)
        inverse = lax.rsqrt(jnp.mean(residual * residual, axis=-1, keepdims=True) + epsilon)
        grad = norm_input_grad(residual, inverse, gain_ref[...], grad_second[...])
        grad = grad + g_ref[...].astype(jnp.float32)
        grad_ref[...] = grad
        grad_low = grad.astype(low)
        term_out[...] = product_tn(attended_ref[...], grad_low).astype(low)
        grad_attended_ref[...] = product_nt(grad_low, out_ref[...]).astype(low)


def dense(x, grads, attended, w_out, gain, w_gate, w_up, w_down, tile=256):
    tokens, depth = x.shape
    hidden = w_gate.shape[1]
    tile = math.gcd(tile, hidden)
    low = jnp.bfloat16
    shape = jax.ShapeDtypeStruct

    def whole(rows, columns):
        return pl.BlockSpec((rows, columns), lambda j: (0, 0))

    across = pl.BlockSpec((depth, tile), lambda j: (0, j))
    down = pl.BlockSpec((tile, depth), lambda j: (j, 0))
    activation = whole(tokens, depth)
    return pl.pallas_call(
        dense_kernel,
        grid=(hidden // tile,),
        in_specs=[activation] * 3 + [whole(depth, depth), whole(1, depth), across, across, down],
        out_specs=[activation] * 3 + [down, across, across, whole(depth, depth)],
        out_shape=[
            shape((tokens, depth), low),
            shape((tokens, depth), jnp.float32),
            shape((tokens, depth), low),
            shape((hidden, depth), low),
            shape((depth, hidden), low),
            shape((depth, hidden), low),
            shape((depth, depth), low),
        ],
        scratch_shapes=[
            pltpu.VMEM((tokens, depth), jnp.float32),
            pltpu.VMEM((tokens, depth), low),
            pltpu.VMEM((depth, tokens), low),
            pltpu.VMEM((tokens, depth), jnp.float32),
            pltpu.VMEM((tokens, depth), jnp.float32),
        ],
        compiler_params=pltpu.CompilerParams(vmem_limit_bytes=VMEM_BYTES),
        cost_estimate=pl.CostEstimate(
            flops=16 * tokens * depth * hidden + 6 * tokens * depth * depth,
            transcendentals=tokens * hidden,
            bytes_accessed=12 * depth * hidden + 20 * tokens * depth,
        ),
        name="dense",
    )(x, grads, attended, w_out, gain, w_gate, w_up, w_down)


def tail_kernel(
    down_hbm,
    gate_hbm,
    up_hbm,
    out_hbm,
    qkv_hbm,
    first_hbm,
    x_hbm,
    grad_hbm,
    w_hbm,
    w_gate_hbm,
    w_up_hbm,
    gain1_ref,
    gain2_ref,
    input_out,
    norm1_ref,
    norm2_ref,
    qkv_out,
    out_out,
    gate_out,
    up_out,
    down_out,
    down,
    gate,
    up,
    out,
    qkv,
    first,
    x,
    grad,
    w,
    w_gate,
    w_up,
    input_wide,
    qkv_wide,
    out_wide,
    gate_wide,
    up_wide,
    down_wide,
    dots1,
    dots2,
    loaded,
    stored,
):
    seq = lax.axis_index("seq")
    count = gate.shape[0]
    block = pl.ds(pl.multiple_of(seq * count, count), count)
    pairs = [
        (gate_hbm, gate),
        (w_gate_hbm.at[block, :], w_gate),
        (up_hbm, up),
        (w_up_hbm.at[block, :], w_up),
        (down_hbm, down),
        (out_hbm, out),
        (w_hbm.at[block, :], w),
        (qkv_hbm, qkv),
        (first_hbm, first),
        (x_hbm, x),
        (grad_hbm, grad),
    ]
    loads = [
        pltpu.make_async_copy(source, target, loaded.at[n]) for n, (source, target) in enumerate(pairs)
    ]
    wides = [gate_wide, up_wide, down_wide, out_wide, qkv_wide, input_wide]
    outs = [gate_out, up_out, down_out, out_out, qkv_out, input_out]
    stores = [
        pltpu.make_async_copy(source, target, stored.at[n])
        for n, (source, target) in enumerate(zip(wides, outs))
    ]
    for copy in loads:
        copy.start()

    def by_rows(count, step, body):
        def turn(index, carry):
            body(pl.ds(pl.multiple_of(index * step, step), step))
            return carry

        lax.fori_loop(0, count // step, turn, 0)

    def widen(former, latter):
        def body(rows):
            latter[rows, :] = former[rows, :].astype(jnp.float32)

        by_rows(former.shape[0], 16, body)

    def dot_rows(values, weights):
        return lane_fold(jnp.add, values * weights.astype(jnp.float32), None)

    def gate_body(rows):
        values = gate[rows, :].astype(jnp.float32)
        gate_wide[rows, :] = values
        dots2[rows, :] = dot_rows(values, w_gate[rows, :])

    def up_body(rows):
        values = up[rows, :].astype(jnp.float32)
        up_wide[rows, :] = values
        dots2[rows, :] += dot_rows(values, w_up[rows, :])

    def qkv_body(rows):
        values = qkv[rows, :].astype(jnp.float32)
        qkv_wide[rows, :] = values
        dots1[rows, :] = dot_rows(values, w[rows, :])

    def gain_grads(dots, gain_ref):
        columns = jnp.broadcast_to(jnp.sum(dots[...], axis=1, keepdims=True), dots.shape)
        return columns.T[:1, :] / gain_ref[:, block]

    def wait(*numbers):
        for number in numbers:
            loads[number].wait()

    wait(0, 1)
    by_rows(count, 16, gate_body)
    stores[0].start()
    wait(2, 3)
    by_rows(count, 16, up_body)
    stores[1].start()
    norm2_ref[...] = gain_grads(dots2, gain2_ref)
    wait(4)
    widen(down, down_wide)
    stores[2].start()
    wait(5)
    widen(out, out_wide)
    stores[3].start()
    wait(6, 7)
    by_rows(count, 16, qkv_body)
    stores[4].start()
    norm1_ref[...] = gain_grads(dots1, gain1_ref)
    wait(8, 9, 10)

    def input_body(rows):
        values = x[rows, :].astype(jnp.float32)
        inverse = lax.rsqrt(jnp.mean(values * values, axis=-1, keepdims=True) + epsilon)
        input_wide[rows, :] = grad[rows, :] + norm_input_grad(
            values, inverse, gain1_ref[...], first[rows, :].astype(jnp.float32)
        )

    by_rows(x.shape[0], 32, input_body)
    stores[5].start()
    for copy in stores:
        copy.wait()


def tail(sums, first, x, grad, w_qkv, w_gate, w_up, gain1, gain2):
    down, gate, up, out, qkv = sums
    tokens, depth = x.shape
    count = gate.shape[0]
    low, wide = jnp.bfloat16, jnp.float32
    anywhere = pl.BlockSpec(memory_space=pl.ANY)
    inside = pl.BlockSpec(memory_space=pltpu.VMEM)
    shapes = [(tokens, depth), qkv.shape, out.shape, gate.shape, up.shape, down.shape]
    results = [shapes[0], (1, count), (1, count)] + shapes[1:]
    return pl.pallas_call(
        tail_kernel,
        in_specs=[anywhere] * 11 + [inside] * 2,
        out_specs=[anywhere] + [inside] * 2 + [anywhere] * 5,
        out_shape=[jax.ShapeDtypeStruct(shape, wide) for shape in results],
        scratch_shapes=[pltpu.VMEM(total.shape, low) for total in sums]
        + [
            pltpu.VMEM(first.shape, low),
            pltpu.VMEM(x.shape, low),
            pltpu.VMEM(x.shape, wide),
            pltpu.VMEM(qkv.shape, low),
            pltpu.VMEM(gate.shape, low),
            pltpu.VMEM(up.shape, low),
        ]
        + [pltpu.VMEM(shape, wide) for shape in shapes]
        + [pltpu.VMEM((count, HEAD_DIM), wide)] * 2
        + [pltpu.SemaphoreType.DMA((11,)), pltpu.SemaphoreType.DMA((6,))],
        compiler_params=pltpu.CompilerParams(vmem_limit_bytes=VMEM_BYTES),
        name="tail",
    )(*sums, first, x, grad, w_qkv, w_gate, w_up, gain1, gain2)


def head_plan(
    seg_size,
    seq_size,
    layer_input,
    output_grad,
    norm1_gain,
    norm2_gain,
    w_qkv,
    w_out,
    w_gate,
    w_up,
    w_down,
    mem_keys,
    mem_values,
    memory_flags,
    sources,
):
    tokens = layer_input.shape[1]
    length = tokens * seq_size
    width = D // seq_size
    inputs = layer_input[0].astype(jnp.float32)
    first_low = norm_forward(inputs, norm1_gain)[0].astype(jnp.bfloat16)
    table = turn_table(length)
    every_low, chosen_memory, attended_low, queries, keys, values, heads_low, log_totals = front(
        memory_flags, sources, first_low, mem_keys[0], mem_values[0], w_qkv, table, seg_size, seq_size, 1
    )

    output, grad_residual, grad_attended, term_down, term_gate, term_up, term_out = dense(
        layer_input[0], output_grad[0], attended_low, w_out, norm2_gain[None], w_gate, w_up, w_down
    )
    *sums, qkv_rows, first_rows = back(
        memory_flags,
        grad_attended,
        queries,
        keys,
        values,
        chosen_memory,
        every_low,
        [term_down, term_gate, term_up, term_out],
        w_qkv,
        heads_low,
        log_totals,
        table,
        2,
    )
    sums = [total.reshape(2 * total.shape[1], total.shape[2]) for total in sums]
    sums.append(qkv_rows.reshape(width, 3 * D))
    input_grad, grad_norm1, grad_norm2, grad_qkv, grad_out, grad_gate, grad_up, grad_down = tail(
        sums, first_rows, layer_input[0], grad_residual, w_qkv, w_gate, w_up, norm1_gain[None], norm2_gain[None]
    )
    return (
        output[None],
        input_grad[None],
        grad_norm1[0],
        grad_norm2[0],
        grad_qkv,
        grad_out,
        grad_gate,
        grad_up,
        grad_down,
    )


def solution(mesh):
    seq_size = mesh.shape["seq"]
    heads_fit = seq_size == 4 and mesh.shape["seg"] == 8
    plan = functools.partial(head_plan, mesh.shape["seg"], seq_size) if heads_fit else general_plan
    placed = (
        P("seg", "seq", None),
        P("seg", "seq", None),
        P(),
        P(),
        P(),
        P(),
        P(),
        P(),
        P(),
        P("seg", "seq", None),
        P("seg", "seq", None),
        P(),
        P(),
    )
    return jax.shard_map(
        plan,
        mesh=mesh,
        in_specs=placed,
        out_specs=(
            P("seg", "seq", None),
            P("seg", "seq", None),
            P("seq"),
            P("seq"),
            P("seq", None),
            P("seq", None),
            P("seq", None),
            P("seq", None),
            P("seq", None),
        ),
        check_vma=False,
    )
```

```python
import functools
import math

import jax
import jax.numpy as jnp
import numpy as np
from jax import lax
from jax.experimental import pallas as pl
from jax.experimental.pallas import tpu as pltpu
from jax.sharding import PartitionSpec as P

D = 1024
HEADS = 8
HEAD_DIM = 128


masked_score = -1e30
epsilon = 1e-06
rotary_base = 10000.0


def product(former, latter):
    return jnp.dot(former, latter, preferred_element_type=jnp.float32)


def product_nt(former, latter):
    return lax.dot_general(
        former, latter, (((1,), (1,)), ((), ())), preferred_element_type=jnp.float32
    )


def product_tn(former, latter):
    return lax.dot_general(
        former, latter, (((0,), (0,)), ((), ())), preferred_element_type=jnp.float32
    )


def norm_forward(values, norm_gain):
    inverse = lax.rsqrt(jnp.mean(values * values, axis=-1, keepdims=True) + epsilon)
    return (values * inverse * norm_gain, inverse)


def norm_backward(values, inverse, norm_gain, upstream):
    weighted = upstream * norm_gain
    inner_mean = jnp.mean(weighted * values, axis=-1, keepdims=True)
    grad_values = inverse * weighted - inverse * inverse * inverse * values * inner_mean
    grad_gain = jnp.sum(upstream * values * inverse, axis=0)
    return (grad_values, grad_gain)


def turn_tables(positions):
    half_dim = HEAD_DIM // 2
    exponent = -2.0 * jnp.arange(half_dim, dtype=jnp.float32) / HEAD_DIM
    angles = positions[:, None] * jnp.power(rotary_base, exponent)[None, :]
    angles = jnp.concatenate([angles, angles], axis=1)
    return (jnp.cos(angles)[:, None, :], jnp.sin(angles)[:, None, :])


def rotate(matrix, cosine_table, sine_table, direction):
    row_count = matrix.shape[0]
    half_dim = HEAD_DIM // 2
    shaped = matrix.reshape(row_count, HEADS, HEAD_DIM)
    turned = jnp.concatenate([-shaped[..., half_dim:], shaped[..., :half_dim]], axis=-1)
    return (shaped * cosine_table + direction * turned * sine_table).reshape(
        row_count, HEADS * HEAD_DIM
    )


def general_plan(
    layer_input,
    output_grad,
    norm1_gain,
    norm2_gain,
    w_qkv,
    w_out,
    w_gate,
    w_up,
    w_down,
    mem_keys,
    mem_values,
    memory_flags,
    sources,
):
    seg_index = lax.axis_index("seg")
    seq_index = lax.axis_index("seq")
    tokens = layer_input.shape[1]
    score_scale = HEAD_DIM ** (-0.5)
    flag_on = lax.dynamic_index_in_dim(memory_flags, seg_index, 0, keepdims=False) > 0
    listed = lax.dynamic_index_in_dim(sources, seg_index, 0, keepdims=False)
    picked = jnp.concatenate([jnp.reshape(seg_index, (1,)), listed])
    every_keys, every_values = (
        lax.all_gather(mem_keys, "seg", axis=0, tiled=True),
        lax.all_gather(mem_values, "seg", axis=0, tiled=True),
    )
    chosen_keys = jnp.take(every_keys, picked, axis=0)
    chosen_values = jnp.take(every_values, picked, axis=0)
    memory_keys, memory_values = (
        lax.all_gather(chosen_keys, "seq", axis=1, tiled=True),
        lax.all_gather(chosen_values, "seq", axis=1, tiled=True),
    )
    memory_key_blocks = memory_keys.reshape(-1, tokens, HEADS, HEAD_DIM)
    memory_value_blocks = memory_values.reshape(-1, tokens, HEADS, HEAD_DIM)
    memory_blocks = memory_key_blocks.shape[0]
    inputs = layer_input[0].astype(jnp.float32)
    first_norm, first_inverse = norm_forward(inputs, norm1_gain)
    first_low = first_norm.astype(jnp.bfloat16)
    projected = product(first_low, w_qkv)
    positions = seq_index * tokens + lax.iota(jnp.int32, tokens)
    cosine_table, sine_table = turn_tables(positions.astype(jnp.float32))
    queries = rotate(projected[:, :D], cosine_table, sine_table, 1.0).astype(jnp.bfloat16)
    own_keys = rotate(projected[:, D : 2 * D], cosine_table, sine_table, 1.0).astype(jnp.bfloat16)
    own_values = projected[:, 2 * D :].astype(jnp.bfloat16)
    all_keys, all_values = (
        lax.all_gather(own_keys, "seq", axis=0, tiled=True),
        lax.all_gather(own_values, "seq", axis=0, tiled=True),
    )
    key_blocks = all_keys.reshape(-1, tokens, HEADS, HEAD_DIM)
    value_blocks = all_values.reshape(-1, tokens, HEADS, HEAD_DIM)
    query_heads = queries.reshape(tokens, HEADS, HEAD_DIM)
    memory_open = jnp.broadcast_to(flag_on, (tokens, tokens))
    own_count = seq_index + 1
    key_offsets = lax.iota(jnp.int32, tokens)

    def own_open(block):
        return (block * tokens + key_offsets)[None, :] <= positions[:, None]

    def block_scores(key_block, open_mask):
        raw = (
            jnp.einsum("qhd,khd->hqk", query_heads, key_block, preferred_element_type=jnp.float32)
            * score_scale
        )
        return jnp.where(open_mask[None], raw, masked_score)

    def sweep(step, carry):

        def memory_turn(block, state):
            return step(
                state,
                block,
                memory_key_blocks[block],
                memory_value_blocks[block],
                memory_open,
                False,
            )

        def own_turn(block, state):
            return step(state, block, key_blocks[block], value_blocks[block], own_open(block), True)

        carry = lax.fori_loop(0, memory_blocks, memory_turn, carry)
        return lax.fori_loop(0, own_count, own_turn, carry)

    def max_step(carry, block, key_block, value_block, open_mask, own):
        row_max, row_sum = carry
        scores = block_scores(key_block, open_mask)
        new_max = jnp.maximum(row_max, jnp.max(scores, axis=2))
        row_sum = row_sum * jnp.exp(row_max - new_max) + jnp.sum(
            jnp.exp(scores - new_max[..., None]), axis=2
        )
        return (new_max, row_sum)

    start_max = jnp.full((HEADS, tokens), masked_score, jnp.float32)
    row_max, row_sum = sweep(max_step, (start_max, jnp.zeros((HEADS, tokens), jnp.float32)))
    log_totals = row_max + jnp.log(row_sum)

    def mix_step(total, block, key_block, value_block, open_mask, own):
        weights_low = jnp.exp(block_scores(key_block, open_mask) - log_totals[..., None]).astype(
            jnp.bfloat16
        )
        return total + jnp.einsum(
            "hqk,khd->qhd", weights_low, value_block, preferred_element_type=jnp.float32
        )

    attended = sweep(mix_step, jnp.zeros((tokens, HEADS, HEAD_DIM), jnp.float32))
    attended_low = attended.reshape(tokens, D).astype(jnp.bfloat16)
    residual = inputs + product(attended_low, w_out)
    second_norm, second_inverse = norm_forward(residual, norm2_gain)
    second_low = second_norm.astype(jnp.bfloat16)
    gate_values = product(second_low, w_gate)
    up_values = product(second_low, w_up)
    sigmoid_gate = jax.nn.sigmoid(gate_values)
    activated = gate_values * sigmoid_gate
    hidden_low = (activated * up_values).astype(jnp.bfloat16)
    output = (residual + product(hidden_low, w_down)).astype(jnp.bfloat16)
    upstream = output_grad[0]
    grad_down = product_tn(hidden_low, upstream)
    grad_hidden = product_nt(upstream, w_down)
    grad_gate_low = (
        grad_hidden * up_values * sigmoid_gate * (1.0 + gate_values * (1.0 - sigmoid_gate))
    ).astype(jnp.bfloat16)
    grad_up_low = (grad_hidden * activated).astype(jnp.bfloat16)
    grad_gate = product_tn(second_low, grad_gate_low)
    grad_up = product_tn(second_low, grad_up_low)
    grad_second = product_nt(grad_gate_low, w_gate) + product_nt(grad_up_low, w_up)
    grad_residual, grad_norm2 = norm_backward(residual, second_inverse, norm2_gain, grad_second)
    grad_residual = grad_residual + upstream.astype(jnp.float32)
    residual_low = grad_residual.astype(jnp.bfloat16)
    grad_out = product_tn(attended_low, residual_low)
    grad_attended = product_nt(residual_low, w_out).astype(jnp.bfloat16)
    grad_heads = grad_attended.reshape(tokens, HEADS, HEAD_DIM)

    def probs_pair(key_block, value_block, open_mask):
        probs = jnp.exp(block_scores(key_block, open_mask) - log_totals[..., None])
        dprobs = jnp.einsum(
            "qhd,khd->hqk", grad_heads, value_block, preferred_element_type=jnp.float32
        )
        return (probs, dprobs)

    def delta_step(total, block, key_block, value_block, open_mask, own):
        probs, dprobs = probs_pair(key_block, value_block, open_mask)
        return total + jnp.sum(probs * dprobs, axis=2)

    delta_rows = sweep(delta_step, jnp.zeros((HEADS, tokens), jnp.float32))

    def grad_step(carry, block, key_block, value_block, open_mask, own):
        grad_query, key_terms, value_terms = carry
        probs, dprobs = probs_pair(key_block, value_block, open_mask)
        dscores = (probs * (dprobs - delta_rows[..., None])).astype(jnp.bfloat16)
        grad_query = grad_query + jnp.einsum(
            "hqk,khd->qhd", dscores, key_block, preferred_element_type=jnp.float32
        )
        if own:
            key_part = (
                jnp.einsum("hqk,qhd->khd", dscores, query_heads, preferred_element_type=jnp.float32)
                * score_scale
            )
            value_part = jnp.einsum(
                "hqk,qhd->khd",
                probs.astype(jnp.bfloat16),
                grad_heads,
                preferred_element_type=jnp.float32,
            )
            key_terms = lax.dynamic_update_index_in_dim(key_terms, key_part, block, 0)
            value_terms = lax.dynamic_update_index_in_dim(value_terms, value_part, block, 0)
        return (grad_query, key_terms, value_terms)

    term_shape = key_blocks.shape
    start_grads = (
        jnp.zeros((tokens, HEADS, HEAD_DIM), jnp.float32),
        jnp.zeros(term_shape, jnp.float32),
        jnp.zeros(term_shape, jnp.float32),
    )
    grad_query, key_terms, value_terms = sweep(grad_step, start_grads)
    grad_queries = (grad_query * score_scale).reshape(tokens, D)
    grad_keys, grad_values = (
        lax.psum_scatter(
            key_terms.astype(jnp.bfloat16), "seq", scatter_dimension=0, tiled=True
        ).astype(jnp.float32),
        lax.psum_scatter(
            value_terms.astype(jnp.bfloat16), "seq", scatter_dimension=0, tiled=True
        ).astype(jnp.float32),
    )
    grad_projected = jnp.concatenate(
        [
            rotate(grad_queries, cosine_table, sine_table, -1.0),
            rotate(grad_keys.reshape(tokens, D), cosine_table, sine_table, -1.0),
            grad_values.reshape(tokens, D),
        ],
        axis=1,
    ).astype(jnp.bfloat16)
    grad_qkv = product_tn(first_low, grad_projected)
    grad_first = product_nt(grad_projected, w_qkv)
    grad_inputs, grad_norm1 = norm_backward(inputs, first_inverse, norm1_gain, grad_first)
    input_grad = (grad_inputs + grad_residual)[None]
    shares = (
        lax.psum_scatter(
            grad_norm1.astype(jnp.bfloat16), "seq", scatter_dimension=0, tiled=True
        ).astype(jnp.float32),
        lax.psum_scatter(
            grad_norm2.astype(jnp.bfloat16), "seq", scatter_dimension=0, tiled=True
        ).astype(jnp.float32),
        lax.psum_scatter(
            grad_qkv.astype(jnp.bfloat16), "seq", scatter_dimension=0, tiled=True
        ).astype(jnp.float32),
        lax.psum_scatter(
            grad_out.astype(jnp.bfloat16), "seq", scatter_dimension=0, tiled=True
        ).astype(jnp.float32),
        lax.psum_scatter(
            grad_gate.astype(jnp.bfloat16), "seq", scatter_dimension=0, tiled=True
        ).astype(jnp.float32),
        lax.psum_scatter(
            grad_up.astype(jnp.bfloat16), "seq", scatter_dimension=0, tiled=True
        ).astype(jnp.float32),
        lax.psum_scatter(
            grad_down.astype(jnp.bfloat16), "seq", scatter_dimension=0, tiled=True
        ).astype(jnp.float32),
    )
    totals = (
        lax.psum(shares[0].astype(jnp.bfloat16), "seg").astype(jnp.float32),
        lax.psum(shares[1].astype(jnp.bfloat16), "seg").astype(jnp.float32),
        lax.psum(shares[2].astype(jnp.bfloat16), "seg").astype(jnp.float32),
        lax.psum(shares[3].astype(jnp.bfloat16), "seg").astype(jnp.float32),
        lax.psum(shares[4].astype(jnp.bfloat16), "seg").astype(jnp.float32),
        lax.psum(shares[5].astype(jnp.bfloat16), "seg").astype(jnp.float32),
        lax.psum(shares[6].astype(jnp.bfloat16), "seg").astype(jnp.float32),
    )
    return (
        output[None],
        input_grad,
        totals[0],
        totals[1],
        totals[2],
        totals[3],
        totals[4],
        totals[5],
        totals[6],
    )


VMEM_BYTES = 60 * 1024 * 1024
VMEM_MOST = 67043328
LN2 = math.log(2.0)
SCORE_SCALE = HEAD_DIM ** (-0.5)


def lane_fold(op, tile, running):
    for column in range(tile.shape[1] // HEAD_DIM):
        piece = tile[:, column * HEAD_DIM : (column + 1) * HEAD_DIM]
        running = piece if running is None else op(running, piece)
    return running


def causal(scores):
    rows = lax.broadcasted_iota(jnp.int32, scores.shape, 0)
    columns = lax.broadcasted_iota(jnp.int32, scores.shape, 1)
    return jnp.where(columns <= rows, scores, masked_score)


def attend(query, pairs, diagonal, carried, closed=0.0):
    every, lane_max = [], None
    for index, (keys, _) in enumerate(pairs):
        scores = product_nt(query, keys)
        if diagonal and index == len(pairs) - 1:
            scores = causal(scores)
        lane_max = lane_fold(jnp.maximum, scores, lane_max)
        every.append(scores)
    row_max = jnp.max(lane_max, axis=1, keepdims=True) - closed
    if carried is not None:
        row_max = jnp.maximum(row_max, carried[0])
    shift = row_max + closed
    lane_sum, mixed = None, None
    for scores, (_, values) in zip(every, pairs):
        probs = jnp.exp2(scores - shift)
        lane_sum = lane_fold(jnp.add, probs, lane_sum)
        part = product(probs.astype(jnp.bfloat16), values)
        mixed = part if mixed is None else mixed + part
    row_sum = jnp.sum(lane_sum, axis=1, keepdims=True)
    if carried is not None:
        shrink = jnp.exp2(carried[0] - row_max)
        row_sum = carried[1] * shrink + row_sum
        mixed = carried[2] * shrink + mixed
    return row_max, row_sum, mixed


def turn_block(matrix, cosine, sine):
    return matrix * cosine + pltpu.roll(matrix, HEAD_DIM // 2, 1) * sine


def turn_factors(both):
    swapped = pltpu.roll(both, HEAD_DIM // 2, 1)
    first = lax.broadcasted_iota(jnp.int32, both.shape, 1) < HEAD_DIM // 2
    return jnp.where(first, both, swapped), jnp.where(first, swapped, -both)


def turn_table(length, step=64):
    frequency = rotary_base ** (-2.0 * np.arange(HEAD_DIM // 2) / HEAD_DIM)
    coarse = np.arange(length // step)[:, None] * step * frequency
    fine = np.arange(step)[:, None] * frequency

    def pair(former, latter):
        return jnp.asarray(np.concatenate([former, latter], axis=1), jnp.float32)

    table = (
        pair(np.cos(coarse), np.sin(coarse))[:, None, :] * pair(np.cos(fine), np.cos(fine))[None]
        + pair(-np.sin(coarse), np.cos(coarse))[:, None, :] * pair(np.sin(fine), np.sin(fine))[None]
    )
    return table.reshape(length, HEAD_DIM)


LINK_RATE = {"core": 300e3, "x": 49e3, "y": 49e3, "z": 49e3}


class Place:
    def __init__(self):
        seg, seq = lax.axis_index("seg"), lax.axis_index("seq")
        self.core, self.z = lax.rem(seg, 2), lax.div(seg, 2)
        self.x, self.y = lax.rem(seq, 2), lax.div(seq, 2)
        odd = lax.rem(self.z, 2)
        self.inner = jnp.logical_or(self.z == 1, self.z == 2)
        self.outer = jnp.logical_not(self.inner)
        self.peer = {
            "core": (seg + 1 - 2 * self.core, seq),
            "x": (seg, seq + 1 - 2 * self.x),
            "y": (seg, seq + 2 - 4 * self.y),
            "xy": (seg, 3 - seq),
            "pair": (seg + 2 - 4 * odd, seq),
            "middle": (seg - 2 + 4 * odd, seq),
        }

    def greet(self, names):
        barrier = pltpu.get_barrier_semaphore()

        def hail(name):
            pl.semaphore_signal(
                barrier, inc=1, device_id=self.peer[name], device_id_type=pl.DeviceIdType.MESH
            )

        for name in names:
            hail(name)

        @pl.when(self.inner)
        def _():
            hail("middle")

        pl.semaphore_wait(barrier, len(names) + self.inner.astype(jnp.int32))


def add_into(total, addend, step=16):
    def turn(index, carry):
        rows = pl.ds(pl.multiple_of(index * step, step), step)
        total[rows, :] = total[rows, :] + addend[rows, :]
        return carry

    lax.fori_loop(0, total.shape[0] // step, turn, 0)


def add_to(result, former, latter, step=16):
    def turn(index, carry):
        rows = pl.ds(pl.multiple_of(index * step, step), step)
        result[rows, :] = former[rows, :] + latter[rows, :]
        return carry

    lax.fori_loop(0, result.shape[0] // step, turn, 0)


def weight_copies(whole, part, seq, semaphores, first):
    width = part.shape[1] // 3
    depth = whole.shape[1] // 3
    return [
        pltpu.make_async_copy(
            whole.at[:, pl.ds(pl.multiple_of(kind * depth + seq * width, HEAD_DIM), width)],
            part.at[:, pl.ds(kind * width, width)],
            semaphores.at[first + kind],
        )
        for kind in range(3)
    ]


class Chunk:
    def __init__(self, term, offset, rows, columns, gather=False):
        self.term, self.offset, self.rows, self.columns = term, offset, rows, columns
        self.gather = gather

    def scratch(self):
        rows, columns, half = self.rows, self.columns, self.columns // 2
        low = jnp.bfloat16
        four = pltpu.VMEM((2, 2, rows, columns), low)
        one = four if self.gather else pltpu.VMEM((rows, columns), low)
        last = pltpu.VMEM((rows, 4 * columns), low) if self.gather else one
        if self.gather:
            middle = [four]
        else:
            middle = [
                pltpu.VMEM((2, rows, half), low),
                pltpu.VMEM((2, rows, half), low),
                pltpu.VMEM((rows, half), low),
                pltpu.VMEM((rows, half), low),
            ]
        ends = [one, one, last] if self.gather else [one, one]
        return [four, four] + middle + ends + [
            pltpu.SemaphoreType.DMA((9,)),
            pltpu.SemaphoreType.DMA((9,)),
            pltpu.SemaphoreType.DMA((3,)),
        ]

    def bind(self, place, source, result, refs):
        self.place, self.source, self.result = place, source, result
        self.mine, self.core_in = refs[0], refs[1]
        ends = 3 if self.gather else 2
        self.middle = refs[2 : -3 - ends]
        self.z_last, self.z_second = refs[-4], refs[-5]
        self.z_first = refs[-6] if self.gather else self.z_last
        self.sent, self.received, self.local = refs[-3:]

    def remote(self, slot, source, target, peer):
        return pltpu.make_async_remote_copy(
            src_ref=source,
            dst_ref=target,
            send_sem=self.sent.at[slot],
            recv_sem=self.received.at[slot],
            device_id=self.place.peer[peer],
            device_id_type=pl.DeviceIdType.MESH,
        )

    def core_copy(self):
        rows = pl.ds(self.offset, self.rows)
        return self.remote(
            0, self.source.at[:, :, 1 - self.place.core, rows, :], self.core_in, "core"
        )

    def load(self):
        rows = pl.ds(self.offset, self.rows)
        return pltpu.make_async_copy(
            self.source.at[:, :, self.place.core, rows, :], self.mine, self.local.at[0]
        )

    def halves(self):
        half = self.columns // 2
        return pl.ds(0, half), pl.ds(half, half)

    def wide_copies(self):
        p, (left, right) = self.place, self.halves()
        if self.gather:
            return [
                self.remote(1, self.mine.at[p.y, 1 - p.x], self.middle[0].at[p.y, p.x], "x"),
                self.remote(2, self.mine.at[1 - p.y, p.x], self.middle[0].at[p.y, p.x], "y"),
                self.remote(3, self.mine.at[1 - p.y, 1 - p.x], self.middle[0].at[p.y, p.x], "xy"),
            ]
        return [
            self.remote(1, self.mine.at[:, 1 - p.x, :, left], self.middle[0], "x"),
            self.remote(2, self.mine.at[1 - p.y, :, :, right], self.middle[1], "y"),
        ]

    def narrow_copies(self):
        p, (left, right) = self.place, self.halves()
        return [
            self.remote(3, self.mine.at[1 - p.y, p.x, :, left], self.middle[2], "y"),
            self.remote(4, self.mine.at[p.y, 1 - p.x, :, right], self.middle[3], "x"),
        ]

    def summed(self):
        return self.middle[0] if self.gather else self.mine.at[self.place.y, self.place.x]

    def pair_copy(self):
        return self.remote(5, self.summed(), self.z_first, "pair")

    def middle_copy(self):
        return self.remote(6, self.summed(), self.z_second, "middle")

    def last_copy(self):
        return self.remote(7, self.z_last, self.z_last, "pair")

    def out_copies(self):
        rows = pl.ds(self.offset, self.rows)
        core = self.place.core
        target = self.result.at[core, rows, :]
        return (
            self.remote(8, self.z_last, target, "core"),
            pltpu.make_async_copy(self.z_last, target, self.local.at[1]),
        )

    def parts(self, ref):
        if self.gather:
            return [ref.at[a, b] for a in range(2) for b in range(2)]
        return [ref]

    def lay_out(self):
        part = self.columns // 3
        for owner in range(4):
            for kind in range(3):
                lanes = pl.ds(kind * part, part)
                former = self.middle[0].at[owner // 2, owner % 2, :, lanes]
                latter = self.z_second.at[owner // 2, owner % 2, :, lanes]
                add_to(self.z_last.at[:, pl.ds((4 * kind + owner) * part, part)], former, latter)

    def stage_start(self):
        self.core_copy().start()
        self.load().start()

    def stage_core(self):
        self.core_copy().wait_recv()
        self.load().wait()
        for a in range(2):
            for b in range(2):
                add_into(self.mine.at[a, b], self.core_in.at[a, b])
        for copy in self.wide_copies():
            copy.start()

    def stage_wide(self):
        p, (left, right) = self.place, self.halves()
        if self.gather:
            stay = pltpu.make_async_copy(
                self.mine.at[p.y, p.x], self.middle[0].at[p.y, p.x], self.local.at[2]
            )
            stay.start()
            for copy in self.wide_copies():
                copy.wait_recv()
            stay.wait()
            self.z_start()
            return
        for copy in self.wide_copies():
            copy.wait_recv()
        for a in range(2):
            add_into(self.mine.at[a, p.x, :, left], self.middle[0].at[a])
            add_into(self.mine.at[p.y, a, :, right], self.middle[1].at[a])
        for copy in self.narrow_copies():
            copy.start()

    def stage_narrow(self):
        p, (left, right) = self.place, self.halves()
        for copy in self.narrow_copies():
            copy.wait_recv()
        add_into(self.mine.at[p.y, p.x, :, left], self.middle[2])
        add_into(self.mine.at[p.y, p.x, :, right], self.middle[3])
        self.z_start()

    def z_start(self):
        @pl.when(self.place.outer)
        def _():
            self.pair_copy().start()

    def stage_pair(self):
        @pl.when(self.place.inner)
        def _():
            self.pair_copy().wait_recv()
            for total, addend in zip(self.parts(self.summed()), self.parts(self.z_first)):
                add_into(total, addend)
            self.middle_copy().start()

    def stage_middle(self):
        @pl.when(self.place.inner)
        def _():
            self.middle_copy().wait_recv()
            if self.gather:
                self.lay_out()
            else:
                add_to(self.z_last, self.summed(), self.z_second)
            self.last_copy().start()
            for copy in self.out_copies():
                copy.start()

    def stage_last(self):
        @pl.when(self.place.outer)
        def _():
            self.last_copy().wait_recv()
            for copy in self.out_copies():
                copy.start()

    def stage_end(self):
        remote_out, local_out = self.out_copies()
        remote_out.wait()
        local_out.wait()
        self.core_copy().wait_send()
        for copy in self.wide_copies():
            copy.wait_send()
        if not self.gather:
            for copy in self.narrow_copies():
                copy.wait_send()

        @pl.when(self.place.outer)
        def _():
            self.pair_copy().wait_send()

        @pl.when(self.place.inner)
        def _():
            self.middle_copy().wait_send()
            self.last_copy().wait_send()

    def plan(self):
        piece = 2 * self.rows * self.columns
        if self.gather:
            return [
                (self.stage_core, [("x", 1.5 * piece), ("y", 1.5 * piece)]),
                (self.stage_wide, [("z", 4 * piece)]),
                (self.stage_pair, [("z", 4 * piece)]),
                (self.stage_middle, [("z", 4 * piece)]),
                (self.stage_last, [("core", 4 * piece)]),
                (self.stage_end, []),
            ]
        return [
            (self.stage_core, [("x", piece), ("y", piece)]),
            (self.stage_wide, [("x", piece / 2), ("y", piece / 2)]),
            (self.stage_narrow, [("z1", piece)]),
            (self.stage_pair, [("z2", piece)]),
            (self.stage_middle, [("z3", piece)]),
            (self.stage_last, [("core", piece)]),
            (self.stage_end, []),
        ]

    def opening(self):
        return [("core", 8 * self.rows * self.columns)]


class RowChunk:
    def __init__(self, term, offset, rows, columns):
        self.term, self.offset, self.rows, self.columns = term, offset, rows, columns

    def scratch(self):
        rows, columns, half = self.rows, self.columns, self.columns // 2
        low = jnp.bfloat16
        return [
            pltpu.VMEM((2, rows, half), low),
            pltpu.VMEM((2, rows, half), low),
            pltpu.VMEM((rows, half), low),
            pltpu.VMEM((rows, half), low),
            pltpu.SemaphoreType.DMA((6,)),
            pltpu.SemaphoreType.DMA((6,)),
            pltpu.SemaphoreType.DMA((1,)),
        ]

    def bind(self, place, source, result, refs):
        self.place, self.result = place, result
        self.blocks = source
        self.middle = refs[:4]
        self.sent, self.received, self.local = refs[4:]

    def mine(self, y, x, lanes):
        return self.blocks.at[2 * y + x, pl.ds(self.offset, self.rows), lanes]

    remote = Chunk.remote
    halves = Chunk.halves

    def wide_copies(self):
        p, (left, right) = self.place, self.halves()
        copies = []
        for a in range(2):
            copies.append(
                self.remote(a, self.mine(a, 1 - p.x, left), self.middle[0].at[a], "x")
            )
            copies.append(
                self.remote(2 + a, self.mine(1 - p.y, a, right), self.middle[1].at[a], "y")
            )
        return copies

    def narrow_copies(self):
        p, (left, right) = self.place, self.halves()
        return [
            self.remote(4, self.mine(1 - p.y, p.x, left), self.middle[2], "y"),
            self.remote(5, self.mine(p.y, 1 - p.x, right), self.middle[3], "x"),
        ]

    def out_copy(self):
        p = self.place
        whole = pl.ds(0, self.columns)
        return pltpu.make_async_copy(
            self.mine(p.y, p.x, whole),
            self.result.at[pl.ds(self.offset, self.rows), :],
            self.local.at[0],
        )

    def stage_start(self):
        for copy in self.wide_copies():
            copy.start()

    def stage_wide(self):
        p, (left, right) = self.place, self.halves()
        for copy in self.wide_copies():
            copy.wait_recv()
        for a in range(2):
            add_into(self.mine(a, p.x, left), self.middle[0].at[a])
            add_into(self.mine(p.y, a, right), self.middle[1].at[a])
        for copy in self.narrow_copies():
            copy.start()

    def stage_narrow(self):
        p, (left, right) = self.place, self.halves()
        for copy in self.narrow_copies():
            copy.wait_recv()
        add_into(self.mine(p.y, p.x, left), self.middle[2])
        add_into(self.mine(p.y, p.x, right), self.middle[3])
        self.out_copy().start()

    def stage_end(self):
        self.out_copy().wait()
        for copy in self.wide_copies() + self.narrow_copies():
            copy.wait_send()

    def plan(self):
        piece = 2 * self.rows * self.columns
        return [
            (self.stage_wide, [("x", piece / 2), ("y", piece / 2)]),
            (self.stage_narrow, [("core", 0.0)]),
            (self.stage_end, []),
        ]

    def opening(self):
        piece = 2 * self.rows * self.columns
        return [("x", piece), ("y", piece)]


class Steps:
    def __init__(self, start):
        self.now, self.free, self.waiting, self.held = start, {}, [], []

    def send(self, transfers):
        ends = [self.now]
        for link, size in transfers:
            start = max(self.now, self.free.get(link, 0.0))
            self.free[link] = start + size / LINK_RATE.get(link, LINK_RATE["z"])
            ends.append(self.free[link] + 2.0)
        return max(ends)

    def open(self, chunks, depth=None):
        entries = [(self.send(chunk.opening()), n, chunk, 0) for n, chunk in enumerate(chunks)]
        self.waiting += entries[:depth]
        self.held += entries[depth:] if depth else []

    def due(self, everything=False):
        stages = []
        while self.waiting:
            self.waiting.sort(key=lambda entry: entry[:2])
            when, number, chunk, index = self.waiting[0]
            if when > self.now and not everything:
                break
            self.waiting.pop(0)
            self.now = max(self.now, when) + 0.4
            stage, transfers = chunk.plan()[index]
            stages.append(stage)
            if index == 1 and self.held:
                ready, *rest = self.held.pop(0)
                self.waiting.append((max(ready, self.now), *rest))
            if index + 1 < len(chunk.plan()):
                self.waiting.append((self.send(transfers), number, chunk, index + 1))
        return stages

    def spend(self, duration):
        self.now += duration


def back_kernel(
    chunks,
    first_chunks,
    heads,
    flag_ref,
    g_ref,
    q_hbm,
    k_hbm,
    v_hbm,
    memory_hbm,
    every_hbm,
    down_ref,
    gate_ref,
    up_ref,
    out_ref,
    w_hbm,
    mix_ref,
    log_ref,
    table_ref,
    sum_down,
    sum_gate,
    sum_up,
    sum_out,
    sum_qkv,
    sum_first,
    w_ref,
    q,
    k,
    v,
    upstream,
    shared,
    dk,
    dv,
    total,
    delta,
    part_qkv,
    trade_sent,
    trade_received,
    local,
    *refs,
):
    place = Place()
    seq = lax.axis_index("seq")
    tokens = g_ref.shape[0]
    width = heads * HEAD_DIM
    used = 0
    sources = [down_ref, gate_ref, up_ref, out_ref, part_qkv, shared]
    results = [sum_down, sum_gate, sum_up, sum_out, sum_qkv, sum_first]
    for chunk in chunks + first_chunks:
        count = len(chunk.scratch())
        chunk.bind(place, sources[chunk.term], results[chunk.term], refs[used : used + count])
        used += count

    def owner_at(turn):
        low, high = lax.rem(turn, 2), lax.div(turn, 2)
        x = place.x + low - 2 * place.x * low
        y = place.y + high - 2 * place.y * high
        return 2 * y + x

    def columns(owner):
        return pl.ds(pl.multiple_of(owner * width, HEAD_DIM), width)

    def span(block):
        return pl.ds(pl.multiple_of(block * tokens, tokens), tokens)

    def lanes(head):
        return pl.ds(pl.multiple_of(head * HEAD_DIM, HEAD_DIM), HEAD_DIM)

    across = {"x": seq + 1 - 2 * place.x, "y": seq + 2 - 4 * place.y, "xy": 3 - seq}
    trades = [
        pltpu.make_async_remote_copy(
            src_ref=g_ref.at[:, columns(across[peer])],
            dst_ref=upstream.at[span(seq), :],
            send_sem=trade_sent.at[slot],
            recv_sem=trade_received.at[slot],
            device_id=place.peer[peer],
            device_id_type=pl.DeviceIdType.MESH,
        )
        for slot, peer in enumerate(("x", "y", "xy"))
    ]
    loads = [
        pltpu.make_async_copy(g_ref.at[:, columns(seq)], upstream.at[span(seq), :], local.at[0]),
        pltpu.make_async_copy(q_hbm, q, local.at[1]),
        pltpu.make_async_copy(k_hbm, k, local.at[2]),
        pltpu.make_async_copy(v_hbm, v, local.at[3]),
        pltpu.make_async_copy(memory_hbm, shared, local.at[4]),
    ] + weight_copies(w_hbm, w_ref, seq, local, 6)
    load_every = pltpu.make_async_copy(every_hbm, shared, local.at[5])

    def turn_back(matrix, rows):
        cosine, sine = turn_factors(table_ref[rows, :])
        return turn_block(matrix, cosine, sine).astype(jnp.bfloat16)

    def memory_part(head, block):
        rows, mine = span(block), lanes(head)
        query, grads = q[rows, mine], upstream[rows, mine]
        row_delta = jnp.sum(
            grads.astype(jnp.float32) * mix_ref[rows, mine].astype(jnp.float32), axis=1, keepdims=True
        )
        delta[...] = jnp.broadcast_to(row_delta, delta.shape)
        closed = (1 - flag_ref[lax.axis_index("seg")]).astype(jnp.float32) * 1e30
        log_total = log_ref[rows, mine][:, :1] + closed
        result = jnp.zeros(total.shape, jnp.float32)
        for slot in range(shared.shape[0]):
            for run in range(2):

                def tile(kind):
                    start = pl.multiple_of((2 * run + kind) * width + head * HEAD_DIM, HEAD_DIM)
                    return shared[slot, :, pl.ds(start, HEAD_DIM)]

                keys, values = tile(0), tile(1)
                probs = jnp.exp2(product_nt(query, keys) - log_total)
                dscores = probs * (product_nt(grads, values) - row_delta)
                result = result + product(dscores.astype(jnp.bfloat16), keys)
        total[...] = result

    def own_part(head, block):
        rows, mine = span(block), lanes(head)
        query, grads = q[rows, mine], upstream[rows, mine]
        log_total, row_delta = log_ref[rows, mine][:, :1], delta[:, :1]

        def turn(other, result, diagonal):
            keys = k[span(other), mine]
            scores = product_nt(query, keys)
            if diagonal:
                scores = causal(scores)
            probs = jnp.exp2(scores - log_total)
            dscores = (probs * (product_nt(grads, v[span(other), mine]) - row_delta)).astype(
                jnp.bfloat16
            )
            dv[span(other), :] += product_tn(probs.astype(jnp.bfloat16), grads)
            dk[span(other), :] += product_tn(dscores, query)
            return result + product(dscores, keys)

        result = turn(block, total[...], True)
        result = lax.fori_loop(0, block, lambda other, r: turn(other, r, False), result)
        q[rows, mine] = turn_back(result * SCORE_SCALE, rows)

    def close_head(head):
        mine = lanes(head)

        def turn(block, carry):
            rows = span(block)
            k[rows, mine] = turn_back(dk[rows, :] * LN2, rows)
            v[rows, mine] = dv[rows, :].astype(jnp.bfloat16)
            return carry

        lax.fori_loop(0, 4, turn, 0)

    def multiply_qkv(index, carry):
        cut = pl.ds(pl.multiple_of(index * width, HEAD_DIM), width)
        for kind, part in enumerate((q, k, v)):
            term = None
            for block in range(shared.shape[0]):
                product_part = product_tn(shared[block, :, cut], part[block * tokens : (block + 1) * tokens, :])
                term = product_part if term is None else term + product_part
            term = term.astype(jnp.bfloat16)
            half = term.shape[0] // 2
            place_y, place_x = lax.div(index, 2), lax.rem(index, 2)
            for core in range(2):
                part_qkv[place_y, place_x, core, :, kind * width : (kind + 1) * width] = term[
                    core * half : (core + 1) * half, :
                ]
        return carry

    def multiply_first(block, carry):
        rows = span(block)
        result = None
        for kind, part in enumerate((q, k, v)):
            term = product_nt(part[rows, :], w_ref[:, kind * width : (kind + 1) * width])
            result = term if result is None else result + term
        shared[block] = result.astype(jnp.bfloat16)
        return carry

    place.greet(("core", "x", "y", "xy", "pair"))
    for copy in trades + loads:
        copy.start()
    for chunk in chunks:
        chunk.stage_start()
    steps = Steps(3.0)
    steps.free.update(x=11.0, y=11.0)
    steps.open(chunks, 3)
    for copy in loads:
        copy.wait()
    slots = []
    for unit in range(2 * 4 * heads):
        slots.append(steps.due())
        steps.spend(4.3 if unit % 2 == 0 else 3.2)

    def run(stages):
        for stage in stages:
            stage()

    def unit(index, carry):
        head, turn = lax.div(index, 4), lax.rem(index, 4)
        block = owner_at(turn)
        for number in range(4 * heads):
            if slots[2 * number] or number in (1, 2, 3):

                @pl.when(index == number)
                def _(number=number):
                    run(slots[2 * number])
                    if number in (1, 2, 3):
                        trades[number - 1].wait_recv()

        @pl.when(turn == 0)
        def _():
            dk[...] = jnp.zeros_like(dk)
            dv[...] = jnp.zeros_like(dv)

        memory_part(head, block)
        for number in range(4 * heads):
            if slots[2 * number + 1]:

                @pl.when(index == number)
                def _(number=number):
                    run(slots[2 * number + 1])

        own_part(head, block)

        @pl.when(turn == 3)
        def _():
            close_head(head)

        return carry

    lax.fori_loop(0, 4 * heads, unit, 0)
    load_every.start()
    run(steps.due())
    load_every.wait()
    lax.fori_loop(0, 4, multiply_qkv, 0)
    steps.spend(8.0)
    qkv_chunks = [chunk for chunk in first_chunks if chunk.term == 4]
    row_chunks = [chunk for chunk in first_chunks if chunk.term == 5]
    for chunk in qkv_chunks:
        chunk.stage_start()
    steps.open(qkv_chunks)
    run(steps.due())
    lax.fori_loop(0, 4, multiply_first, 0)
    steps.spend(6.0)
    for chunk in row_chunks:
        chunk.stage_start()
    steps.open(row_chunks)
    run(steps.due(True))
    for copy in trades:
        copy.wait_send()


def back(
    flags, grads, queries, keys, values, memory, every, terms, w_qkv, attended, log_totals, table, collective_id
):
    tokens, depth = grads.shape
    length, width = queries.shape
    low = jnp.bfloat16
    chunks, shapes = [], []
    for index, term in enumerate(terms):
        rows, columns = term.shape[0] // 8, term.shape[1]
        parts = (2, 4, 4, 2)[index]
        chunks += [Chunk(index, n * rows // parts, rows // parts, columns) for n in range(parts)]
        shapes.append((2, rows, columns))
    rows = depth // 8
    first_chunks = [Chunk(4, n * rows // 4, rows // 4, 3 * width, True) for n in range(4)]
    first_chunks += [RowChunk(5, n * tokens // 4, tokens // 4, depth) for n in range(4)]
    shapes += [(2, rows, 12 * width), (tokens, depth)]
    anywhere = pl.BlockSpec(memory_space=pl.ANY)
    inside = pl.BlockSpec(memory_space=pltpu.VMEM)
    scratch = (
        [pltpu.VMEM((depth, 3 * width), low)]
        + [pltpu.VMEM((length, width), low)] * 4
        + [pltpu.VMEM((4, tokens, depth), low)]
        + [pltpu.VMEM((length, HEAD_DIM), jnp.float32)] * 2
        + [pltpu.VMEM((tokens, HEAD_DIM), jnp.float32)] * 2
        + [pltpu.VMEM((2, 2, 2, rows, 3 * width), low)]
        + [pltpu.SemaphoreType.DMA((3,))] * 2
        + [pltpu.SemaphoreType.DMA((9,))]
    )
    return pl.pallas_call(
        functools.partial(back_kernel, chunks, first_chunks, width // HEAD_DIM),
        in_specs=[pl.BlockSpec(memory_space=pltpu.SMEM)] + [anywhere] * 11 + [inside] * 3,
        out_specs=[anywhere] * len(shapes),
        out_shape=[jax.ShapeDtypeStruct(shape, low) for shape in shapes],
        scratch_shapes=scratch + [ref for chunk in chunks + first_chunks for ref in chunk.scratch()],
        compiler_params=pltpu.CompilerParams(
            collective_id=collective_id, has_side_effects=True, vmem_limit_bytes=VMEM_MOST
        ),
        name="back",
    )(
        flags,
        grads,
        queries,
        keys,
        values,
        memory,
        every,
        *[term.reshape((2, 2, 2, term.shape[0] // 8, term.shape[1])) for term in terms],
        w_qkv,
        attended,
        log_totals,
        table,
    )


class Line:
    def __init__(self, place, seg, memory, spans, refs):
        self.place, self.seg, self.memory, self.spans = place, seg, memory, spans
        self.runs = len(spans)
        self.sent, self.received, self.core_sent, self.core_received = refs

    def span(self, run):
        return self.spans[run]

    def there(self, way, step):
        return self.place.z >= step if way == 0 else self.place.z + step <= 3

    def goes(self, way, step):
        has = self.there(way, step - 1)
        return jnp.logical_and(has, self.place.z <= 2 if way == 0 else self.place.z >= 1)

    def index(self, way, step):
        return self.seg - 2 * step if way == 0 else self.seg + 2 * step

    def hop(self, way, step, run):
        name = self.index(way, step - 1)
        target = self.memory.at[name, self.span(run), :]
        slot = (way * 3 + step - 1) * self.runs + run
        seg, seq = lax.axis_index("seg"), lax.axis_index("seq")
        return pltpu.make_async_remote_copy(
            src_ref=target,
            dst_ref=target,
            send_sem=self.sent.at[slot],
            recv_sem=self.received.at[slot],
            device_id=(seg + 2 - 4 * way, seq),
            device_id_type=pl.DeviceIdType.MESH,
        )

    def arrival(self, way, step, run):
        target = self.memory.at[self.index(way, step), self.span(run), :]
        slot = (way * 3 + step - 1) * self.runs + run
        return pltpu.make_async_remote_copy(
            src_ref=target,
            dst_ref=target,
            send_sem=self.sent.at[slot],
            recv_sem=self.received.at[slot],
            device_id=self.place.peer["core"],
            device_id_type=pl.DeviceIdType.MESH,
        )

    def share(self, way, step, run):
        name = self.index(way, step)
        target = self.memory.at[name, self.span(run), :]
        slot = (way * 3 + step) * self.runs + run
        return pltpu.make_async_remote_copy(
            src_ref=target,
            dst_ref=target,
            send_sem=self.core_sent.at[slot],
            recv_sem=self.core_received.at[slot],
            device_id=self.place.peer["core"],
            device_id_type=pl.DeviceIdType.MESH,
        )

    def start(self, run):
        for way in range(2):

            @pl.when(self.goes(way, 1))
            def _(way=way):
                self.hop(way, 1, run).start()

        self.share(0, 0, run).start()

    def advance(self, step, run):
        for way in range(2):

            @pl.when(self.there(way, step))
            def _(way=way):
                self.arrival(way, step, run).wait_recv()

            if step < 3:

                @pl.when(self.goes(way, step + 1))
                def _(way=way):
                    self.hop(way, step + 1, run).start()

            @pl.when(self.there(way, step))
            def _(way=way):
                self.share(way, step, run).start()

    def finish(self):
        for run in range(self.runs):
            self.share(0, 0, run).wait()
            for way in range(2):
                for step in range(1, 4):

                    @pl.when(self.there(way, step))
                    def _(way=way, step=step, run=run):
                        self.share(way, step, run).wait()

                    @pl.when(self.goes(way, step))
                    def _(way=way, step=step, run=run):
                        self.hop(way, step, run).wait_send()


def front_kernel(
    heads,
    flag_ref,
    source_ref,
    x_ref,
    mem_k_ref,
    mem_v_ref,
    w_hbm,
    table_ref,
    every_ref,
    chosen_ref,
    attended_ref,
    q_ref,
    k_ref,
    v_ref,
    low_ref,
    log_ref,
    w_ref,
    rows,
    memory,
    listed,
    mix_ref,
    max_ref,
    sum_ref,
    trade_sent,
    trade_received,
    rows_sent,
    rows_received,
    line_sent,
    line_received,
    core_sent,
    core_received,
    back_sent,
    back_received,
    local,
):
    place = Place()
    seg, seq = lax.axis_index("seg"), lax.axis_index("seq")
    width = heads * HEAD_DIM
    count = mem_k_ref.shape[0]
    tokens, depth = x_ref.shape
    across = {"x": seq + 1 - 2 * place.x, "y": seq + 2 - 4 * place.y, "xy": 3 - seq}

    def remote(source, target, sent, received, slot, peer):
        return pltpu.make_async_remote_copy(
            src_ref=source,
            dst_ref=target,
            send_sem=sent.at[slot],
            recv_sem=received.at[slot],
            device_id=place.peer[peer],
            device_id_type=pl.DeviceIdType.MESH,
        )

    def columns(owner, start=0):
        return pl.ds(pl.multiple_of(start + owner * width, HEAD_DIM), width)

    def seat(owner):
        return pl.ds(pl.multiple_of(owner * count, 16), count)

    def owner_at(turn):
        low, high = lax.rem(turn, 2), lax.div(turn, 2)
        x = place.x + low - 2 * place.x * low
        y = place.y + high - 2 * place.y * high
        return 2 * y + x

    def block_rows(block):
        return pl.ds(pl.multiple_of(block * tokens, 16), tokens)

    peers = ("x", "y", "xy")
    trades = []
    for number, peer in enumerate(peers):
        for kind, source in enumerate((mem_k_ref, mem_v_ref)):
            lanes = pl.ds(kind * width, width)
            trades.append(
                remote(
                    source.at[:, columns(across[peer])],
                    memory.at[seg, seat(seq), lanes],
                    trade_sent,
                    trade_received,
                    2 * number + kind,
                    peer,
                )
            )
    keeps = [
        pltpu.make_async_copy(
            source.at[:, columns(seq)],
            memory.at[seg, seat(seq), pl.ds(kind * width, width)],
            local.at[kind],
        )
        for kind, source in enumerate((mem_k_ref, mem_v_ref))
    ]
    half = depth // 2
    left, right = pl.ds(0, half), pl.ds(half, half)
    load = pltpu.make_async_copy(x_ref, rows.at[seq], local.at[2])
    loads = weight_copies(w_hbm, w_ref, seq, local, 3)
    direct = [
        remote(x_ref.at[:, left], rows.at[seq, :, left], rows_sent, rows_received, 0, "x"),
        remote(x_ref.at[:, right], rows.at[seq, :, right], rows_sent, rows_received, 1, "y"),
        remote(x_ref.at[:, right], rows.at[seq, :, right], rows_sent, rows_received, 2, "x"),
        remote(x_ref.at[:, left], rows.at[seq, :, left], rows_sent, rows_received, 3, "y"),
    ]
    onward = [
        remote(
            rows.at[across["x"], :, left], rows.at[across["x"], :, left], rows_sent, rows_received, 4, "y"
        ),
        remote(
            rows.at[across["y"], :, right], rows.at[across["y"], :, right], rows_sent, rows_received, 5, "x"
        ),
    ]
    line = Line(
        place,
        seg,
        memory,
        [seat(owner) for owner in (seq, across["x"], across["y"], across["xy"])],
        (line_sent, line_received, core_sent, core_received),
    )
    keep_rows = pltpu.make_async_copy(rows, every_ref, local.at[6])
    run_rows = memory.shape[1] // 2
    keep_chosen = []
    for run in range(2):
        span, lanes = pl.ds(run * run_rows, run_rows), pl.ds(2 * run * width, 2 * width)
        keep_chosen.append(
            pltpu.make_async_copy(memory.at[seg, span, :], chosen_ref.at[0, :, lanes], local.at[7 + run])
        )
        keep_chosen.append(
            pltpu.make_async_copy(
                listed.at[:, span, :],
                chosen_ref.at[pl.ds(1, listed.shape[0]), :, lanes],
                local.at[9 + run],
            )
        )
    returns = [
        remote(
            low_ref.at[block_rows(across[peer]), :],
            attended_ref.at[:, columns(seq)],
            back_sent,
            back_received,
            slot,
            peer,
        )
        for slot, peer in enumerate(peers)
    ]
    keep_attended = pltpu.make_async_copy(
        low_ref.at[block_rows(seq), :], attended_ref.at[:, columns(seq)], local.at[11]
    )

    def project_rows(owner):
        block = rows[owner]
        span = block_rows(owner)
        cosine, sine = turn_factors(table_ref[span, :])
        scale = SCORE_SCALE / LN2
        queries = product(block, w_ref[:, :width])
        keys = product(block, w_ref[:, width : 2 * width])
        for head in range(heads):
            lanes = slice(head * HEAD_DIM, (head + 1) * HEAD_DIM)
            q_ref[span, lanes] = turn_block(
                queries[:, lanes], cosine * scale, sine * (-scale)
            ).astype(jnp.bfloat16)
            k_ref[span, lanes] = turn_block(keys[:, lanes], cosine, -sine).astype(jnp.bfloat16)
        v_ref[span, :] = product(block, w_ref[:, 2 * width :]).astype(jnp.bfloat16)

    def head_lanes(head, start=0):
        return pl.ds(pl.multiple_of(start + head * HEAD_DIM, HEAD_DIM), HEAD_DIM)

    def keep(span, lanes, row_max, row_sum, mixed):
        mix_ref[span, lanes] = mixed
        max_ref[span, lanes] = jnp.broadcast_to(row_max, mixed.shape)
        sum_ref[span, lanes] = jnp.broadcast_to(row_sum, mixed.shape)

    def own_rows(block):
        def turn(head, carry):
            lanes = head_lanes(head)
            span = pl.ds(block * tokens, tokens)
            pairs = [
                (k_ref[pl.ds(n * tokens, tokens), lanes], v_ref[pl.ds(n * tokens, tokens), lanes])
                for n in range(block + 1)
            ]
            keep(span, lanes, *attend(q_ref[span, lanes], pairs, True, None))
            return carry

        lax.fori_loop(0, heads, turn, 0)

    closed = (1 - flag_ref[seg]).astype(jnp.float32) * 1e30

    def carried(span, lanes):
        return max_ref[span, lanes][:, :1], sum_ref[span, lanes][:, :1], mix_ref[span, lanes]

    def own_memory(first, last):
        def turn(index, carry):
            head = lax.rem(index, heads)
            lanes, span = head_lanes(head), block_rows(lax.div(index, heads))
            pair = (memory[seg, :, lanes], memory[seg, :, head_lanes(head, width)])
            keep(span, lanes, *attend(q_ref[span, lanes], [pair], False, carried(span, lanes), closed))
            return carry

        lax.fori_loop(first * heads, last * heads, turn, 0)

    barrier = pltpu.get_barrier_semaphore()

    def hail(device):
        pl.semaphore_signal(barrier, inc=1, device_id=device, device_id_type=pl.DeviceIdType.MESH)

    for copy in keeps + [load] + loads:
        copy.start()
    for peer in ("x", "y", "xy", "core"):
        hail(place.peer[peer])
    below, above = place.z >= 1, place.z <= 2

    @pl.when(below)
    def _():
        hail((seg - 2, seq))

    @pl.when(above)
    def _():
        hail((seg + 2, seq))

    pl.semaphore_wait(barrier, 4 + below.astype(jnp.int32) + above.astype(jnp.int32))

    for copy in trades + direct:
        copy.start()
    for copy in keeps:
        copy.wait()
    line.start(0)
    load.wait()
    for copy in loads:
        copy.wait()
    project_rows(seq)
    for number in range(3):
        for kind in range(2):
            trades[2 * number + kind].wait_recv()
        line.start(number + 1)
        line.advance(1, number)
    direct[0].wait_recv()
    direct[1].wait_recv()
    for copy in onward:
        copy.start()
    line.advance(1, 3)
    line.advance(2, 0)
    direct[2].wait_recv()
    direct[3].wait_recv()
    project_rows(across["x"])
    line.advance(2, 1)
    project_rows(across["y"])
    line.advance(2, 2)
    for copy in onward:
        copy.wait_recv()
    project_rows(3 - seq)
    keep_rows.start()
    line.advance(2, 3)
    own_rows(0)
    own_rows(1)
    line.advance(3, 0)
    own_rows(2)
    line.advance(3, 1)
    own_rows(3)
    line.advance(3, 2)
    own_memory(0, 2)
    line.advance(3, 3)
    own_memory(2, 4)
    line.finish()
    for n in range(listed.shape[0]):
        listed[n] = memory[source_ref[seg, n]]

    def unit(index, carry):
        turn, head = lax.div(index, heads), lax.rem(index, heads)

        @pl.when(index == heads // 2)
        def _():
            for copy in keep_chosen:
                copy.start()

        for number in range(3):

            @pl.when(index == heads * (3 - number))
            def _(number=number):
                returns[number].start()

        lanes, span = head_lanes(head), block_rows(owner_at(3 - turn))
        pairs = [
            (listed[n, :, lanes], listed[n, :, head_lanes(head, width)])
            for n in range(listed.shape[0])
        ]
        row_max, row_sum, mixed = attend(
            q_ref[span, lanes], pairs, False, carried(span, lanes), closed
        )
        low_ref[span, lanes] = (mixed * (1.0 / row_sum)).astype(jnp.bfloat16)
        log_ref[span, lanes] = jnp.broadcast_to(row_max + jnp.log2(row_sum), mixed.shape)
        return carry

    lax.fori_loop(0, 4 * heads, unit, 0)
    keep_attended.start()
    for copy in returns:
        copy.wait()
    for copy in keep_chosen + [keep_rows, keep_attended]:
        copy.wait()
    for copy in trades + direct + onward:
        copy.wait_send()


def front(
    flags, sources, first_low, mem_keys, mem_values, w_qkv, table, seg_size, seq_size, collective_id
):
    tokens, depth = first_low.shape
    length = tokens * seq_size
    width = depth // seq_size
    count = mem_keys.shape[0] * seq_size
    slots = sources.shape[1]
    anywhere = pl.BlockSpec(memory_space=pl.ANY)
    inside = pl.BlockSpec(memory_space=pltpu.VMEM)
    scalars = pl.BlockSpec(memory_space=pltpu.SMEM)
    low = jnp.bfloat16
    shape = jax.ShapeDtypeStruct
    dma = pltpu.SemaphoreType.DMA
    return pl.pallas_call(
        functools.partial(front_kernel, width // HEAD_DIM),
        in_specs=[scalars] * 2 + [anywhere] * 4 + [inside],
        out_specs=[anywhere] * 3 + [inside] * 5,
        out_shape=[
            shape((seq_size, tokens, depth), low),
            shape((slots + 1, count // 2, 4 * width), low),
            shape((tokens, depth), low),
        ]
        + [shape((length, width), low)] * 4
        + [shape((length, width), jnp.float32)],
        scratch_shapes=[
            pltpu.VMEM((depth, 3 * width), low),
            pltpu.VMEM((seq_size, tokens, depth), low),
            pltpu.VMEM((seg_size, count, 2 * width), low),
            pltpu.VMEM((slots, count, 2 * width), low),
        ]
        + [pltpu.VMEM((length, width), jnp.float32)] * 3
        + [dma((6,))] * 4
        + [dma((24,))] * 2
        + [dma((28,))] * 2
        + [dma((3,))] * 2
        + [dma((12,))],
        compiler_params=pltpu.CompilerParams(
            collective_id=collective_id, has_side_effects=True, vmem_limit_bytes=VMEM_BYTES
        ),
        name="front",
    )(flags, sources, first_low, mem_keys, mem_values, w_qkv, table)


def norm_input_grad(values, inverse, norm_gain, upstream):
    weighted = upstream * norm_gain
    inner_mean = jnp.mean(weighted * values, axis=-1, keepdims=True)
    return inverse * weighted - inverse * inverse * inverse * values * inner_mean


def dense_kernel(
    x_ref,
    g_ref,
    attended_ref,
    out_ref,
    gain_ref,
    gate_ref,
    up_ref,
    down_ref,
    output_ref,
    grad_ref,
    grad_attended_ref,
    term_down,
    term_gate,
    term_up,
    term_out,
    residual_ref,
    second,
    second_t,
    total,
    grad_second,
):
    index = pl.program_id(0)
    low = jnp.bfloat16

    @pl.when(index == 0)
    def _():
        residual = x_ref[...].astype(jnp.float32) + product(attended_ref[...], out_ref[...])
        residual_ref[...] = residual
        second_low = norm_forward(residual, gain_ref[...])[0].astype(low)
        second[...] = second_low
        second_t[...] = second_low.T

    gate, up = product(second[...], gate_ref[...]), product(second[...], up_ref[...])
    grad_hidden = product_nt(g_ref[...], down_ref[...])
    sigmoid_gate = jax.nn.sigmoid(gate)
    activated = gate * sigmoid_gate
    hidden = (activated * up).astype(low)
    grad_gate = (grad_hidden * up * sigmoid_gate * (1.0 + gate * (1.0 - sigmoid_gate))).astype(low)
    grad_up = (grad_hidden * activated).astype(low)
    term_down[...] = product_tn(hidden, g_ref[...]).astype(low)
    term_gate[...] = product(second_t[...], grad_gate).astype(low)
    term_up[...] = product(second_t[...], grad_up).astype(low)
    part = product(hidden, down_ref[...])
    grad_part = product_nt(grad_gate, gate_ref[...]) + product_nt(grad_up, up_ref[...])

    @pl.when(index == 0)
    def _():
        total[...] = part
        grad_second[...] = grad_part

    @pl.when(index > 0)
    def _():
        total[...] += part
        grad_second[...] += grad_part

    @pl.when(index == pl.num_programs(0) - 1)
    def _():
        residual = residual_ref[...]
        output_ref[...] = (residual + total[...]).astype(low)
        inverse = lax.rsqrt(jnp.mean(residual * residual, axis=-1, keepdims=True) + epsilon)
        grad = norm_input_grad(residual, inverse, gain_ref[...], grad_second[...])
        grad = grad + g_ref[...].astype(jnp.float32)
        grad_ref[...] = grad
        grad_low = grad.astype(low)
        term_out[...] = product_tn(attended_ref[...], grad_low).astype(low)
        grad_attended_ref[...] = product_nt(grad_low, out_ref[...]).astype(low)


def dense(x, grads, attended, w_out, gain, w_gate, w_up, w_down, tile=256):
    tokens, depth = x.shape
    hidden = w_gate.shape[1]
    tile = math.gcd(tile, hidden)
    low = jnp.bfloat16
    shape = jax.ShapeDtypeStruct

    def whole(rows, columns):
        return pl.BlockSpec((rows, columns), lambda j: (0, 0))

    across = pl.BlockSpec((depth, tile), lambda j: (0, j))
    down = pl.BlockSpec((tile, depth), lambda j: (j, 0))
    activation = whole(tokens, depth)
    return pl.pallas_call(
        dense_kernel,
        grid=(hidden // tile,),
        in_specs=[activation] * 3 + [whole(depth, depth), whole(1, depth), across, across, down],
        out_specs=[activation] * 3 + [down, across, across, whole(depth, depth)],
        out_shape=[
            shape((tokens, depth), low),
            shape((tokens, depth), jnp.float32),
            shape((tokens, depth), low),
            shape((hidden, depth), low),
            shape((depth, hidden), low),
            shape((depth, hidden), low),
            shape((depth, depth), low),
        ],
        scratch_shapes=[
            pltpu.VMEM((tokens, depth), jnp.float32),
            pltpu.VMEM((tokens, depth), low),
            pltpu.VMEM((depth, tokens), low),
            pltpu.VMEM((tokens, depth), jnp.float32),
            pltpu.VMEM((tokens, depth), jnp.float32),
        ],
        compiler_params=pltpu.CompilerParams(vmem_limit_bytes=VMEM_BYTES),
        cost_estimate=pl.CostEstimate(
            flops=16 * tokens * depth * hidden + 6 * tokens * depth * depth,
            transcendentals=tokens * hidden,
            bytes_accessed=12 * depth * hidden + 20 * tokens * depth,
        ),
        name="dense",
    )(x, grads, attended, w_out, gain, w_gate, w_up, w_down)


def tail_kernel(
    down_hbm,
    gate_hbm,
    up_hbm,
    out_hbm,
    qkv_hbm,
    first_hbm,
    x_hbm,
    grad_hbm,
    w_hbm,
    w_gate_hbm,
    w_up_hbm,
    gain1_ref,
    gain2_ref,
    input_out,
    norm1_ref,
    norm2_ref,
    qkv_out,
    out_out,
    gate_out,
    up_out,
    down_out,
    down,
    gate,
    up,
    out,
    qkv,
    first,
    x,
    grad,
    w,
    w_gate,
    w_up,
    input_wide,
    qkv_wide,
    out_wide,
    gate_wide,
    up_wide,
    down_wide,
    dots1,
    dots2,
    loaded,
    stored,
):
    seq = lax.axis_index("seq")
    count = gate.shape[0]
    block = pl.ds(pl.multiple_of(seq * count, count), count)
    pairs = [
        (gate_hbm, gate),
        (w_gate_hbm.at[block, :], w_gate),
        (up_hbm, up),
        (w_up_hbm.at[block, :], w_up),
        (down_hbm, down),
        (out_hbm, out),
        (w_hbm.at[block, :], w),
        (qkv_hbm, qkv),
        (first_hbm, first),
        (x_hbm, x),
        (grad_hbm, grad),
    ]
    loads = [
        pltpu.make_async_copy(source, target, loaded.at[n]) for n, (source, target) in enumerate(pairs)
    ]
    wides = [gate_wide, up_wide, down_wide, out_wide, qkv_wide, input_wide]
    outs = [gate_out, up_out, down_out, out_out, qkv_out, input_out]
    stores = [
        pltpu.make_async_copy(source, target, stored.at[n])
        for n, (source, target) in enumerate(zip(wides, outs))
    ]
    for copy in loads:
        copy.start()

    def by_rows(count, step, body):
        def turn(index, carry):
            body(pl.ds(pl.multiple_of(index * step, step), step))
            return carry

        lax.fori_loop(0, count // step, turn, 0)

    def widen(former, latter):
        def body(rows):
            latter[rows, :] = former[rows, :].astype(jnp.float32)

        by_rows(former.shape[0], 16, body)

    def dot_rows(values, weights):
        return lane_fold(jnp.add, values * weights.astype(jnp.float32), None)

    def gate_body(rows):
        values = gate[rows, :].astype(jnp.float32)
        gate_wide[rows, :] = values
        dots2[rows, :] = dot_rows(values, w_gate[rows, :])

    def up_body(rows):
        values = up[rows, :].astype(jnp.float32)
        up_wide[rows, :] = values
        dots2[rows, :] += dot_rows(values, w_up[rows, :])

    def qkv_body(rows):
        values = qkv[rows, :].astype(jnp.float32)
        qkv_wide[rows, :] = values
        dots1[rows, :] = dot_rows(values, w[rows, :])

    def gain_grads(dots, gain_ref):
        columns = jnp.broadcast_to(jnp.sum(dots[...], axis=1, keepdims=True), dots.shape)
        return columns.T[:1, :] / gain_ref[:, block]

    def wait(*numbers):
        for number in numbers:
            loads[number].wait()

    wait(0, 1)
    by_rows(count, 16, gate_body)
    stores[0].start()
    wait(2, 3)
    by_rows(count, 16, up_body)
    stores[1].start()
    norm2_ref[...] = gain_grads(dots2, gain2_ref)
    wait(4)
    widen(down, down_wide)
    stores[2].start()
    wait(5)
    widen(out, out_wide)
    stores[3].start()
    wait(6, 7)
    by_rows(count, 16, qkv_body)
    stores[4].start()
    norm1_ref[...] = gain_grads(dots1, gain1_ref)
    wait(8, 9, 10)

    def input_body(rows):
        values = x[rows, :].astype(jnp.float32)
        inverse = lax.rsqrt(jnp.mean(values * values, axis=-1, keepdims=True) + epsilon)
        input_wide[rows, :] = grad[rows, :] + norm_input_grad(
            values, inverse, gain1_ref[...], first[rows, :].astype(jnp.float32)
        )

    by_rows(x.shape[0], 32, input_body)
    stores[5].start()
    for copy in stores:
        copy.wait()


def tail(sums, first, x, grad, w_qkv, w_gate, w_up, gain1, gain2):
    down, gate, up, out, qkv = sums
    tokens, depth = x.shape
    count = gate.shape[0]
    low, wide = jnp.bfloat16, jnp.float32
    anywhere = pl.BlockSpec(memory_space=pl.ANY)
    inside = pl.BlockSpec(memory_space=pltpu.VMEM)
    shapes = [(tokens, depth), qkv.shape, out.shape, gate.shape, up.shape, down.shape]
    results = [shapes[0], (1, count), (1, count)] + shapes[1:]
    return pl.pallas_call(
        tail_kernel,
        in_specs=[anywhere] * 11 + [inside] * 2,
        out_specs=[anywhere] + [inside] * 2 + [anywhere] * 5,
        out_shape=[jax.ShapeDtypeStruct(shape, wide) for shape in results],
        scratch_shapes=[pltpu.VMEM(total.shape, low) for total in sums]
        + [
            pltpu.VMEM(first.shape, low),
            pltpu.VMEM(x.shape, low),
            pltpu.VMEM(x.shape, wide),
            pltpu.VMEM(qkv.shape, low),
            pltpu.VMEM(gate.shape, low),
            pltpu.VMEM(up.shape, low),
        ]
        + [pltpu.VMEM(shape, wide) for shape in shapes]
        + [pltpu.VMEM((count, HEAD_DIM), wide)] * 2
        + [pltpu.SemaphoreType.DMA((11,)), pltpu.SemaphoreType.DMA((6,))],
        compiler_params=pltpu.CompilerParams(vmem_limit_bytes=VMEM_BYTES),
        name="tail",
    )(*sums, first, x, grad, w_qkv, w_gate, w_up, gain1, gain2)


def head_plan(
    seg_size,
    seq_size,
    layer_input,
    output_grad,
    norm1_gain,
    norm2_gain,
    w_qkv,
    w_out,
    w_gate,
    w_up,
    w_down,
    mem_keys,
    mem_values,
    memory_flags,
    sources,
):
    tokens = layer_input.shape[1]
    length = tokens * seq_size
    width = D // seq_size
    inputs = layer_input[0].astype(jnp.float32)
    first_low = norm_forward(inputs, norm1_gain)[0].astype(jnp.bfloat16)
    table = turn_table(length)
    every_low, chosen_memory, attended_low, queries, keys, values, heads_low, log_totals = front(
        memory_flags, sources, first_low, mem_keys[0], mem_values[0], w_qkv, table, seg_size, seq_size, 1
    )

    output, grad_residual, grad_attended, term_down, term_gate, term_up, term_out = dense(
        layer_input[0], output_grad[0], attended_low, w_out, norm2_gain[None], w_gate, w_up, w_down
    )
    *sums, qkv_rows, first_rows = back(
        memory_flags,
        grad_attended,
        queries,
        keys,
        values,
        chosen_memory,
        every_low,
        [term_down, term_gate, term_up, term_out],
        w_qkv,
        heads_low,
        log_totals,
        table,
        2,
    )
    sums = [total.reshape(2 * total.shape[1], total.shape[2]) for total in sums]
    sums.append(qkv_rows.reshape(width, 3 * D))
    input_grad, grad_norm1, grad_norm2, grad_qkv, grad_out, grad_gate, grad_up, grad_down = tail(
        sums, first_rows, layer_input[0], grad_residual, w_qkv, w_gate, w_up, norm1_gain[None], norm2_gain[None]
    )
    return (
        output[None],
        input_grad[None],
        grad_norm1[0],
        grad_norm2[0],
        grad_qkv,
        grad_out,
        grad_gate,
        grad_up,
        grad_down,
    )


def solution(mesh):
    seq_size = mesh.shape["seq"]
    heads_fit = seq_size == 4 and mesh.shape["seg"] == 8
    plan = functools.partial(head_plan, mesh.shape["seg"], seq_size) if heads_fit else general_plan
    placed = (
        P("seg", "seq", None),
        P("seg", "seq", None),
        P(),
        P(),
        P(),
        P(),
        P(),
        P(),
        P(),
        P("seg", "seq", None),
        P("seg", "seq", None),
        P(),
        P(),
    )
    return jax.shard_map(
        plan,
        mesh=mesh,
        in_specs=placed,
        out_specs=(
            P("seg", "seq", None),
            P("seg", "seq", None),
            P("seq"),
            P("seq"),
            P("seq", None),
            P("seq", None),
            P("seq", None),
            P("seq", None),
            P("seq", None),
        ),
        check_vma=False,
    )
```

```python
import functools
import math

import jax
import jax.numpy as jnp
import numpy as np
from jax import lax
from jax.experimental import pallas as pl
from jax.experimental.pallas import tpu as pltpu
from jax.sharding import PartitionSpec as P

D = 1024
HEADS = 8
HEAD_DIM = 128


masked_score = -1e30
epsilon = 1e-06
rotary_base = 10000.0


def product(former, latter):
    return jnp.dot(former, latter, preferred_element_type=jnp.float32)


def product_nt(former, latter):
    return lax.dot_general(
        former, latter, (((1,), (1,)), ((), ())), preferred_element_type=jnp.float32
    )


def product_tn(former, latter):
    return lax.dot_general(
        former, latter, (((0,), (0,)), ((), ())), preferred_element_type=jnp.float32
    )


def norm_forward(values, norm_gain):
    inverse = lax.rsqrt(jnp.mean(values * values, axis=-1, keepdims=True) + epsilon)
    return (values * inverse * norm_gain, inverse)


def norm_backward(values, inverse, norm_gain, upstream):
    weighted = upstream * norm_gain
    inner_mean = jnp.mean(weighted * values, axis=-1, keepdims=True)
    grad_values = inverse * weighted - inverse * inverse * inverse * values * inner_mean
    grad_gain = jnp.sum(upstream * values * inverse, axis=0)
    return (grad_values, grad_gain)


def turn_tables(positions):
    half_dim = HEAD_DIM // 2
    exponent = -2.0 * jnp.arange(half_dim, dtype=jnp.float32) / HEAD_DIM
    angles = positions[:, None] * jnp.power(rotary_base, exponent)[None, :]
    angles = jnp.concatenate([angles, angles], axis=1)
    return (jnp.cos(angles)[:, None, :], jnp.sin(angles)[:, None, :])


def rotate(matrix, cosine_table, sine_table, direction):
    row_count = matrix.shape[0]
    half_dim = HEAD_DIM // 2
    shaped = matrix.reshape(row_count, HEADS, HEAD_DIM)
    turned = jnp.concatenate([-shaped[..., half_dim:], shaped[..., :half_dim]], axis=-1)
    return (shaped * cosine_table + direction * turned * sine_table).reshape(
        row_count, HEADS * HEAD_DIM
    )


def general_plan(
    layer_input,
    output_grad,
    norm1_gain,
    norm2_gain,
    w_qkv,
    w_out,
    w_gate,
    w_up,
    w_down,
    mem_keys,
    mem_values,
    memory_flags,
    sources,
):
    seg_index = lax.axis_index("seg")
    seq_index = lax.axis_index("seq")
    tokens = layer_input.shape[1]
    score_scale = HEAD_DIM ** (-0.5)
    flag_on = lax.dynamic_index_in_dim(memory_flags, seg_index, 0, keepdims=False) > 0
    listed = lax.dynamic_index_in_dim(sources, seg_index, 0, keepdims=False)
    picked = jnp.concatenate([jnp.reshape(seg_index, (1,)), listed])
    every_keys, every_values = (
        lax.all_gather(mem_keys, "seg", axis=0, tiled=True),
        lax.all_gather(mem_values, "seg", axis=0, tiled=True),
    )
    chosen_keys = jnp.take(every_keys, picked, axis=0)
    chosen_values = jnp.take(every_values, picked, axis=0)
    memory_keys, memory_values = (
        lax.all_gather(chosen_keys, "seq", axis=1, tiled=True),
        lax.all_gather(chosen_values, "seq", axis=1, tiled=True),
    )
    memory_key_blocks = memory_keys.reshape(-1, tokens, HEADS, HEAD_DIM)
    memory_value_blocks = memory_values.reshape(-1, tokens, HEADS, HEAD_DIM)
    memory_blocks = memory_key_blocks.shape[0]
    inputs = layer_input[0].astype(jnp.float32)
    first_norm, first_inverse = norm_forward(inputs, norm1_gain)
    first_low = first_norm.astype(jnp.bfloat16)
    projected = product(first_low, w_qkv)
    positions = seq_index * tokens + lax.iota(jnp.int32, tokens)
    cosine_table, sine_table = turn_tables(positions.astype(jnp.float32))
    queries = rotate(projected[:, :D], cosine_table, sine_table, 1.0).astype(jnp.bfloat16)
    own_keys = rotate(projected[:, D : 2 * D], cosine_table, sine_table, 1.0).astype(jnp.bfloat16)
    own_values = projected[:, 2 * D :].astype(jnp.bfloat16)
    all_keys, all_values = (
        lax.all_gather(own_keys, "seq", axis=0, tiled=True),
        lax.all_gather(own_values, "seq", axis=0, tiled=True),
    )
    key_blocks = all_keys.reshape(-1, tokens, HEADS, HEAD_DIM)
    value_blocks = all_values.reshape(-1, tokens, HEADS, HEAD_DIM)
    query_heads = queries.reshape(tokens, HEADS, HEAD_DIM)
    memory_open = jnp.broadcast_to(flag_on, (tokens, tokens))
    own_count = seq_index + 1
    key_offsets = lax.iota(jnp.int32, tokens)

    def own_open(block):
        return (block * tokens + key_offsets)[None, :] <= positions[:, None]

    def block_scores(key_block, open_mask):
        raw = (
            jnp.einsum("qhd,khd->hqk", query_heads, key_block, preferred_element_type=jnp.float32)
            * score_scale
        )
        return jnp.where(open_mask[None], raw, masked_score)

    def sweep(step, carry):

        def memory_turn(block, state):
            return step(
                state,
                block,
                memory_key_blocks[block],
                memory_value_blocks[block],
                memory_open,
                False,
            )

        def own_turn(block, state):
            return step(state, block, key_blocks[block], value_blocks[block], own_open(block), True)

        carry = lax.fori_loop(0, memory_blocks, memory_turn, carry)
        return lax.fori_loop(0, own_count, own_turn, carry)

    def max_step(carry, block, key_block, value_block, open_mask, own):
        row_max, row_sum = carry
        scores = block_scores(key_block, open_mask)
        new_max = jnp.maximum(row_max, jnp.max(scores, axis=2))
        row_sum = row_sum * jnp.exp(row_max - new_max) + jnp.sum(
            jnp.exp(scores - new_max[..., None]), axis=2
        )
        return (new_max, row_sum)

    start_max = jnp.full((HEADS, tokens), masked_score, jnp.float32)
    row_max, row_sum = sweep(max_step, (start_max, jnp.zeros((HEADS, tokens), jnp.float32)))
    log_totals = row_max + jnp.log(row_sum)

    def mix_step(total, block, key_block, value_block, open_mask, own):
        weights_low = jnp.exp(block_scores(key_block, open_mask) - log_totals[..., None]).astype(
            jnp.bfloat16
        )
        return total + jnp.einsum(
            "hqk,khd->qhd", weights_low, value_block, preferred_element_type=jnp.float32
        )

    attended = sweep(mix_step, jnp.zeros((tokens, HEADS, HEAD_DIM), jnp.float32))
    attended_low = attended.reshape(tokens, D).astype(jnp.bfloat16)
    residual = inputs + product(attended_low, w_out)
    second_norm, second_inverse = norm_forward(residual, norm2_gain)
    second_low = second_norm.astype(jnp.bfloat16)
    gate_values = product(second_low, w_gate)
    up_values = product(second_low, w_up)
    sigmoid_gate = jax.nn.sigmoid(gate_values)
    activated = gate_values * sigmoid_gate
    hidden_low = (activated * up_values).astype(jnp.bfloat16)
    output = (residual + product(hidden_low, w_down)).astype(jnp.bfloat16)
    upstream = output_grad[0]
    grad_down = product_tn(hidden_low, upstream)
    grad_hidden = product_nt(upstream, w_down)
    grad_gate_low = (
        grad_hidden * up_values * sigmoid_gate * (1.0 + gate_values * (1.0 - sigmoid_gate))
    ).astype(jnp.bfloat16)
    grad_up_low = (grad_hidden * activated).astype(jnp.bfloat16)
    grad_gate = product_tn(second_low, grad_gate_low)
    grad_up = product_tn(second_low, grad_up_low)
    grad_second = product_nt(grad_gate_low, w_gate) + product_nt(grad_up_low, w_up)
    grad_residual, grad_norm2 = norm_backward(residual, second_inverse, norm2_gain, grad_second)
    grad_residual = grad_residual + upstream.astype(jnp.float32)
    residual_low = grad_residual.astype(jnp.bfloat16)
    grad_out = product_tn(attended_low, residual_low)
    grad_attended = product_nt(residual_low, w_out).astype(jnp.bfloat16)
    grad_heads = grad_attended.reshape(tokens, HEADS, HEAD_DIM)

    def probs_pair(key_block, value_block, open_mask):
        probs = jnp.exp(block_scores(key_block, open_mask) - log_totals[..., None])
        dprobs = jnp.einsum(
            "qhd,khd->hqk", grad_heads, value_block, preferred_element_type=jnp.float32
        )
        return (probs, dprobs)

    def delta_step(total, block, key_block, value_block, open_mask, own):
        probs, dprobs = probs_pair(key_block, value_block, open_mask)
        return total + jnp.sum(probs * dprobs, axis=2)

    delta_rows = sweep(delta_step, jnp.zeros((HEADS, tokens), jnp.float32))

    def grad_step(carry, block, key_block, value_block, open_mask, own):
        grad_query, key_terms, value_terms = carry
        probs, dprobs = probs_pair(key_block, value_block, open_mask)
        dscores = (probs * (dprobs - delta_rows[..., None])).astype(jnp.bfloat16)
        grad_query = grad_query + jnp.einsum(
            "hqk,khd->qhd", dscores, key_block, preferred_element_type=jnp.float32
        )
        if own:
            key_part = (
                jnp.einsum("hqk,qhd->khd", dscores, query_heads, preferred_element_type=jnp.float32)
                * score_scale
            )
            value_part = jnp.einsum(
                "hqk,qhd->khd",
                probs.astype(jnp.bfloat16),
                grad_heads,
                preferred_element_type=jnp.float32,
            )
            key_terms = lax.dynamic_update_index_in_dim(key_terms, key_part, block, 0)
            value_terms = lax.dynamic_update_index_in_dim(value_terms, value_part, block, 0)
        return (grad_query, key_terms, value_terms)

    term_shape = key_blocks.shape
    start_grads = (
        jnp.zeros((tokens, HEADS, HEAD_DIM), jnp.float32),
        jnp.zeros(term_shape, jnp.float32),
        jnp.zeros(term_shape, jnp.float32),
    )
    grad_query, key_terms, value_terms = sweep(grad_step, start_grads)
    grad_queries = (grad_query * score_scale).reshape(tokens, D)
    grad_keys, grad_values = (
        lax.psum_scatter(
            key_terms.astype(jnp.bfloat16), "seq", scatter_dimension=0, tiled=True
        ).astype(jnp.float32),
        lax.psum_scatter(
            value_terms.astype(jnp.bfloat16), "seq", scatter_dimension=0, tiled=True
        ).astype(jnp.float32),
    )
    grad_projected = jnp.concatenate(
        [
            rotate(grad_queries, cosine_table, sine_table, -1.0),
            rotate(grad_keys.reshape(tokens, D), cosine_table, sine_table, -1.0),
            grad_values.reshape(tokens, D),
        ],
        axis=1,
    ).astype(jnp.bfloat16)
    grad_qkv = product_tn(first_low, grad_projected)
    grad_first = product_nt(grad_projected, w_qkv)
    grad_inputs, grad_norm1 = norm_backward(inputs, first_inverse, norm1_gain, grad_first)
    input_grad = (grad_inputs + grad_residual)[None]
    shares = (
        lax.psum_scatter(
            grad_norm1.astype(jnp.bfloat16), "seq", scatter_dimension=0, tiled=True
        ).astype(jnp.float32),
        lax.psum_scatter(
            grad_norm2.astype(jnp.bfloat16), "seq", scatter_dimension=0, tiled=True
        ).astype(jnp.float32),
        lax.psum_scatter(
            grad_qkv.astype(jnp.bfloat16), "seq", scatter_dimension=0, tiled=True
        ).astype(jnp.float32),
        lax.psum_scatter(
            grad_out.astype(jnp.bfloat16), "seq", scatter_dimension=0, tiled=True
        ).astype(jnp.float32),
        lax.psum_scatter(
            grad_gate.astype(jnp.bfloat16), "seq", scatter_dimension=0, tiled=True
        ).astype(jnp.float32),
        lax.psum_scatter(
            grad_up.astype(jnp.bfloat16), "seq", scatter_dimension=0, tiled=True
        ).astype(jnp.float32),
        lax.psum_scatter(
            grad_down.astype(jnp.bfloat16), "seq", scatter_dimension=0, tiled=True
        ).astype(jnp.float32),
    )
    totals = (
        lax.psum(shares[0].astype(jnp.bfloat16), "seg").astype(jnp.float32),
        lax.psum(shares[1].astype(jnp.bfloat16), "seg").astype(jnp.float32),
        lax.psum(shares[2].astype(jnp.bfloat16), "seg").astype(jnp.float32),
        lax.psum(shares[3].astype(jnp.bfloat16), "seg").astype(jnp.float32),
        lax.psum(shares[4].astype(jnp.bfloat16), "seg").astype(jnp.float32),
        lax.psum(shares[5].astype(jnp.bfloat16), "seg").astype(jnp.float32),
        lax.psum(shares[6].astype(jnp.bfloat16), "seg").astype(jnp.float32),
    )
    return (
        output[None],
        input_grad,
        totals[0],
        totals[1],
        totals[2],
        totals[3],
        totals[4],
        totals[5],
        totals[6],
    )


VMEM_BYTES = 60 * 1024 * 1024
VMEM_MOST = 67043328
LN2 = math.log(2.0)
SCORE_SCALE = HEAD_DIM ** (-0.5)


def lane_fold(op, tile, running):
    for column in range(tile.shape[1] // HEAD_DIM):
        piece = tile[:, column * HEAD_DIM : (column + 1) * HEAD_DIM]
        running = piece if running is None else op(running, piece)
    return running


def causal(scores):
    rows = lax.broadcasted_iota(jnp.int32, scores.shape, 0)
    columns = lax.broadcasted_iota(jnp.int32, scores.shape, 1)
    return jnp.where(columns <= rows, scores, masked_score)


def attend(query, pairs, diagonal, carried, closed=0.0):
    every, lane_max = [], None
    for index, (keys, _) in enumerate(pairs):
        scores = product_nt(query, keys)
        if diagonal and index == len(pairs) - 1:
            scores = causal(scores)
        lane_max = lane_fold(jnp.maximum, scores, lane_max)
        every.append(scores)
    row_max = jnp.max(lane_max, axis=1, keepdims=True) - closed
    if carried is not None:
        row_max = jnp.maximum(row_max, carried[0])
    shift = row_max + closed
    lane_sum, mixed = None, None
    for scores, (_, values) in zip(every, pairs):
        probs = jnp.exp2(scores - shift)
        lane_sum = lane_fold(jnp.add, probs, lane_sum)
        part = product(probs.astype(jnp.bfloat16), values)
        mixed = part if mixed is None else mixed + part
    row_sum = jnp.sum(lane_sum, axis=1, keepdims=True)
    if carried is not None:
        shrink = jnp.exp2(carried[0] - row_max)
        row_sum = carried[1] * shrink + row_sum
        mixed = carried[2] * shrink + mixed
    return row_max, row_sum, mixed


def turn_block(matrix, cosine, sine):
    return matrix * cosine + pltpu.roll(matrix, HEAD_DIM // 2, 1) * sine


def turn_factors(both):
    swapped = pltpu.roll(both, HEAD_DIM // 2, 1)
    first = lax.broadcasted_iota(jnp.int32, both.shape, 1) < HEAD_DIM // 2
    return jnp.where(first, both, swapped), jnp.where(first, swapped, -both)


def turn_table(length, step=64):
    frequency = rotary_base ** (-2.0 * np.arange(HEAD_DIM // 2) / HEAD_DIM)
    coarse = np.arange(length // step)[:, None] * step * frequency
    fine = np.arange(step)[:, None] * frequency

    def pair(former, latter):
        return jnp.asarray(np.concatenate([former, latter], axis=1), jnp.float32)

    table = (
        pair(np.cos(coarse), np.sin(coarse))[:, None, :] * pair(np.cos(fine), np.cos(fine))[None]
        + pair(-np.sin(coarse), np.cos(coarse))[:, None, :] * pair(np.sin(fine), np.sin(fine))[None]
    )
    return table.reshape(length, HEAD_DIM)


LINK_RATE = {"core": 300e3, "x": 49e3, "y": 49e3, "z": 49e3}


class Place:
    def __init__(self):
        seg, seq = lax.axis_index("seg"), lax.axis_index("seq")
        self.core, self.z = lax.rem(seg, 2), lax.div(seg, 2)
        self.x, self.y = lax.rem(seq, 2), lax.div(seq, 2)
        odd = lax.rem(self.z, 2)
        self.inner = jnp.logical_or(self.z == 1, self.z == 2)
        self.outer = jnp.logical_not(self.inner)
        self.peer = {
            "core": (seg + 1 - 2 * self.core, seq),
            "x": (seg, seq + 1 - 2 * self.x),
            "y": (seg, seq + 2 - 4 * self.y),
            "xy": (seg, 3 - seq),
            "pair": (seg + 2 - 4 * odd, seq),
            "middle": (seg - 2 + 4 * odd, seq),
        }

    def greet(self, names):
        barrier = pltpu.get_barrier_semaphore()

        def hail(name):
            pl.semaphore_signal(
                barrier, inc=1, device_id=self.peer[name], device_id_type=pl.DeviceIdType.MESH
            )

        for name in names:
            hail(name)

        @pl.when(self.inner)
        def _():
            hail("middle")

        pl.semaphore_wait(barrier, len(names) + self.inner.astype(jnp.int32))


def add_into(total, addend, step=16):
    def turn(index, carry):
        rows = pl.ds(pl.multiple_of(index * step, step), step)
        total[rows, :] = total[rows, :] + addend[rows, :]
        return carry

    lax.fori_loop(0, total.shape[0] // step, turn, 0)


def add_to(result, former, latter, step=16):
    def turn(index, carry):
        rows = pl.ds(pl.multiple_of(index * step, step), step)
        result[rows, :] = former[rows, :] + latter[rows, :]
        return carry

    lax.fori_loop(0, result.shape[0] // step, turn, 0)


def weight_copies(whole, part, seq, semaphores, first):
    width = part.shape[1] // 3
    depth = whole.shape[1] // 3
    return [
        pltpu.make_async_copy(
            whole.at[:, pl.ds(pl.multiple_of(kind * depth + seq * width, HEAD_DIM), width)],
            part.at[:, pl.ds(kind * width, width)],
            semaphores.at[first + kind],
        )
        for kind in range(3)
    ]


class Chunk:
    def __init__(self, term, offset, rows, columns, gather=False):
        self.term, self.offset, self.rows, self.columns = term, offset, rows, columns
        self.gather = gather

    def scratch(self):
        rows, columns, half = self.rows, self.columns, self.columns // 2
        low = jnp.bfloat16
        four = pltpu.VMEM((2, 2, rows, columns), low)
        one = four if self.gather else pltpu.VMEM((rows, columns), low)
        last = pltpu.VMEM((rows, 4 * columns), low) if self.gather else one
        if self.gather:
            middle = [four]
        else:
            middle = [
                pltpu.VMEM((2, rows, half), low),
                pltpu.VMEM((2, rows, half), low),
                pltpu.VMEM((rows, half), low),
                pltpu.VMEM((rows, half), low),
            ]
        ends = [one, one, last] if self.gather else [one, one]
        return [four, four] + middle + ends + [
            pltpu.SemaphoreType.DMA((9,)),
            pltpu.SemaphoreType.DMA((9,)),
            pltpu.SemaphoreType.DMA((3,)),
        ]

    def bind(self, place, source, result, refs):
        self.place, self.source, self.result = place, source, result
        self.mine, self.core_in = refs[0], refs[1]
        ends = 3 if self.gather else 2
        self.middle = refs[2 : -3 - ends]
        self.z_last, self.z_second = refs[-4], refs[-5]
        self.z_first = refs[-6] if self.gather else self.z_last
        self.sent, self.received, self.local = refs[-3:]

    def remote(self, slot, source, target, peer):
        return pltpu.make_async_remote_copy(
            src_ref=source,
            dst_ref=target,
            send_sem=self.sent.at[slot],
            recv_sem=self.received.at[slot],
            device_id=self.place.peer[peer],
            device_id_type=pl.DeviceIdType.MESH,
        )

    def core_copy(self):
        rows = pl.ds(self.offset, self.rows)
        return self.remote(
            0, self.source.at[:, :, 1 - self.place.core, rows, :], self.core_in, "core"
        )

    def load(self):
        rows = pl.ds(self.offset, self.rows)
        return pltpu.make_async_copy(
            self.source.at[:, :, self.place.core, rows, :], self.mine, self.local.at[0]
        )

    def halves(self):
        half = self.columns // 2
        return pl.ds(0, half), pl.ds(half, half)

    def wide_copies(self):
        p, (left, right) = self.place, self.halves()
        if self.gather:
            return [
                self.remote(1, self.mine.at[p.y, 1 - p.x], self.middle[0].at[p.y, p.x], "x"),
                self.remote(2, self.mine.at[1 - p.y, p.x], self.middle[0].at[p.y, p.x], "y"),
                self.remote(3, self.mine.at[1 - p.y, 1 - p.x], self.middle[0].at[p.y, p.x], "xy"),
            ]
        return [
            self.remote(1, self.mine.at[:, 1 - p.x, :, left], self.middle[0], "x"),
            self.remote(2, self.mine.at[1 - p.y, :, :, right], self.middle[1], "y"),
        ]

    def narrow_copies(self):
        p, (left, right) = self.place, self.halves()
        return [
            self.remote(3, self.mine.at[1 - p.y, p.x, :, left], self.middle[2], "y"),
            self.remote(4, self.mine.at[p.y, 1 - p.x, :, right], self.middle[3], "x"),
        ]

    def summed(self):
        return self.middle[0] if self.gather else self.mine.at[self.place.y, self.place.x]

    def pair_copy(self):
        return self.remote(5, self.summed(), self.z_first, "pair")

    def middle_copy(self):
        return self.remote(6, self.summed(), self.z_second, "middle")

    def last_copy(self):
        return self.remote(7, self.z_last, self.z_last, "pair")

    def out_copies(self):
        rows = pl.ds(self.offset, self.rows)
        core = self.place.core
        target = self.result.at[core, rows, :]
        return (
            self.remote(8, self.z_last, target, "core"),
            pltpu.make_async_copy(self.z_last, target, self.local.at[1]),
        )

    def parts(self, ref):
        if self.gather:
            return [ref.at[a, b] for a in range(2) for b in range(2)]
        return [ref]

    def lay_out(self):
        part = self.columns // 3
        for owner in range(4):
            for kind in range(3):
                lanes = pl.ds(kind * part, part)
                former = self.middle[0].at[owner // 2, owner % 2, :, lanes]
                latter = self.z_second.at[owner // 2, owner % 2, :, lanes]
                add_to(self.z_last.at[:, pl.ds((4 * kind + owner) * part, part)], former, latter)

    def stage_start(self):
        self.core_copy().start()
        self.load().start()

    def stage_core(self):
        self.core_copy().wait_recv()
        self.load().wait()
        for a in range(2):
            for b in range(2):
                add_into(self.mine.at[a, b], self.core_in.at[a, b])
        for copy in self.wide_copies():
            copy.start()

    def stage_wide(self):
        p, (left, right) = self.place, self.halves()
        if self.gather:
            stay = pltpu.make_async_copy(
                self.mine.at[p.y, p.x], self.middle[0].at[p.y, p.x], self.local.at[2]
            )
            stay.start()
            for copy in self.wide_copies():
                copy.wait_recv()
            stay.wait()
            self.z_start()
            return
        for copy in self.wide_copies():
            copy.wait_recv()
        for a in range(2):
            add_into(self.mine.at[a, p.x, :, left], self.middle[0].at[a])
            add_into(self.mine.at[p.y, a, :, right], self.middle[1].at[a])
        for copy in self.narrow_copies():
            copy.start()

    def stage_narrow(self):
        p, (left, right) = self.place, self.halves()
        for copy in self.narrow_copies():
            copy.wait_recv()
        add_into(self.mine.at[p.y, p.x, :, left], self.middle[2])
        add_into(self.mine.at[p.y, p.x, :, right], self.middle[3])
        self.z_start()

    def z_start(self):
        @pl.when(self.place.outer)
        def _():
            self.pair_copy().start()

    def stage_pair(self):
        @pl.when(self.place.inner)
        def _():
            self.pair_copy().wait_recv()
            for total, addend in zip(self.parts(self.summed()), self.parts(self.z_first)):
                add_into(total, addend)
            self.middle_copy().start()

    def stage_middle(self):
        @pl.when(self.place.inner)
        def _():
            self.middle_copy().wait_recv()
            if self.gather:
                self.lay_out()
            else:
                add_to(self.z_last, self.summed(), self.z_second)
            self.last_copy().start()
            for copy in self.out_copies():
                copy.start()

    def stage_last(self):
        @pl.when(self.place.outer)
        def _():
            self.last_copy().wait_recv()
            for copy in self.out_copies():
                copy.start()

    def stage_end(self):
        remote_out, local_out = self.out_copies()
        remote_out.wait()
        local_out.wait()
        self.core_copy().wait_send()
        for copy in self.wide_copies():
            copy.wait_send()
        if not self.gather:
            for copy in self.narrow_copies():
                copy.wait_send()

        @pl.when(self.place.outer)
        def _():
            self.pair_copy().wait_send()

        @pl.when(self.place.inner)
        def _():
            self.middle_copy().wait_send()
            self.last_copy().wait_send()

    def plan(self):
        piece = 2 * self.rows * self.columns
        if self.gather:
            return [
                (self.stage_core, [("x", 1.5 * piece), ("y", 1.5 * piece)]),
                (self.stage_wide, [("z", 4 * piece)]),
                (self.stage_pair, [("z", 4 * piece)]),
                (self.stage_middle, [("z", 4 * piece)]),
                (self.stage_last, [("core", 4 * piece)]),
                (self.stage_end, []),
            ]
        return [
            (self.stage_core, [("x", piece), ("y", piece)]),
            (self.stage_wide, [("x", piece / 2), ("y", piece / 2)]),
            (self.stage_narrow, [("z1", piece)]),
            (self.stage_pair, [("z2", piece)]),
            (self.stage_middle, [("z3", piece)]),
            (self.stage_last, [("core", piece)]),
            (self.stage_end, []),
        ]

    def opening(self):
        return [("core", 8 * self.rows * self.columns)]


class RowChunk:
    def __init__(self, term, offset, rows, columns):
        self.term, self.offset, self.rows, self.columns = term, offset, rows, columns

    def scratch(self):
        rows, columns, half = self.rows, self.columns, self.columns // 2
        low = jnp.bfloat16
        return [
            pltpu.VMEM((2, rows, half), low),
            pltpu.VMEM((2, rows, half), low),
            pltpu.VMEM((rows, half), low),
            pltpu.VMEM((rows, half), low),
            pltpu.SemaphoreType.DMA((6,)),
            pltpu.SemaphoreType.DMA((6,)),
            pltpu.SemaphoreType.DMA((1,)),
        ]

    def bind(self, place, source, result, refs):
        self.place, self.result = place, result
        self.blocks = source
        self.middle = refs[:4]
        self.sent, self.received, self.local = refs[4:]

    def mine(self, y, x, lanes):
        return self.blocks.at[2 * y + x, pl.ds(self.offset, self.rows), lanes]

    remote = Chunk.remote
    halves = Chunk.halves

    def wide_copies(self):
        p, (left, right) = self.place, self.halves()
        copies = []
        for a in range(2):
            copies.append(
                self.remote(a, self.mine(a, 1 - p.x, left), self.middle[0].at[a], "x")
            )
            copies.append(
                self.remote(2 + a, self.mine(1 - p.y, a, right), self.middle[1].at[a], "y")
            )
        return copies

    def narrow_copies(self):
        p, (left, right) = self.place, self.halves()
        return [
            self.remote(4, self.mine(1 - p.y, p.x, left), self.middle[2], "y"),
            self.remote(5, self.mine(p.y, 1 - p.x, right), self.middle[3], "x"),
        ]

    def out_copy(self):
        p = self.place
        whole = pl.ds(0, self.columns)
        return pltpu.make_async_copy(
            self.mine(p.y, p.x, whole),
            self.result.at[pl.ds(self.offset, self.rows), :],
            self.local.at[0],
        )

    def stage_start(self):
        for copy in self.wide_copies():
            copy.start()

    def stage_wide(self):
        p, (left, right) = self.place, self.halves()
        for copy in self.wide_copies():
            copy.wait_recv()
        for a in range(2):
            add_into(self.mine(a, p.x, left), self.middle[0].at[a])
            add_into(self.mine(p.y, a, right), self.middle[1].at[a])
        for copy in self.narrow_copies():
            copy.start()

    def stage_narrow(self):
        p, (left, right) = self.place, self.halves()
        for copy in self.narrow_copies():
            copy.wait_recv()
        add_into(self.mine(p.y, p.x, left), self.middle[2])
        add_into(self.mine(p.y, p.x, right), self.middle[3])
        self.out_copy().start()

    def stage_end(self):
        self.out_copy().wait()
        for copy in self.wide_copies() + self.narrow_copies():
            copy.wait_send()

    def plan(self):
        piece = 2 * self.rows * self.columns
        return [
            (self.stage_wide, [("x", piece / 2), ("y", piece / 2)]),
            (self.stage_narrow, [("core", 0.0)]),
            (self.stage_end, []),
        ]

    def opening(self):
        piece = 2 * self.rows * self.columns
        return [("x", piece), ("y", piece)]


class Steps:
    def __init__(self, start):
        self.now, self.free, self.waiting, self.held = start, {}, [], []

    def send(self, transfers):
        ends = [self.now]
        for link, size in transfers:
            start = max(self.now, self.free.get(link, 0.0))
            self.free[link] = start + size / LINK_RATE.get(link, LINK_RATE["z"])
            ends.append(self.free[link] + 2.0)
        return max(ends)

    def open(self, chunks, depth=None):
        entries = [(self.send(chunk.opening()), n, chunk, 0) for n, chunk in enumerate(chunks)]
        self.waiting += entries[:depth]
        self.held += entries[depth:] if depth else []

    def due(self, everything=False):
        stages = []
        while self.waiting:
            self.waiting.sort(key=lambda entry: entry[:2])
            when, number, chunk, index = self.waiting[0]
            if when > self.now and not everything:
                break
            self.waiting.pop(0)
            self.now = max(self.now, when) + 0.4
            stage, transfers = chunk.plan()[index]
            stages.append(stage)
            if index == 1 and self.held:
                ready, *rest = self.held.pop(0)
                self.waiting.append((max(ready, self.now), *rest))
            if index + 1 < len(chunk.plan()):
                self.waiting.append((self.send(transfers), number, chunk, index + 1))
        return stages

    def spend(self, duration):
        self.now += duration


def back_kernel(
    chunks,
    first_chunks,
    heads,
    flag_ref,
    g_ref,
    q_hbm,
    k_hbm,
    v_hbm,
    memory_hbm,
    every_hbm,
    down_ref,
    gate_ref,
    up_ref,
    out_ref,
    w_hbm,
    mix_ref,
    log_ref,
    table_ref,
    sum_down,
    sum_gate,
    sum_up,
    sum_out,
    sum_qkv,
    sum_first,
    w_ref,
    q,
    k,
    v,
    upstream,
    shared,
    dk,
    dv,
    total,
    delta,
    part_qkv,
    trade_sent,
    trade_received,
    local,
    *refs,
):
    place = Place()
    seq = lax.axis_index("seq")
    tokens = g_ref.shape[0]
    width = heads * HEAD_DIM
    used = 0
    sources = [down_ref, gate_ref, up_ref, out_ref, part_qkv, shared]
    results = [sum_down, sum_gate, sum_up, sum_out, sum_qkv, sum_first]
    for chunk in chunks + first_chunks:
        count = len(chunk.scratch())
        chunk.bind(place, sources[chunk.term], results[chunk.term], refs[used : used + count])
        used += count

    def owner_at(turn):
        low, high = lax.rem(turn, 2), lax.div(turn, 2)
        x = place.x + low - 2 * place.x * low
        y = place.y + high - 2 * place.y * high
        return 2 * y + x

    def columns(owner):
        return pl.ds(pl.multiple_of(owner * width, HEAD_DIM), width)

    def span(block):
        return pl.ds(pl.multiple_of(block * tokens, tokens), tokens)

    def lanes(head):
        return pl.ds(pl.multiple_of(head * HEAD_DIM, HEAD_DIM), HEAD_DIM)

    across = {"x": seq + 1 - 2 * place.x, "y": seq + 2 - 4 * place.y, "xy": 3 - seq}
    trades = [
        pltpu.make_async_remote_copy(
            src_ref=g_ref.at[:, columns(across[peer])],
            dst_ref=upstream.at[span(seq), :],
            send_sem=trade_sent.at[slot],
            recv_sem=trade_received.at[slot],
            device_id=place.peer[peer],
            device_id_type=pl.DeviceIdType.MESH,
        )
        for slot, peer in enumerate(("x", "y", "xy"))
    ]
    loads = [
        pltpu.make_async_copy(g_ref.at[:, columns(seq)], upstream.at[span(seq), :], local.at[0]),
        pltpu.make_async_copy(q_hbm, q, local.at[1]),
        pltpu.make_async_copy(k_hbm, k, local.at[2]),
        pltpu.make_async_copy(v_hbm, v, local.at[3]),
        pltpu.make_async_copy(memory_hbm, shared, local.at[4]),
    ] + weight_copies(w_hbm, w_ref, seq, local, 6)
    load_every = pltpu.make_async_copy(every_hbm, shared, local.at[5])

    def turn_back(matrix, rows):
        cosine, sine = turn_factors(table_ref[rows, :])
        return turn_block(matrix, cosine, sine).astype(jnp.bfloat16)

    def memory_part(head, block):
        rows, mine = span(block), lanes(head)
        query, grads = q[rows, mine], upstream[rows, mine]
        row_delta = jnp.sum(
            grads.astype(jnp.float32) * mix_ref[rows, mine].astype(jnp.float32), axis=1, keepdims=True
        )
        delta[...] = jnp.broadcast_to(row_delta, delta.shape)
        closed = (1 - flag_ref[lax.axis_index("seg")]).astype(jnp.float32) * 1e30
        log_total = log_ref[rows, mine][:, :1] + closed
        result = jnp.zeros(total.shape, jnp.float32)
        for slot in range(shared.shape[0]):
            for run in range(2):

                def tile(kind):
                    start = pl.multiple_of((2 * run + kind) * width + head * HEAD_DIM, HEAD_DIM)
                    return shared[slot, :, pl.ds(start, HEAD_DIM)]

                keys, values = tile(0), tile(1)
                probs = jnp.exp2(product_nt(query, keys) - log_total)
                dscores = probs * (product_nt(grads, values) - row_delta)
                result = result + product(dscores.astype(jnp.bfloat16), keys)
        total[...] = result

    def own_part(head, block):
        rows, mine = span(block), lanes(head)
        query, grads = q[rows, mine], upstream[rows, mine]
        log_total, row_delta = log_ref[rows, mine][:, :1], delta[:, :1]

        def turn(other, result, diagonal):
            keys = k[span(other), mine]
            scores = product_nt(query, keys)
            if diagonal:
                scores = causal(scores)
            probs = jnp.exp2(scores - log_total)
            dscores = (probs * (product_nt(grads, v[span(other), mine]) - row_delta)).astype(
                jnp.bfloat16
            )
            dv[span(other), :] += product_tn(probs.astype(jnp.bfloat16), grads)
            dk[span(other), :] += product_tn(dscores, query)
            return result + product(dscores, keys)

        result = turn(block, total[...], True)
        result = lax.fori_loop(0, block, lambda other, r: turn(other, r, False), result)
        q[rows, mine] = turn_back(result * SCORE_SCALE, rows)

    def close_head(head):
        mine = lanes(head)

        def turn(block, carry):
            rows = span(block)
            k[rows, mine] = turn_back(dk[rows, :] * LN2, rows)
            v[rows, mine] = dv[rows, :].astype(jnp.bfloat16)
            return carry

        lax.fori_loop(0, 4, turn, 0)

    def multiply_qkv(index, carry):
        cut = pl.ds(pl.multiple_of(index * width, HEAD_DIM), width)
        for kind, part in enumerate((q, k, v)):
            term = None
            for block in range(shared.shape[0]):
                product_part = product_tn(shared[block, :, cut], part[block * tokens : (block + 1) * tokens, :])
                term = product_part if term is None else term + product_part
            term = term.astype(jnp.bfloat16)
            half = term.shape[0] // 2
            place_y, place_x = lax.div(index, 2), lax.rem(index, 2)
            for core in range(2):
                part_qkv[place_y, place_x, core, :, kind * width : (kind + 1) * width] = term[
                    core * half : (core + 1) * half, :
                ]
        return carry

    def multiply_first(block, carry):
        rows = span(block)
        result = None
        for kind, part in enumerate((q, k, v)):
            term = product_nt(part[rows, :], w_ref[:, kind * width : (kind + 1) * width])
            result = term if result is None else result + term
        shared[block] = result.astype(jnp.bfloat16)
        return carry

    place.greet(("core", "x", "y", "xy", "pair"))
    for copy in trades + loads:
        copy.start()
    for chunk in chunks:
        chunk.stage_start()
    steps = Steps(3.0)
    steps.free.update(x=11.0, y=11.0)
    steps.open(chunks, 2)
    for copy in loads:
        copy.wait()
    slots = []
    for unit in range(2 * 4 * heads):
        slots.append(steps.due())
        steps.spend(4.3 if unit % 2 == 0 else 3.2)

    def run(stages):
        for stage in stages:
            stage()

    def unit(index, carry):
        head, turn = lax.div(index, 4), lax.rem(index, 4)
        block = owner_at(turn)
        for number in range(4 * heads):
            if slots[2 * number] or number in (1, 2, 3):

                @pl.when(index == number)
                def _(number=number):
                    run(slots[2 * number])
                    if number in (1, 2, 3):
                        trades[number - 1].wait_recv()

        @pl.when(turn == 0)
        def _():
            dk[...] = jnp.zeros_like(dk)
            dv[...] = jnp.zeros_like(dv)

        memory_part(head, block)
        for number in range(4 * heads):
            if slots[2 * number + 1]:

                @pl.when(index == number)
                def _(number=number):
                    run(slots[2 * number + 1])

        own_part(head, block)

        @pl.when(turn == 3)
        def _():
            close_head(head)

        return carry

    lax.fori_loop(0, 4 * heads, unit, 0)
    load_every.start()
    run(steps.due())
    load_every.wait()
    lax.fori_loop(0, 4, multiply_qkv, 0)
    steps.spend(8.0)
    qkv_chunks = [chunk for chunk in first_chunks if chunk.term == 4]
    row_chunks = [chunk for chunk in first_chunks if chunk.term == 5]
    for chunk in qkv_chunks:
        chunk.stage_start()
    steps.open(qkv_chunks)
    run(steps.due())
    lax.fori_loop(0, 4, multiply_first, 0)
    steps.spend(6.0)
    for chunk in row_chunks:
        chunk.stage_start()
    steps.open(row_chunks)
    run(steps.due(True))
    for copy in trades:
        copy.wait_send()


def back(
    flags, grads, queries, keys, values, memory, every, terms, w_qkv, attended, log_totals, table, collective_id
):
    tokens, depth = grads.shape
    length, width = queries.shape
    low = jnp.bfloat16
    chunks, shapes = [], []
    for index, term in enumerate(terms):
        rows, columns = term.shape[0] // 8, term.shape[1]
        parts = (2, 4, 4, 2)[index]
        chunks += [Chunk(index, n * rows // parts, rows // parts, columns) for n in range(parts)]
        shapes.append((2, rows, columns))
    rows = depth // 8
    first_chunks = [Chunk(4, n * rows // 4, rows // 4, 3 * width, True) for n in range(4)]
    first_chunks += [RowChunk(5, n * tokens // 4, tokens // 4, depth) for n in range(4)]
    shapes += [(2, rows, 12 * width), (tokens, depth)]
    anywhere = pl.BlockSpec(memory_space=pl.ANY)
    inside = pl.BlockSpec(memory_space=pltpu.VMEM)
    scratch = (
        [pltpu.VMEM((depth, 3 * width), low)]
        + [pltpu.VMEM((length, width), low)] * 4
        + [pltpu.VMEM((4, tokens, depth), low)]
        + [pltpu.VMEM((length, HEAD_DIM), jnp.float32)] * 2
        + [pltpu.VMEM((tokens, HEAD_DIM), jnp.float32)] * 2
        + [pltpu.VMEM((2, 2, 2, rows, 3 * width), low)]
        + [pltpu.SemaphoreType.DMA((3,))] * 2
        + [pltpu.SemaphoreType.DMA((9,))]
    )
    return pl.pallas_call(
        functools.partial(back_kernel, chunks, first_chunks, width // HEAD_DIM),
        in_specs=[pl.BlockSpec(memory_space=pltpu.SMEM)] + [anywhere] * 11 + [inside] * 3,
        out_specs=[anywhere] * len(shapes),
        out_shape=[jax.ShapeDtypeStruct(shape, low) for shape in shapes],
        scratch_shapes=scratch + [ref for chunk in chunks + first_chunks for ref in chunk.scratch()],
        compiler_params=pltpu.CompilerParams(
            collective_id=collective_id, has_side_effects=True, vmem_limit_bytes=VMEM_MOST
        ),
        name="back",
    )(
        flags,
        grads,
        queries,
        keys,
        values,
        memory,
        every,
        *[term.reshape((2, 2, 2, term.shape[0] // 8, term.shape[1])) for term in terms],
        w_qkv,
        attended,
        log_totals,
        table,
    )


class Line:
    def __init__(self, place, seg, memory, spans, refs):
        self.place, self.seg, self.memory, self.spans = place, seg, memory, spans
        self.runs = len(spans)
        self.sent, self.received, self.core_sent, self.core_received = refs

    def span(self, run):
        return self.spans[run]

    def there(self, way, step):
        return self.place.z >= step if way == 0 else self.place.z + step <= 3

    def goes(self, way, step):
        has = self.there(way, step - 1)
        return jnp.logical_and(has, self.place.z <= 2 if way == 0 else self.place.z >= 1)

    def index(self, way, step):
        return self.seg - 2 * step if way == 0 else self.seg + 2 * step

    def hop(self, way, step, run):
        name = self.index(way, step - 1)
        target = self.memory.at[name, self.span(run), :]
        slot = (way * 3 + step - 1) * self.runs + run
        seg, seq = lax.axis_index("seg"), lax.axis_index("seq")
        return pltpu.make_async_remote_copy(
            src_ref=target,
            dst_ref=target,
            send_sem=self.sent.at[slot],
            recv_sem=self.received.at[slot],
            device_id=(seg + 2 - 4 * way, seq),
            device_id_type=pl.DeviceIdType.MESH,
        )

    def arrival(self, way, step, run):
        target = self.memory.at[self.index(way, step), self.span(run), :]
        slot = (way * 3 + step - 1) * self.runs + run
        return pltpu.make_async_remote_copy(
            src_ref=target,
            dst_ref=target,
            send_sem=self.sent.at[slot],
            recv_sem=self.received.at[slot],
            device_id=self.place.peer["core"],
            device_id_type=pl.DeviceIdType.MESH,
        )

    def share(self, way, step, run):
        name = self.index(way, step)
        target = self.memory.at[name, self.span(run), :]
        slot = (way * 3 + step) * self.runs + run
        return pltpu.make_async_remote_copy(
            src_ref=target,
            dst_ref=target,
            send_sem=self.core_sent.at[slot],
            recv_sem=self.core_received.at[slot],
            device_id=self.place.peer["core"],
            device_id_type=pl.DeviceIdType.MESH,
        )

    def start(self, run):
        for way in range(2):

            @pl.when(self.goes(way, 1))
            def _(way=way):
                self.hop(way, 1, run).start()

        self.share(0, 0, run).start()

    def advance(self, step, run):
        for way in range(2):

            @pl.when(self.there(way, step))
            def _(way=way):
                self.arrival(way, step, run).wait_recv()

            if step < 3:

                @pl.when(self.goes(way, step + 1))
                def _(way=way):
                    self.hop(way, step + 1, run).start()

            @pl.when(self.there(way, step))
            def _(way=way):
                self.share(way, step, run).start()

    def finish(self):
        for run in range(self.runs):
            self.share(0, 0, run).wait()
            for way in range(2):
                for step in range(1, 4):

                    @pl.when(self.there(way, step))
                    def _(way=way, step=step, run=run):
                        self.share(way, step, run).wait()

                    @pl.when(self.goes(way, step))
                    def _(way=way, step=step, run=run):
                        self.hop(way, step, run).wait_send()


def front_kernel(
    heads,
    flag_ref,
    source_ref,
    x_ref,
    mem_k_ref,
    mem_v_ref,
    w_hbm,
    table_ref,
    every_ref,
    chosen_ref,
    attended_ref,
    q_ref,
    k_ref,
    v_ref,
    low_ref,
    log_ref,
    w_ref,
    rows,
    memory,
    listed,
    mix_ref,
    max_ref,
    sum_ref,
    trade_sent,
    trade_received,
    rows_sent,
    rows_received,
    line_sent,
    line_received,
    core_sent,
    core_received,
    back_sent,
    back_received,
    local,
):
    place = Place()
    seg, seq = lax.axis_index("seg"), lax.axis_index("seq")
    width = heads * HEAD_DIM
    count = mem_k_ref.shape[0]
    tokens, depth = x_ref.shape
    across = {"x": seq + 1 - 2 * place.x, "y": seq + 2 - 4 * place.y, "xy": 3 - seq}

    def remote(source, target, sent, received, slot, peer):
        return pltpu.make_async_remote_copy(
            src_ref=source,
            dst_ref=target,
            send_sem=sent.at[slot],
            recv_sem=received.at[slot],
            device_id=place.peer[peer],
            device_id_type=pl.DeviceIdType.MESH,
        )

    def columns(owner, start=0):
        return pl.ds(pl.multiple_of(start + owner * width, HEAD_DIM), width)

    def seat(owner):
        return pl.ds(pl.multiple_of(owner * count, 16), count)

    def owner_at(turn):
        low, high = lax.rem(turn, 2), lax.div(turn, 2)
        x = place.x + low - 2 * place.x * low
        y = place.y + high - 2 * place.y * high
        return 2 * y + x

    def block_rows(block):
        return pl.ds(pl.multiple_of(block * tokens, 16), tokens)

    peers = ("x", "y", "xy")
    trades = []
    for number, peer in enumerate(peers):
        for kind, source in enumerate((mem_k_ref, mem_v_ref)):
            lanes = pl.ds(kind * width, width)
            trades.append(
                remote(
                    source.at[:, columns(across[peer])],
                    memory.at[seg, seat(seq), lanes],
                    trade_sent,
                    trade_received,
                    2 * number + kind,
                    peer,
                )
            )
    keeps = [
        pltpu.make_async_copy(
            source.at[:, columns(seq)],
            memory.at[seg, seat(seq), pl.ds(kind * width, width)],
            local.at[kind],
        )
        for kind, source in enumerate((mem_k_ref, mem_v_ref))
    ]
    half = depth // 2
    left, right = pl.ds(0, half), pl.ds(half, half)
    load = pltpu.make_async_copy(x_ref, rows.at[seq], local.at[2])
    loads = weight_copies(w_hbm, w_ref, seq, local, 3)
    direct = [
        remote(x_ref.at[:, left], rows.at[seq, :, left], rows_sent, rows_received, 0, "x"),
        remote(x_ref.at[:, right], rows.at[seq, :, right], rows_sent, rows_received, 1, "y"),
        remote(x_ref.at[:, right], rows.at[seq, :, right], rows_sent, rows_received, 2, "x"),
        remote(x_ref.at[:, left], rows.at[seq, :, left], rows_sent, rows_received, 3, "y"),
    ]
    onward = [
        remote(
            rows.at[across["x"], :, left], rows.at[across["x"], :, left], rows_sent, rows_received, 4, "y"
        ),
        remote(
            rows.at[across["y"], :, right], rows.at[across["y"], :, right], rows_sent, rows_received, 5, "x"
        ),
    ]
    line = Line(
        place,
        seg,
        memory,
        [seat(owner) for owner in (seq, across["x"], across["y"], across["xy"])],
        (line_sent, line_received, core_sent, core_received),
    )
    keep_rows = pltpu.make_async_copy(rows, every_ref, local.at[6])
    run_rows = memory.shape[1] // 2
    keep_chosen = []
    for run in range(2):
        span, lanes = pl.ds(run * run_rows, run_rows), pl.ds(2 * run * width, 2 * width)
        keep_chosen.append(
            pltpu.make_async_copy(memory.at[seg, span, :], chosen_ref.at[0, :, lanes], local.at[7 + run])
        )
        keep_chosen.append(
            pltpu.make_async_copy(
                listed.at[:, span, :],
                chosen_ref.at[pl.ds(1, listed.shape[0]), :, lanes],
                local.at[9 + run],
            )
        )
    returns = [
        remote(
            low_ref.at[block_rows(across[peer]), :],
            attended_ref.at[:, columns(seq)],
            back_sent,
            back_received,
            slot,
            peer,
        )
        for slot, peer in enumerate(peers)
    ]
    keep_attended = pltpu.make_async_copy(
        low_ref.at[block_rows(seq), :], attended_ref.at[:, columns(seq)], local.at[11]
    )

    def project_rows(owner):
        block = rows[owner]
        span = block_rows(owner)
        cosine, sine = turn_factors(table_ref[span, :])
        scale = SCORE_SCALE / LN2
        queries = product(block, w_ref[:, :width])
        keys = product(block, w_ref[:, width : 2 * width])
        for head in range(heads):
            lanes = slice(head * HEAD_DIM, (head + 1) * HEAD_DIM)
            q_ref[span, lanes] = turn_block(
                queries[:, lanes], cosine * scale, sine * (-scale)
            ).astype(jnp.bfloat16)
            k_ref[span, lanes] = turn_block(keys[:, lanes], cosine, -sine).astype(jnp.bfloat16)
        v_ref[span, :] = product(block, w_ref[:, 2 * width :]).astype(jnp.bfloat16)

    def head_lanes(head, start=0):
        return pl.ds(pl.multiple_of(start + head * HEAD_DIM, HEAD_DIM), HEAD_DIM)

    def keep(span, lanes, row_max, row_sum, mixed):
        mix_ref[span, lanes] = mixed
        max_ref[span, lanes] = jnp.broadcast_to(row_max, mixed.shape)
        sum_ref[span, lanes] = jnp.broadcast_to(row_sum, mixed.shape)

    def own_rows(block):
        def turn(head, carry):
            lanes = head_lanes(head)
            span = pl.ds(block * tokens, tokens)
            pairs = [
                (k_ref[pl.ds(n * tokens, tokens), lanes], v_ref[pl.ds(n * tokens, tokens), lanes])
                for n in range(block + 1)
            ]
            keep(span, lanes, *attend(q_ref[span, lanes], pairs, True, None))
            return carry

        lax.fori_loop(0, heads, turn, 0)

    closed = (1 - flag_ref[seg]).astype(jnp.float32) * 1e30

    def carried(span, lanes):
        return max_ref[span, lanes][:, :1], sum_ref[span, lanes][:, :1], mix_ref[span, lanes]

    def own_memory(first, last):
        def turn(index, carry):
            head = lax.rem(index, heads)
            lanes, span = head_lanes(head), block_rows(lax.div(index, heads))
            pair = (memory[seg, :, lanes], memory[seg, :, head_lanes(head, width)])
            keep(span, lanes, *attend(q_ref[span, lanes], [pair], False, carried(span, lanes), closed))
            return carry

        lax.fori_loop(first * heads, last * heads, turn, 0)

    barrier = pltpu.get_barrier_semaphore()

    def hail(device):
        pl.semaphore_signal(barrier, inc=1, device_id=device, device_id_type=pl.DeviceIdType.MESH)

    for copy in keeps + [load] + loads:
        copy.start()
    for peer in ("x", "y", "xy", "core"):
        hail(place.peer[peer])
    below, above = place.z >= 1, place.z <= 2

    @pl.when(below)
    def _():
        hail((seg - 2, seq))

    @pl.when(above)
    def _():
        hail((seg + 2, seq))

    pl.semaphore_wait(barrier, 4 + below.astype(jnp.int32) + above.astype(jnp.int32))

    for copy in trades + direct:
        copy.start()
    for copy in keeps:
        copy.wait()
    line.start(0)
    load.wait()
    for copy in loads:
        copy.wait()
    project_rows(seq)
    for number in range(3):
        for kind in range(2):
            trades[2 * number + kind].wait_recv()
        line.start(number + 1)
        line.advance(1, number)
    direct[0].wait_recv()
    direct[1].wait_recv()
    for copy in onward:
        copy.start()
    line.advance(1, 3)
    line.advance(2, 0)
    direct[2].wait_recv()
    direct[3].wait_recv()
    project_rows(across["x"])
    line.advance(2, 1)
    project_rows(across["y"])
    line.advance(2, 2)
    for copy in onward:
        copy.wait_recv()
    project_rows(3 - seq)
    keep_rows.start()
    line.advance(2, 3)
    own_rows(0)
    own_rows(1)
    line.advance(3, 0)
    own_rows(2)
    line.advance(3, 1)
    own_rows(3)
    line.advance(3, 2)
    own_memory(0, 2)
    line.advance(3, 3)
    own_memory(2, 4)
    line.finish()
    for n in range(listed.shape[0]):
        listed[n] = memory[source_ref[seg, n]]

    def unit(index, carry):
        turn, head = lax.div(index, heads), lax.rem(index, heads)

        @pl.when(index == heads // 2)
        def _():
            for copy in keep_chosen:
                copy.start()

        for number in range(3):

            @pl.when(index == heads * (3 - number))
            def _(number=number):
                returns[number].start()

        lanes, span = head_lanes(head), block_rows(owner_at(3 - turn))
        pairs = [
            (listed[n, :, lanes], listed[n, :, head_lanes(head, width)])
            for n in range(listed.shape[0])
        ]
        row_max, row_sum, mixed = attend(
            q_ref[span, lanes], pairs, False, carried(span, lanes), closed
        )
        low_ref[span, lanes] = (mixed * (1.0 / row_sum)).astype(jnp.bfloat16)
        log_ref[span, lanes] = jnp.broadcast_to(row_max + jnp.log2(row_sum), mixed.shape)
        return carry

    lax.fori_loop(0, 4 * heads, unit, 0)
    keep_attended.start()
    for copy in returns:
        copy.wait()
    for copy in keep_chosen + [keep_rows, keep_attended]:
        copy.wait()
    for copy in trades + direct + onward:
        copy.wait_send()


def front(
    flags, sources, first_low, mem_keys, mem_values, w_qkv, table, seg_size, seq_size, collective_id
):
    tokens, depth = first_low.shape
    length = tokens * seq_size
    width = depth // seq_size
    count = mem_keys.shape[0] * seq_size
    slots = sources.shape[1]
    anywhere = pl.BlockSpec(memory_space=pl.ANY)
    inside = pl.BlockSpec(memory_space=pltpu.VMEM)
    scalars = pl.BlockSpec(memory_space=pltpu.SMEM)
    low = jnp.bfloat16
    shape = jax.ShapeDtypeStruct
    dma = pltpu.SemaphoreType.DMA
    return pl.pallas_call(
        functools.partial(front_kernel, width // HEAD_DIM),
        in_specs=[scalars] * 2 + [anywhere] * 4 + [inside],
        out_specs=[anywhere] * 3 + [inside] * 5,
        out_shape=[
            shape((seq_size, tokens, depth), low),
            shape((slots + 1, count // 2, 4 * width), low),
            shape((tokens, depth), low),
        ]
        + [shape((length, width), low)] * 4
        + [shape((length, width), jnp.float32)],
        scratch_shapes=[
            pltpu.VMEM((depth, 3 * width), low),
            pltpu.VMEM((seq_size, tokens, depth), low),
            pltpu.VMEM((seg_size, count, 2 * width), low),
            pltpu.VMEM((slots, count, 2 * width), low),
        ]
        + [pltpu.VMEM((length, width), jnp.float32)] * 3
        + [dma((6,))] * 4
        + [dma((24,))] * 2
        + [dma((28,))] * 2
        + [dma((3,))] * 2
        + [dma((12,))],
        compiler_params=pltpu.CompilerParams(
            collective_id=collective_id, has_side_effects=True, vmem_limit_bytes=VMEM_BYTES
        ),
        name="front",
    )(flags, sources, first_low, mem_keys, mem_values, w_qkv, table)


def norm_input_grad(values, inverse, norm_gain, upstream):
    weighted = upstream * norm_gain
    inner_mean = jnp.mean(weighted * values, axis=-1, keepdims=True)
    return inverse * weighted - inverse * inverse * inverse * values * inner_mean


def dense_kernel(
    x_ref,
    g_ref,
    attended_ref,
    out_ref,
    gain_ref,
    gate_ref,
    up_ref,
    down_ref,
    output_ref,
    grad_ref,
    grad_attended_ref,
    term_down,
    term_gate,
    term_up,
    term_out,
    residual_ref,
    second,
    second_t,
    total,
    grad_second,
):
    index = pl.program_id(0)
    low = jnp.bfloat16

    @pl.when(index == 0)
    def _():
        residual = x_ref[...].astype(jnp.float32) + product(attended_ref[...], out_ref[...])
        residual_ref[...] = residual
        second_low = norm_forward(residual, gain_ref[...])[0].astype(low)
        second[...] = second_low
        second_t[...] = second_low.T

    gate, up = product(second[...], gate_ref[...]), product(second[...], up_ref[...])
    grad_hidden = product_nt(g_ref[...], down_ref[...])
    sigmoid_gate = jax.nn.sigmoid(gate)
    activated = gate * sigmoid_gate
    hidden = (activated * up).astype(low)
    grad_gate = (grad_hidden * up * sigmoid_gate * (1.0 + gate * (1.0 - sigmoid_gate))).astype(low)
    grad_up = (grad_hidden * activated).astype(low)
    term_down[...] = product_tn(hidden, g_ref[...]).astype(low)
    term_gate[...] = product(second_t[...], grad_gate).astype(low)
    term_up[...] = product(second_t[...], grad_up).astype(low)
    part = product(hidden, down_ref[...])
    grad_part = product_nt(grad_gate, gate_ref[...]) + product_nt(grad_up, up_ref[...])

    @pl.when(index == 0)
    def _():
        total[...] = part
        grad_second[...] = grad_part

    @pl.when(index > 0)
    def _():
        total[...] += part
        grad_second[...] += grad_part

    @pl.when(index == pl.num_programs(0) - 1)
    def _():
        residual = residual_ref[...]
        output_ref[...] = (residual + total[...]).astype(low)
        inverse = lax.rsqrt(jnp.mean(residual * residual, axis=-1, keepdims=True) + epsilon)
        grad = norm_input_grad(residual, inverse, gain_ref[...], grad_second[...])
        grad = grad + g_ref[...].astype(jnp.float32)
        grad_ref[...] = grad
        grad_low = grad.astype(low)
        term_out[...] = product_tn(attended_ref[...], grad_low).astype(low)
        grad_attended_ref[...] = product_nt(grad_low, out_ref[...]).astype(low)


def dense(x, grads, attended, w_out, gain, w_gate, w_up, w_down, tile=256):
    tokens, depth = x.shape
    hidden = w_gate.shape[1]
    tile = math.gcd(tile, hidden)
    low = jnp.bfloat16
    shape = jax.ShapeDtypeStruct

    def whole(rows, columns):
        return pl.BlockSpec((rows, columns), lambda j: (0, 0))

    across = pl.BlockSpec((depth, tile), lambda j: (0, j))
    down = pl.BlockSpec((tile, depth), lambda j: (j, 0))
    activation = whole(tokens, depth)
    return pl.pallas_call(
        dense_kernel,
        grid=(hidden // tile,),
        in_specs=[activation] * 3 + [whole(depth, depth), whole(1, depth), across, across, down],
        out_specs=[activation] * 3 + [down, across, across, whole(depth, depth)],
        out_shape=[
            shape((tokens, depth), low),
            shape((tokens, depth), jnp.float32),
            shape((tokens, depth), low),
            shape((hidden, depth), low),
            shape((depth, hidden), low),
            shape((depth, hidden), low),
            shape((depth, depth), low),
        ],
        scratch_shapes=[
            pltpu.VMEM((tokens, depth), jnp.float32),
            pltpu.VMEM((tokens, depth), low),
            pltpu.VMEM((depth, tokens), low),
            pltpu.VMEM((tokens, depth), jnp.float32),
            pltpu.VMEM((tokens, depth), jnp.float32),
        ],
        compiler_params=pltpu.CompilerParams(vmem_limit_bytes=VMEM_BYTES),
        cost_estimate=pl.CostEstimate(
            flops=16 * tokens * depth * hidden + 6 * tokens * depth * depth,
            transcendentals=tokens * hidden,
            bytes_accessed=12 * depth * hidden + 20 * tokens * depth,
        ),
        name="dense",
    )(x, grads, attended, w_out, gain, w_gate, w_up, w_down)


def tail_kernel(
    down_hbm,
    gate_hbm,
    up_hbm,
    out_hbm,
    qkv_hbm,
    first_hbm,
    x_hbm,
    grad_hbm,
    w_hbm,
    w_gate_hbm,
    w_up_hbm,
    gain1_ref,
    gain2_ref,
    input_out,
    norm1_ref,
    norm2_ref,
    qkv_out,
    out_out,
    gate_out,
    up_out,
    down_out,
    down,
    gate,
    up,
    out,
    qkv,
    first,
    x,
    grad,
    w,
    w_gate,
    w_up,
    input_wide,
    qkv_wide,
    out_wide,
    gate_wide,
    up_wide,
    down_wide,
    dots1,
    dots2,
    loaded,
    stored,
):
    seq = lax.axis_index("seq")
    count = gate.shape[0]
    block = pl.ds(pl.multiple_of(seq * count, count), count)
    pairs = [
        (gate_hbm, gate),
        (w_gate_hbm.at[block, :], w_gate),
        (up_hbm, up),
        (w_up_hbm.at[block, :], w_up),
        (down_hbm, down),
        (out_hbm, out),
        (w_hbm.at[block, :], w),
        (qkv_hbm, qkv),
        (first_hbm, first),
        (x_hbm, x),
        (grad_hbm, grad),
    ]
    loads = [
        pltpu.make_async_copy(source, target, loaded.at[n]) for n, (source, target) in enumerate(pairs)
    ]
    wides = [gate_wide, up_wide, down_wide, out_wide, qkv_wide, input_wide]
    outs = [gate_out, up_out, down_out, out_out, qkv_out, input_out]
    stores = [
        pltpu.make_async_copy(source, target, stored.at[n])
        for n, (source, target) in enumerate(zip(wides, outs))
    ]
    for copy in loads:
        copy.start()

    def by_rows(count, step, body):
        def turn(index, carry):
            body(pl.ds(pl.multiple_of(index * step, step), step))
            return carry

        lax.fori_loop(0, count // step, turn, 0)

    def widen(former, latter):
        def body(rows):
            latter[rows, :] = former[rows, :].astype(jnp.float32)

        by_rows(former.shape[0], 16, body)

    def dot_rows(values, weights):
        return lane_fold(jnp.add, values * weights.astype(jnp.float32), None)

    def gate_body(rows):
        values = gate[rows, :].astype(jnp.float32)
        gate_wide[rows, :] = values
        dots2[rows, :] = dot_rows(values, w_gate[rows, :])

    def up_body(rows):
        values = up[rows, :].astype(jnp.float32)
        up_wide[rows, :] = values
        dots2[rows, :] += dot_rows(values, w_up[rows, :])

    def qkv_body(rows):
        values = qkv[rows, :].astype(jnp.float32)
        qkv_wide[rows, :] = values
        dots1[rows, :] = dot_rows(values, w[rows, :])

    def gain_grads(dots, gain_ref):
        columns = jnp.broadcast_to(jnp.sum(dots[...], axis=1, keepdims=True), dots.shape)
        return columns.T[:1, :] / gain_ref[:, block]

    def wait(*numbers):
        for number in numbers:
            loads[number].wait()

    wait(0, 1)
    by_rows(count, 16, gate_body)
    stores[0].start()
    wait(2, 3)
    by_rows(count, 16, up_body)
    stores[1].start()
    norm2_ref[...] = gain_grads(dots2, gain2_ref)
    wait(4)
    widen(down, down_wide)
    stores[2].start()
    wait(5)
    widen(out, out_wide)
    stores[3].start()
    wait(6, 7)
    by_rows(count, 16, qkv_body)
    stores[4].start()
    norm1_ref[...] = gain_grads(dots1, gain1_ref)
    wait(8, 9, 10)

    def input_body(rows):
        values = x[rows, :].astype(jnp.float32)
        inverse = lax.rsqrt(jnp.mean(values * values, axis=-1, keepdims=True) + epsilon)
        input_wide[rows, :] = grad[rows, :] + norm_input_grad(
            values, inverse, gain1_ref[...], first[rows, :].astype(jnp.float32)
        )

    by_rows(x.shape[0], 32, input_body)
    stores[5].start()
    for copy in stores:
        copy.wait()


def tail(sums, first, x, grad, w_qkv, w_gate, w_up, gain1, gain2):
    down, gate, up, out, qkv = sums
    tokens, depth = x.shape
    count = gate.shape[0]
    low, wide = jnp.bfloat16, jnp.float32
    anywhere = pl.BlockSpec(memory_space=pl.ANY)
    inside = pl.BlockSpec(memory_space=pltpu.VMEM)
    shapes = [(tokens, depth), qkv.shape, out.shape, gate.shape, up.shape, down.shape]
    results = [shapes[0], (1, count), (1, count)] + shapes[1:]
    return pl.pallas_call(
        tail_kernel,
        in_specs=[anywhere] * 11 + [inside] * 2,
        out_specs=[anywhere] + [inside] * 2 + [anywhere] * 5,
        out_shape=[jax.ShapeDtypeStruct(shape, wide) for shape in results],
        scratch_shapes=[pltpu.VMEM(total.shape, low) for total in sums]
        + [
            pltpu.VMEM(first.shape, low),
            pltpu.VMEM(x.shape, low),
            pltpu.VMEM(x.shape, wide),
            pltpu.VMEM(qkv.shape, low),
            pltpu.VMEM(gate.shape, low),
            pltpu.VMEM(up.shape, low),
        ]
        + [pltpu.VMEM(shape, wide) for shape in shapes]
        + [pltpu.VMEM((count, HEAD_DIM), wide)] * 2
        + [pltpu.SemaphoreType.DMA((11,)), pltpu.SemaphoreType.DMA((6,))],
        compiler_params=pltpu.CompilerParams(vmem_limit_bytes=VMEM_BYTES),
        name="tail",
    )(*sums, first, x, grad, w_qkv, w_gate, w_up, gain1, gain2)


def head_plan(
    seg_size,
    seq_size,
    layer_input,
    output_grad,
    norm1_gain,
    norm2_gain,
    w_qkv,
    w_out,
    w_gate,
    w_up,
    w_down,
    mem_keys,
    mem_values,
    memory_flags,
    sources,
):
    tokens = layer_input.shape[1]
    length = tokens * seq_size
    width = D // seq_size
    inputs = layer_input[0].astype(jnp.float32)
    first_low = norm_forward(inputs, norm1_gain)[0].astype(jnp.bfloat16)
    table = turn_table(length)
    every_low, chosen_memory, attended_low, queries, keys, values, heads_low, log_totals = front(
        memory_flags, sources, first_low, mem_keys[0], mem_values[0], w_qkv, table, seg_size, seq_size, 1
    )

    output, grad_residual, grad_attended, term_down, term_gate, term_up, term_out = dense(
        layer_input[0], output_grad[0], attended_low, w_out, norm2_gain[None], w_gate, w_up, w_down
    )
    *sums, qkv_rows, first_rows = back(
        memory_flags,
        grad_attended,
        queries,
        keys,
        values,
        chosen_memory,
        every_low,
        [term_down, term_gate, term_up, term_out],
        w_qkv,
        heads_low,
        log_totals,
        table,
        2,
    )
    sums = [total.reshape(2 * total.shape[1], total.shape[2]) for total in sums]
    sums.append(qkv_rows.reshape(width, 3 * D))
    input_grad, grad_norm1, grad_norm2, grad_qkv, grad_out, grad_gate, grad_up, grad_down = tail(
        sums, first_rows, layer_input[0], grad_residual, w_qkv, w_gate, w_up, norm1_gain[None], norm2_gain[None]
    )
    return (
        output[None],
        input_grad[None],
        grad_norm1[0],
        grad_norm2[0],
        grad_qkv,
        grad_out,
        grad_gate,
        grad_up,
        grad_down,
    )


def solution(mesh):
    seq_size = mesh.shape["seq"]
    heads_fit = seq_size == 4 and mesh.shape["seg"] == 8
    plan = functools.partial(head_plan, mesh.shape["seg"], seq_size) if heads_fit else general_plan
    placed = (
        P("seg", "seq", None),
        P("seg", "seq", None),
        P(),
        P(),
        P(),
        P(),
        P(),
        P(),
        P(),
        P("seg", "seq", None),
        P("seg", "seq", None),
        P(),
        P(),
    )
    return jax.shard_map(
        plan,
        mesh=mesh,
        in_specs=placed,
        out_specs=(
            P("seg", "seq", None),
            P("seg", "seq", None),
            P("seq"),
            P("seq"),
            P("seq", None),
            P("seq", None),
            P("seq", None),
            P("seq", None),
            P("seq", None),
        ),
        check_vma=False,
    )
```
